32 devices in a mesh: dom: 32 (over z, y, x, core).
Axes of the slice: x: 2, y: 2, z: 4, core: 2. Of those that a mesh axis runs over, the one named last changes fastest.
Arguments:
- rhs: float32 [8, 212992], P(None, 'dom'), may hold values from -25 to 25, as said below
- potential: float32 [212992], P('dom'), may hold values from 0.5 to 2
- precond: float32 [212992], P('dom'), may hold values from 0.05 to 0.5
- shift: float32 [8], replicated, may hold values from 0.3 to 3
- stiffness: float32 [343, 343], replicated, may hold values from -0.4 to 2, as said below
- cell_scale: float32 [1024], P('dom'), may hold values from 0.5 to 2
- conn: int32 [1024, 343], P('dom'), may hold values from 0 to 7487, as said below
- cell_count: int32 [32], replicated, may hold values from 1 to 32, as said below
- projector: float32 [256, 8, 343], P('dom'), may hold values from -0.6 to 0.6
- support_cell: int32 [256], P('dom'), may hold values from 0 to 31, as said below
- support_atom: int32 [256], P('dom'), may hold values from 0 to 63, as said below
- support_count: int32 [32], replicated, may hold values from 4 to 8, as said below
- atom_matrix: float32 [64, 8, 8], P('dom'), may hold values from -2 to 15, as said below
Outputs:
- solution: float32 [8, 212992], P(None, 'dom')
- residual: float32 [8, 212992], P(None, 'dom')
The draws below stay inside these ranges and needn't reach their ends.
Inputs may be any that keep to these rules, and one draw needn't show every extreme that they name: `rhs`: row v rises in scale along the nodes. `stiffness`: symmetric positive definite. `atom_matrix`: each atom's matrix is symmetric positive definite. Block b's live cells are its slots 0 to cell_count[b] - 1; blocks 2k and 2k + 1 together hold at most 40 live cells, and some block holds 32. `conn`: a local index i of block b is column b * 6656 + i of the field padded by 416 zero columns at each end: indices below 416 are the previous block's last nodes, indices from 7072 on the next block's first nodes. `support_cell`: every entry names a live cell of its block. `support_atom`: atom a is owned by block a // 2; an entry of block b names an atom owned by block b - 1, b or b + 1. Block b's live entries are its first support_count[b]; some block has 8.
All inputs are finite; a program needn't handle non-finite values.
Results may differ from the reference program's by a relative error of at most 0.0003.
Values sent between devices are 32-bit elements; how exact they have to be, the bound alone decides.
No kernel may reach another device: no remote copies, remote signals or barrier semaphores. Data moves between devices by JAX's collectives and lax.ppermute only.
A program may use at most 64 MiB of HBM per device.

```python
import math
import jax
import jax.numpy as jnp
from jax import lax

ELEM = 343
NPROJ = 8
VEC = 8
ITERS = 2
CELL_DEV = 32
NODE_DEV = 6656
GHOST = 416
HALF = 20
PSUP_DEV = 8
ATOM_DEV = 2
NODES = 212992
CELLS = 1024
PSUPS = 256
ATOMS = 64
N_DOM = 32


def pair_counts(key):
    pairs = N_DOM // 2
    keys = jax.random.split(key, 4)
    totals = jax.random.randint(keys[0], (pairs,), HALF, 2 * HALF + 1)
    upper = jnp.minimum(totals - 1, CELL_DEV)
    lower = (totals + 1) // 2
    heavy = jax.random.randint(keys[1], (pairs,), lower, upper + 1)
    chosen = jax.random.randint(keys[2], (), 0, pairs)
    marked = jnp.arange(pairs) == chosen
    totals = jnp.where(marked, 2 * HALF, totals)
    heavy = jnp.where(marked, CELL_DEV, heavy)
    light = totals - heavy
    first = jax.random.randint(keys[3], (pairs,), 0, 2)
    even = jnp.where(first == 1, heavy, light)
    odd = jnp.where(first == 1, light, heavy)
    return jnp.stack([even, odd], axis=1).reshape(N_DOM).astype(jnp.int32)


def draw_cell_count(key, part):
    return pair_counts(jax.random.fold_in(key, 7))


def draw_support_cell(key, part):
    counts = pair_counts(jax.random.fold_in(key, 7))
    owner = jnp.arange(PSUPS) // PSUP_DEV
    return jax.random.randint(jax.random.fold_in(key, 13), (PSUPS,), 0, counts[owner]).astype(jnp.int32)


def draw_support_atom(key, part):
    keys = jax.random.split(jax.random.fold_in(key, 17), 2)
    block = jnp.arange(PSUPS) // PSUP_DEV
    offset = jax.random.randint(keys[0], (PSUPS,), -1, 2)
    owner = jnp.clip(block + offset, 0, N_DOM - 1)
    local = jax.random.randint(keys[1], (PSUPS,), 0, ATOM_DEV)
    return (owner * ATOM_DEV + local).astype(jnp.int32)


def draw_support_count(key, part):
    keys = jax.random.split(jax.random.fold_in(key, 19), 2)
    counts = jax.random.randint(keys[0], (N_DOM,), PSUP_DEV // 2, PSUP_DEV + 1)
    chosen = jax.random.randint(keys[1], (), 0, N_DOM)
    return jnp.where(jnp.arange(N_DOM) == chosen, PSUP_DEV, counts).astype(jnp.int32)


def draw_conn(key, part):
    keys = jax.random.split(jax.random.fold_in(key, 23), 4)
    reach = NODE_DEV // 4
    base = jax.random.randint(keys[0], (CELLS, 1), 0, NODE_DEV + 2 * GHOST - reach + 1)
    spread = jax.random.randint(keys[1], (CELLS, ELEM), 0, reach)
    nodes = base + spread
    low_rim = jax.random.randint(keys[2], (CELLS,), 0, GHOST)
    high_rim = jax.random.randint(keys[3], (CELLS,), GHOST + NODE_DEV, NODE_DEV + 2 * GHOST)
    nodes = nodes.at[:, 0].set(low_rim)
    nodes = nodes.at[:, ELEM - 1].set(high_rim)
    return nodes.astype(jnp.int32)


def draw_rhs(key, part):
    keys = jax.random.split(jax.random.fold_in(key, 29), 1)
    ramp = 1.0 + 2.0 * jnp.arange(NODES, dtype=jnp.float32) / NODES
    rough = jax.random.truncated_normal(keys[0], -4.0, 4.0, (VEC, NODES), jnp.float32)
    return (rough * ramp[None, :]).astype(jnp.float32)


def draw_stiffness(key, part):
    inner = jax.random.fold_in(key, 31)
    raw = jnp.clip(jax.random.normal(inner, (ELEM, ELEM), jnp.float32), -4.0, 4.0)
    sym = 0.5 * (raw + raw.T)
    outside = sym * (1.0 - jnp.eye(ELEM, dtype=jnp.float32))
    diagonal = 1.0 + jnp.sum(jnp.abs(outside), axis=1)
    matrix = outside + jnp.diag(diagonal)
    return (matrix / jnp.mean(diagonal)).astype(jnp.float32)


def draw_atom_matrix(key, part):
    inner = jax.random.fold_in(key, 37)
    raw = 0.5 * jnp.clip(jax.random.normal(inner, (ATOMS, NPROJ, NPROJ), jnp.float32), -4.0, 4.0)
    sym = 0.5 * (raw + jnp.swapaxes(raw, 1, 2))
    outside = sym * (1.0 - jnp.eye(NPROJ, dtype=jnp.float32))[None, :, :]
    diagonal = 0.5 + jnp.sum(jnp.abs(outside), axis=2)
    matrix = outside + diagonal[:, :, None] * jnp.eye(NPROJ, dtype=jnp.float32)[None, :, :]
    return matrix.astype(jnp.float32)


def shard_levels(stream_key, shape, pieces, least, top_value):
    level, own = 1.0, jax.random.fold_in(stream_key, 6)
    for dim, parts in pieces:
        draws = jnp.exp(jax.random.uniform(jax.random.fold_in(own, dim), (parts,), jnp.float32, least / len(pieces), top_value / len(pieces)))
        level = level * jnp.repeat(draws, shape[dim] // parts).reshape([-1 if axis == dim else 1 for axis in range(len(shape))])
    return level


def bell_draw(key, shape, deviation, limit, cuts=(), held_as=jnp.bfloat16):
    result = jax.random.normal(key, shape, jnp.float32) * deviation
    if len(cuts) > 0:
        result = shard_levels(key, shape, cuts, -0.22, 0.18) * result
    return jnp.clip(result, min=-limit, max=limit).astype(held_as)


def setup_inputs(seed: int = 0) -> dict:
    streams_of = jax.random.split(jax.random.key(seed), 14)
    return {
        "rhs": draw_rhs(jax.random.fold_in(streams_of[13], 71), 0),
        "potential": jnp.clip(0.5 + 1.5 * jax.random.uniform(streams_of[1], (NODES,), jnp.float32) ** shard_levels(streams_of[1], (NODES,), ((0, 32),), -0.2, 0.2), 0.5, 2.0),
        "precond": jnp.clip(jnp.exp(math.log(0.5) - 2.3025851 * jax.random.uniform(streams_of[2], (NODES,), jnp.float32) ** shard_levels(streams_of[2], (NODES,), ((0, 32),), -0.2, 0.2)), 0.05, 0.5),
        "shift": jnp.clip(jnp.exp(jax.random.uniform(streams_of[3], (VEC,), jnp.float32, math.log(0.3), math.log(3.0))), 0.3, 3.0),
        "stiffness": draw_stiffness(jax.random.fold_in(streams_of[13], 71), 0),
        "cell_scale": jnp.clip(jnp.exp(math.log(2.0) - 1.3862944 * jax.random.uniform(streams_of[5], (CELLS,), jnp.float32) ** shard_levels(streams_of[5], (CELLS,), ((0, 32),), -0.2, 0.2)), 0.5, 2.0),
        "conn": draw_conn(jax.random.fold_in(streams_of[13], 71), 0),
        "cell_count": draw_cell_count(jax.random.fold_in(streams_of[13], 71), 0),
        "projector": bell_draw(streams_of[8], (PSUPS, NPROJ, ELEM), 0.1, 0.6, ((0, 32),), jnp.float32),
        "support_cell": draw_support_cell(jax.random.fold_in(streams_of[13], 71), 0),
        "support_atom": draw_support_atom(jax.random.fold_in(streams_of[13], 71), 0),
        "support_count": draw_support_count(jax.random.fold_in(streams_of[13], 71), 0),
        "atom_matrix": draw_atom_matrix(jax.random.fold_in(streams_of[13], 71), 0),
    }


HIGH = lax.Precision.HIGHEST


def apply_operator(field, potential, shift, stiffness, cell_scale, conn, cell_count, projector, support_cell, support_atom, support_count, atom_matrix):
    padded = jnp.pad(field, ((0, 0), (GHOST, GHOST)))
    conn_blocks = conn.reshape(N_DOM, CELL_DEV, ELEM)
    scale_blocks = cell_scale.reshape(N_DOM, CELL_DEV)
    proj_blocks = projector.reshape(N_DOM, PSUP_DEV, NPROJ, ELEM)
    cell_blocks = support_cell.reshape(N_DOM, PSUP_DEV)
    blocks = jnp.arange(N_DOM, dtype=jnp.int32)
    entry_live = (jnp.arange(PSUP_DEV, dtype=jnp.int32)[None, :] < support_count[:, None]).astype(field.dtype)

    def window_of(index):
        return lax.dynamic_slice_in_dim(padded, (index * NODE_DEV).astype(jnp.int32), NODE_DEV + 2 * GHOST, 1)

    def partials(index):
        window = window_of(index)
        rows = conn_blocks[index][cell_blocks[index]]
        values = window[:, rows]
        return jnp.einsum("sjn,vsn->sjv", proj_blocks[index], values, precision=HIGH)

    weights = lax.map(partials, blocks)
    weights = weights * entry_live[:, :, None, None]
    flat = weights.reshape(N_DOM * PSUP_DEV, NPROJ, VEC)
    coef = jax.ops.segment_sum(flat, support_atom, num_segments=ATOMS)
    term = jnp.einsum("aij,ajv->aiv", atom_matrix, coef, precision=HIGH)
    picked = term[support_atom] * entry_live.reshape(-1)[:, None, None]
    picked = picked.reshape(N_DOM, PSUP_DEV, NPROJ, VEC)

    def local(index):
        window = window_of(index)
        connect = conn_blocks[index]
        live = (jnp.arange(CELL_DEV, dtype=jnp.int32) < cell_count[index]).astype(field.dtype)
        values = window[:, connect] * (scale_blocks[index] * live)[None, :, None]
        product = jnp.einsum("vcn,mn->vcm", values, stiffness, precision=HIGH)
        rows = connect[cell_blocks[index]]
        back = jnp.einsum("sjn,sjv->vsn", proj_blocks[index], picked[index], precision=HIGH)
        total = jnp.zeros_like(window)
        total = total.at[:, connect].add(product)
        total = total.at[:, rows].add(back)
        return total

    stacked = lax.map(local, blocks)
    inner = jnp.transpose(stacked[:, :, GHOST:GHOST + NODE_DEV], (1, 0, 2))
    left = jnp.transpose(stacked[:, :, :GHOST], (1, 0, 2))
    right = jnp.transpose(stacked[:, :, GHOST + NODE_DEV:], (1, 0, 2))
    inner = inner.at[:, :-1, NODE_DEV - GHOST:].add(left[:, 1:])
    inner = inner.at[:, 1:, :GHOST].add(right[:, :-1])
    return inner.reshape(VEC, NODES) + (potential[None, :] + shift[:, None]) * field


def reference(rhs, potential, precond, shift, stiffness, cell_scale, conn, cell_count, projector, support_cell, support_atom, support_count, atom_matrix):
    def operator(field):
        return apply_operator(field, potential, shift, stiffness, cell_scale, conn, cell_count, projector, support_cell, support_atom, support_count, atom_matrix)

    solution = jnp.zeros_like(rhs)
    residual = rhs
    search = precond[None, :] * residual
    gamma = jnp.sum(residual * search, axis=1)
    for step in range(ITERS):
        image = operator(search)
        step_size = gamma / jnp.sum(search * image, axis=1)
        solution = solution + step_size[:, None] * search
        residual = residual - step_size[:, None] * image
        if step + 1 < ITERS:
            smoothed = precond[None, :] * residual
            fresh = jnp.sum(residual * smoothed, axis=1)
            search = smoothed + (fresh / gamma)[:, None] * search
            gamma = fresh
    return solution, residual
```

```python
import functools

import jax
import jax.numpy as jnp
from jax import lax
from jax.experimental import pallas as pl
from jax.experimental.pallas import tpu as pltpu
from jax.sharding import PartitionSpec as P

LANES = 128
ROWS = 8
WIDE = 256
F32 = jnp.float32
BF16 = jnp.bfloat16
HIGHEST = lax.Precision.HIGHEST
NT = (((1,), (1,)), ((), ()))
VMEM = pl.BlockSpec(memory_space=pltpu.VMEM)
SMEM = pl.BlockSpec(memory_space=pltpu.SMEM)


def round_up(value, step):
    return -(-value // step) * step


class Sizes:
    def __init__(self, count, rhs, conn, projector, atom_matrix):
        self.devices = count
        self.vectors, self.nodes = rhs.shape
        self.slots, self.elem = conn.shape
        self.entries, self.channels = projector.shape[:2]
        self.owned = atom_matrix.shape[0]
        self.ghost = self.nodes // 16
        self.rim = round_up(self.ghost, WIDE)
        self.shift = self.rim - self.ghost
        self.window = self.nodes + 2 * self.rim
        self.width = round_up(self.elem, LANES)
        self.tiles = self.width // LANES
        self.pairs = self.channels * self.vectors
        assert self.vectors == ROWS and self.channels == ROWS
        assert self.nodes % WIDE == 0 and self.owned * self.pairs == LANES


def lane_gather(values, index):
    return jnp.take_along_axis(values, index, axis=1, mode="promise_in_bounds")


def iota(shape, dim):
    return lax.broadcasted_iota(jnp.int32, shape, dim)


def split(values):
    high = values.astype(BF16)
    return high, (values - high.astype(F32)).astype(BF16)


def lanes_by_vector(z, values):
    total = jnp.sum(values, axis=1, keepdims=True)
    spread = jnp.broadcast_to(total, (ROWS, LANES))
    return jnp.sum(jnp.where(iota((ROWS, LANES), 1) == iota((ROWS, LANES), 0), spread, 0.0), axis=0, keepdims=True)


def load_index(z, conn_ref, index_ref):
    index_ref[...] = jnp.zeros_like(index_ref)
    for c in range(z.slots):
        index_ref[c, :, : z.elem] = conn_ref[c : c + 1, :] + z.shift


def gather_cells(z, index_ref, window_ref, scale_ref, live, u_ref, uw_ref):
    def cell(c, _):
        weight = jnp.where(c < live, scale_ref[c], 0.0)
        rows = pl.ds(pl.multiple_of(c * ROWS, ROWS), ROWS)
        for t in range(z.tiles):
            lanes = slice(t * LANES, (t + 1) * LANES)
            index = jnp.broadcast_to(index_ref[c, :, lanes], (ROWS, LANES))
            low, high = index & (LANES - 1), index >> 7
            value = jnp.zeros((ROWS, LANES), F32)
            for h in range(z.window // LANES):
                got = lane_gather(window_ref[:, h * LANES : (h + 1) * LANES], low)
                value = jnp.where(high == h, got, value)
            u_ref[rows, lanes] = value
            uw_ref[rows, lanes] = value * weight
        return 0

    lax.fori_loop(0, z.slots, cell, 0)


def stiffness_product(z, stiffness_ref, k_ref, uw_ref, e_ref):
    k_ref[...] = jnp.zeros_like(k_ref)
    k_ref[: z.elem, : z.elem] = stiffness_ref[...]
    k_high, k_low = split(k_ref[...])
    u_high, u_low = split(uw_ref[...])
    dot = functools.partial(lax.dot_general, dimension_numbers=NT, preferred_element_type=F32)
    e_ref[...] = dot(u_high, k_high) + (dot(u_high, k_low) + dot(u_low, k_high))


def entry_facts(z, position, atom_ref, count_ref, s):
    atom = atom_ref[s]
    owner = atom // z.owned
    return owner, atom - owner * z.owned, s < count_ref[position]


def contributions(z, position, projector_ref, pj_ref, cell_ref, atom_ref, count_ref, u_ref):
    pj_ref[...] = jnp.zeros_like(pj_ref)
    pj_ref[:, : z.elem] = projector_ref[...]
    values = [u_ref[pl.ds(pl.multiple_of(cell_ref[s] * ROWS, ROWS), ROWS), :] for s in range(z.entries)]
    sums = lax.dot_general(
        pj_ref[...], jnp.concatenate(values, axis=0), NT, precision=HIGHEST, preferred_element_type=F32
    )
    sums = jnp.concatenate([sums, jnp.zeros((sums.shape[0], LANES - sums.shape[1]), F32)], axis=1)
    lane, row = iota((ROWS, LANES), 1), iota((ROWS, LANES), 0)
    parts = [jnp.zeros((ROWS, LANES), F32)] * 3
    for s in range(z.entries):
        owner, local, alive = entry_facts(z, position, atom_ref, count_ref, s)
        got = lane_gather(sums[s * ROWS : (s + 1) * ROWS], s * ROWS + lane % ROWS)
        here = (lane // ROWS % ROWS == row) & (lane // z.pairs == local) & alive
        for k in range(3):
            parts[k] = parts[k] + jnp.where(here & (owner == position - 1 + k), got, 0.0)
    return [jnp.sum(part, axis=0, keepdims=True) for part in parts]


def first_kernel(
    z, pos_ref, count_ref, scale_ref, cell_ref, atom_ref, scount_ref, rhs_ref, precond_ref, potential_ref, shift_ref,
    halo_a_ref, halo_b_ref, conn_ref, stiffness_ref, projector_ref, coupling_ref,
    p_ref, diag_ref, out_ref, e_ref, pj_ref, k_ref, index_ref, gamma_ref, u_ref, uw_ref,
):
    position = pos_ref[0]
    even = position % 2 == 0
    a, b = halo_a_ref[...], halo_b_ref[...]
    left, right = jnp.where(even, b, a), jnp.where(even, a, b)
    own = slice(z.rim, z.rim + z.nodes)
    first, last = slice(0, z.rim), slice(z.rim + z.nodes, z.window)
    for where, side in ((first, left), (last, right)):
        p_ref[:, where] = side[:ROWS] * side[ROWS : ROWS + 1]
        diag_ref[0:1, where] = side[ROWS : ROWS + 1]
        diag_ref[1:2, where] = side[ROWS + 1 : ROWS + 2]
    diag_ref[0:1, own] = precond_ref[...]
    diag_ref[1:2, own] = potential_ref[...]
    product = rhs_ref[...] * precond_ref[...]
    p_ref[:, own] = product
    gamma_ref[...] = lanes_by_vector(z, product * rhs_ref[...])
    load_index(z, conn_ref, index_ref)
    gather_cells(z, index_ref, p_ref, scale_ref, count_ref[position], u_ref, uw_ref)
    parts = contributions(z, position, projector_ref, pj_ref, cell_ref, atom_ref, scount_ref, u_ref)
    message = jnp.concatenate(parts + [coupling_ref[...]], axis=0)
    for d in range(z.devices):
        out_ref[d] = message
    stiffness_product(z, stiffness_ref, k_ref, uw_ref, e_ref)


def second_kernel(
    z, pos_ref, count_ref, scale_ref, cell_ref, atom_ref, scount_ref, p_ref, diag_ref, shift_ref, gamma_ref,
    image_ref, halo_a_ref, halo_b_ref, index_ref, stiffness_ref, projector_ref,
    y_ref, q_ref, out_ref, e_ref, pj_ref, k_ref, u_ref, uw_ref,
):
    position = pos_ref[0]
    even = position % 2 == 0
    a, b = halo_a_ref[...], halo_b_ref[...]
    left, right = jnp.where(even, b, a), jnp.where(even, a, b)
    diagonal = diag_ref[1:2, :] + shift_ref[...]
    y_ref[...] = image_ref[...] + diagonal * p_ref[...]
    y_ref[:, : 2 * z.rim] += left
    y_ref[:, z.window - 2 * z.rim :] += right
    q_ref[...] = y_ref[...] * diag_ref[0:1, :]
    own = slice(z.rim, z.rim + z.nodes)
    y, q = y_ref[:, own], q_ref[:, own]
    dots = [
        gamma_ref[...],
        lanes_by_vector(z, y * p_ref[:, own]),
        lanes_by_vector(z, y * q),
    ]
    energy = jnp.sum(q * q * (diag_ref[1:2, own] + shift_ref[...]), axis=1, keepdims=True)
    gather_cells(z, index_ref, q_ref, scale_ref, count_ref[position], u_ref, uw_ref)
    parts = contributions(z, position, projector_ref, pj_ref, cell_ref, atom_ref, scount_ref, u_ref)
    stiffness_product(z, stiffness_ref, k_ref, uw_ref, e_ref)
    elements = jnp.zeros((ROWS, z.width), F32)
    for c in range(z.slots):
        rows = slice(c * ROWS, (c + 1) * ROWS)
        elements = elements + u_ref[rows, :] * e_ref[rows, :]
    energy = energy + jnp.sum(elements, axis=1, keepdims=True)
    dots.append(lanes_by_vector(z, energy))
    line = dots[0]
    for k in range(1, len(dots)):
        line = line + pltpu.roll(dots[k], k * ROWS, 1)
    message = jnp.concatenate(parts + [line], axis=0)
    for d in range(z.devices):
        out_ref[d] = message


def scatter_kernel(
    z, last, pos_ref, cell_ref, atom_ref, scount_ref, sums_ref, coupling_ref, e_in_ref, index_ref, pj_ref, *refs,
):
    if last:
        image_ref, send_a_ref, send_b_ref, dots_ref, e_ref, lhs_ref, hot_ref, acc_ref = refs
    else:
        image_ref, send_a_ref, send_b_ref, e_ref, lhs_ref, hot_ref, acc_ref = refs
    position = pos_ref[0]
    wanted = (
        pltpu.roll(sums_ref[:, 0, :], z.devices - 1, 0) + sums_ref[:, 1, :] + pltpu.roll(sums_ref[:, 2, :], 1, 0)
    )
    coupling = coupling_ref[:, 3, :]
    shape = (z.devices, LANES)
    lane = iota(shape, 1)
    term = jnp.zeros(shape, F32)
    for j in range(z.channels):
        matrix = lane_gather(coupling, lane // ROWS * ROWS + j)
        vector = lane_gather(wanted, lane // z.pairs * z.pairs + j * ROWS + lane % ROWS)
        term = term + matrix * vector
    if last:
        energy = jnp.sum(term * wanted, axis=0, keepdims=True)
        energy = jnp.broadcast_to(energy, (ROWS, LANES))
        step = ROWS
        while step < LANES:
            energy = energy + pltpu.roll(energy, step, 1)
            step *= 2
        line = iota((1, LANES), 1)
        dots_ref[...] = jnp.sum(sums_ref[:, 3, :], axis=0, keepdims=True) + jnp.where(
            line // ROWS == 3, energy[0:1], 0.0
        )
    block = iota(shape, 0)
    small_lane, small_row = iota((ROWS, LANES), 1), iota((ROWS, LANES), 0)
    spread = []
    for s in range(z.entries):
        owner, local, alive = entry_facts(z, position, atom_ref, scount_ref, s)
        mine = jnp.sum(jnp.where(block == owner, term, 0.0), axis=0, keepdims=True)
        got = lane_gather(
            jnp.broadcast_to(mine, (ROWS, LANES)), local * z.pairs + small_lane % ROWS * ROWS + small_row
        )
        spread.append(jnp.where((small_lane // ROWS == s) & alive, got, 0.0)[:, : z.entries * ROWS])
    support = jnp.dot(
        jnp.concatenate(spread, axis=0), pj_ref[...], precision=HIGHEST, preferred_element_type=F32
    )
    e_ref[...] = e_in_ref[...]
    for s in range(z.entries):
        rows = pl.ds(pl.multiple_of(cell_ref[s] * ROWS, ROWS), ROWS)
        e_ref[rows, :] += support[s * ROWS : (s + 1) * ROWS]

    groups = z.window // WIDE
    chunk = lhs_ref.shape[1] // z.width
    acc_ref[...] = jnp.zeros_like(acc_ref)
    sub = iota((2 * ROWS, LANES), 0)
    lows = [(sub + k * 2 * ROWS).astype(jnp.int16) for k in range(WIDE // (2 * ROWS))]
    one, none = jnp.ones((2 * ROWS, LANES), BF16), jnp.zeros((2 * ROWS, LANES), BF16)

    def some_cells(g, _):
        for cc in range(chunk):
            c = g * chunk + cc
            rows = pl.ds(pl.multiple_of(c * ROWS, ROWS), ROWS)
            for t in range(z.tiles):
                lanes = slice(t * LANES, (t + 1) * LANES)
                to = slice(cc * z.width + t * LANES, cc * z.width + (t + 1) * LANES)
                index = jnp.broadcast_to(index_ref[c, :, lanes], (2 * ROWS, LANES))
                low, high = (index & (WIDE - 1)).astype(jnp.int16), (index >> 8).astype(jnp.int16)
                value = e_ref[rows, lanes]
                rounded = value.astype(BF16).astype(F32)
                both = jnp.concatenate([rounded, value - rounded], axis=0).astype(BF16)
                for h in range(groups):
                    lhs_ref[h * 2 * ROWS : (h + 1) * 2 * ROWS, to] = jnp.where(high == jnp.int16(h), both, none)
                for k, ref_low in enumerate(lows):
                    hot_ref[k * 2 * ROWS : (k + 1) * 2 * ROWS, to] = jnp.where(low == ref_low, one, none)
        acc_ref[...] += lax.dot_general(lhs_ref[...], hot_ref[...], NT, preferred_element_type=F32)
        return 0

    lax.fori_loop(0, z.slots // chunk, some_cells, 0)
    for h in range(groups):
        at = h * 2 * ROWS
        image_ref[:, h * WIDE : (h + 1) * WIDE] = acc_ref[at : at + ROWS] + acc_ref[at + ROWS : at + 2 * ROWS]
    low_rim, high_rim = image_ref[:, : 2 * z.rim], image_ref[:, z.window - 2 * z.rim :]
    even = position % 2 == 0
    send_a_ref[...] = jnp.where(even, high_rim, low_rim)
    send_b_ref[...] = jnp.where(even, low_rim, high_rim)


def last_kernel(
    z, pos_ref, rhs_ref, p_ref, diag_ref, shift_ref, y_ref, q_ref, image_ref, halo_a_ref, halo_b_ref, dots_ref,
    solution_ref, residual_ref, z_ref,
):
    even = pos_ref[0] % 2 == 0
    a, b = halo_a_ref[...], halo_b_ref[...]
    left, right = jnp.where(even, b, a), jnp.where(even, a, b)
    own = slice(z.rim, z.rim + z.nodes)
    z_ref[...] = image_ref[...]
    z_ref[:, : 2 * z.rim] += left
    z_ref[:, z.window - 2 * z.rim :] += right
    lane, row = iota((ROWS, LANES), 1), iota((ROWS, LANES), 0)
    line = jnp.broadcast_to(dots_ref[...], (ROWS, LANES))

    def column(k):
        return jnp.sum(jnp.where(lane == k * ROWS + row, line, 0.0), axis=1, keepdims=True)

    gamma, py, qy, qq = (column(k) for k in range(4))
    alpha = gamma / py
    fresh = gamma - 2.0 * alpha * py + alpha * alpha * qy
    beta = fresh / gamma
    more = 1.0 + beta
    step = fresh / (more * more * py - 2.0 * more * alpha * qy + alpha * alpha * qq)
    p, q, y = p_ref[:, own], q_ref[:, own], y_ref[:, own]
    second = z_ref[:, own] + (diag_ref[1:2, own] + shift_ref[...]) * q
    search = (p - alpha * q) + beta * p
    solution_ref[...] = alpha * p + step * search
    residual_ref[...] = (rhs_ref[...] - alpha * y) - step * (more * y - alpha * second)


def on_device(
    rhs, potential, precond, shift, stiffness, cell_scale, conn, cell_count, projector, support_cell, support_atom,
    support_count, atom_matrix,
):
    count = lax.axis_size("dom")
    z = Sizes(count, rhs, conn, projector, atom_matrix)
    position = lax.axis_index("dom")
    even = position % 2 == 0
    pos = position.astype(jnp.int32).reshape(1)
    near = [(i, i ^ 1) for i in range(count)]
    far = [(i, j) for i in range(1, count - 1) for j in [i + 1 if i % 2 else i - 1]]

    def exchange(a, b):
        return lax.ppermute(a, "dom", near), lax.ppermute(b, "dom", far)

    def call(kernel, outs, scratch, specs, *args):
        return pl.pallas_call(
            functools.partial(kernel),
            out_shape=[jax.ShapeDtypeStruct(s, d) for s, d in outs],
            in_specs=specs,
            out_specs=[VMEM] * len(outs),
            scratch_shapes=[pltpu.VMEM(s, d) for s, d in scratch],
        )(*args)

    precond_row, potential_row = precond[None, :], potential[None, :]
    shift_column = shift[:, None]
    packed = jnp.concatenate([rhs, precond_row, potential_row], axis=0)
    head, tail = packed[:, : z.rim], packed[:, z.nodes - z.rim :]
    halo = exchange(jnp.where(even, tail, head), jnp.where(even, head, tail))
    flat_projector = projector.reshape(z.entries * z.channels, z.elem)
    coupling = atom_matrix.reshape(1, LANES)

    cells = (z.slots * ROWS, z.width)
    window = (z.vectors, z.window)
    message = (z.devices, 4, LANES)
    cell_scratch = [(cells, F32), (cells, F32)]
    p, diag, sums, e, pj, k_pad, index, gamma = call(
        functools.partial(first_kernel, z),
        [(window, F32), ((2, z.window), F32), (message, F32), (cells, F32), ((z.entries * ROWS, z.width), F32),
         ((z.width, z.width), F32), ((z.slots, 1, z.width), jnp.int32), ((1, LANES), F32)],
        cell_scratch,
        [SMEM] * 6 + [VMEM] * 10,
        pos, cell_count, cell_scale, support_cell, support_atom, support_count, rhs, precond_row, potential_row,
        shift_column, *halo, conn, stiffness, flat_projector, coupling,
    )
    chunk = 4 if z.slots % 4 == 0 else 1
    groups = z.window // WIDE
    scatter_scratch = [
        (cells, F32), ((groups * 2 * ROWS, chunk * z.width), BF16), ((WIDE, chunk * z.width), BF16),
        ((groups * 2 * ROWS, WIDE), F32),
    ]
    rim = (z.vectors, 2 * z.rim)
    coupled = lax.all_to_all(sums, "dom", 0, 0)
    image, send_a, send_b = call(
        functools.partial(scatter_kernel, z, False),
        [(window, F32), (rim, F32), (rim, F32)],
        scatter_scratch,
        [SMEM] * 4 + [VMEM] * 5,
        pos, support_cell, support_atom, support_count, coupled, coupled, e, index, pj,
    )
    halo = exchange(send_a, send_b)
    y, q, sums, e = call(
        functools.partial(second_kernel, z),
        [(window, F32), (window, F32), (message, F32), (cells, F32)],
        [((z.entries * ROWS, z.width), F32), ((z.width, z.width), F32)] + cell_scratch,
        [SMEM] * 6 + [VMEM] * 10 + [],
        pos, cell_count, cell_scale, support_cell, support_atom, support_count, p, diag, shift_column, gamma,
        image, *halo, index, stiffness, flat_projector,
    )
    totals = lax.all_to_all(sums, "dom", 0, 0)
    image, send_a, send_b, dots = call(
        functools.partial(scatter_kernel, z, True),
        [(window, F32), (rim, F32), (rim, F32), ((1, LANES), F32)],
        scatter_scratch,
        [SMEM] * 4 + [VMEM] * 5,
        pos, support_cell, support_atom, support_count, totals, coupled, e, index, pj,
    )
    halo = exchange(send_a, send_b)
    own = (z.vectors, z.nodes)
    return tuple(
        call(
            functools.partial(last_kernel, z),
            [(own, F32), (own, F32)],
            [(window, F32)],
            [SMEM] + [VMEM] * 10,
            pos, rhs, p, diag, shift_column, y, q, image, *halo, dots,
        )
    )


def solution(mesh):
    placed = (
        P(None, "dom"),
        P("dom"),
        P("dom"),
        P(),
        P(),
        P("dom"),
        P("dom", None),
        P(),
        P("dom", None, None),
        P("dom"),
        P("dom"),
        P(),
        P("dom", None, None),
    )
    return jax.shard_map(
        on_device,
        mesh=mesh,
        in_specs=placed,
        out_specs=(P(None, "dom"), P(None, "dom")),
        check_vma=False,
    )
```

```python
import functools

import jax
import jax.numpy as jnp
from jax import lax
from jax.experimental import pallas as pl
from jax.experimental.pallas import tpu as pltpu
from jax.sharding import PartitionSpec as P

LANES = 128
ROWS = 8
WIDE = 256
CHAINS = 4
F32 = jnp.float32
BF16 = jnp.bfloat16
HIGHEST = lax.Precision.HIGHEST
NT = (((1,), (1,)), ((), ()))
VMEM = pl.BlockSpec(memory_space=pltpu.VMEM)
SMEM = pl.BlockSpec(memory_space=pltpu.SMEM)


def round_up(value, step):
    return -(-value // step) * step


class Sizes:
    def __init__(self, count, rhs, conn, projector, atom_matrix):
        self.devices = count
        self.vectors, self.nodes = rhs.shape
        self.slots, self.elem = conn.shape
        self.entries, self.channels = projector.shape[:2]
        self.owned = atom_matrix.shape[0]
        self.ghost = self.nodes // 16
        self.rim = round_up(self.ghost, WIDE)
        self.shift = self.rim - self.ghost
        self.window = self.nodes + 2 * self.rim
        self.width = round_up(self.elem, LANES)
        self.tiles = self.width // LANES
        self.pairs = self.channels * self.vectors
        assert self.vectors == ROWS and self.channels == ROWS
        assert self.nodes % WIDE == 0 and self.owned * self.pairs == LANES


def lane_gather(values, index):
    return jnp.take_along_axis(values, index, axis=1, mode="promise_in_bounds")


def iota(shape, dim):
    return lax.broadcasted_iota(jnp.int32, shape, dim)


def split(values):
    high = values.astype(BF16)
    return high, (values - high.astype(F32)).astype(BF16)


def lanes_by_vector(z, values):
    total = jnp.sum(values, axis=1, keepdims=True)
    spread = jnp.broadcast_to(total, (ROWS, LANES))
    return jnp.sum(jnp.where(iota((ROWS, LANES), 1) == iota((ROWS, LANES), 0), spread, 0.0), axis=0, keepdims=True)


def load_index(z, conn_ref, index_ref):
    index_ref[...] = jnp.zeros_like(index_ref)
    for c in range(z.slots):
        index_ref[c, :, : z.elem] = conn_ref[c : c + 1, :] + z.shift


def gather_cells(z, index_ref, window_ref, scale_ref, live, u_ref, uw_ref):
    def cell(c, _):
        weight = jnp.where(c < live, scale_ref[c], 0.0)
        rows = pl.ds(pl.multiple_of(c * ROWS, ROWS), ROWS)
        for t in range(z.tiles):
            lanes = slice(t * LANES, (t + 1) * LANES)
            index = jnp.broadcast_to(index_ref[c, :, lanes], (ROWS, LANES))
            low, high = index & (LANES - 1), index >> 7
            chains = [jnp.zeros((ROWS, LANES), F32)] * CHAINS
            for h in range(z.window // LANES):
                got = lane_gather(window_ref[:, h * LANES : (h + 1) * LANES], low)
                chains[h % CHAINS] = jnp.where(high == h, got, chains[h % CHAINS])
            value = functools.reduce(jnp.add, chains)
            u_ref[rows, lanes] = value
            uw_ref[rows, lanes] = value * weight
        return 0

    lax.fori_loop(0, z.slots, cell, 0)


def stiffness_product(z, stiffness_ref, k_ref, uw_ref, e_ref):
    k_ref[...] = jnp.zeros_like(k_ref)
    k_ref[: z.elem, : z.elem] = stiffness_ref[...]
    k_high, k_low = split(k_ref[...])
    u_high, u_low = split(uw_ref[...])
    dot = functools.partial(lax.dot_general, dimension_numbers=NT, preferred_element_type=F32)
    e_ref[...] = dot(u_high, k_high) + (dot(u_high, k_low) + dot(u_low, k_high))


def entry_facts(z, position, atom_ref, count_ref, s):
    atom = atom_ref[s]
    owner = atom // z.owned
    return owner, atom - owner * z.owned, s < count_ref[position]


def contributions(z, position, projector_ref, pj_ref, cell_ref, atom_ref, count_ref, u_ref):
    pj_ref[...] = jnp.zeros_like(pj_ref)
    pj_ref[:, : z.elem] = projector_ref[...]
    values = [u_ref[pl.ds(pl.multiple_of(cell_ref[s] * ROWS, ROWS), ROWS), :] for s in range(z.entries)]
    sums = lax.dot_general(
        pj_ref[...], jnp.concatenate(values, axis=0), NT, precision=HIGHEST, preferred_element_type=F32
    )
    sums = jnp.concatenate([sums, jnp.zeros((sums.shape[0], LANES - sums.shape[1]), F32)], axis=1)
    lane, row = iota((ROWS, LANES), 1), iota((ROWS, LANES), 0)
    parts = [jnp.zeros((ROWS, LANES), F32)] * 3
    for s in range(z.entries):
        owner, local, alive = entry_facts(z, position, atom_ref, count_ref, s)
        got = lane_gather(sums[s * ROWS : (s + 1) * ROWS], s * ROWS + lane % ROWS)
        here = (lane // ROWS % ROWS == row) & (lane // z.pairs == local) & alive
        for k in range(3):
            parts[k] = parts[k] + jnp.where(here & (owner == position - 1 + k), got, 0.0)
    return [jnp.sum(part, axis=0, keepdims=True) for part in parts]


def first_kernel(
    z, pos_ref, count_ref, scale_ref, cell_ref, atom_ref, scount_ref, rhs_ref, precond_ref, potential_ref, shift_ref,
    halo_a_ref, halo_b_ref, conn_ref, stiffness_ref, projector_ref, coupling_ref,
    p_ref, diag_ref, out_ref, e_ref, pj_ref, k_ref, index_ref, gamma_ref, u_ref, uw_ref,
):
    position = pos_ref[0]
    even = position % 2 == 0
    a, b = halo_a_ref[...], halo_b_ref[...]
    left, right = jnp.where(even, b, a), jnp.where(even, a, b)
    own = slice(z.rim, z.rim + z.nodes)
    first, last = slice(0, z.rim), slice(z.rim + z.nodes, z.window)
    for where, side in ((first, left), (last, right)):
        p_ref[:, where] = side[:ROWS] * side[ROWS : ROWS + 1]
        diag_ref[0:1, where] = side[ROWS : ROWS + 1]
        diag_ref[1:2, where] = side[ROWS + 1 : ROWS + 2]
    diag_ref[0:1, own] = precond_ref[...]
    diag_ref[1:2, own] = potential_ref[...]
    product = rhs_ref[...] * precond_ref[...]
    p_ref[:, own] = product
    gamma_ref[...] = lanes_by_vector(z, product * rhs_ref[...])
    load_index(z, conn_ref, index_ref)
    gather_cells(z, index_ref, p_ref, scale_ref, count_ref[position], u_ref, uw_ref)
    parts = contributions(z, position, projector_ref, pj_ref, cell_ref, atom_ref, scount_ref, u_ref)
    message = jnp.concatenate(parts + [coupling_ref[...]], axis=0)
    for d in range(z.devices):
        out_ref[d] = message
    stiffness_product(z, stiffness_ref, k_ref, uw_ref, e_ref)


def second_kernel(
    z, pos_ref, count_ref, scale_ref, cell_ref, atom_ref, scount_ref, p_ref, diag_ref, shift_ref, gamma_ref,
    image_ref, halo_a_ref, halo_b_ref, index_ref, stiffness_ref, projector_ref,
    y_ref, q_ref, out_ref, e_ref, pj_ref, k_ref, u_ref, uw_ref,
):
    position = pos_ref[0]
    even = position % 2 == 0
    a, b = halo_a_ref[...], halo_b_ref[...]
    left, right = jnp.where(even, b, a), jnp.where(even, a, b)
    diagonal = diag_ref[1:2, :] + shift_ref[...]
    y_ref[...] = image_ref[...] + diagonal * p_ref[...]
    y_ref[:, : 2 * z.rim] += left
    y_ref[:, z.window - 2 * z.rim :] += right
    q_ref[...] = y_ref[...] * diag_ref[0:1, :]
    own = slice(z.rim, z.rim + z.nodes)
    y, q = y_ref[:, own], q_ref[:, own]
    dots = [
        gamma_ref[...],
        lanes_by_vector(z, y * p_ref[:, own]),
        lanes_by_vector(z, y * q),
    ]
    energy = jnp.sum(q * q * (diag_ref[1:2, own] + shift_ref[...]), axis=1, keepdims=True)
    gather_cells(z, index_ref, q_ref, scale_ref, count_ref[position], u_ref, uw_ref)
    parts = contributions(z, position, projector_ref, pj_ref, cell_ref, atom_ref, scount_ref, u_ref)
    stiffness_product(z, stiffness_ref, k_ref, uw_ref, e_ref)
    elements = jnp.zeros((ROWS, z.width), F32)
    for c in range(z.slots):
        rows = slice(c * ROWS, (c + 1) * ROWS)
        elements = elements + u_ref[rows, :] * e_ref[rows, :]
    energy = energy + jnp.sum(elements, axis=1, keepdims=True)
    dots.append(lanes_by_vector(z, energy))
    line = dots[0]
    for k in range(1, len(dots)):
        line = line + pltpu.roll(dots[k], k * ROWS, 1)
    message = jnp.concatenate(parts + [line], axis=0)
    for d in range(z.devices):
        out_ref[d] = message


def scatter_kernel(
    z, last, pos_ref, cell_ref, atom_ref, scount_ref, sums_ref, coupling_ref, e_in_ref, index_ref, pj_ref, *refs,
):
    if last:
        image_ref, send_a_ref, send_b_ref, dots_ref, e_ref, lhs_ref, hot_ref, acc_ref = refs
    else:
        image_ref, send_a_ref, send_b_ref, e_ref, lhs_ref, hot_ref, acc_ref = refs
    position = pos_ref[0]
    wanted = (
        pltpu.roll(sums_ref[:, 0, :], z.devices - 1, 0) + sums_ref[:, 1, :] + pltpu.roll(sums_ref[:, 2, :], 1, 0)
    )
    coupling = coupling_ref[:, 3, :]
    shape = (z.devices, LANES)
    lane = iota(shape, 1)
    term = jnp.zeros(shape, F32)
    for j in range(z.channels):
        matrix = lane_gather(coupling, lane // ROWS * ROWS + j)
        vector = lane_gather(wanted, lane // z.pairs * z.pairs + j * ROWS + lane % ROWS)
        term = term + matrix * vector
    if last:
        energy = jnp.sum(term * wanted, axis=0, keepdims=True)
        energy = jnp.broadcast_to(energy, (ROWS, LANES))
        step = ROWS
        while step < LANES:
            energy = energy + pltpu.roll(energy, step, 1)
            step *= 2
        line = iota((1, LANES), 1)
        dots_ref[...] = jnp.sum(sums_ref[:, 3, :], axis=0, keepdims=True) + jnp.where(
            line // ROWS == 3, energy[0:1], 0.0
        )
    block = iota(shape, 0)
    small_lane, small_row = iota((ROWS, LANES), 1), iota((ROWS, LANES), 0)
    spread = []
    for s in range(z.entries):
        owner, local, alive = entry_facts(z, position, atom_ref, scount_ref, s)
        mine = jnp.sum(jnp.where(block == owner, term, 0.0), axis=0, keepdims=True)
        got = lane_gather(
            jnp.broadcast_to(mine, (ROWS, LANES)), local * z.pairs + small_lane % ROWS * ROWS + small_row
        )
        spread.append(jnp.where((small_lane // ROWS == s) & alive, got, 0.0)[:, : z.entries * ROWS])
    support = jnp.dot(
        jnp.concatenate(spread, axis=0), pj_ref[...], precision=HIGHEST, preferred_element_type=F32
    )
    e_ref[...] = e_in_ref[...]
    for s in range(z.entries):
        rows = pl.ds(pl.multiple_of(cell_ref[s] * ROWS, ROWS), ROWS)
        e_ref[rows, :] += support[s * ROWS : (s + 1) * ROWS]

    groups = z.window // WIDE
    chunk = lhs_ref.shape[1] // z.width
    acc_ref[...] = jnp.zeros_like(acc_ref)
    sub = iota((2 * ROWS, LANES), 0)
    lows = [(sub + k * 2 * ROWS).astype(jnp.int16) for k in range(WIDE // (2 * ROWS))]
    one, none = jnp.ones((2 * ROWS, LANES), BF16), jnp.zeros((2 * ROWS, LANES), BF16)

    def some_cells(g, _):
        for cc in range(chunk):
            c = g * chunk + cc
            rows = pl.ds(pl.multiple_of(c * ROWS, ROWS), ROWS)
            for t in range(z.tiles):
                lanes = slice(t * LANES, (t + 1) * LANES)
                to = slice(cc * z.width + t * LANES, cc * z.width + (t + 1) * LANES)
                index = jnp.broadcast_to(index_ref[c, :, lanes], (2 * ROWS, LANES))
                low, high = (index & (WIDE - 1)).astype(jnp.int16), (index >> 8).astype(jnp.int16)
                value = e_ref[rows, lanes]
                rounded = value.astype(BF16).astype(F32)
                both = jnp.concatenate([rounded, value - rounded], axis=0).astype(BF16)
                for h in range(groups):
                    lhs_ref[h * 2 * ROWS : (h + 1) * 2 * ROWS, to] = jnp.where(high == jnp.int16(h), both, none)
                for k, ref_low in enumerate(lows):
                    hot_ref[k * 2 * ROWS : (k + 1) * 2 * ROWS, to] = jnp.where(low == ref_low, one, none)
        acc_ref[...] += lax.dot_general(lhs_ref[...], hot_ref[...], NT, preferred_element_type=F32)
        return 0

    lax.fori_loop(0, z.slots // chunk, some_cells, 0)
    for h in range(groups):
        at = h * 2 * ROWS
        image_ref[:, h * WIDE : (h + 1) * WIDE] = acc_ref[at : at + ROWS] + acc_ref[at + ROWS : at + 2 * ROWS]
    low_rim, high_rim = image_ref[:, : 2 * z.rim], image_ref[:, z.window - 2 * z.rim :]
    even = position % 2 == 0
    send_a_ref[...] = jnp.where(even, high_rim, low_rim)
    send_b_ref[...] = jnp.where(even, low_rim, high_rim)


def last_kernel(
    z, pos_ref, rhs_ref, p_ref, diag_ref, shift_ref, y_ref, q_ref, image_ref, halo_a_ref, halo_b_ref, dots_ref,
    solution_ref, residual_ref, z_ref,
):
    even = pos_ref[0] % 2 == 0
    a, b = halo_a_ref[...], halo_b_ref[...]
    left, right = jnp.where(even, b, a), jnp.where(even, a, b)
    own = slice(z.rim, z.rim + z.nodes)
    z_ref[...] = image_ref[...]
    z_ref[:, : 2 * z.rim] += left
    z_ref[:, z.window - 2 * z.rim :] += right
    lane, row = iota((ROWS, LANES), 1), iota((ROWS, LANES), 0)
    line = jnp.broadcast_to(dots_ref[...], (ROWS, LANES))

    def column(k):
        return jnp.sum(jnp.where(lane == k * ROWS + row, line, 0.0), axis=1, keepdims=True)

    gamma, py, qy, qq = (column(k) for k in range(4))
    alpha = gamma / py
    fresh = gamma - 2.0 * alpha * py + alpha * alpha * qy
    beta = fresh / gamma
    more = 1.0 + beta
    step = fresh / (more * more * py - 2.0 * more * alpha * qy + alpha * alpha * qq)
    p, q, y = p_ref[:, own], q_ref[:, own], y_ref[:, own]
    second = z_ref[:, own] + (diag_ref[1:2, own] + shift_ref[...]) * q
    search = (p - alpha * q) + beta * p
    solution_ref[...] = alpha * p + step * search
    residual_ref[...] = (rhs_ref[...] - alpha * y) - step * (more * y - alpha * second)


def on_device(
    rhs, potential, precond, shift, stiffness, cell_scale, conn, cell_count, projector, support_cell, support_atom,
    support_count, atom_matrix,
):
    count = lax.axis_size("dom")
    z = Sizes(count, rhs, conn, projector, atom_matrix)
    position = lax.axis_index("dom")
    even = position % 2 == 0
    pos = position.astype(jnp.int32).reshape(1)
    near = [(i, i ^ 1) for i in range(count)]
    far = [(i, j) for i in range(1, count - 1) for j in [i + 1 if i % 2 else i - 1]]

    def exchange(a, b):
        return lax.ppermute(a, "dom", near), lax.ppermute(b, "dom", far)

    def call(kernel, outs, scratch, specs, *args):
        return pl.pallas_call(
            functools.partial(kernel),
            out_shape=[jax.ShapeDtypeStruct(s, d) for s, d in outs],
            in_specs=specs,
            out_specs=[VMEM] * len(outs),
            scratch_shapes=[pltpu.VMEM(s, d) for s, d in scratch],
        )(*args)

    precond_row, potential_row = precond[None, :], potential[None, :]
    shift_column = shift[:, None]
    packed = jnp.concatenate([rhs, precond_row, potential_row], axis=0)
    head, tail = packed[:, : z.rim], packed[:, z.nodes - z.rim :]
    halo = exchange(jnp.where(even, tail, head), jnp.where(even, head, tail))
    flat_projector = projector.reshape(z.entries * z.channels, z.elem)
    coupling = atom_matrix.reshape(1, LANES)

    cells = (z.slots * ROWS, z.width)
    window = (z.vectors, z.window)
    message = (z.devices, 4, LANES)
    cell_scratch = [(cells, F32), (cells, F32)]
    p, diag, sums, e, pj, k_pad, index, gamma = call(
        functools.partial(first_kernel, z),
        [(window, F32), ((2, z.window), F32), (message, F32), (cells, F32), ((z.entries * ROWS, z.width), F32),
         ((z.width, z.width), F32), ((z.slots, 1, z.width), jnp.int32), ((1, LANES), F32)],
        cell_scratch,
        [SMEM] * 6 + [VMEM] * 10,
        pos, cell_count, cell_scale, support_cell, support_atom, support_count, rhs, precond_row, potential_row,
        shift_column, *halo, conn, stiffness, flat_projector, coupling,
    )
    chunk = 4 if z.slots % 4 == 0 else 1
    groups = z.window // WIDE
    scatter_scratch = [
        (cells, F32), ((groups * 2 * ROWS, chunk * z.width), BF16), ((WIDE, chunk * z.width), BF16),
        ((groups * 2 * ROWS, WIDE), F32),
    ]
    rim = (z.vectors, 2 * z.rim)
    coupled = lax.all_to_all(sums, "dom", 0, 0)
    image, send_a, send_b = call(
        functools.partial(scatter_kernel, z, False),
        [(window, F32), (rim, F32), (rim, F32)],
        scatter_scratch,
        [SMEM] * 4 + [VMEM] * 5,
        pos, support_cell, support_atom, support_count, coupled, coupled, e, index, pj,
    )
    halo = exchange(send_a, send_b)
    y, q, sums, e = call(
        functools.partial(second_kernel, z),
        [(window, F32), (window, F32), (message, F32), (cells, F32)],
        [((z.entries * ROWS, z.width), F32), ((z.width, z.width), F32)] + cell_scratch,
        [SMEM] * 6 + [VMEM] * 10 + [],
        pos, cell_count, cell_scale, support_cell, support_atom, support_count, p, diag, shift_column, gamma,
        image, *halo, index, stiffness, flat_projector,
    )
    totals = lax.all_to_all(sums, "dom", 0, 0)
    image, send_a, send_b, dots = call(
        functools.partial(scatter_kernel, z, True),
        [(window, F32), (rim, F32), (rim, F32), ((1, LANES), F32)],
        scatter_scratch,
        [SMEM] * 4 + [VMEM] * 5,
        pos, support_cell, support_atom, support_count, totals, coupled, e, index, pj,
    )
    halo = exchange(send_a, send_b)
    own = (z.vectors, z.nodes)
    return tuple(
        call(
            functools.partial(last_kernel, z),
            [(own, F32), (own, F32)],
            [(window, F32)],
            [SMEM] + [VMEM] * 10,
            pos, rhs, p, diag, shift_column, y, q, image, *halo, dots,
        )
    )


def solution(mesh):
    placed = (
        P(None, "dom"),
        P("dom"),
        P("dom"),
        P(),
        P(),
        P("dom"),
        P("dom", None),
        P(),
        P("dom", None, None),
        P("dom"),
        P("dom"),
        P(),
        P("dom", None, None),
    )
    return jax.shard_map(
        on_device,
        mesh=mesh,
        in_specs=placed,
        out_specs=(P(None, "dom"), P(None, "dom")),
        check_vma=False,
    )
```

```python
import functools

import jax
import jax.numpy as jnp
from jax import lax
from jax.experimental import pallas as pl
from jax.experimental.pallas import tpu as pltpu
from jax.sharding import PartitionSpec as P

LANES = 128
ROWS = 8
WIDE = 256
CHAINS = 4
SPAN = 14
BAND = 8
TOGETHER = 4
F32 = jnp.float32
BF16 = jnp.bfloat16
HIGHEST = lax.Precision.HIGHEST
NT = (((1,), (1,)), ((), ()))
VMEM = pl.BlockSpec(memory_space=pltpu.VMEM)
SMEM = pl.BlockSpec(memory_space=pltpu.SMEM)


def round_up(value, step):
    return -(-value // step) * step


class Sizes:
    def __init__(self, count, rhs, conn, projector, atom_matrix):
        self.devices = count
        self.vectors, self.nodes = rhs.shape
        self.slots, self.elem = conn.shape
        self.entries, self.channels = projector.shape[:2]
        self.owned = atom_matrix.shape[0]
        self.ghost = self.nodes // 16
        self.rim = round_up(self.ghost, WIDE)
        self.shift = self.rim - self.ghost
        self.window = self.nodes + 2 * self.rim
        self.width = round_up(self.elem, LANES)
        self.tiles = self.width // LANES
        self.pairs = self.channels * self.vectors
        self.reach = self.window + SPAN * LANES
        self.together = TOGETHER if self.slots % TOGETHER == 0 else 1
        assert self.vectors == ROWS and self.channels == ROWS and 2 * self.slots <= LANES
        assert self.nodes % WIDE == 0 and self.owned * self.pairs == LANES


def lane_gather(values, index):
    return jnp.take_along_axis(values, index, axis=1, mode="promise_in_bounds")


def iota(shape, dim):
    return lax.broadcasted_iota(jnp.int32, shape, dim)


def split(values):
    high = values.astype(BF16)
    return high, (values - high.astype(F32)).astype(BF16)


def lanes_by_vector(z, values):
    total = jnp.sum(values, axis=1, keepdims=True)
    spread = jnp.broadcast_to(total, (ROWS, LANES))
    return jnp.sum(jnp.where(iota((ROWS, LANES), 1) == iota((ROWS, LANES), 0), spread, 0.0), axis=0, keepdims=True)


def prepare_kernel(z, conn_ref, stiffness_ref, projector_ref, index_ref, k_high_ref, k_low_ref, pj_ref, k_ref):
    index_ref[...] = jnp.zeros_like(index_ref)
    for c in range(z.slots):
        index_ref[c, :, : z.elem] = conn_ref[c : c + 1, :] + z.shift
    k_ref[...] = jnp.zeros_like(k_ref)
    k_ref[: z.elem, : z.elem] = stiffness_ref[...]
    k_high_ref[...], k_low_ref[...] = split(k_ref[...])
    pj_ref[...] = jnp.zeros_like(pj_ref)
    pj_ref[:, : z.elem] = projector_ref[...]


def gather_cells(z, index_ref, corner_ref, range_ref, window_ref, scale_ref, live, u_ref, uw_ref):
    total = z.window // LANES
    tile = (ROWS, LANES)
    corner = jnp.broadcast_to(corner_ref[...], tile)
    low, high = corner & (LANES - 1), corner >> 7
    chains = [jnp.zeros(tile, F32)] * CHAINS
    for h in range(total):
        got = lane_gather(window_ref[:, h * LANES : (h + 1) * LANES], low)
        chains[h % CHAINS] = jnp.where(high == h, got, chains[h % CHAINS])
    corners = functools.reduce(jnp.add, chains)
    lane = iota(tile, 1)
    last = (z.elem - 1) % LANES

    def some_cells(g, _):
        cells = [g * z.together + i for i in range(z.together)]
        starts = [range_ref[0, c] >> 7 for c in cells]
        ends = [range_ref[1, c] >> 7 for c in cells]
        passes = functools.reduce(jnp.maximum, [(e - s) // SPAN + 1 for s, e in zip(starts, ends)])

        def one_pass(k, values):
            values = list(values)
            for i, c in enumerate(cells):
                start = jnp.minimum(starts[i] + k * SPAN, total)
                for t in range(z.tiles):
                    index = jnp.broadcast_to(index_ref[c, :, t * LANES : (t + 1) * LANES], tile)
                    low, high = index & (LANES - 1), (index >> 7) - start
                    value = values[i * z.tiles + t]
                    for h in range(SPAN):
                        at = pl.ds(pl.multiple_of((start + h) * LANES, LANES), LANES)
                        value = jnp.where(high == h, lane_gather(window_ref[:, at], low), value)
                    values[i * z.tiles + t] = value
            return tuple(values)

        values = lax.fori_loop(0, passes, one_pass, (jnp.zeros(tile, F32),) * (z.together * z.tiles))
        for i, c in enumerate(cells):
            weight = jnp.where(c < live, scale_ref[c], 0.0)
            rows = pl.ds(pl.multiple_of(c * ROWS, ROWS), ROWS)
            for t in range(z.tiles):
                value = values[i * z.tiles + t]
                if t == 0:
                    value = jnp.where(lane == 0, lane_gather(corners, jnp.full(tile, 0, jnp.int32) + c), value)
                if t == z.tiles - 1:
                    got = lane_gather(corners, jnp.full(tile, z.slots, jnp.int32) + c)
                    value = jnp.where(lane == last, got, value)
                u_ref[rows, t * LANES : (t + 1) * LANES] = value
                uw_ref[rows, t * LANES : (t + 1) * LANES] = value * weight
        return 0

    lax.fori_loop(0, z.slots // z.together, some_cells, 0)


def stiffness_product(k_high_ref, k_low_ref, uw_ref, e_ref):
    k_high, k_low = k_high_ref[...], k_low_ref[...]
    u_high, u_low = split(uw_ref[...])
    dot = functools.partial(lax.dot_general, dimension_numbers=NT, preferred_element_type=F32)
    e_ref[...] = dot(u_high, k_high) + (dot(u_high, k_low) + dot(u_low, k_high))


def entry_facts(z, position, atom_ref, count_ref, s):
    atom = atom_ref[s]
    owner = atom // z.owned
    return owner, atom - owner * z.owned, s < count_ref[position]


def contributions(z, position, pj_ref, cell_ref, atom_ref, count_ref, u_ref):
    values = [u_ref[pl.ds(pl.multiple_of(cell_ref[s] * ROWS, ROWS), ROWS), :] for s in range(z.entries)]
    sums = lax.dot_general(
        pj_ref[...], jnp.concatenate(values, axis=0), NT, precision=HIGHEST, preferred_element_type=F32
    )
    sums = jnp.concatenate([sums, jnp.zeros((sums.shape[0], LANES - sums.shape[1]), F32)], axis=1)
    lane, row = iota((ROWS, LANES), 1), iota((ROWS, LANES), 0)
    parts = [jnp.zeros((ROWS, LANES), F32)] * 3
    for s in range(z.entries):
        owner, local, alive = entry_facts(z, position, atom_ref, count_ref, s)
        got = lane_gather(sums[s * ROWS : (s + 1) * ROWS], s * ROWS + lane % ROWS)
        here = (lane // ROWS % ROWS == row) & (lane // z.pairs == local) & alive
        for k in range(3):
            parts[k] = parts[k] + jnp.where(here & (owner == position - 1 + k), got, 0.0)
    return [jnp.sum(part, axis=0, keepdims=True) for part in parts]


def first_kernel(
    z, pos_ref, count_ref, scale_ref, cell_ref, atom_ref, scount_ref, range_ref, rhs_ref, precond_ref, potential_ref,
    halo_a_ref, halo_b_ref, index_ref, corner_ref, k_high_ref, k_low_ref, pj_ref, coupling_ref,
    p_ref, diag_ref, out_ref, e_ref, gamma_ref, u_ref, uw_ref,
):
    position = pos_ref[0]
    even = position % 2 == 0
    a, b = halo_a_ref[...], halo_b_ref[...]
    left, right = jnp.where(even, b, a), jnp.where(even, a, b)
    own = slice(z.rim, z.rim + z.nodes)
    first, last = slice(0, z.rim), slice(z.rim + z.nodes, z.window)
    for where, side in ((first, left), (last, right)):
        p_ref[:, where] = side[:ROWS] * side[ROWS : ROWS + 1]
        diag_ref[0:1, where] = side[ROWS : ROWS + 1]
        diag_ref[1:2, where] = side[ROWS + 1 : ROWS + 2]
    diag_ref[0:1, own] = precond_ref[...]
    diag_ref[1:2, own] = potential_ref[...]
    product = rhs_ref[...] * precond_ref[...]
    p_ref[:, own] = product
    gamma_ref[...] = lanes_by_vector(z, product * rhs_ref[...])
    p_ref[:, z.window :] = jnp.zeros((ROWS, z.reach - z.window), F32)
    gather_cells(z, index_ref, corner_ref, range_ref, p_ref, scale_ref, count_ref[position], u_ref, uw_ref)
    parts = contributions(z, position, pj_ref, cell_ref, atom_ref, scount_ref, u_ref)
    message = jnp.concatenate(parts + [coupling_ref[...]], axis=0)
    for d in range(z.devices):
        out_ref[d] = message
    stiffness_product(k_high_ref, k_low_ref, uw_ref, e_ref)


def second_kernel(
    z, pos_ref, count_ref, scale_ref, cell_ref, atom_ref, scount_ref, range_ref, p_ref, diag_ref, shift_ref, gamma_ref,
    image_ref, halo_a_ref, halo_b_ref, index_ref, corner_ref, k_high_ref, k_low_ref, pj_ref,
    y_ref, q_ref, out_ref, e_ref, u_ref, uw_ref,
):
    position = pos_ref[0]
    even = position % 2 == 0
    a, b = halo_a_ref[...], halo_b_ref[...]
    left, right = jnp.where(even, b, a), jnp.where(even, a, b)
    diagonal = diag_ref[1:2, :] + shift_ref[...]
    y_ref[...] = image_ref[...] + diagonal * p_ref[:, : z.window]
    y_ref[:, : 2 * z.rim] += left
    y_ref[:, z.window - 2 * z.rim :] += right
    q_ref[:, : z.window] = y_ref[...] * diag_ref[0:1, :]
    q_ref[:, z.window :] = jnp.zeros((ROWS, z.reach - z.window), F32)
    own = slice(z.rim, z.rim + z.nodes)
    y, q = y_ref[:, own], q_ref[:, own]
    dots = [
        gamma_ref[...],
        lanes_by_vector(z, y * p_ref[:, own]),
        lanes_by_vector(z, y * q),
    ]
    energy = jnp.sum(q * q * (diag_ref[1:2, own] + shift_ref[...]), axis=1, keepdims=True)
    gather_cells(z, index_ref, corner_ref, range_ref, q_ref, scale_ref, count_ref[position], u_ref, uw_ref)
    parts = contributions(z, position, pj_ref, cell_ref, atom_ref, scount_ref, u_ref)
    stiffness_product(k_high_ref, k_low_ref, uw_ref, e_ref)
    elements = jnp.zeros((ROWS, z.width), F32)
    for c in range(z.slots):
        rows = slice(c * ROWS, (c + 1) * ROWS)
        elements = elements + u_ref[rows, :] * e_ref[rows, :]
    energy = energy + jnp.sum(elements, axis=1, keepdims=True)
    dots.append(lanes_by_vector(z, energy))
    line = dots[0]
    for k in range(1, len(dots)):
        line = line + pltpu.roll(dots[k], k * ROWS, 1)
    message = jnp.concatenate(parts + [line], axis=0)
    for d in range(z.devices):
        out_ref[d] = message


def scatter_kernel(
    z, last, pos_ref, cell_ref, atom_ref, scount_ref, range_ref, sums_ref, coupling_ref, e_in_ref, index_ref,
    corner_ref, pj_ref, *refs,
):
    if last:
        image_ref, send_a_ref, send_b_ref, dots_ref, e_ref, acc_ref = refs
    else:
        image_ref, send_a_ref, send_b_ref, e_ref, acc_ref = refs
    position = pos_ref[0]
    wanted = (
        pltpu.roll(sums_ref[:, 0, :], z.devices - 1, 0) + sums_ref[:, 1, :] + pltpu.roll(sums_ref[:, 2, :], 1, 0)
    )
    coupling = coupling_ref[:, 3, :]
    shape = (z.devices, LANES)
    lane = iota(shape, 1)
    term = jnp.zeros(shape, F32)
    for j in range(z.channels):
        matrix = lane_gather(coupling, lane // ROWS * ROWS + j)
        vector = lane_gather(wanted, lane // z.pairs * z.pairs + j * ROWS + lane % ROWS)
        term = term + matrix * vector
    if last:
        energy = jnp.sum(term * wanted, axis=0, keepdims=True)
        energy = jnp.broadcast_to(energy, (ROWS, LANES))
        step = ROWS
        while step < LANES:
            energy = energy + pltpu.roll(energy, step, 1)
            step *= 2
        line = iota((1, LANES), 1)
        dots_ref[...] = jnp.sum(sums_ref[:, 3, :], axis=0, keepdims=True) + jnp.where(
            line // ROWS == 3, energy[0:1], 0.0
        )
    block = iota(shape, 0)
    small_lane, small_row = iota((ROWS, LANES), 1), iota((ROWS, LANES), 0)
    spread = []
    for s in range(z.entries):
        owner, local, alive = entry_facts(z, position, atom_ref, scount_ref, s)
        mine = jnp.sum(jnp.where(block == owner, term, 0.0), axis=0, keepdims=True)
        got = lane_gather(
            jnp.broadcast_to(mine, (ROWS, LANES)), local * z.pairs + small_lane % ROWS * ROWS + small_row
        )
        spread.append(jnp.where((small_lane // ROWS == s) & alive, got, 0.0)[:, : z.entries * ROWS])
    support = jnp.dot(
        jnp.concatenate(spread, axis=0), pj_ref[...], precision=HIGHEST, preferred_element_type=F32
    )
    e_ref[...] = e_in_ref[...]
    for s in range(z.entries):
        rows = pl.ds(pl.multiple_of(cell_ref[s] * ROWS, ROWS), ROWS)
        e_ref[rows, :] += support[s * ROWS : (s + 1) * ROWS]

    groups = z.window // WIDE
    pair = (2 * ROWS, LANES)
    sub, lane = iota(pair, 0), iota(pair, 1)
    lows = [(sub + k * 2 * ROWS).astype(jnp.int16) for k in range(WIDE // (2 * ROWS))]
    one, none = jnp.ones(pair, BF16), jnp.zeros(pair, BF16)

    def two_parts(value):
        rounded = value.astype(BF16).astype(F32)
        return jnp.concatenate([rounded, value - rounded], axis=0).astype(BF16)

    def hot_rows(index):
        low = (index & (WIDE - 1)).astype(jnp.int16)
        return jnp.concatenate([jnp.where(low == k, one, none) for k in lows], axis=0)

    def masked(high, both, rows):
        high = high.astype(jnp.int16)
        return jnp.concatenate([jnp.where(high == jnp.int16(h), both, none) for h in range(rows)], axis=0)

    def product(lhs, hot):
        return lax.dot_general(lhs, hot, NT, preferred_element_type=F32)

    corners = jnp.zeros((ROWS, LANES), F32)
    end = (z.elem - 1) % LANES
    for c in range(z.slots):
        tiles = e_ref[c * ROWS : (c + 1) * ROWS, :]
        at = (z.tiles - 1) * LANES + end
        corners = jnp.where(small_lane == c, tiles[:, 0:1], corners)
        corners = jnp.where(small_lane == z.slots + c, tiles[:, at : at + 1], corners)
    index = jnp.broadcast_to(corner_ref[...], pair)
    acc_ref[: groups * 2 * ROWS, :] = product(masked(index >> 8, two_parts(corners), groups), hot_rows(index))
    acc_ref[groups * 2 * ROWS :, :] = jnp.zeros((BAND * 2 * ROWS, WIDE), F32)

    def some_cells(g, _):
        cells = [g * z.together + i for i in range(z.together)]
        starts = [range_ref[0, c] >> 8 for c in cells]
        ends = [range_ref[1, c] >> 8 for c in cells]
        passes = functools.reduce(jnp.maximum, [(e - s) // BAND + 1 for s, e in zip(starts, ends)])

        def one_pass(k, _):
            for i, c in enumerate(cells):
                start = jnp.minimum(starts[i] + k * BAND, groups)
                rows = pl.ds(pl.multiple_of(c * ROWS, ROWS), ROWS)
                lhs, hot = [], []
                for t in range(z.tiles):
                    lanes = slice(t * LANES, (t + 1) * LANES)
                    index = jnp.broadcast_to(index_ref[c, :, lanes], pair)
                    value = e_ref[rows, lanes]
                    if t == 0:
                        value = jnp.where(small_lane == 0, 0.0, value)
                    if t == z.tiles - 1:
                        value = jnp.where(small_lane == end, 0.0, value)
                    lhs.append(masked((index >> 8) - start, two_parts(value), BAND))
                    hot.append(hot_rows(index))
                to = pl.ds(pl.multiple_of(start * 2 * ROWS, 2 * ROWS), BAND * 2 * ROWS)
                acc_ref[to, :] += product(jnp.concatenate(lhs, axis=1), jnp.concatenate(hot, axis=1))
            return 0

        lax.fori_loop(0, passes, one_pass, 0)
        return 0

    lax.fori_loop(0, z.slots // z.together, some_cells, 0)
    for h in range(groups):
        at = h * 2 * ROWS
        image_ref[:, h * WIDE : (h + 1) * WIDE] = acc_ref[at : at + ROWS] + acc_ref[at + ROWS : at + 2 * ROWS]
    low_rim, high_rim = image_ref[:, : 2 * z.rim], image_ref[:, z.window - 2 * z.rim :]
    even = position % 2 == 0
    send_a_ref[...] = jnp.where(even, high_rim, low_rim)
    send_b_ref[...] = jnp.where(even, low_rim, high_rim)


def last_kernel(
    z, rhs_ref, p_ref, diag_ref, shift_ref, y_ref, q_ref, image_ref, dots_ref, solution_ref, residual_ref, factor_ref,
):
    own = slice(z.rim, z.rim + z.nodes)
    lane, row = iota((ROWS, LANES), 1), iota((ROWS, LANES), 0)
    line = jnp.broadcast_to(dots_ref[...], (ROWS, LANES))

    def column(k):
        return jnp.sum(jnp.where(lane == k * ROWS + row, line, 0.0), axis=1, keepdims=True)

    gamma, py, qy, qq = (column(k) for k in range(4))
    alpha = gamma / py
    fresh = gamma - 2.0 * alpha * py + alpha * alpha * qy
    beta = fresh / gamma
    more = 1.0 + beta
    step = fresh / (more * more * py - 2.0 * more * alpha * qy + alpha * alpha * qq)
    p, q, y = p_ref[:, own], q_ref[:, own], y_ref[:, own]
    second = image_ref[:, own] + (diag_ref[1:2, own] + shift_ref[...]) * q
    search = (p - alpha * q) + beta * p
    solution_ref[...] = alpha * p + step * search
    residual_ref[...] = (rhs_ref[...] - alpha * y) - step * (more * y - alpha * second)
    factor_ref[...] = jnp.broadcast_to(step * alpha, (ROWS, LANES))


def rim_kernel(z, pos_ref, residual_in_ref, halo_a_ref, halo_b_ref, factor_ref, residual_ref):
    even = pos_ref[0] % 2 == 0
    a, b = halo_a_ref[...], halo_b_ref[...]
    left, right = jnp.where(even, b, a), jnp.where(even, a, b)
    side = jnp.where(pl.program_id(0) == 0, left[:, z.rim :], right[:, : z.rim])
    residual_ref[...] = residual_in_ref[...] + factor_ref[:, 0:1] * side


def on_device(
    rhs, potential, precond, shift, stiffness, cell_scale, conn, cell_count, projector, support_cell, support_atom,
    support_count, atom_matrix,
):
    count = lax.axis_size("dom")
    z = Sizes(count, rhs, conn, projector, atom_matrix)
    position = lax.axis_index("dom")
    even = position % 2 == 0
    pos = position.astype(jnp.int32).reshape(1)
    near = [(i, i ^ 1) for i in range(count)]
    far = [(i, j) for i in range(1, count - 1) for j in [i + 1 if i % 2 else i - 1]]

    def exchange(a, b):
        return lax.ppermute(a, "dom", near), lax.ppermute(b, "dom", far)

    def call(kernel, outs, scratch, specs, *args):
        return pl.pallas_call(
            functools.partial(kernel),
            out_shape=[jax.ShapeDtypeStruct(s, d) for s, d in outs],
            in_specs=specs,
            out_specs=[VMEM] * len(outs),
            scratch_shapes=[pltpu.VMEM(s, d) for s, d in scratch],
        )(*args)

    precond_row, potential_row = precond[None, :], potential[None, :]
    shift_column = shift[:, None]
    packed = jnp.concatenate([rhs, precond_row, potential_row], axis=0)
    head, tail = packed[:, : z.rim], packed[:, z.nodes - z.rim :]
    halo = exchange(jnp.where(even, tail, head), jnp.where(even, head, tail))
    flat_projector = projector.reshape(z.entries * z.channels, z.elem)
    coupling = atom_matrix.reshape(1, LANES)
    middle = conn[:, 1:-1] + z.shift
    ranges = jnp.stack([jnp.min(middle, axis=1), jnp.max(middle, axis=1)])
    corner = jnp.concatenate([conn[:, 0], conn[:, -1]]) + z.shift
    corner = jnp.pad(corner, (0, LANES - 2 * z.slots))[None, :]

    cells = (z.slots * ROWS, z.width)
    window, reach = (z.vectors, z.window), (z.vectors, z.reach)
    message = (z.devices, 4, LANES)
    cell_scratch = [(cells, F32), (cells, F32)]
    square = (z.width, z.width)
    index, k_high, k_low, pj = call(
        functools.partial(prepare_kernel, z),
        [((z.slots, 1, z.width), jnp.int32), (square, BF16), (square, BF16), ((z.entries * ROWS, z.width), F32)],
        [(square, F32)],
        [VMEM] * 3,
        conn, stiffness, flat_projector,
    )
    p, diag, sums, e, gamma = call(
        functools.partial(first_kernel, z),
        [(reach, F32), ((2, z.window), F32), (message, F32), (cells, F32), ((1, LANES), F32)],
        cell_scratch,
        [SMEM] * 7 + [VMEM] * 11,
        pos, cell_count, cell_scale, support_cell, support_atom, support_count, ranges, rhs, precond_row,
        potential_row, *halo, index, corner, k_high, k_low, pj, coupling,
    )
    groups = z.window // WIDE
    scatter_scratch = [(cells, F32), (((groups + BAND) * 2 * ROWS, WIDE), F32)]
    rim = (z.vectors, 2 * z.rim)
    coupled = lax.all_to_all(sums, "dom", 0, 0)
    image, send_a, send_b = call(
        functools.partial(scatter_kernel, z, False),
        [(window, F32), (rim, F32), (rim, F32)],
        scatter_scratch,
        [SMEM] * 5 + [VMEM] * 6,
        pos, support_cell, support_atom, support_count, ranges, coupled, coupled, e, index, corner, pj,
    )
    halo = exchange(send_a, send_b)
    y, q, sums, e = call(
        functools.partial(second_kernel, z),
        [(window, F32), (reach, F32), (message, F32), (cells, F32)],
        cell_scratch,
        [SMEM] * 7 + [VMEM] * 12,
        pos, cell_count, cell_scale, support_cell, support_atom, support_count, ranges, p, diag, shift_column, gamma,
        image, *halo, index, corner, k_high, k_low, pj,
    )
    totals = lax.all_to_all(sums, "dom", 0, 0)
    image, send_a, send_b, dots = call(
        functools.partial(scatter_kernel, z, True),
        [(window, F32), (rim, F32), (rim, F32), ((1, LANES), F32)],
        scatter_scratch,
        [SMEM] * 5 + [VMEM] * 6,
        pos, support_cell, support_atom, support_count, ranges, totals, coupled, e, index, corner, pj,
    )
    halo = exchange(send_a, send_b)
    own = (z.vectors, z.nodes)
    answer, residual, factor = call(
        functools.partial(last_kernel, z),
        [(own, F32), (own, F32), ((ROWS, LANES), F32)],
        [],
        [VMEM] * 8,
        rhs, p, diag, shift_column, y, q, image, dots,
    )
    ends = pl.BlockSpec((ROWS, z.rim), lambda i: (0, i * (z.nodes // z.rim - 1)))
    residual = pl.pallas_call(
        functools.partial(rim_kernel, z),
        grid=(2,),
        out_shape=jax.ShapeDtypeStruct(own, F32),
        in_specs=[SMEM, ends, VMEM, VMEM, VMEM],
        out_specs=ends,
        input_output_aliases={1: 0},
    )(pos, residual, *halo, factor)
    return answer, residual


def solution(mesh):
    placed = (
        P(None, "dom"),
        P("dom"),
        P("dom"),
        P(),
        P(),
        P("dom"),
        P("dom", None),
        P(),
        P("dom", None, None),
        P("dom"),
        P("dom"),
        P(),
        P("dom", None, None),
    )
    return jax.shard_map(
        on_device,
        mesh=mesh,
        in_specs=placed,
        out_specs=(P(None, "dom"), P(None, "dom")),
        check_vma=False,
    )
```

```python
import functools

import jax
import jax.numpy as jnp
from jax import lax
from jax.experimental import pallas as pl
from jax.experimental.pallas import tpu as pltpu
from jax.sharding import PartitionSpec as P

LANES = 128
ROWS = 8
WIDE = 256
CHAINS = 4
SPAN = 14
BAND = 8
TOGETHER = 4
F32 = jnp.float32
BF16 = jnp.bfloat16
HIGHEST = lax.Precision.HIGHEST
NT = (((1,), (1,)), ((), ()))
VMEM = pl.BlockSpec(memory_space=pltpu.VMEM)
SMEM = pl.BlockSpec(memory_space=pltpu.SMEM)


def round_up(value, step):
    return -(-value // step) * step


class Sizes:
    def __init__(self, count, rhs, conn, projector, atom_matrix):
        self.devices = count
        self.vectors, self.nodes = rhs.shape
        self.slots, self.elem = conn.shape
        self.entries, self.channels = projector.shape[:2]
        self.owned = atom_matrix.shape[0]
        self.ghost = self.nodes // 16
        self.rim = round_up(self.ghost, WIDE)
        self.shift = self.rim - self.ghost
        self.window = self.nodes + 2 * self.rim
        self.width = round_up(self.elem, LANES)
        self.tiles = self.width // LANES
        self.pairs = self.channels * self.vectors
        self.reach = self.window + SPAN * LANES
        self.together = TOGETHER if self.slots % TOGETHER == 0 else 1
        assert self.vectors == ROWS and self.channels == ROWS and 2 * self.slots <= LANES
        assert self.nodes % WIDE == 0 and self.owned * self.pairs == LANES


def lane_gather(values, index):
    return jnp.take_along_axis(values, index, axis=1, mode="promise_in_bounds")


def iota(shape, dim):
    return lax.broadcasted_iota(jnp.int32, shape, dim)


def split(values):
    high = values.astype(BF16)
    return high, (values - high.astype(F32)).astype(BF16)


def lanes_by_vector(z, values):
    total = jnp.sum(values, axis=1, keepdims=True)
    spread = jnp.broadcast_to(total, (ROWS, LANES))
    return jnp.sum(jnp.where(iota((ROWS, LANES), 1) == iota((ROWS, LANES), 0), spread, 0.0), axis=0, keepdims=True)


def prepare_kernel(
    z, conn_ref, stiffness_ref, projector_ref, index_ref, corner_ref, k_high_ref, k_low_ref, pj_ref, k_ref
):
    line = iota((1, LANES), 1)
    corner = jnp.zeros((1, LANES), jnp.int32)
    index_ref[...] = jnp.zeros_like(index_ref)
    for c in range(z.slots):
        row = conn_ref[c : c + 1, :] + z.shift
        index_ref[c, :, : z.elem] = row
        corner = jnp.where(line == c, row[:, :1], corner)
        corner = jnp.where(line == z.slots + c, row[:, z.elem - 1 :], corner)
    corner_ref[...] = corner
    k_ref[...] = jnp.zeros_like(k_ref)
    k_ref[: z.elem, : z.elem] = stiffness_ref[...]
    k_high_ref[...], k_low_ref[...] = split(k_ref[...])
    pj_ref[...] = jnp.zeros_like(pj_ref)
    pj_ref[:, : z.elem] = projector_ref[...]


def gather_cells(
    z, index_ref, corner_ref, low_ref, high_ref, window_ref, scale_ref, live, u_ref, uw_ref
):
    total = z.window // LANES
    tile = (ROWS, LANES)
    corner = jnp.broadcast_to(corner_ref[...], tile)
    low, high = corner & (LANES - 1), corner >> 7
    chains = [jnp.zeros(tile, F32)] * CHAINS
    for h in range(total):
        got = lane_gather(window_ref[:, h * LANES : (h + 1) * LANES], low)
        chains[h % CHAINS] = jnp.where(high == h, got, chains[h % CHAINS])
    corners = functools.reduce(jnp.add, chains)
    lane = iota(tile, 1)
    last = (z.elem - 1) % LANES

    def some_cells(g, _):
        cells = [g * z.together + i for i in range(z.together)]
        starts = [(low_ref[c] + z.shift) >> 7 for c in cells]
        ends = [(high_ref[c] + z.shift) >> 7 for c in cells]
        passes = functools.reduce(jnp.maximum, [(e - s) // SPAN + 1 for s, e in zip(starts, ends)])

        def one_pass(k, values):
            values = list(values)
            for i, c in enumerate(cells):
                start = jnp.minimum(starts[i] + k * SPAN, total)
                for t in range(z.tiles):
                    index = jnp.broadcast_to(index_ref[c, :, t * LANES : (t + 1) * LANES], tile)
                    low, high = index & (LANES - 1), (index >> 7) - start
                    value = values[i * z.tiles + t]
                    for h in range(SPAN):
                        at = pl.ds(pl.multiple_of((start + h) * LANES, LANES), LANES)
                        value = jnp.where(high == h, lane_gather(window_ref[:, at], low), value)
                    values[i * z.tiles + t] = value
            return tuple(values)

        values = lax.fori_loop(0, passes, one_pass, (jnp.zeros(tile, F32),) * (z.together * z.tiles))
        for i, c in enumerate(cells):
            weight = jnp.where(c < live, scale_ref[c], 0.0)
            rows = pl.ds(pl.multiple_of(c * ROWS, ROWS), ROWS)
            for t in range(z.tiles):
                value = values[i * z.tiles + t]
                if t == 0:
                    value = jnp.where(lane == 0, lane_gather(corners, jnp.full(tile, 0, jnp.int32) + c), value)
                if t == z.tiles - 1:
                    got = lane_gather(corners, jnp.full(tile, z.slots, jnp.int32) + c)
                    value = jnp.where(lane == last, got, value)
                u_ref[rows, t * LANES : (t + 1) * LANES] = value
                uw_ref[rows, t * LANES : (t + 1) * LANES] = value * weight
        return 0

    lax.fori_loop(0, z.slots // z.together, some_cells, 0)


def stiffness_product(k_high_ref, k_low_ref, uw_ref, e_ref):
    k_high, k_low = k_high_ref[...], k_low_ref[...]
    u_high, u_low = split(uw_ref[...])
    dot = functools.partial(lax.dot_general, dimension_numbers=NT, preferred_element_type=F32)
    e_ref[...] = dot(u_high, k_high) + (dot(u_high, k_low) + dot(u_low, k_high))


def entry_facts(z, position, atom_ref, count_ref, s):
    atom = atom_ref[s]
    owner = atom // z.owned
    return owner, atom - owner * z.owned, s < count_ref[position]


def contributions(z, position, pj_ref, cell_ref, atom_ref, count_ref, u_ref):
    values = [u_ref[pl.ds(pl.multiple_of(cell_ref[s] * ROWS, ROWS), ROWS), :] for s in range(z.entries)]
    sums = lax.dot_general(
        pj_ref[...], jnp.concatenate(values, axis=0), NT, precision=HIGHEST, preferred_element_type=F32
    )
    sums = jnp.concatenate([sums, jnp.zeros((sums.shape[0], LANES - sums.shape[1]), F32)], axis=1)
    lane, row = iota((ROWS, LANES), 1), iota((ROWS, LANES), 0)
    parts = [jnp.zeros((ROWS, LANES), F32)] * 3
    for s in range(z.entries):
        owner, local, alive = entry_facts(z, position, atom_ref, count_ref, s)
        got = lane_gather(sums[s * ROWS : (s + 1) * ROWS], s * ROWS + lane % ROWS)
        here = (lane // ROWS % ROWS == row) & (lane // z.pairs == local) & alive
        for k in range(3):
            parts[k] = parts[k] + jnp.where(here & (owner == position - 1 + k), got, 0.0)
    return [jnp.sum(part, axis=0, keepdims=True) for part in parts]


def sides(position, near, far):
    even = position % 2 == 0
    return jnp.where(even, far, near), jnp.where(even, near, far)


def first_kernel(
    z, pos_ref, count_ref, scale_ref, cell_ref, atom_ref, scount_ref, low_ref, high_ref, rhs_ref, precond_ref,
    potential_ref, halo_a_ref, halo_b_ref, index_ref, corner_ref, k_high_ref, k_low_ref, pj_ref, coupling_ref,
    p_ref, diag_ref, out_ref, e_ref, gamma_ref, u_ref, uw_ref,
):
    position = pos_ref[0]
    own = slice(z.rim, z.rim + z.nodes)
    p_ref[:, : z.rim], p_ref[:, z.rim + z.nodes : z.window] = sides(position, halo_a_ref[...], halo_b_ref[...])
    diag_ref[...] = jnp.zeros_like(diag_ref)
    diag_ref[0:1, own] = precond_ref[...]
    diag_ref[1:2, own] = potential_ref[...]
    product = rhs_ref[...] * precond_ref[...]
    p_ref[:, own] = product
    gamma_ref[...] = lanes_by_vector(z, product * rhs_ref[...])
    p_ref[:, z.window :] = jnp.zeros((ROWS, z.reach - z.window), F32)
    gather_cells(z, index_ref, corner_ref, low_ref, high_ref, p_ref, scale_ref, count_ref[position], u_ref, uw_ref)
    parts = contributions(z, position, pj_ref, cell_ref, atom_ref, scount_ref, u_ref)
    small_lane, small_row = iota((ROWS, LANES), 1), iota((ROWS, LANES), 0)
    matrices = jnp.zeros((ROWS, LANES), F32)
    for atom in range(z.owned):
        block = jnp.concatenate([coupling_ref[atom], jnp.zeros((ROWS, LANES - z.channels), F32)], axis=1)
        got = lane_gather(block, small_lane % ROWS)
        matrices = jnp.where(small_lane // ROWS == atom * ROWS + small_row, got, matrices)
    message = jnp.concatenate(parts + [jnp.sum(matrices, axis=0, keepdims=True)], axis=0)
    for d in range(z.devices):
        out_ref[d] = message
    stiffness_product(k_high_ref, k_low_ref, uw_ref, e_ref)


def second_kernel(
    z, pos_ref, count_ref, scale_ref, cell_ref, atom_ref, scount_ref, low_ref, high_ref, p_ref, diag_in_ref, shift_ref,
    gamma_ref, image_ref, halo_a_ref, halo_b_ref, index_ref, corner_ref, k_high_ref, k_low_ref, pj_ref,
    y_ref, q_ref, out_ref, e_ref, diag_ref, u_ref, uw_ref,
):
    position = pos_ref[0]
    left, right = sides(position, halo_a_ref[...], halo_b_ref[...])
    own = slice(z.rim, z.rim + z.nodes)
    diag_ref[:, own] = diag_in_ref[:, own]
    diag_ref[:, : z.rim] = left[ROWS : ROWS + 2, : z.rim]
    diag_ref[:, z.rim + z.nodes :] = right[ROWS : ROWS + 2, z.rim :]
    y_ref[...] = image_ref[...] + (diag_ref[1:2, :] + shift_ref[...]) * p_ref[:, : z.window]
    y_ref[:, : 2 * z.rim] += left[:ROWS]
    y_ref[:, z.window - 2 * z.rim :] += right[:ROWS]
    q_ref[:, : z.window] = y_ref[...] * diag_ref[0:1, :]
    q_ref[:, z.window :] = jnp.zeros((ROWS, z.reach - z.window), F32)
    y, q = y_ref[:, own], q_ref[:, own]
    dots = [
        gamma_ref[...],
        lanes_by_vector(z, y * p_ref[:, own]),
        lanes_by_vector(z, y * q),
    ]
    energy = jnp.sum(q * q * (diag_ref[1:2, own] + shift_ref[...]), axis=1, keepdims=True)
    gather_cells(z, index_ref, corner_ref, low_ref, high_ref, q_ref, scale_ref, count_ref[position], u_ref, uw_ref)
    parts = contributions(z, position, pj_ref, cell_ref, atom_ref, scount_ref, u_ref)
    stiffness_product(k_high_ref, k_low_ref, uw_ref, e_ref)
    elements = jnp.zeros((ROWS, z.width), F32)
    for c in range(z.slots):
        rows = slice(c * ROWS, (c + 1) * ROWS)
        elements = elements + u_ref[rows, :] * e_ref[rows, :]
    energy = energy + jnp.sum(elements, axis=1, keepdims=True)
    dots.append(lanes_by_vector(z, energy))
    line = dots[0]
    for k in range(1, len(dots)):
        line = line + pltpu.roll(dots[k], k * ROWS, 1)
    message = jnp.concatenate(parts + [line], axis=0)
    for d in range(z.devices):
        out_ref[d] = message


def scatter_kernel(
    z, last, pos_ref, cell_ref, atom_ref, scount_ref, low_ref, high_ref, sums_ref, coupling_ref, e_in_ref, index_ref,
    corner_ref, pj_ref, diag_ref, *refs,
):
    if last:
        image_ref, send_a_ref, send_b_ref, dots_ref, e_ref, acc_ref = refs
    else:
        image_ref, send_a_ref, send_b_ref, e_ref, acc_ref = refs
    position = pos_ref[0]
    wanted = (
        pltpu.roll(sums_ref[:, 0, :], z.devices - 1, 0) + sums_ref[:, 1, :] + pltpu.roll(sums_ref[:, 2, :], 1, 0)
    )
    coupling = coupling_ref[:, 3, :]
    shape = (z.devices, LANES)
    lane = iota(shape, 1)
    term = jnp.zeros(shape, F32)
    for j in range(z.channels):
        matrix = lane_gather(coupling, lane // ROWS * ROWS + j)
        vector = lane_gather(wanted, lane // z.pairs * z.pairs + j * ROWS + lane % ROWS)
        term = term + matrix * vector
    if last:
        energy = jnp.sum(term * wanted, axis=0, keepdims=True)
        energy = jnp.broadcast_to(energy, (ROWS, LANES))
        step = ROWS
        while step < LANES:
            energy = energy + pltpu.roll(energy, step, 1)
            step *= 2
        line = iota((1, LANES), 1)
        dots_ref[...] = jnp.sum(sums_ref[:, 3, :], axis=0, keepdims=True) + jnp.where(
            line // ROWS == 3, energy[0:1], 0.0
        )
    block = iota(shape, 0)
    small_lane, small_row = iota((ROWS, LANES), 1), iota((ROWS, LANES), 0)
    spread = []
    for s in range(z.entries):
        owner, local, alive = entry_facts(z, position, atom_ref, scount_ref, s)
        mine = jnp.sum(jnp.where(block == owner, term, 0.0), axis=0, keepdims=True)
        got = lane_gather(
            jnp.broadcast_to(mine, (ROWS, LANES)), local * z.pairs + small_lane % ROWS * ROWS + small_row
        )
        spread.append(jnp.where((small_lane // ROWS == s) & alive, got, 0.0)[:, : z.entries * ROWS])
    support = jnp.dot(
        jnp.concatenate(spread, axis=0), pj_ref[...], precision=HIGHEST, preferred_element_type=F32
    )
    e_ref[...] = e_in_ref[...]
    for s in range(z.entries):
        rows = pl.ds(pl.multiple_of(cell_ref[s] * ROWS, ROWS), ROWS)
        e_ref[rows, :] += support[s * ROWS : (s + 1) * ROWS]

    groups = z.window // WIDE
    pair = (2 * ROWS, LANES)
    sub, lane = iota(pair, 0), iota(pair, 1)
    lows = [(sub + k * 2 * ROWS).astype(jnp.int16) for k in range(WIDE // (2 * ROWS))]
    one, none = jnp.ones(pair, BF16), jnp.zeros(pair, BF16)

    def two_parts(value):
        rounded = value.astype(BF16).astype(F32)
        return jnp.concatenate([rounded, value - rounded], axis=0).astype(BF16)

    def hot_rows(index):
        low = (index & (WIDE - 1)).astype(jnp.int16)
        return jnp.concatenate([jnp.where(low == k, one, none) for k in lows], axis=0)

    def masked(high, both, rows):
        high = high.astype(jnp.int16)
        return jnp.concatenate([jnp.where(high == jnp.int16(h), both, none) for h in range(rows)], axis=0)

    def product(lhs, hot):
        return lax.dot_general(lhs, hot, NT, preferred_element_type=F32)

    corners = jnp.zeros((ROWS, LANES), F32)
    end = (z.elem - 1) % LANES
    for c in range(z.slots):
        tiles = e_ref[c * ROWS : (c + 1) * ROWS, :]
        at = (z.tiles - 1) * LANES + end
        corners = jnp.where(small_lane == c, tiles[:, 0:1], corners)
        corners = jnp.where(small_lane == z.slots + c, tiles[:, at : at + 1], corners)
    index = jnp.broadcast_to(corner_ref[...], pair)
    acc_ref[: groups * 2 * ROWS, :] = product(masked(index >> 8, two_parts(corners), groups), hot_rows(index))
    acc_ref[groups * 2 * ROWS :, :] = jnp.zeros((BAND * 2 * ROWS, WIDE), F32)

    def some_cells(g, _):
        cells = [g * z.together + i for i in range(z.together)]
        starts = [(low_ref[c] + z.shift) >> 8 for c in cells]
        ends = [(high_ref[c] + z.shift) >> 8 for c in cells]
        passes = functools.reduce(jnp.maximum, [(e - s) // BAND + 1 for s, e in zip(starts, ends)])

        def one_pass(k, _):
            for i, c in enumerate(cells):
                start = jnp.minimum(starts[i] + k * BAND, groups)
                rows = pl.ds(pl.multiple_of(c * ROWS, ROWS), ROWS)
                lhs, hot = [], []
                for t in range(z.tiles):
                    lanes = slice(t * LANES, (t + 1) * LANES)
                    index = jnp.broadcast_to(index_ref[c, :, lanes], pair)
                    value = e_ref[rows, lanes]
                    if t == 0:
                        value = jnp.where(small_lane == 0, 0.0, value)
                    if t == z.tiles - 1:
                        value = jnp.where(small_lane == end, 0.0, value)
                    lhs.append(masked((index >> 8) - start, two_parts(value), BAND))
                    hot.append(hot_rows(index))
                to = pl.ds(pl.multiple_of(start * 2 * ROWS, 2 * ROWS), BAND * 2 * ROWS)
                acc_ref[to, :] += product(jnp.concatenate(lhs, axis=1), jnp.concatenate(hot, axis=1))
            return 0

        lax.fori_loop(0, passes, one_pass, 0)
        return 0

    lax.fori_loop(0, z.slots // z.together, some_cells, 0)
    for h in range(groups):
        at = h * 2 * ROWS
        image_ref[:, h * WIDE : (h + 1) * WIDE] = acc_ref[at : at + ROWS] + acc_ref[at + ROWS : at + 2 * ROWS]
    even = position % 2 == 0
    ends = [slice(0, 2 * z.rim), slice(z.window - 2 * z.rim, z.window)]
    for source_ref, rows in ((image_ref, slice(0, ROWS)),) + (() if last else ((diag_ref, slice(ROWS, ROWS + 2)),)):
        low_rim, high_rim = (source_ref[:, end] for end in ends)
        send_a_ref[rows, :] = jnp.where(even, high_rim, low_rim)
        send_b_ref[rows, :] = jnp.where(even, low_rim, high_rim)


def last_kernel(
    z, rhs_ref, p_ref, diag_ref, shift_ref, y_ref, q_ref, image_ref, dots_ref, solution_ref, residual_ref, factor_ref,
):
    own = slice(z.rim, z.rim + z.nodes)
    lane, row = iota((ROWS, LANES), 1), iota((ROWS, LANES), 0)
    line = jnp.broadcast_to(dots_ref[...], (ROWS, LANES))

    def column(k):
        return jnp.sum(jnp.where(lane == k * ROWS + row, line, 0.0), axis=1, keepdims=True)

    gamma, py, qy, qq = (column(k) for k in range(4))
    alpha = gamma / py
    fresh = gamma - 2.0 * alpha * py + alpha * alpha * qy
    beta = fresh / gamma
    more = 1.0 + beta
    step = fresh / (more * more * py - 2.0 * more * alpha * qy + alpha * alpha * qq)
    p, q, y = p_ref[:, own], q_ref[:, own], y_ref[:, own]
    second = image_ref[:, own] + (diag_ref[1:2, own] + shift_ref[...]) * q
    search = (p - alpha * q) + beta * p
    solution_ref[...] = alpha * p + step * search
    residual_ref[...] = (rhs_ref[...] - alpha * y) - step * (more * y - alpha * second)
    factor_ref[...] = jnp.broadcast_to(step * alpha, (ROWS, LANES))


def on_device(
    rhs, potential, precond, shift, stiffness, cell_scale, conn, cell_count, projector, support_cell, support_atom,
    support_count, atom_matrix,
):
    count = lax.axis_size("dom")
    z = Sizes(count, rhs, conn, projector, atom_matrix)
    position = lax.axis_index("dom")
    even = position % 2 == 0
    pos = position.astype(jnp.int32).reshape(1)
    near = [(i, i ^ 1) for i in range(count)]
    far = [(i, j) for i in range(1, count - 1) for j in [i + 1 if i % 2 else i - 1]]

    def exchange(a, b):
        return lax.ppermute(a, "dom", near), lax.ppermute(b, "dom", far)

    def call(kernel, outs, scratch, specs, *args, final=False):
        args = [
            x if spec is SMEM else pltpu.with_memory_space_constraint(x, pltpu.VMEM) for x, spec in zip(args, specs)
        ]
        shapes = [jax.ShapeDtypeStruct(s, d) if final else pltpu.VMEM(s, d) for s, d in outs]
        return pl.pallas_call(
            kernel,
            out_shape=shapes,
            in_specs=specs,
            out_specs=[VMEM] * len(outs),
            scratch_shapes=[pltpu.VMEM(s, d) for s, d in scratch],
            compiler_params=pltpu.CompilerParams(vmem_limit_bytes=16 * 1024 * 1024),
        )(*args)

    precond_row, potential_row = precond[None, :], potential[None, :]
    shift_column = shift[:, None]
    head = rhs[:, : z.rim] * precond[: z.rim]
    tail = rhs[:, z.nodes - z.rim :] * precond[z.nodes - z.rim :]
    halo = exchange(jnp.where(even, tail, head), jnp.where(even, head, tail))
    flat_projector = projector.reshape(z.entries * z.channels, z.elem)
    middle = conn[:, 1:-1]
    ranges = jnp.min(middle, axis=1), jnp.max(middle, axis=1)

    cells = (z.slots * ROWS, z.width)
    window, reach = (z.vectors, z.window), (z.vectors, z.reach)
    message = (z.devices, 4, LANES)
    cell_scratch = [(cells, F32), (cells, F32)]
    square = (z.width, z.width)
    index, corner, k_high, k_low, pj = call(
        functools.partial(prepare_kernel, z),
        [((z.slots, 1, z.width), jnp.int32), ((1, LANES), jnp.int32), (square, BF16), (square, BF16),
         ((z.entries * ROWS, z.width), F32)],
        [(square, F32)],
        [VMEM] * 3,
        conn, stiffness, flat_projector,
    )
    p, diag, sums, e, gamma = call(
        functools.partial(first_kernel, z),
        [(reach, F32), ((2, z.window), F32), (message, F32), (cells, F32), ((1, LANES), F32)],
        cell_scratch,
        [SMEM] * 8 + [VMEM] * 11,
        pos, cell_count, cell_scale, support_cell, support_atom, support_count, *ranges, rhs, precond_row,
        potential_row, *halo, index, corner, k_high, k_low, pj, atom_matrix,
    )
    groups = z.window // WIDE
    scatter_scratch = [(cells, F32), (((groups + BAND) * 2 * ROWS, WIDE), F32)]
    rim, more_rim = (z.vectors, 2 * z.rim), (z.vectors + 2, 2 * z.rim)
    coupled = lax.all_to_all(sums, "dom", 0, 0)
    image, send_a, send_b = call(
        functools.partial(scatter_kernel, z, False),
        [(window, F32), (more_rim, F32), (more_rim, F32)],
        scatter_scratch,
        [SMEM] * 6 + [VMEM] * 7,
        pos, support_cell, support_atom, support_count, *ranges, coupled, coupled, e, index, corner, pj, diag,
    )
    halo = exchange(send_a, send_b)
    y, q, sums, e = call(
        functools.partial(second_kernel, z),
        [(window, F32), (reach, F32), (message, F32), (cells, F32)],
        [((2, z.window), F32)] + cell_scratch,
        [SMEM] * 8 + [VMEM] * 12,
        pos, cell_count, cell_scale, support_cell, support_atom, support_count, *ranges, p, diag, shift_column, gamma,
        image, *halo, index, corner, k_high, k_low, pj,
    )
    totals = lax.all_to_all(sums, "dom", 0, 0)
    image, send_a, send_b, dots = call(
        functools.partial(scatter_kernel, z, True),
        [(window, F32), (rim, F32), (rim, F32), ((1, LANES), F32)],
        scatter_scratch,
        [SMEM] * 6 + [VMEM] * 7,
        pos, support_cell, support_atom, support_count, *ranges, totals, coupled, e, index, corner, pj, diag,
    )
    halo = exchange(send_a, send_b)
    own = (z.vectors, z.nodes)
    answer, residual, factor = call(
        functools.partial(last_kernel, z),
        [(own, F32), (own, F32), ((ROWS, LANES), F32)],
        [],
        [VMEM] * 8,
        rhs, p, diag, shift_column, y, q, image, dots, final=True,
    )
    left, right = sides(position, *halo)
    residual = residual.at[:, : z.rim].add(factor[:, :1] * left[:, z.rim :])
    residual = residual.at[:, z.nodes - z.rim :].add(factor[:, :1] * right[:, : z.rim])
    return answer, residual


def solution(mesh):
    placed = (
        P(None, "dom"),
        P("dom"),
        P("dom"),
        P(),
        P(),
        P("dom"),
        P("dom", None),
        P(),
        P("dom", None, None),
        P("dom"),
        P("dom"),
        P(),
        P("dom", None, None),
    )
    return jax.shard_map(
        on_device,
        mesh=mesh,
        in_specs=placed,
        out_specs=(P(None, "dom"), P(None, "dom")),
        check_vma=False,
    )
```

```python
import functools

import jax
import jax.numpy as jnp
from jax import lax
from jax.experimental import pallas as pl
from jax.experimental.pallas import tpu as pltpu
from jax.sharding import PartitionSpec as P

LANES = 128
ROWS = 8
WIDE = 256
CHAINS = 4
SPAN = 14
BAND = 8
TOGETHER = 4
F32 = jnp.float32
BF16 = jnp.bfloat16
HIGHEST = lax.Precision.HIGHEST
NT = (((1,), (1,)), ((), ()))
VMEM = pl.BlockSpec(memory_space=pltpu.VMEM)
SMEM = pl.BlockSpec(memory_space=pltpu.SMEM)


def round_up(value, step):
    return -(-value // step) * step


class Sizes:
    def __init__(self, count, rhs, conn, projector, atom_matrix):
        self.devices = count
        self.vectors, self.nodes = rhs.shape
        self.slots, self.elem = conn.shape
        self.entries, self.channels = projector.shape[:2]
        self.owned = atom_matrix.shape[0]
        self.ghost = self.nodes // 16
        self.rim = round_up(self.ghost, WIDE)
        self.shift = self.rim - self.ghost
        self.window = self.nodes + 2 * self.rim
        self.width = round_up(self.elem, LANES)
        self.tiles = self.width // LANES
        self.pairs = self.channels * self.vectors
        self.reach = self.window + SPAN * LANES
        self.together = TOGETHER if self.slots % TOGETHER == 0 else 1
        assert self.vectors == ROWS and self.channels == ROWS and 2 * self.slots <= LANES
        assert self.nodes % WIDE == 0 and self.owned * self.pairs == LANES


def lane_gather(values, index):
    return jnp.take_along_axis(values, index, axis=1, mode="promise_in_bounds")


def iota(shape, dim):
    return lax.broadcasted_iota(jnp.int32, shape, dim)


def split(values):
    high = values.astype(BF16)
    return high, (values - high.astype(F32)).astype(BF16)


def lanes_by_vector(z, values):
    total = jnp.sum(values, axis=1, keepdims=True)
    spread = jnp.broadcast_to(total, (ROWS, LANES))
    return jnp.sum(jnp.where(iota((ROWS, LANES), 1) == iota((ROWS, LANES), 0), spread, 0.0), axis=0, keepdims=True)


def prepare_kernel(
    z, conn_ref, stiffness_ref, projector_ref, index_ref, corner_ref, k_high_ref, k_low_ref, pj_ref, k_ref
):
    line = iota((1, LANES), 1)
    corner = jnp.zeros((1, LANES), jnp.int32)
    index_ref[...] = jnp.zeros_like(index_ref)
    for c in range(z.slots):
        row = conn_ref[c : c + 1, :] + z.shift
        index_ref[c, :, : z.elem] = row
        corner = jnp.where(line == c, row[:, :1], corner)
        corner = jnp.where(line == z.slots + c, row[:, z.elem - 1 :], corner)
    corner_ref[...] = corner
    k_ref[...] = jnp.zeros_like(k_ref)
    k_ref[: z.elem, : z.elem] = stiffness_ref[...]
    k_high_ref[...], k_low_ref[...] = split(k_ref[...])
    pj_ref[...] = jnp.zeros_like(pj_ref)
    pj_ref[:, : z.elem] = projector_ref[...]


def gather_cells(
    z, index_ref, corner_ref, low_ref, high_ref, window_ref, scale_ref, live, u_ref, uw_ref
):
    total = z.window // LANES
    tile = (ROWS, LANES)
    corner = jnp.broadcast_to(corner_ref[...], tile)
    low, high = corner & (LANES - 1), corner >> 7
    chains = [jnp.zeros(tile, F32)] * CHAINS
    for h in range(total):
        got = lane_gather(window_ref[:, h * LANES : (h + 1) * LANES], low)
        chains[h % CHAINS] = jnp.where(high == h, got, chains[h % CHAINS])
    corners = functools.reduce(jnp.add, chains)
    lane = iota(tile, 1)
    last = (z.elem - 1) % LANES

    def some_cells(g, _):
        cells = [g * z.together + i for i in range(z.together)]
        starts = [(low_ref[c] + z.shift) >> 7 for c in cells]
        ends = [(high_ref[c] + z.shift) >> 7 for c in cells]
        passes = functools.reduce(jnp.maximum, [(e - s) // SPAN + 1 for s, e in zip(starts, ends)])

        def one_pass(k, values):
            values = list(values)
            for i, c in enumerate(cells):
                start = jnp.minimum(starts[i] + k * SPAN, total)
                for t in range(z.tiles):
                    index = jnp.broadcast_to(index_ref[c, :, t * LANES : (t + 1) * LANES], tile)
                    low, high = index & (LANES - 1), (index >> 7) - start
                    value = values[i * z.tiles + t]
                    for h in range(SPAN):
                        at = pl.ds(pl.multiple_of((start + h) * LANES, LANES), LANES)
                        value = jnp.where(high == h, lane_gather(window_ref[:, at], low), value)
                    values[i * z.tiles + t] = value
            return tuple(values)

        values = lax.fori_loop(0, passes, one_pass, (jnp.zeros(tile, F32),) * (z.together * z.tiles))
        for i, c in enumerate(cells):
            weight = jnp.where(c < live, scale_ref[c], 0.0)
            rows = pl.ds(pl.multiple_of(c * ROWS, ROWS), ROWS)
            for t in range(z.tiles):
                value = values[i * z.tiles + t]
                if t == 0:
                    value = jnp.where(lane == 0, lane_gather(corners, jnp.full(tile, 0, jnp.int32) + c), value)
                if t == z.tiles - 1:
                    got = lane_gather(corners, jnp.full(tile, z.slots, jnp.int32) + c)
                    value = jnp.where(lane == last, got, value)
                u_ref[rows, t * LANES : (t + 1) * LANES] = value
                uw_ref[rows, t * LANES : (t + 1) * LANES] = value * weight
        return 0

    lax.fori_loop(0, z.slots // z.together, some_cells, 0)


def stiffness_product(k_high_ref, k_low_ref, uw_ref, e_ref):
    k_high, k_low = k_high_ref[...], k_low_ref[...]
    u_high, u_low = split(uw_ref[...])
    dot = functools.partial(lax.dot_general, dimension_numbers=NT, preferred_element_type=F32)
    e_ref[...] = dot(u_high, k_high) + (dot(u_high, k_low) + dot(u_low, k_high))


def entry_facts(z, position, atom_ref, count_ref, s):
    atom = atom_ref[s]
    owner = atom // z.owned
    return owner, atom - owner * z.owned, s < count_ref[position]


def contributions(z, position, pj_ref, cell_ref, atom_ref, count_ref, u_ref):
    values = [u_ref[pl.ds(pl.multiple_of(cell_ref[s] * ROWS, ROWS), ROWS), :] for s in range(z.entries)]
    sums = lax.dot_general(
        pj_ref[...], jnp.concatenate(values, axis=0), NT, precision=HIGHEST, preferred_element_type=F32
    )
    sums = jnp.concatenate([sums, jnp.zeros((sums.shape[0], LANES - sums.shape[1]), F32)], axis=1)
    lane, row = iota((ROWS, LANES), 1), iota((ROWS, LANES), 0)
    parts = [jnp.zeros((ROWS, LANES), F32)] * 3
    for s in range(z.entries):
        owner, local, alive = entry_facts(z, position, atom_ref, count_ref, s)
        got = lane_gather(sums[s * ROWS : (s + 1) * ROWS], s * ROWS + lane % ROWS)
        here = (lane // ROWS % ROWS == row) & (lane // z.pairs == local) & alive
        for k in range(3):
            parts[k] = parts[k] + jnp.where(here & (owner == position - 1 + k), got, 0.0)
    return [jnp.sum(part, axis=0, keepdims=True) for part in parts]


def sides(position, near, far):
    even = position % 2 == 0
    return jnp.where(even, far, near), jnp.where(even, near, far)


def first_kernel(
    z, pos_ref, count_ref, scale_ref, cell_ref, atom_ref, scount_ref, low_ref, high_ref, rhs_ref, precond_ref,
    potential_ref, halo_a_ref, halo_b_ref, index_ref, corner_ref, pj_ref, coupling_ref,
    p_ref, diag_ref, out_ref, uw_ref, gamma_ref, u_ref,
):
    position = pos_ref[0]
    own = slice(z.rim, z.rim + z.nodes)
    p_ref[:, : z.rim], p_ref[:, z.rim + z.nodes : z.window] = sides(position, halo_a_ref[...], halo_b_ref[...])
    diag_ref[...] = jnp.zeros_like(diag_ref)
    diag_ref[0:1, own] = precond_ref[...]
    diag_ref[1:2, own] = potential_ref[...]
    product = rhs_ref[...] * precond_ref[...]
    p_ref[:, own] = product
    gamma_ref[...] = lanes_by_vector(z, product * rhs_ref[...])
    p_ref[:, z.window :] = jnp.zeros((ROWS, z.reach - z.window), F32)
    gather_cells(z, index_ref, corner_ref, low_ref, high_ref, p_ref, scale_ref, count_ref[position], u_ref, uw_ref)
    parts = contributions(z, position, pj_ref, cell_ref, atom_ref, scount_ref, u_ref)
    small_lane, small_row = iota((ROWS, LANES), 1), iota((ROWS, LANES), 0)
    matrices = jnp.zeros((ROWS, LANES), F32)
    for atom in range(z.owned):
        block = jnp.concatenate([coupling_ref[atom], jnp.zeros((ROWS, LANES - z.channels), F32)], axis=1)
        got = lane_gather(block, small_lane % ROWS)
        matrices = jnp.where(small_lane // ROWS == atom * ROWS + small_row, got, matrices)
    message = jnp.concatenate(parts + [jnp.sum(matrices, axis=0, keepdims=True)], axis=0)
    for d in range(z.devices):
        out_ref[d] = message


def second_kernel(
    z, pos_ref, count_ref, scale_ref, cell_ref, atom_ref, scount_ref, low_ref, high_ref, p_ref, diag_in_ref, shift_ref,
    gamma_ref, image_ref, halo_a_ref, halo_b_ref, index_ref, corner_ref, k_high_ref, k_low_ref, pj_ref,
    y_ref, q_ref, out_ref, e_ref, diag_ref, u_ref, uw_ref,
):
    position = pos_ref[0]
    left, right = sides(position, halo_a_ref[...], halo_b_ref[...])
    own = slice(z.rim, z.rim + z.nodes)
    diag_ref[:, own] = diag_in_ref[:, own]
    diag_ref[:, : z.rim] = left[ROWS : ROWS + 2, : z.rim]
    diag_ref[:, z.rim + z.nodes :] = right[ROWS : ROWS + 2, z.rim :]
    y_ref[...] = image_ref[...] + (diag_ref[1:2, :] + shift_ref[...]) * p_ref[:, : z.window]
    y_ref[:, : 2 * z.rim] += left[:ROWS]
    y_ref[:, z.window - 2 * z.rim :] += right[:ROWS]
    q_ref[:, : z.window] = y_ref[...] * diag_ref[0:1, :]
    q_ref[:, z.window :] = jnp.zeros((ROWS, z.reach - z.window), F32)
    y, q = y_ref[:, own], q_ref[:, own]
    dots = [
        gamma_ref[...],
        lanes_by_vector(z, y * p_ref[:, own]),
        lanes_by_vector(z, y * q),
    ]
    energy = jnp.sum(q * q * (diag_ref[1:2, own] + shift_ref[...]), axis=1, keepdims=True)
    gather_cells(z, index_ref, corner_ref, low_ref, high_ref, q_ref, scale_ref, count_ref[position], u_ref, uw_ref)
    parts = contributions(z, position, pj_ref, cell_ref, atom_ref, scount_ref, u_ref)
    stiffness_product(k_high_ref, k_low_ref, uw_ref, e_ref)
    elements = jnp.zeros((ROWS, z.width), F32)
    for c in range(z.slots):
        rows = slice(c * ROWS, (c + 1) * ROWS)
        elements = elements + u_ref[rows, :] * e_ref[rows, :]
    energy = energy + jnp.sum(elements, axis=1, keepdims=True)
    dots.append(lanes_by_vector(z, energy))
    line = dots[0]
    for k in range(1, len(dots)):
        line = line + pltpu.roll(dots[k], k * ROWS, 1)
    message = jnp.concatenate(parts + [line], axis=0)
    for d in range(z.devices):
        out_ref[d] = message


class Scatter:
    def __init__(self, z, index_ref, corner_ref, low_ref, high_ref, acc_ref):
        self.z, self.index_ref, self.corner_ref, self.acc_ref = z, index_ref, corner_ref, acc_ref
        self.low_ref, self.high_ref = low_ref, high_ref
        self.groups = z.window // WIDE
        self.pair = (2 * ROWS, LANES)
        sub = iota(self.pair, 0)
        self.lows = [(sub + k * 2 * ROWS).astype(jnp.int16) for k in range(WIDE // (2 * ROWS))]
        self.one, self.none = jnp.ones(self.pair, BF16), jnp.zeros(self.pair, BF16)
        self.lane = iota((ROWS, LANES), 1)
        self.end = (z.elem - 1) % LANES

    def two_parts(self, value):
        rounded = value.astype(BF16).astype(F32)
        return jnp.concatenate([rounded, value - rounded], axis=0).astype(BF16)

    def hot_rows(self, index):
        low = (index & (WIDE - 1)).astype(jnp.int16)
        return jnp.concatenate([jnp.where(low == k, self.one, self.none) for k in self.lows], axis=0)

    def masked(self, high, both, rows):
        high = high.astype(jnp.int16)
        return jnp.concatenate([jnp.where(high == jnp.int16(h), both, self.none) for h in range(rows)], axis=0)

    def product(self, lhs, hot):
        return lax.dot_general(lhs, hot, NT, preferred_element_type=F32)

    def start(self, sources):
        z = self.z
        corners = jnp.zeros((ROWS, LANES), F32)
        at = (z.tiles - 1) * LANES + self.end
        for cell, values in sources:
            corners = corners + jnp.where(self.lane == cell, values[:, 0:1], 0.0)
            corners = corners + jnp.where(self.lane == z.slots + cell, values[:, at : at + 1], 0.0)
        index = jnp.broadcast_to(self.corner_ref[...], self.pair)
        rows = self.groups * 2 * ROWS
        self.acc_ref[:rows, :] = self.product(
            self.masked(index >> 8, self.two_parts(corners), self.groups), self.hot_rows(index)
        )
        self.acc_ref[rows:, :] = jnp.zeros((BAND * 2 * ROWS, WIDE), F32)

    def add(self, cells, value_of):
        z = self.z
        starts = [(self.low_ref[c] + z.shift) >> 8 for c in cells]
        ends = [(self.high_ref[c] + z.shift) >> 8 for c in cells]
        passes = functools.reduce(jnp.maximum, [(e - s) // BAND + 1 for s, e in zip(starts, ends)])

        def one_pass(k, _):
            for i, c in enumerate(cells):
                start = jnp.minimum(starts[i] + k * BAND, self.groups)
                lhs, hot = [], []
                for t in range(z.tiles):
                    index = jnp.broadcast_to(self.index_ref[c, :, t * LANES : (t + 1) * LANES], self.pair)
                    value = value_of(i, t)
                    if t == 0:
                        value = jnp.where(self.lane == 0, 0.0, value)
                    if t == z.tiles - 1:
                        value = jnp.where(self.lane == self.end, 0.0, value)
                    lhs.append(self.masked((index >> 8) - start, self.two_parts(value), BAND))
                    hot.append(self.hot_rows(index))
                to = pl.ds(pl.multiple_of(start * 2 * ROWS, 2 * ROWS), BAND * 2 * ROWS)
                self.acc_ref[to, :] += self.product(jnp.concatenate(lhs, axis=1), jnp.concatenate(hot, axis=1))
            return 0

        lax.fori_loop(0, passes, one_pass, 0)

    def result(self, h):
        at = h * 2 * ROWS
        return self.acc_ref[at : at + ROWS] + self.acc_ref[at + ROWS : at + 2 * ROWS]


def cells_kernel(z, multiply, low_ref, high_ref, index_ref, corner_ref, *refs):
    if multiply:
        uw_ref, k_high_ref, k_low_ref, image_ref, e_ref, acc_ref = refs
        stiffness_product(k_high_ref, k_low_ref, uw_ref, e_ref)
    else:
        e_ref, image_ref, acc_ref = refs
    scatter = Scatter(z, index_ref, corner_ref, low_ref, high_ref, acc_ref)
    scatter.start([(c, e_ref[c * ROWS : (c + 1) * ROWS, :]) for c in range(z.slots)])

    def some_cells(g, _):
        cells = [g * z.together + i for i in range(z.together)]

        def value_of(i, t):
            rows = pl.ds(pl.multiple_of(cells[i] * ROWS, ROWS), ROWS)
            return e_ref[rows, t * LANES : (t + 1) * LANES]

        scatter.add(cells, value_of)
        return 0

    lax.fori_loop(0, z.slots // z.together, some_cells, 0)
    for h in range(scatter.groups):
        image_ref[:, h * WIDE : (h + 1) * WIDE] = scatter.result(h)


def support_kernel(
    z, last, pos_ref, cell_ref, atom_ref, scount_ref, low_ref, high_ref, sums_ref, coupling_ref, index_ref, corner_ref,
    pj_ref, diag_ref, cells_ref, *refs,
):
    if last:
        image_ref, send_a_ref, send_b_ref, dots_ref, support_ref, acc_ref = refs
    else:
        image_ref, send_a_ref, send_b_ref, support_ref, acc_ref = refs
    position = pos_ref[0]
    wanted = (
        pltpu.roll(sums_ref[:, 0, :], z.devices - 1, 0) + sums_ref[:, 1, :] + pltpu.roll(sums_ref[:, 2, :], 1, 0)
    )
    coupling = coupling_ref[:, 3, :]
    shape = (z.devices, LANES)
    lane = iota(shape, 1)
    term = jnp.zeros(shape, F32)
    for j in range(z.channels):
        matrix = lane_gather(coupling, lane // ROWS * ROWS + j)
        vector = lane_gather(wanted, lane // z.pairs * z.pairs + j * ROWS + lane % ROWS)
        term = term + matrix * vector
    if last:
        energy = jnp.sum(term * wanted, axis=0, keepdims=True)
        energy = jnp.broadcast_to(energy, (ROWS, LANES))
        step = ROWS
        while step < LANES:
            energy = energy + pltpu.roll(energy, step, 1)
            step *= 2
        line = iota((1, LANES), 1)
        dots_ref[...] = jnp.sum(sums_ref[:, 3, :], axis=0, keepdims=True) + jnp.where(
            line // ROWS == 3, energy[0:1], 0.0
        )
    block = iota(shape, 0)
    small_lane, small_row = iota((ROWS, LANES), 1), iota((ROWS, LANES), 0)
    spread = []
    for s in range(z.entries):
        owner, local, alive = entry_facts(z, position, atom_ref, scount_ref, s)
        mine = jnp.sum(jnp.where(block == owner, term, 0.0), axis=0, keepdims=True)
        got = lane_gather(
            jnp.broadcast_to(mine, (ROWS, LANES)), local * z.pairs + small_lane % ROWS * ROWS + small_row
        )
        spread.append(jnp.where((small_lane // ROWS == s) & alive, got, 0.0)[:, : z.entries * ROWS])
    support_ref[...] = jnp.dot(
        jnp.concatenate(spread, axis=0), pj_ref[...], precision=HIGHEST, preferred_element_type=F32
    )
    scatter = Scatter(z, index_ref, corner_ref, low_ref, high_ref, acc_ref)
    cells = [cell_ref[s] for s in range(z.entries)]
    scatter.start([(cell, support_ref[s * ROWS : (s + 1) * ROWS, :]) for s, cell in enumerate(cells)])
    for first in range(0, z.entries, z.together):
        some = cells[first : first + z.together]

        def value_of(i, t):
            s = first + i
            return support_ref[s * ROWS : (s + 1) * ROWS, t * LANES : (t + 1) * LANES]

        scatter.add(some, value_of)
    for h in range(scatter.groups):
        at = slice(h * WIDE, (h + 1) * WIDE)
        image_ref[:, at] = cells_ref[:, at] + scatter.result(h)
    even = position % 2 == 0
    ends = [slice(0, 2 * z.rim), slice(z.window - 2 * z.rim, z.window)]
    for source_ref, rows in ((image_ref, slice(0, ROWS)),) + (() if last else ((diag_ref, slice(ROWS, ROWS + 2)),)):
        low_rim, high_rim = (source_ref[:, end] for end in ends)
        send_a_ref[rows, :] = jnp.where(even, high_rim, low_rim)
        send_b_ref[rows, :] = jnp.where(even, low_rim, high_rim)


def last_kernel(
    z, rhs_ref, p_ref, diag_ref, shift_ref, y_ref, q_ref, image_ref, dots_ref, solution_ref, residual_ref, factor_ref,
):
    own = slice(z.rim, z.rim + z.nodes)
    lane, row = iota((ROWS, LANES), 1), iota((ROWS, LANES), 0)
    line = jnp.broadcast_to(dots_ref[...], (ROWS, LANES))

    def column(k):
        return jnp.sum(jnp.where(lane == k * ROWS + row, line, 0.0), axis=1, keepdims=True)

    gamma, py, qy, qq = (column(k) for k in range(4))
    alpha = gamma / py
    fresh = gamma - 2.0 * alpha * py + alpha * alpha * qy
    beta = fresh / gamma
    more = 1.0 + beta
    step = fresh / (more * more * py - 2.0 * more * alpha * qy + alpha * alpha * qq)
    p, q, y = p_ref[:, own], q_ref[:, own], y_ref[:, own]
    second = image_ref[:, own] + (diag_ref[1:2, own] + shift_ref[...]) * q
    search = (p - alpha * q) + beta * p
    solution_ref[...] = alpha * p + step * search
    residual_ref[...] = (rhs_ref[...] - alpha * y) - step * (more * y - alpha * second)
    factor_ref[...] = jnp.broadcast_to(step * alpha, (ROWS, LANES))


def rim_kernel(z, pos_ref, residual_in_ref, halo_a_ref, halo_b_ref, factor_ref, residual_ref):
    left, right = sides(pos_ref[0], halo_a_ref[...], halo_b_ref[...])
    factor = factor_ref[:, :1]
    first, last = slice(0, z.rim), slice(z.nodes - z.rim, z.nodes)
    residual_ref[:, z.rim : z.nodes - z.rim] = residual_in_ref[:, z.rim : z.nodes - z.rim]
    residual_ref[:, first] = residual_in_ref[:, first] + factor * left[:, z.rim :]
    residual_ref[:, last] = residual_in_ref[:, last] + factor * right[:, : z.rim]


def on_device(
    rhs, potential, precond, shift, stiffness, cell_scale, conn, cell_count, projector, support_cell, support_atom,
    support_count, atom_matrix,
):
    count = lax.axis_size("dom")
    z = Sizes(count, rhs, conn, projector, atom_matrix)
    position = lax.axis_index("dom")
    even = position % 2 == 0
    pos = position.astype(jnp.int32).reshape(1)
    near = [(i, i ^ 1) for i in range(count)]
    far = [(i, j) for i in range(1, count - 1) for j in [i + 1 if i % 2 else i - 1]]

    def exchange(a, b):
        return lax.ppermute(a, "dom", near), lax.ppermute(b, "dom", far)

    def call(kernel, outs, scratch, scalars, *args, in_hbm=()):
        args = [pltpu.with_memory_space_constraint(x, pltpu.VMEM) for x in args]
        return pl.pallas_call(
            kernel,
            out_shape=[
                jax.ShapeDtypeStruct(s, d) if i in in_hbm else pltpu.VMEM(s, d) for i, (s, d) in enumerate(outs)
            ],
            in_specs=[SMEM] * len(scalars) + [VMEM] * len(args),
            out_specs=[VMEM] * len(outs),
            scratch_shapes=[pltpu.VMEM(s, d) for s, d in scratch],
            compiler_params=pltpu.CompilerParams(vmem_limit_bytes=16 * 1024 * 1024),
        )(*scalars, *args)

    precond_row, potential_row = precond[None, :], potential[None, :]
    shift_column = shift[:, None]
    head = rhs[:, : z.rim] * precond[: z.rim]
    tail = rhs[:, z.nodes - z.rim :] * precond[z.nodes - z.rim :]
    halo = exchange(jnp.where(even, tail, head), jnp.where(even, head, tail))
    flat_projector = projector.reshape(z.entries * z.channels, z.elem)
    middle = conn[:, 1:-1]
    ranges = jnp.min(middle, axis=1), jnp.max(middle, axis=1)

    cells = (z.slots * ROWS, z.width)
    window, reach, own = (z.vectors, z.window), (z.vectors, z.reach), (z.vectors, z.nodes)
    message = (z.devices, 4, LANES)
    square, entries = (z.width, z.width), (z.entries * ROWS, z.width)
    rim, more_rim = (z.vectors, 2 * z.rim), (z.vectors + 2, 2 * z.rim)
    acc = ((z.window // WIDE + BAND) * 2 * ROWS, WIDE)
    supports = support_cell, support_atom, support_count

    index, corner, k_high, k_low, pj = call(
        functools.partial(prepare_kernel, z),
        [((z.slots, 1, z.width), jnp.int32), ((1, LANES), jnp.int32), (square, BF16), (square, BF16), (entries, F32)],
        [(square, F32)],
        (),
        conn, stiffness, flat_projector,
    )
    p, diag, sums, uw, gamma = call(
        functools.partial(first_kernel, z),
        [(reach, F32), ((2, z.window), F32), (message, F32), (cells, F32), ((1, LANES), F32)],
        [(cells, F32)],
        (pos, cell_count, cell_scale, *supports, *ranges),
        rhs, precond_row, potential_row, *halo, index, corner, pj, atom_matrix,
    )
    coupled = lax.all_to_all(sums, "dom", 0, 0)
    (image,) = call(
        functools.partial(cells_kernel, z, True),
        [(window, F32)],
        [(cells, F32), (acc, F32)],
        ranges,
        index, corner, uw, k_high, k_low,
    )
    image, send_a, send_b = call(
        functools.partial(support_kernel, z, False),
        [(window, F32), (more_rim, F32), (more_rim, F32)],
        [(entries, F32), (acc, F32)],
        (pos, *supports, *ranges),
        coupled, coupled, index, corner, pj, diag, image,
    )
    halo = exchange(send_a, send_b)
    y, q, sums, e = call(
        functools.partial(second_kernel, z),
        [(window, F32), (reach, F32), (message, F32), (cells, F32)],
        [((2, z.window), F32), (cells, F32), (cells, F32)],
        (pos, cell_count, cell_scale, *supports, *ranges),
        p, diag, shift_column, gamma, image, *halo, index, corner, k_high, k_low, pj,
    )
    totals = lax.all_to_all(sums, "dom", 0, 0)
    (image,) = call(functools.partial(cells_kernel, z, False), [(window, F32)], [(acc, F32)], ranges, index, corner, e)
    image, send_a, send_b, dots = call(
        functools.partial(support_kernel, z, True),
        [(window, F32), (rim, F32), (rim, F32), ((1, LANES), F32)],
        [(entries, F32), (acc, F32)],
        (pos, *supports, *ranges),
        totals, coupled, index, corner, pj, diag, image,
    )
    halo = exchange(send_a, send_b)
    answer, residual, factor = call(
        functools.partial(last_kernel, z),
        [(own, F32), (own, F32), ((ROWS, LANES), F32)],
        [],
        (),
        rhs, p, diag, shift_column, y, q, image, dots, in_hbm=(0,),
    )
    (residual,) = call(functools.partial(rim_kernel, z), [(own, F32)], [], (pos,), residual, *halo, factor, in_hbm=(0,))
    return answer, residual


def solution(mesh):
    placed = (
        P(None, "dom"),
        P("dom"),
        P("dom"),
        P(),
        P(),
        P("dom"),
        P("dom", None),
        P(),
        P("dom", None, None),
        P("dom"),
        P("dom"),
        P(),
        P("dom", None, None),
    )
    return jax.shard_map(
        on_device,
        mesh=mesh,
        in_specs=placed,
        out_specs=(P(None, "dom"), P(None, "dom")),
        check_vma=False,
    )
```

```python
import functools

import jax
import jax.numpy as jnp
from jax import lax
from jax.experimental import pallas as pl
from jax.experimental.pallas import tpu as pltpu
from jax.sharding import PartitionSpec as P

LANES = 128
ROWS = 8
WIDE = 256
CHAINS = 4
SPAN = 14
BAND = 8
TOGETHER = 4
F32 = jnp.float32
BF16 = jnp.bfloat16
HIGHEST = lax.Precision.HIGHEST
NT = (((1,), (1,)), ((), ()))
VMEM = pl.BlockSpec(memory_space=pltpu.VMEM)
SMEM = pl.BlockSpec(memory_space=pltpu.SMEM)


def round_up(value, step):
    return -(-value // step) * step


class Sizes:
    def __init__(self, count, rhs, conn, projector, atom_matrix):
        self.devices = count
        self.vectors, self.nodes = rhs.shape
        self.slots, self.elem = conn.shape
        self.entries, self.channels = projector.shape[:2]
        self.owned = atom_matrix.shape[0]
        self.ghost = self.nodes // 16
        self.rim = round_up(self.ghost, WIDE)
        self.shift = self.rim - self.ghost
        self.window = self.nodes + 2 * self.rim
        self.width = round_up(self.elem, LANES)
        self.tiles = self.width // LANES
        self.pairs = self.channels * self.vectors
        self.reach = self.window + SPAN * LANES
        self.together = TOGETHER if self.slots % TOGETHER == 0 else 1
        assert self.vectors == ROWS and self.channels == ROWS and 2 * self.slots <= LANES
        assert self.nodes % WIDE == 0 and self.owned * self.pairs == LANES


def lane_gather(values, index):
    return jnp.take_along_axis(values, index, axis=1, mode="promise_in_bounds")


def iota(shape, dim):
    return lax.broadcasted_iota(jnp.int32, shape, dim)


def split(values):
    high = values.astype(BF16)
    return high, (values - high.astype(F32)).astype(BF16)


def lanes_by_vector(z, values):
    total = jnp.sum(values, axis=1, keepdims=True)
    spread = jnp.broadcast_to(total, (ROWS, LANES))
    return jnp.sum(jnp.where(iota((ROWS, LANES), 1) == iota((ROWS, LANES), 0), spread, 0.0), axis=0, keepdims=True)


def list_cells(z, margin, low_ref, high_ref, list_ref):
    def place(c, counts):
        inside, outside = counts
        good = (low_ref[c] + z.shift >= margin) & (high_ref[c] + z.shift < z.window - margin)
        list_ref[jnp.where(good, inside, z.slots - 1 - outside)] = c
        one = good.astype(jnp.int32)
        return inside + one, outside + 1 - one

    inside, _ = lax.fori_loop(0, z.slots, place, (jnp.int32(0), jnp.int32(0)))
    list_ref[z.slots] = inside // z.together


def prepare_kernel(z, low_ref, high_ref, conn_ref, index_ref, corner_ref, first_list_ref, second_list_ref):
    line = iota((1, LANES), 1)
    corner = jnp.zeros((1, LANES), jnp.int32)
    index_ref[...] = jnp.zeros_like(index_ref)
    for c in range(z.slots):
        row = conn_ref[c : c + 1, :] + z.shift
        index_ref[c, :, : z.elem] = row
        corner = jnp.where(line == c, row[:, :1], corner)
        corner = jnp.where(line == z.slots + c, row[:, z.elem - 1 :], corner)
    corner_ref[...] = corner
    list_cells(z, z.rim, low_ref, high_ref, first_list_ref)
    list_cells(z, 2 * z.rim, low_ref, high_ref, second_list_ref)


def pad_kernel(z, stiffness_ref, projector_ref, k_high_ref, k_low_ref, pj_ref, k_ref):
    k_ref[...] = jnp.zeros_like(k_ref)
    k_ref[: z.elem, : z.elem] = stiffness_ref[...]
    k_high_ref[...], k_low_ref[...] = split(k_ref[...])
    pj_ref[...] = jnp.zeros_like(pj_ref)
    pj_ref[:, : z.elem] = projector_ref[...]


def gather_middle(z, groups, list_ref, index_ref, low_ref, high_ref, window_ref, u_ref):
    total = z.window // LANES
    tile = (ROWS, LANES)

    def some_cells(g, _):
        cells = [list_ref[g * z.together + i] for i in range(z.together)]
        starts = [(low_ref[c] + z.shift) >> 7 for c in cells]
        ends = [(high_ref[c] + z.shift) >> 7 for c in cells]
        passes = functools.reduce(jnp.maximum, [(e - s) // SPAN + 1 for s, e in zip(starts, ends)])

        def one_pass(k, values):
            values = list(values)
            for i, c in enumerate(cells):
                start = jnp.minimum(starts[i] + k * SPAN, total)
                for t in range(z.tiles):
                    index = jnp.broadcast_to(index_ref[c, :, t * LANES : (t + 1) * LANES], tile)
                    low, high = index & (LANES - 1), (index >> 7) - start
                    value = values[i * z.tiles + t]
                    for h in range(SPAN):
                        at = pl.ds(pl.multiple_of((start + h) * LANES, LANES), LANES)
                        value = jnp.where(high == h, lane_gather(window_ref[:, at], low), value)
                    values[i * z.tiles + t] = value
            return tuple(values)

        values = lax.fori_loop(0, passes, one_pass, (jnp.zeros(tile, F32),) * (z.together * z.tiles))
        for i, c in enumerate(cells):
            rows = pl.ds(pl.multiple_of(c * ROWS, ROWS), ROWS)
            for t in range(z.tiles):
                u_ref[rows, t * LANES : (t + 1) * LANES] = values[i * z.tiles + t]
        return 0

    lax.fori_loop(*groups, some_cells, 0)


def gather_corners(z, corner_ref, window_ref, scale_ref, live, u_ref, uw_ref):
    tile = (ROWS, LANES)
    corner = jnp.broadcast_to(corner_ref[...], tile)
    low, high = corner & (LANES - 1), corner >> 7
    chains = [jnp.zeros(tile, F32)] * CHAINS
    for h in range(z.window // LANES):
        got = lane_gather(window_ref[:, h * LANES : (h + 1) * LANES], low)
        chains[h % CHAINS] = jnp.where(high == h, got, chains[h % CHAINS])
    corners = functools.reduce(jnp.add, chains)
    lane = iota(tile, 1)
    last = (z.elem - 1) % LANES
    for c in range(z.slots):
        weight = jnp.where(c < live, scale_ref[c], 0.0)
        rows = slice(c * ROWS, (c + 1) * ROWS)
        for t in range(z.tiles):
            lanes = slice(t * LANES, (t + 1) * LANES)
            value = u_ref[rows, lanes]
            if t == 0:
                value = jnp.where(lane == 0, corners[:, c : c + 1], value)
            if t == z.tiles - 1:
                value = jnp.where(lane == last, corners[:, z.slots + c : z.slots + c + 1], value)
            u_ref[rows, lanes] = value
            uw_ref[rows, lanes] = value * weight


def stiffness_product(k_high_ref, k_low_ref, uw_ref, e_ref):
    k_high, k_low = k_high_ref[...], k_low_ref[...]
    u_high, u_low = split(uw_ref[...])
    dot = functools.partial(lax.dot_general, dimension_numbers=NT, preferred_element_type=F32)
    e_ref[...] = dot(u_high, k_high) + (dot(u_high, k_low) + dot(u_low, k_high))


def entry_facts(z, position, atom_ref, count_ref, s):
    atom = atom_ref[s]
    owner = atom // z.owned
    return owner, atom - owner * z.owned, s < count_ref[position]


def contributions(z, position, pj_ref, cell_ref, atom_ref, count_ref, u_ref):
    values = [u_ref[pl.ds(pl.multiple_of(cell_ref[s] * ROWS, ROWS), ROWS), :] for s in range(z.entries)]
    sums = lax.dot_general(
        pj_ref[...], jnp.concatenate(values, axis=0), NT, precision=HIGHEST, preferred_element_type=F32
    )
    sums = jnp.concatenate([sums, jnp.zeros((sums.shape[0], LANES - sums.shape[1]), F32)], axis=1)
    lane, row = iota((ROWS, LANES), 1), iota((ROWS, LANES), 0)
    parts = [jnp.zeros((ROWS, LANES), F32)] * 3
    for s in range(z.entries):
        owner, local, alive = entry_facts(z, position, atom_ref, count_ref, s)
        got = lane_gather(sums[s * ROWS : (s + 1) * ROWS], s * ROWS + lane % ROWS)
        here = (lane // ROWS % ROWS == row) & (lane // z.pairs == local) & alive
        for k in range(3):
            parts[k] = parts[k] + jnp.where(here & (owner == position - 1 + k), got, 0.0)
    return [jnp.sum(part, axis=0, keepdims=True) for part in parts]


def sides(position, near, far):
    even = position % 2 == 0
    return jnp.where(even, far, near), jnp.where(even, near, far)


def first_window_kernel(
    z, low_ref, high_ref, list_ref, rhs_ref, precond_ref, index_ref, p_ref, u_ref, gamma_ref,
):
    product = rhs_ref[...] * precond_ref[...]
    p_ref[:, z.rim : z.rim + z.nodes] = product
    gamma_ref[...] = lanes_by_vector(z, product * rhs_ref[...])
    p_ref[:, z.window :] = jnp.zeros((ROWS, z.reach - z.window), F32)
    gather_middle(z, (0, list_ref[z.slots]), list_ref, index_ref, low_ref, high_ref, p_ref, u_ref)


def first_kernel(
    z, pos_ref, count_ref, scale_ref, cell_ref, atom_ref, scount_ref, low_ref, high_ref, list_ref, p_in_ref, u_in_ref,
    precond_ref, potential_ref, halo_a_ref, halo_b_ref, index_ref, corner_ref, pj_ref, coupling_ref,
    p_ref, diag_ref, out_ref, uw_ref, u_ref,
):
    position = pos_ref[0]
    own = slice(z.rim, z.rim + z.nodes)
    p_ref[:, : z.rim], p_ref[:, z.rim + z.nodes : z.window] = sides(position, halo_a_ref[...], halo_b_ref[...])
    p_ref[:, own] = p_in_ref[:, own]
    p_ref[:, z.window :] = p_in_ref[:, z.window :]
    u_ref[...] = u_in_ref[...]
    diag_ref[...] = jnp.zeros_like(diag_ref)
    diag_ref[0:1, own] = precond_ref[...]
    diag_ref[1:2, own] = potential_ref[...]
    groups = list_ref[z.slots], z.slots // z.together
    gather_middle(z, groups, list_ref, index_ref, low_ref, high_ref, p_ref, u_ref)
    gather_corners(z, corner_ref, p_ref, scale_ref, count_ref[position], u_ref, uw_ref)
    parts = contributions(z, position, pj_ref, cell_ref, atom_ref, scount_ref, u_ref)
    small_lane, small_row = iota((ROWS, LANES), 1), iota((ROWS, LANES), 0)
    matrices = jnp.zeros((ROWS, LANES), F32)
    for atom in range(z.owned):
        block = jnp.concatenate([coupling_ref[atom], jnp.zeros((ROWS, LANES - z.channels), F32)], axis=1)
        got = lane_gather(block, small_lane % ROWS)
        matrices = jnp.where(small_lane // ROWS == atom * ROWS + small_row, got, matrices)
    message = jnp.concatenate(parts + [jnp.sum(matrices, axis=0, keepdims=True)], axis=0)
    for d in range(z.devices):
        out_ref[d] = message


def second_window_kernel(
    z, low_ref, high_ref, list_ref, p_ref, diag_ref, shift_ref, image_ref, index_ref, y_ref, q_ref, u_ref,
):
    y_ref[...] = image_ref[...] + (diag_ref[1:2, :] + shift_ref[...]) * p_ref[:, : z.window]
    q_ref[:, : z.window] = y_ref[...] * diag_ref[0:1, :]
    q_ref[:, z.window :] = jnp.zeros((ROWS, z.reach - z.window), F32)
    gather_middle(z, (0, list_ref[z.slots]), list_ref, index_ref, low_ref, high_ref, q_ref, u_ref)


def second_kernel(
    z, pos_ref, count_ref, scale_ref, cell_ref, atom_ref, scount_ref, low_ref, high_ref, list_ref, y_in_ref, q_in_ref,
    u_in_ref, p_ref, diag_in_ref, shift_ref, gamma_ref, halo_a_ref, halo_b_ref, index_ref, corner_ref, k_high_ref,
    k_low_ref, pj_ref, y_ref, q_ref, out_ref, e_ref, diag_ref, u_ref, uw_ref,
):
    position = pos_ref[0]
    left, right = sides(position, halo_a_ref[...], halo_b_ref[...])
    own = slice(z.rim, z.rim + z.nodes)
    ghosts = slice(0, z.rim), slice(z.rim + z.nodes, z.window)
    diag_ref[:, own] = diag_in_ref[:, own]
    diag_ref[:, ghosts[0]] = left[ROWS : ROWS + 2, : z.rim]
    diag_ref[:, ghosts[1]] = right[ROWS : ROWS + 2, z.rim :]
    y_ref[...] = y_in_ref[...]
    for ghost in ghosts:
        y_ref[:, ghost] += (diag_ref[1:2, ghost] - diag_in_ref[1:2, ghost]) * p_ref[:, ghost]
    y_ref[:, : 2 * z.rim] += left[:ROWS]
    y_ref[:, z.window - 2 * z.rim :] += right[:ROWS]
    q_ref[...] = q_in_ref[...]
    for rims in (slice(0, 2 * z.rim), slice(z.window - 2 * z.rim, z.window)):
        q_ref[:, rims] = y_ref[:, rims] * diag_ref[0:1, rims]
    u_ref[...] = u_in_ref[...]
    y, q = y_ref[:, own], q_ref[:, own]
    dots = [
        gamma_ref[...],
        lanes_by_vector(z, y * p_ref[:, own]),
        lanes_by_vector(z, y * q),
    ]
    energy = jnp.sum(q * q * (diag_ref[1:2, own] + shift_ref[...]), axis=1, keepdims=True)
    groups = list_ref[z.slots], z.slots // z.together
    gather_middle(z, groups, list_ref, index_ref, low_ref, high_ref, q_ref, u_ref)
    gather_corners(z, corner_ref, q_ref, scale_ref, count_ref[position], u_ref, uw_ref)
    parts = contributions(z, position, pj_ref, cell_ref, atom_ref, scount_ref, u_ref)
    stiffness_product(k_high_ref, k_low_ref, uw_ref, e_ref)
    elements = jnp.zeros((ROWS, z.width), F32)
    for c in range(z.slots):
        rows = slice(c * ROWS, (c + 1) * ROWS)
        elements = elements + u_ref[rows, :] * e_ref[rows, :]
    energy = energy + jnp.sum(elements, axis=1, keepdims=True)
    dots.append(lanes_by_vector(z, energy))
    line = dots[0]
    for k in range(1, len(dots)):
        line = line + pltpu.roll(dots[k], k * ROWS, 1)
    message = jnp.concatenate(parts + [line], axis=0)
    for d in range(z.devices):
        out_ref[d] = message


class Scatter:
    def __init__(self, z, index_ref, corner_ref, low_ref, high_ref, acc_ref):
        self.z, self.index_ref, self.corner_ref, self.acc_ref = z, index_ref, corner_ref, acc_ref
        self.low_ref, self.high_ref = low_ref, high_ref
        self.groups = z.window // WIDE
        self.pair = (2 * ROWS, LANES)
        sub = iota(self.pair, 0)
        self.lows = [(sub + k * 2 * ROWS).astype(jnp.int16) for k in range(WIDE // (2 * ROWS))]
        self.one, self.none = jnp.ones(self.pair, BF16), jnp.zeros(self.pair, BF16)
        self.lane = iota((ROWS, LANES), 1)
        self.end = (z.elem - 1) % LANES

    def two_parts(self, value):
        rounded = value.astype(BF16).astype(F32)
        return jnp.concatenate([rounded, value - rounded], axis=0).astype(BF16)

    def hot_rows(self, index):
        low = (index & (WIDE - 1)).astype(jnp.int16)
        return jnp.concatenate([jnp.where(low == k, self.one, self.none) for k in self.lows], axis=0)

    def masked(self, high, both, rows):
        high = high.astype(jnp.int16)
        return jnp.concatenate([jnp.where(high == jnp.int16(h), both, self.none) for h in range(rows)], axis=0)

    def product(self, lhs, hot):
        return lax.dot_general(lhs, hot, NT, preferred_element_type=F32)

    def start(self, sources):
        z = self.z
        corners = jnp.zeros((ROWS, LANES), F32)
        at = (z.tiles - 1) * LANES + self.end
        for cell, values in sources:
            corners = corners + jnp.where(self.lane == cell, values[:, 0:1], 0.0)
            corners = corners + jnp.where(self.lane == z.slots + cell, values[:, at : at + 1], 0.0)
        index = jnp.broadcast_to(self.corner_ref[...], self.pair)
        rows = self.groups * 2 * ROWS
        self.acc_ref[:rows, :] = self.product(
            self.masked(index >> 8, self.two_parts(corners), self.groups), self.hot_rows(index)
        )
        self.acc_ref[rows:, :] = jnp.zeros((BAND * 2 * ROWS, WIDE), F32)

    def add(self, cells, value_of):
        z = self.z
        starts = [(self.low_ref[c] + z.shift) >> 8 for c in cells]
        ends = [(self.high_ref[c] + z.shift) >> 8 for c in cells]
        passes = functools.reduce(jnp.maximum, [(e - s) // BAND + 1 for s, e in zip(starts, ends)])

        def one_pass(k, _):
            for i, c in enumerate(cells):
                start = jnp.minimum(starts[i] + k * BAND, self.groups)
                lhs, hot = [], []
                for t in range(z.tiles):
                    index = jnp.broadcast_to(self.index_ref[c, :, t * LANES : (t + 1) * LANES], self.pair)
                    value = value_of(i, t)
                    if t == 0:
                        value = jnp.where(self.lane == 0, 0.0, value)
                    if t == z.tiles - 1:
                        value = jnp.where(self.lane == self.end, 0.0, value)
                    lhs.append(self.masked((index >> 8) - start, self.two_parts(value), BAND))
                    hot.append(self.hot_rows(index))
                to = pl.ds(pl.multiple_of(start * 2 * ROWS, 2 * ROWS), BAND * 2 * ROWS)
                self.acc_ref[to, :] += self.product(jnp.concatenate(lhs, axis=1), jnp.concatenate(hot, axis=1))
            return 0

        lax.fori_loop(0, passes, one_pass, 0)

    def result(self, h):
        at = h * 2 * ROWS
        return self.acc_ref[at : at + ROWS] + self.acc_ref[at + ROWS : at + 2 * ROWS]


def cells_kernel(z, multiply, low_ref, high_ref, index_ref, corner_ref, *refs):
    if multiply:
        uw_ref, k_high_ref, k_low_ref, image_ref, e_ref, acc_ref = refs
        stiffness_product(k_high_ref, k_low_ref, uw_ref, e_ref)
    else:
        e_ref, image_ref, acc_ref = refs
    scatter = Scatter(z, index_ref, corner_ref, low_ref, high_ref, acc_ref)
    scatter.start([(c, e_ref[c * ROWS : (c + 1) * ROWS, :]) for c in range(z.slots)])

    def some_cells(g, _):
        cells = [g * z.together + i for i in range(z.together)]

        def value_of(i, t):
            rows = pl.ds(pl.multiple_of(cells[i] * ROWS, ROWS), ROWS)
            return e_ref[rows, t * LANES : (t + 1) * LANES]

        scatter.add(cells, value_of)
        return 0

    lax.fori_loop(0, z.slots // z.together, some_cells, 0)
    for h in range(scatter.groups):
        image_ref[:, h * WIDE : (h + 1) * WIDE] = scatter.result(h)


def support_kernel(
    z, last, pos_ref, cell_ref, atom_ref, scount_ref, low_ref, high_ref, sums_ref, coupling_ref, index_ref, corner_ref,
    pj_ref, diag_ref, cells_ref, *refs,
):
    if last:
        image_ref, send_a_ref, send_b_ref, dots_ref, support_ref, acc_ref = refs
    else:
        image_ref, send_a_ref, send_b_ref, support_ref, acc_ref = refs
    position = pos_ref[0]
    wanted = (
        pltpu.roll(sums_ref[:, 0, :], z.devices - 1, 0) + sums_ref[:, 1, :] + pltpu.roll(sums_ref[:, 2, :], 1, 0)
    )
    coupling = coupling_ref[:, 3, :]
    shape = (z.devices, LANES)
    lane = iota(shape, 1)
    term = jnp.zeros(shape, F32)
    for j in range(z.channels):
        matrix = lane_gather(coupling, lane // ROWS * ROWS + j)
        vector = lane_gather(wanted, lane // z.pairs * z.pairs + j * ROWS + lane % ROWS)
        term = term + matrix * vector
    if last:
        energy = jnp.sum(term * wanted, axis=0, keepdims=True)
        energy = jnp.broadcast_to(energy, (ROWS, LANES))
        step = ROWS
        while step < LANES:
            energy = energy + pltpu.roll(energy, step, 1)
            step *= 2
        line = iota((1, LANES), 1)
        dots_ref[...] = jnp.sum(sums_ref[:, 3, :], axis=0, keepdims=True) + jnp.where(
            line // ROWS == 3, energy[0:1], 0.0
        )
    block = iota(shape, 0)
    small_lane, small_row = iota((ROWS, LANES), 1), iota((ROWS, LANES), 0)
    spread = []
    for s in range(z.entries):
        owner, local, alive = entry_facts(z, position, atom_ref, scount_ref, s)
        mine = jnp.sum(jnp.where(block == owner, term, 0.0), axis=0, keepdims=True)
        got = lane_gather(
            jnp.broadcast_to(mine, (ROWS, LANES)), local * z.pairs + small_lane % ROWS * ROWS + small_row
        )
        spread.append(jnp.where((small_lane // ROWS == s) & alive, got, 0.0)[:, : z.entries * ROWS])
    support_ref[...] = jnp.dot(
        jnp.concatenate(spread, axis=0), pj_ref[...], precision=HIGHEST, preferred_element_type=F32
    )
    scatter = Scatter(z, index_ref, corner_ref, low_ref, high_ref, acc_ref)
    cells = [cell_ref[s] for s in range(z.entries)]
    scatter.start([(cell, support_ref[s * ROWS : (s + 1) * ROWS, :]) for s, cell in enumerate(cells)])
    for first in range(0, z.entries, z.together):
        some = cells[first : first + z.together]

        def value_of(i, t):
            s = first + i
            return support_ref[s * ROWS : (s + 1) * ROWS, t * LANES : (t + 1) * LANES]

        scatter.add(some, value_of)
    for h in range(scatter.groups):
        at = slice(h * WIDE, (h + 1) * WIDE)
        image_ref[:, at] = cells_ref[:, at] + scatter.result(h)
    even = position % 2 == 0
    ends = [slice(0, 2 * z.rim), slice(z.window - 2 * z.rim, z.window)]
    for source_ref, rows in ((image_ref, slice(0, ROWS)),) + (() if last else ((diag_ref, slice(ROWS, ROWS + 2)),)):
        low_rim, high_rim = (source_ref[:, end] for end in ends)
        send_a_ref[rows, :] = jnp.where(even, high_rim, low_rim)
        send_b_ref[rows, :] = jnp.where(even, low_rim, high_rim)


def last_kernel(
    z, rhs_ref, p_ref, diag_ref, shift_ref, y_ref, q_ref, image_ref, dots_ref, solution_ref, residual_ref, factor_ref,
):
    own = slice(z.rim, z.rim + z.nodes)
    lane, row = iota((ROWS, LANES), 1), iota((ROWS, LANES), 0)
    line = jnp.broadcast_to(dots_ref[...], (ROWS, LANES))

    def column(k):
        return jnp.sum(jnp.where(lane == k * ROWS + row, line, 0.0), axis=1, keepdims=True)

    gamma, py, qy, qq = (column(k) for k in range(4))
    alpha = gamma / py
    fresh = gamma - 2.0 * alpha * py + alpha * alpha * qy
    beta = fresh / gamma
    more = 1.0 + beta
    step = fresh / (more * more * py - 2.0 * more * alpha * qy + alpha * alpha * qq)
    p, q, y = p_ref[:, own], q_ref[:, own], y_ref[:, own]
    second = image_ref[:, own] + (diag_ref[1:2, own] + shift_ref[...]) * q
    search = (p - alpha * q) + beta * p
    solution_ref[...] = alpha * p + step * search
    residual_ref[...] = (rhs_ref[...] - alpha * y) - step * (more * y - alpha * second)
    factor_ref[...] = jnp.broadcast_to(step * alpha, (ROWS, LANES))


def rim_kernel(z, pos_ref, residual_in_ref, halo_a_ref, halo_b_ref, factor_ref, residual_ref):
    left, right = sides(pos_ref[0], halo_a_ref[...], halo_b_ref[...])
    factor = factor_ref[:, :1]
    first, last = slice(0, z.rim), slice(z.nodes - z.rim, z.nodes)
    residual_ref[:, z.rim : z.nodes - z.rim] = residual_in_ref[:, z.rim : z.nodes - z.rim]
    residual_ref[:, first] = residual_in_ref[:, first] + factor * left[:, z.rim :]
    residual_ref[:, last] = residual_in_ref[:, last] + factor * right[:, : z.rim]


def on_device(
    rhs, potential, precond, shift, stiffness, cell_scale, conn, cell_count, projector, support_cell, support_atom,
    support_count, atom_matrix,
):
    count = lax.axis_size("dom")
    z = Sizes(count, rhs, conn, projector, atom_matrix)
    position = lax.axis_index("dom")
    even = position % 2 == 0
    pos = position.astype(jnp.int32).reshape(1)
    near = [(i, i ^ 1) for i in range(count)]
    far = [(i, j) for i in range(1, count - 1) for j in [i + 1 if i % 2 else i - 1]]

    def exchange(a, b):
        return lax.ppermute(a, "dom", near), lax.ppermute(b, "dom", far)

    def call(kernel, outs, scratch, scalars, *args, in_hbm=(), in_smem=()):
        args = [pltpu.with_memory_space_constraint(x, pltpu.VMEM) for x in args]
        return pl.pallas_call(
            kernel,
            out_shape=[
                jax.ShapeDtypeStruct(s, d) if i in in_hbm + in_smem else pltpu.VMEM(s, d)
                for i, (s, d) in enumerate(outs)
            ],
            in_specs=[SMEM] * len(scalars) + [VMEM] * len(args),
            out_specs=[SMEM if i in in_smem else VMEM for i in range(len(outs))],
            scratch_shapes=[pltpu.VMEM(s, d) for s, d in scratch],
            compiler_params=pltpu.CompilerParams(vmem_limit_bytes=16 * 1024 * 1024),
        )(*scalars, *args)

    precond_row, potential_row = precond[None, :], potential[None, :]
    shift_column = shift[:, None]
    head = rhs[:, : z.rim] * precond[: z.rim]
    tail = rhs[:, z.nodes - z.rim :] * precond[z.nodes - z.rim :]
    halo = exchange(jnp.where(even, tail, head), jnp.where(even, head, tail))
    flat_projector = projector.reshape(z.entries * z.channels, z.elem)
    middle = conn[:, 1:-1]
    ranges = jnp.min(middle, axis=1), jnp.max(middle, axis=1)

    cells = (z.slots * ROWS, z.width)
    window, reach, own = (z.vectors, z.window), (z.vectors, z.reach), (z.vectors, z.nodes)
    message = (z.devices, 4, LANES)
    square, entries = (z.width, z.width), (z.entries * ROWS, z.width)
    rim, more_rim = (z.vectors, 2 * z.rim), (z.vectors + 2, 2 * z.rim)
    acc = ((z.window // WIDE + BAND) * 2 * ROWS, WIDE)
    supports = support_cell, support_atom, support_count

    index, corner, first_list, second_list = call(
        functools.partial(prepare_kernel, z),
        [((z.slots, 1, z.width), jnp.int32), ((1, LANES), jnp.int32)] + [((z.slots + 1,), jnp.int32)] * 2,
        [],
        ranges,
        conn, in_smem=(2, 3),
    )
    p, u, gamma = call(
        functools.partial(first_window_kernel, z),
        [(reach, F32), (cells, F32), ((1, LANES), F32)],
        [],
        (*ranges, first_list),
        rhs, precond_row, index,
    )
    k_high, k_low, pj = call(
        functools.partial(pad_kernel, z),
        [(square, BF16), (square, BF16), (entries, F32)],
        [(square, F32)],
        (),
        stiffness, flat_projector,
    )
    p, diag, sums, uw = call(
        functools.partial(first_kernel, z),
        [(reach, F32), ((2, z.window), F32), (message, F32), (cells, F32)],
        [(cells, F32)],
        (pos, cell_count, cell_scale, *supports, *ranges, first_list),
        p, u, precond_row, potential_row, *halo, index, corner, pj, atom_matrix,
    )
    coupled = lax.all_to_all(sums, "dom", 0, 0)
    (image,) = call(
        functools.partial(cells_kernel, z, True),
        [(window, F32)],
        [(cells, F32), (acc, F32)],
        ranges,
        index, corner, uw, k_high, k_low,
    )
    image, send_a, send_b = call(
        functools.partial(support_kernel, z, False),
        [(window, F32), (more_rim, F32), (more_rim, F32)],
        [(entries, F32), (acc, F32)],
        (pos, *supports, *ranges),
        coupled, coupled, index, corner, pj, diag, image,
    )
    halo = exchange(send_a, send_b)
    y, q, u = call(
        functools.partial(second_window_kernel, z),
        [(window, F32), (reach, F32), (cells, F32)],
        [],
        (*ranges, second_list),
        p, diag, shift_column, image, index,
    )
    y, q, sums, e = call(
        functools.partial(second_kernel, z),
        [(window, F32), (reach, F32), (message, F32), (cells, F32)],
        [((2, z.window), F32), (cells, F32), (cells, F32)],
        (pos, cell_count, cell_scale, *supports, *ranges, second_list),
        y, q, u, p, diag, shift_column, gamma, *halo, index, corner, k_high, k_low, pj,
    )
    totals = lax.all_to_all(sums, "dom", 0, 0)
    (image,) = call(functools.partial(cells_kernel, z, False), [(window, F32)], [(acc, F32)], ranges, index, corner, e)
    image, send_a, send_b, dots = call(
        functools.partial(support_kernel, z, True),
        [(window, F32), (rim, F32), (rim, F32), ((1, LANES), F32)],
        [(entries, F32), (acc, F32)],
        (pos, *supports, *ranges),
        totals, coupled, index, corner, pj, diag, image,
    )
    halo = exchange(send_a, send_b)
    answer, residual, factor = call(
        functools.partial(last_kernel, z),
        [(own, F32), (own, F32), ((ROWS, LANES), F32)],
        [],
        (),
        rhs, p, diag, shift_column, y, q, image, dots, in_hbm=(0,),
    )
    (residual,) = call(functools.partial(rim_kernel, z), [(own, F32)], [], (pos,), residual, *halo, factor, in_hbm=(0,))
    return answer, residual


def solution(mesh):
    placed = (
        P(None, "dom"),
        P("dom"),
        P("dom"),
        P(),
        P(),
        P("dom"),
        P("dom", None),
        P(),
        P("dom", None, None),
        P("dom"),
        P("dom"),
        P(),
        P("dom", None, None),
    )
    return jax.shard_map(
        on_device,
        mesh=mesh,
        in_specs=placed,
        out_specs=(P(None, "dom"), P(None, "dom")),
        check_vma=False,
    )
```

```python
import functools

import jax
import jax.numpy as jnp
from jax import lax
from jax.experimental import pallas as pl
from jax.experimental.pallas import tpu as pltpu
from jax.sharding import PartitionSpec as P

LANES = 128
ROWS = 8
WIDE = 256
CHAINS = 4
SPAN = 14
BAND = 8
TOGETHER = 8
F32 = jnp.float32
BF16 = jnp.bfloat16
HIGHEST = lax.Precision.HIGHEST
NT = (((1,), (1,)), ((), ()))
VMEM = pl.BlockSpec(memory_space=pltpu.VMEM)
SMEM = pl.BlockSpec(memory_space=pltpu.SMEM)


def round_up(value, step):
    return -(-value // step) * step


class Sizes:
    def __init__(self, count, rhs, conn, projector, atom_matrix):
        self.devices = count
        self.vectors, self.nodes = rhs.shape
        self.slots, self.elem = conn.shape
        self.entries, self.channels = projector.shape[:2]
        self.owned = atom_matrix.shape[0]
        self.ghost = self.nodes // 16
        self.rim = round_up(self.ghost, WIDE)
        self.shift = self.rim - self.ghost
        self.window = self.nodes + 2 * self.rim
        self.width = round_up(self.elem, LANES)
        self.tiles = self.width // LANES
        self.pairs = self.channels * self.vectors
        self.reach = self.window + SPAN * LANES
        self.together = TOGETHER if self.slots % TOGETHER == 0 else 1
        assert self.vectors == ROWS and self.channels == ROWS and 2 * self.slots <= LANES
        assert self.nodes % WIDE == 0 and self.owned * self.pairs == LANES


def lane_gather(values, index):
    return jnp.take_along_axis(values, index, axis=1, mode="promise_in_bounds")


def iota(shape, dim):
    return lax.broadcasted_iota(jnp.int32, shape, dim)


def split(values):
    high = values.astype(BF16)
    return high, (values - high.astype(F32)).astype(BF16)


def lanes_by_vector(z, values):
    total = jnp.sum(values, axis=1, keepdims=True)
    spread = jnp.broadcast_to(total, (ROWS, LANES))
    return jnp.sum(jnp.where(iota((ROWS, LANES), 1) == iota((ROWS, LANES), 0), spread, 0.0), axis=0, keepdims=True)


def prepare_kernel(z, conn_ref, index_ref, corner_ref):
    line = iota((1, LANES), 1)
    corner = jnp.zeros((1, LANES), jnp.int32)
    index_ref[...] = jnp.zeros_like(index_ref)
    for c in range(z.slots):
        row = conn_ref[c : c + 1, :] + z.shift
        index_ref[c, :, : z.elem] = row
        corner = jnp.where(line == c, row[:, :1], corner)
        corner = jnp.where(line == z.slots + c, row[:, z.elem - 1 :], corner)
    corner_ref[...] = corner


def start_kernel(z, pos_ref, rhs_ref, precond_ref, p_ref, send_a_ref, send_b_ref, gamma_ref):
    product = rhs_ref[...] * precond_ref[...]
    own = slice(z.rim, z.rim + z.nodes)
    p_ref[:, own] = product
    p_ref[:, z.window :] = jnp.zeros((ROWS, z.reach - z.window), F32)
    gamma_ref[...] = lanes_by_vector(z, product * rhs_ref[...])
    head, tail = product[:, : z.rim], product[:, z.nodes - z.rim :]
    even = pos_ref[0] % 2 == 0
    send_a_ref[...] = jnp.where(even, tail, head)
    send_b_ref[...] = jnp.where(even, head, tail)


def gather_middle(z, groups, list_ref, index_ref, low_ref, high_ref, window_ref, u_ref):
    total = z.window // LANES
    tile = (ROWS, LANES)

    def some_cells(g, _):
        cells = [list_ref[g * z.together + i] for i in range(z.together)]
        starts = [(low_ref[c] + z.shift) >> 7 for c in cells]
        ends = [(high_ref[c] + z.shift) >> 7 for c in cells]
        passes = functools.reduce(jnp.maximum, [(e - s) // SPAN + 1 for s, e in zip(starts, ends)])

        def one_pass(k, values):
            values = list(values)
            for i, c in enumerate(cells):
                start = jnp.minimum(starts[i] + k * SPAN, total)
                for t in range(z.tiles):
                    index = jnp.broadcast_to(index_ref[c, :, t * LANES : (t + 1) * LANES], tile)
                    low, high = index & (LANES - 1), (index >> 7) - start
                    value = values[i * z.tiles + t]
                    for h in range(SPAN):
                        at = pl.ds(pl.multiple_of((start + h) * LANES, LANES), LANES)
                        value = jnp.where(high == h, lane_gather(window_ref[:, at], low), value)
                    values[i * z.tiles + t] = value
            return tuple(values)

        values = lax.fori_loop(0, passes, one_pass, (jnp.zeros(tile, F32),) * (z.together * z.tiles))
        for i, c in enumerate(cells):
            rows = pl.ds(pl.multiple_of(c * ROWS, ROWS), ROWS)
            for t in range(z.tiles):
                u_ref[rows, t * LANES : (t + 1) * LANES] = values[i * z.tiles + t]
        return 0

    lax.fori_loop(*groups, some_cells, 0)


def gather_corners(z, corner_ref, window_ref, scale_ref, live, u_ref, uw_ref):
    tile = (ROWS, LANES)
    corner = jnp.broadcast_to(corner_ref[...], tile)
    low, high = corner & (LANES - 1), corner >> 7
    chains = [jnp.zeros(tile, F32)] * CHAINS
    for h in range(z.window // LANES):
        got = lane_gather(window_ref[:, h * LANES : (h + 1) * LANES], low)
        chains[h % CHAINS] = jnp.where(high == h, got, chains[h % CHAINS])
    corners = functools.reduce(jnp.add, chains)
    lane = iota(tile, 1)
    last = (z.elem - 1) % LANES
    for c in range(z.slots):
        weight = jnp.where(c < live, scale_ref[c], 0.0)
        rows = slice(c * ROWS, (c + 1) * ROWS)
        for t in range(z.tiles):
            lanes = slice(t * LANES, (t + 1) * LANES)
            value = u_ref[rows, lanes]
            if t == 0:
                value = jnp.where(lane == 0, corners[:, c : c + 1], value)
            if t == z.tiles - 1:
                value = jnp.where(lane == last, corners[:, z.slots + c : z.slots + c + 1], value)
            u_ref[rows, lanes] = value
            uw_ref[rows, lanes] = value * weight


def stiffness_product(k_high_ref, k_low_ref, uw_ref, e_ref):
    k_high, k_low = k_high_ref[...], k_low_ref[...]
    u_high, u_low = split(uw_ref[...])
    dot = functools.partial(lax.dot_general, dimension_numbers=NT, preferred_element_type=F32)
    e_ref[...] = dot(u_high, k_high) + (dot(u_high, k_low) + dot(u_low, k_high))


def entry_facts(z, position, atom_ref, count_ref, s):
    atom = atom_ref[s]
    owner = atom // z.owned
    return owner, atom - owner * z.owned, s < count_ref[position]


def contributions(z, position, pj_ref, cell_ref, atom_ref, count_ref, u_ref):
    values = [u_ref[pl.ds(pl.multiple_of(cell_ref[s] * ROWS, ROWS), ROWS), :] for s in range(z.entries)]
    sums = lax.dot_general(
        pj_ref[...], jnp.concatenate(values, axis=0), NT, precision=HIGHEST, preferred_element_type=F32
    )
    sums = jnp.concatenate([sums, jnp.zeros((sums.shape[0], LANES - sums.shape[1]), F32)], axis=1)
    lane, row = iota((ROWS, LANES), 1), iota((ROWS, LANES), 0)
    parts = [jnp.zeros((ROWS, LANES), F32)] * 3
    for s in range(z.entries):
        owner, local, alive = entry_facts(z, position, atom_ref, count_ref, s)
        got = lane_gather(sums[s * ROWS : (s + 1) * ROWS], s * ROWS + lane % ROWS)
        here = (lane // ROWS % ROWS == row) & (lane // z.pairs == local) & alive
        for k in range(3):
            parts[k] = parts[k] + jnp.where(here & (owner == position - 1 + k), got, 0.0)
    return [jnp.sum(part, axis=0, keepdims=True) for part in parts]


def sides(position, near, far):
    even = position % 2 == 0
    return jnp.where(even, far, near), jnp.where(even, near, far)


def first_window_kernel(z, low_ref, high_ref, list_ref, groups_ref, p_ref, index_ref, u_ref):
    gather_middle(z, (0, groups_ref[0]), list_ref, index_ref, low_ref, high_ref, p_ref, u_ref)


def first_kernel(
    z, pos_ref, count_ref, scale_ref, cell_ref, atom_ref, scount_ref, low_ref, high_ref, list_ref, groups_ref,
    p_in_ref, u_in_ref, precond_ref, potential_ref, halo_a_ref, halo_b_ref, index_ref, corner_ref, projector_ref,
    coupling_ref, p_ref, diag_ref, out_ref, uw_ref, pj_ref, u_ref,
):
    position = pos_ref[0]
    own = slice(z.rim, z.rim + z.nodes)
    p_ref[:, : z.rim], p_ref[:, z.rim + z.nodes : z.window] = sides(position, halo_a_ref[...], halo_b_ref[...])
    p_ref[:, own] = p_in_ref[:, own]
    p_ref[:, z.window :] = p_in_ref[:, z.window :]
    u_ref[...] = u_in_ref[...]
    diag_ref[...] = jnp.zeros_like(diag_ref)
    diag_ref[0:1, own] = precond_ref[...]
    diag_ref[1:2, own] = potential_ref[...]
    pj_ref[...] = jnp.zeros_like(pj_ref)
    pj_ref[:, : z.elem] = projector_ref[...]
    groups = groups_ref[0], z.slots // z.together
    gather_middle(z, groups, list_ref, index_ref, low_ref, high_ref, p_ref, u_ref)
    gather_corners(z, corner_ref, p_ref, scale_ref, count_ref[position], u_ref, uw_ref)
    parts = contributions(z, position, pj_ref, cell_ref, atom_ref, scount_ref, u_ref)
    small_lane, small_row = iota((ROWS, LANES), 1), iota((ROWS, LANES), 0)
    matrices = jnp.zeros((ROWS, LANES), F32)
    for atom in range(z.owned):
        block = jnp.concatenate([coupling_ref[atom], jnp.zeros((ROWS, LANES - z.channels), F32)], axis=1)
        got = lane_gather(block, small_lane % ROWS)
        matrices = jnp.where(small_lane // ROWS == atom * ROWS + small_row, got, matrices)
    message = jnp.concatenate(parts + [jnp.sum(matrices, axis=0, keepdims=True)], axis=0)
    for d in range(z.devices):
        out_ref[d] = message


def second_window_kernel(
    z, low_ref, high_ref, list_ref, groups_ref, p_ref, diag_ref, shift_ref, image_ref, index_ref, y_ref, q_ref, u_ref,
):
    y_ref[...] = image_ref[...] + (diag_ref[1:2, :] + shift_ref[...]) * p_ref[:, : z.window]
    q_ref[:, : z.window] = y_ref[...] * diag_ref[0:1, :]
    q_ref[:, z.window :] = jnp.zeros((ROWS, z.reach - z.window), F32)
    gather_middle(z, (0, groups_ref[0]), list_ref, index_ref, low_ref, high_ref, q_ref, u_ref)


def second_kernel(
    z, pos_ref, count_ref, scale_ref, cell_ref, atom_ref, scount_ref, low_ref, high_ref, list_ref, groups_ref,
    y_in_ref, q_in_ref, u_in_ref, p_ref, diag_in_ref, shift_ref, gamma_ref, halo_a_ref, halo_b_ref, index_ref, corner_ref, k_high_ref,
    k_low_ref, pj_ref, y_ref, q_ref, out_ref, e_ref, diag_ref, u_ref, uw_ref,
):
    position = pos_ref[0]
    left, right = sides(position, halo_a_ref[...], halo_b_ref[...])
    own = slice(z.rim, z.rim + z.nodes)
    ghosts = slice(0, z.rim), slice(z.rim + z.nodes, z.window)
    diag_ref[:, own] = diag_in_ref[:, own]
    diag_ref[:, ghosts[0]] = left[ROWS : ROWS + 2, : z.rim]
    diag_ref[:, ghosts[1]] = right[ROWS : ROWS + 2, z.rim :]
    y_ref[...] = y_in_ref[...]
    for ghost in ghosts:
        y_ref[:, ghost] += (diag_ref[1:2, ghost] - diag_in_ref[1:2, ghost]) * p_ref[:, ghost]
    y_ref[:, : 2 * z.rim] += left[:ROWS]
    y_ref[:, z.window - 2 * z.rim :] += right[:ROWS]
    q_ref[...] = q_in_ref[...]
    for rims in (slice(0, 2 * z.rim), slice(z.window - 2 * z.rim, z.window)):
        q_ref[:, rims] = y_ref[:, rims] * diag_ref[0:1, rims]
    u_ref[...] = u_in_ref[...]
    y, q = y_ref[:, own], q_ref[:, own]
    dots = [
        gamma_ref[...],
        lanes_by_vector(z, y * p_ref[:, own]),
        lanes_by_vector(z, y * q),
    ]
    energy = jnp.sum(q * q * (diag_ref[1:2, own] + shift_ref[...]), axis=1, keepdims=True)
    groups = groups_ref[0], z.slots // z.together
    gather_middle(z, groups, list_ref, index_ref, low_ref, high_ref, q_ref, u_ref)
    gather_corners(z, corner_ref, q_ref, scale_ref, count_ref[position], u_ref, uw_ref)
    parts = contributions(z, position, pj_ref, cell_ref, atom_ref, scount_ref, u_ref)
    stiffness_product(k_high_ref, k_low_ref, uw_ref, e_ref)
    elements = jnp.zeros((ROWS, z.width), F32)
    for c in range(z.slots):
        rows = slice(c * ROWS, (c + 1) * ROWS)
        elements = elements + u_ref[rows, :] * e_ref[rows, :]
    energy = energy + jnp.sum(elements, axis=1, keepdims=True)
    dots.append(lanes_by_vector(z, energy))
    line = dots[0]
    for k in range(1, len(dots)):
        line = line + pltpu.roll(dots[k], k * ROWS, 1)
    message = jnp.concatenate(parts + [line], axis=0)
    for d in range(z.devices):
        out_ref[d] = message


class Scatter:
    def __init__(self, z, index_ref, corner_ref, low_ref, high_ref, acc_ref):
        self.z, self.index_ref, self.corner_ref, self.acc_ref = z, index_ref, corner_ref, acc_ref
        self.low_ref, self.high_ref = low_ref, high_ref
        self.groups = z.window // WIDE
        self.pair = (2 * ROWS, LANES)
        sub = iota(self.pair, 0)
        self.lows = [(sub + k * 2 * ROWS).astype(jnp.int16) for k in range(WIDE // (2 * ROWS))]
        self.one, self.none = jnp.ones(self.pair, BF16), jnp.zeros(self.pair, BF16)
        self.lane = iota((ROWS, LANES), 1)
        self.end = (z.elem - 1) % LANES

    def two_parts(self, value):
        rounded = value.astype(BF16).astype(F32)
        return jnp.concatenate([rounded, value - rounded], axis=0).astype(BF16)

    def hot_rows(self, index):
        low = (index & (WIDE - 1)).astype(jnp.int16)
        return jnp.concatenate([jnp.where(low == k, self.one, self.none) for k in self.lows], axis=0)

    def masked(self, high, both, rows):
        high = high.astype(jnp.int16)
        return jnp.concatenate([jnp.where(high == jnp.int16(h), both, self.none) for h in range(rows)], axis=0)

    def product(self, lhs, hot):
        return lax.dot_general(lhs, hot, NT, preferred_element_type=F32)

    def start(self, sources):
        z = self.z
        corners = jnp.zeros((ROWS, LANES), F32)
        at = (z.tiles - 1) * LANES + self.end
        for cell, values in sources:
            corners = corners + jnp.where(self.lane == cell, values[:, 0:1], 0.0)
            corners = corners + jnp.where(self.lane == z.slots + cell, values[:, at : at + 1], 0.0)
        index = jnp.broadcast_to(self.corner_ref[...], self.pair)
        rows = self.groups * 2 * ROWS
        self.acc_ref[:rows, :] = self.product(
            self.masked(index >> 8, self.two_parts(corners), self.groups), self.hot_rows(index)
        )
        self.acc_ref[rows:, :] = jnp.zeros((BAND * 2 * ROWS, WIDE), F32)

    def add(self, cells, value_of):
        z = self.z
        starts = [(self.low_ref[c] + z.shift) >> 8 for c in cells]
        ends = [(self.high_ref[c] + z.shift) >> 8 for c in cells]
        passes = functools.reduce(jnp.maximum, [(e - s) // BAND + 1 for s, e in zip(starts, ends)])

        def one_pass(k, _):
            for i, c in enumerate(cells):
                start = jnp.minimum(starts[i] + k * BAND, self.groups)
                lhs, hot = [], []
                for t in range(z.tiles):
                    index = jnp.broadcast_to(self.index_ref[c, :, t * LANES : (t + 1) * LANES], self.pair)
                    value = value_of(i, t)
                    if t == 0:
                        value = jnp.where(self.lane == 0, 0.0, value)
                    if t == z.tiles - 1:
                        value = jnp.where(self.lane == self.end, 0.0, value)
                    lhs.append(self.masked((index >> 8) - start, self.two_parts(value), BAND))
                    hot.append(self.hot_rows(index))
                to = pl.ds(pl.multiple_of(start * 2 * ROWS, 2 * ROWS), BAND * 2 * ROWS)
                self.acc_ref[to, :] += self.product(jnp.concatenate(lhs, axis=1), jnp.concatenate(hot, axis=1))
            return 0

        lax.fori_loop(0, passes, one_pass, 0)

    def result(self, h):
        at = h * 2 * ROWS
        return self.acc_ref[at : at + ROWS] + self.acc_ref[at + ROWS : at + 2 * ROWS]


def cells_kernel(z, multiply, low_ref, high_ref, index_ref, corner_ref, *refs):
    if multiply:
        uw_ref, stiffness_ref, image_ref, k_high_ref, k_low_ref, e_ref, k_ref, acc_ref = refs
        k_ref[...] = jnp.zeros_like(k_ref)
        k_ref[: z.elem, : z.elem] = stiffness_ref[...]
        k_high_ref[...], k_low_ref[...] = split(k_ref[...])
        stiffness_product(k_high_ref, k_low_ref, uw_ref, e_ref)
    else:
        e_ref, image_ref, acc_ref = refs
    scatter = Scatter(z, index_ref, corner_ref, low_ref, high_ref, acc_ref)
    scatter.start([(c, e_ref[c * ROWS : (c + 1) * ROWS, :]) for c in range(z.slots)])

    def some_cells(g, _):
        cells = [g * z.together + i for i in range(z.together)]

        def value_of(i, t):
            rows = pl.ds(pl.multiple_of(cells[i] * ROWS, ROWS), ROWS)
            return e_ref[rows, t * LANES : (t + 1) * LANES]

        scatter.add(cells, value_of)
        return 0

    lax.fori_loop(0, z.slots // z.together, some_cells, 0)
    for h in range(scatter.groups):
        image_ref[:, h * WIDE : (h + 1) * WIDE] = scatter.result(h)


def support_kernel(
    z, last, pos_ref, cell_ref, atom_ref, scount_ref, low_ref, high_ref, sums_ref, coupling_ref, index_ref, corner_ref,
    pj_ref, diag_ref, cells_ref, *refs,
):
    if last:
        image_ref, send_a_ref, send_b_ref, dots_ref, support_ref, acc_ref = refs
    else:
        image_ref, send_a_ref, send_b_ref, support_ref, acc_ref = refs
    position = pos_ref[0]
    wanted = (
        pltpu.roll(sums_ref[:, 0, :], z.devices - 1, 0) + sums_ref[:, 1, :] + pltpu.roll(sums_ref[:, 2, :], 1, 0)
    )
    coupling = coupling_ref[:, 3, :]
    shape = (z.devices, LANES)
    lane = iota(shape, 1)
    term = jnp.zeros(shape, F32)
    for j in range(z.channels):
        matrix = lane_gather(coupling, lane // ROWS * ROWS + j)
        vector = lane_gather(wanted, lane // z.pairs * z.pairs + j * ROWS + lane % ROWS)
        term = term + matrix * vector
    if last:
        energy = jnp.sum(term * wanted, axis=0, keepdims=True)
        energy = jnp.broadcast_to(energy, (ROWS, LANES))
        step = ROWS
        while step < LANES:
            energy = energy + pltpu.roll(energy, step, 1)
            step *= 2
        line = iota((1, LANES), 1)
        dots_ref[...] = jnp.sum(sums_ref[:, 3, :], axis=0, keepdims=True) + jnp.where(
            line // ROWS == 3, energy[0:1], 0.0
        )
    block = iota(shape, 0)
    small_lane, small_row = iota((ROWS, LANES), 1), iota((ROWS, LANES), 0)
    spread = []
    for s in range(z.entries):
        owner, local, alive = entry_facts(z, position, atom_ref, scount_ref, s)
        mine = jnp.sum(jnp.where(block == owner, term, 0.0), axis=0, keepdims=True)
        got = lane_gather(
            jnp.broadcast_to(mine, (ROWS, LANES)), local * z.pairs + small_lane % ROWS * ROWS + small_row
        )
        spread.append(jnp.where((small_lane // ROWS == s) & alive, got, 0.0)[:, : z.entries * ROWS])
    support_ref[...] = jnp.dot(
        jnp.concatenate(spread, axis=0), pj_ref[...], precision=HIGHEST, preferred_element_type=F32
    )
    scatter = Scatter(z, index_ref, corner_ref, low_ref, high_ref, acc_ref)
    cells = [cell_ref[s] for s in range(z.entries)]
    scatter.start([(cell, support_ref[s * ROWS : (s + 1) * ROWS, :]) for s, cell in enumerate(cells)])
    for first in range(0, z.entries, z.together):
        some = cells[first : first + z.together]

        def value_of(i, t):
            s = first + i
            return support_ref[s * ROWS : (s + 1) * ROWS, t * LANES : (t + 1) * LANES]

        scatter.add(some, value_of)
    for h in range(scatter.groups):
        at = slice(h * WIDE, (h + 1) * WIDE)
        image_ref[:, at] = cells_ref[:, at] + scatter.result(h)
    even = position % 2 == 0
    ends = [slice(0, 2 * z.rim), slice(z.window - 2 * z.rim, z.window)]
    for source_ref, rows in ((image_ref, slice(0, ROWS)),) + (() if last else ((diag_ref, slice(ROWS, ROWS + 2)),)):
        low_rim, high_rim = (source_ref[:, end] for end in ends)
        send_a_ref[rows, :] = jnp.where(even, high_rim, low_rim)
        send_b_ref[rows, :] = jnp.where(even, low_rim, high_rim)


def last_kernel(
    z, rhs_ref, p_ref, diag_ref, shift_ref, y_ref, q_ref, image_ref, dots_ref, solution_ref, residual_ref, factor_ref,
):
    own = slice(z.rim, z.rim + z.nodes)
    lane, row = iota((ROWS, LANES), 1), iota((ROWS, LANES), 0)
    line = jnp.broadcast_to(dots_ref[...], (ROWS, LANES))

    def column(k):
        return jnp.sum(jnp.where(lane == k * ROWS + row, line, 0.0), axis=1, keepdims=True)

    gamma, py, qy, qq = (column(k) for k in range(4))
    alpha = gamma / py
    fresh = gamma - 2.0 * alpha * py + alpha * alpha * qy
    beta = fresh / gamma
    more = 1.0 + beta
    step = fresh / (more * more * py - 2.0 * more * alpha * qy + alpha * alpha * qq)
    p, q, y = p_ref[:, own], q_ref[:, own], y_ref[:, own]
    second = image_ref[:, own] + (diag_ref[1:2, own] + shift_ref[...]) * q
    search = (p - alpha * q) + beta * p
    solution_ref[...] = alpha * p + step * search
    residual_ref[...] = (rhs_ref[...] - alpha * y) - step * (more * y - alpha * second)
    factor_ref[...] = jnp.broadcast_to(step * alpha, (ROWS, LANES))


def rim_kernel(z, pos_ref, residual_in_ref, halo_a_ref, halo_b_ref, factor_ref, residual_ref):
    left, right = sides(pos_ref[0], halo_a_ref[...], halo_b_ref[...])
    factor = factor_ref[:, :1]
    first, last = slice(0, z.rim), slice(z.nodes - z.rim, z.nodes)
    residual_ref[:, z.rim : z.nodes - z.rim] = residual_in_ref[:, z.rim : z.nodes - z.rim]
    residual_ref[:, first] = residual_in_ref[:, first] + factor * left[:, z.rim :]
    residual_ref[:, last] = residual_in_ref[:, last] + factor * right[:, : z.rim]


def on_device(
    rhs, potential, precond, shift, stiffness, cell_scale, conn, cell_count, projector, support_cell, support_atom,
    support_count, atom_matrix,
):
    count = lax.axis_size("dom")
    z = Sizes(count, rhs, conn, projector, atom_matrix)
    position = lax.axis_index("dom")
    even = position % 2 == 0
    pos = position.astype(jnp.int32).reshape(1)
    near = [(i, i ^ 1) for i in range(count)]
    far = [(i, j) for i in range(1, count - 1) for j in [i + 1 if i % 2 else i - 1]]

    def exchange(a, b):
        return lax.ppermute(a, "dom", near), lax.ppermute(b, "dom", far)

    def call(kernel, outs, scratch, scalars, *args, in_hbm=()):
        args = [pltpu.with_memory_space_constraint(x, pltpu.VMEM) for x in args]
        return pl.pallas_call(
            kernel,
            out_shape=[
                jax.ShapeDtypeStruct(s, d) if i in in_hbm else pltpu.VMEM(s, d) for i, (s, d) in enumerate(outs)
            ],
            in_specs=[SMEM] * len(scalars) + [VMEM] * len(args),
            out_specs=[VMEM] * len(outs),
            scratch_shapes=[pltpu.VMEM(s, d) for s, d in scratch],
            compiler_params=pltpu.CompilerParams(vmem_limit_bytes=16 * 1024 * 1024),
        )(*scalars, *args)

    precond_row, potential_row = precond[None, :], potential[None, :]
    shift_column = shift[:, None]
    flat_projector = projector.reshape(z.entries * z.channels, z.elem)
    middle = conn[:, 1:-1]
    ranges = jnp.min(middle, axis=1), jnp.max(middle, axis=1)

    def listed(margin):
        good = (ranges[0] + z.shift >= margin) & (ranges[1] + z.shift < z.window - margin)
        one = good.astype(jnp.int32)
        number = jnp.arange(z.slots)
        before = jnp.sum(jnp.where(number[None, :] < number[:, None], one[None, :], 0), axis=1)
        total = jnp.sum(one)
        place = jnp.where(good, before, total + number - before)
        order = jnp.sum(jnp.where(place[None, :] == number[:, None], number[None, :], 0), axis=1)
        return order.astype(jnp.int32), (total // z.together).astype(jnp.int32).reshape(1)

    cells = (z.slots * ROWS, z.width)
    window, reach, own = (z.vectors, z.window), (z.vectors, z.reach), (z.vectors, z.nodes)
    message = (z.devices, 4, LANES)
    square, entries = (z.width, z.width), (z.entries * ROWS, z.width)
    rim, more_rim = (z.vectors, 2 * z.rim), (z.vectors + 2, 2 * z.rim)
    acc = ((z.window // WIDE + BAND) * 2 * ROWS, WIDE)
    supports = support_cell, support_atom, support_count

    p, send_a, send_b, gamma = call(
        functools.partial(start_kernel, z),
        [(reach, F32), ((z.vectors, z.rim), F32), ((z.vectors, z.rim), F32), ((1, LANES), F32)],
        [],
        (pos,),
        rhs, precond_row,
    )
    halo = exchange(send_a, send_b)
    first_list, second_list = listed(z.rim), listed(2 * z.rim)
    index, corner = call(
        functools.partial(prepare_kernel, z),
        [((z.slots, 1, z.width), jnp.int32), ((1, LANES), jnp.int32)],
        [],
        (),
        conn,
    )
    (u,) = call(
        functools.partial(first_window_kernel, z), [(cells, F32)], [], (*ranges, *first_list), p, index,
    )
    p, diag, sums, uw, pj = call(
        functools.partial(first_kernel, z),
        [(reach, F32), ((2, z.window), F32), (message, F32), (cells, F32), (entries, F32)],
        [(cells, F32)],
        (pos, cell_count, cell_scale, *supports, *ranges, *first_list),
        p, u, precond_row, potential_row, *halo, index, corner, flat_projector, atom_matrix,
    )
    coupled = lax.all_to_all(sums, "dom", 0, 0)
    image, k_high, k_low = call(
        functools.partial(cells_kernel, z, True),
        [(window, F32), (square, BF16), (square, BF16)],
        [(cells, F32), (square, F32), (acc, F32)],
        ranges,
        index, corner, uw, stiffness,
    )
    image, send_a, send_b = call(
        functools.partial(support_kernel, z, False),
        [(window, F32), (more_rim, F32), (more_rim, F32)],
        [(entries, F32), (acc, F32)],
        (pos, *supports, *ranges),
        coupled, coupled, index, corner, pj, diag, image,
    )
    halo = exchange(send_a, send_b)
    y, q, u = call(
        functools.partial(second_window_kernel, z),
        [(window, F32), (reach, F32), (cells, F32)],
        [],
        (*ranges, *second_list),
        p, diag, shift_column, image, index,
    )
    y, q, sums, e = call(
        functools.partial(second_kernel, z),
        [(window, F32), (reach, F32), (message, F32), (cells, F32)],
        [((2, z.window), F32), (cells, F32), (cells, F32)],
        (pos, cell_count, cell_scale, *supports, *ranges, *second_list),
        y, q, u, p, diag, shift_column, gamma, *halo, index, corner, k_high, k_low, pj,
    )
    totals = lax.all_to_all(sums, "dom", 0, 0)
    (image,) = call(functools.partial(cells_kernel, z, False), [(window, F32)], [(acc, F32)], ranges, index, corner, e)
    image, send_a, send_b, dots = call(
        functools.partial(support_kernel, z, True),
        [(window, F32), (rim, F32), (rim, F32), ((1, LANES), F32)],
        [(entries, F32), (acc, F32)],
        (pos, *supports, *ranges),
        totals, coupled, index, corner, pj, diag, image,
    )
    halo = exchange(send_a, send_b)
    answer, residual, factor = call(
        functools.partial(last_kernel, z),
        [(own, F32), (own, F32), ((ROWS, LANES), F32)],
        [],
        (),
        rhs, p, diag, shift_column, y, q, image, dots, in_hbm=(0,),
    )
    (residual,) = call(functools.partial(rim_kernel, z), [(own, F32)], [], (pos,), residual, *halo, factor, in_hbm=(0,))
    return answer, residual


def solution(mesh):
    placed = (
        P(None, "dom"),
        P("dom"),
        P("dom"),
        P(),
        P(),
        P("dom"),
        P("dom", None),
        P(),
        P("dom", None, None),
        P("dom"),
        P("dom"),
        P(),
        P("dom", None, None),
    )
    return jax.shard_map(
        on_device,
        mesh=mesh,
        in_specs=placed,
        out_specs=(P(None, "dom"), P(None, "dom")),
        check_vma=False,
    )
```

```python
import functools

import jax
import jax.numpy as jnp
from jax import lax
from jax.experimental import pallas as pl
from jax.experimental.pallas import tpu as pltpu
from jax.sharding import PartitionSpec as P

LANES = 128
ROWS = 8
WIDE = 256
CHAINS = 4
SPAN = 14
BAND = 8
TOGETHER = 8
F32 = jnp.float32
BF16 = jnp.bfloat16
HIGHEST = lax.Precision.HIGHEST
NT = (((1,), (1,)), ((), ()))
VMEM = pl.BlockSpec(memory_space=pltpu.VMEM)
SMEM = pl.BlockSpec(memory_space=pltpu.SMEM)


def round_up(value, step):
    return -(-value // step) * step


class Sizes:
    def __init__(self, count, rhs, conn, projector, atom_matrix):
        self.devices = count
        self.vectors, self.nodes = rhs.shape
        self.slots, self.elem = conn.shape
        self.entries, self.channels = projector.shape[:2]
        self.owned = atom_matrix.shape[0]
        self.ghost = self.nodes // 16
        self.rim = round_up(self.ghost, WIDE)
        self.shift = self.rim - self.ghost
        self.window = self.nodes + 2 * self.rim
        self.width = round_up(self.elem, LANES)
        self.tiles = self.width // LANES
        self.pairs = self.channels * self.vectors
        self.reach = self.window + SPAN * LANES
        self.together = TOGETHER if self.slots % TOGETHER == 0 else 1
        assert self.vectors == ROWS and self.channels == ROWS and 2 * self.slots <= LANES
        assert self.nodes % WIDE == 0 and self.owned * self.pairs == LANES


def lane_gather(values, index):
    return jnp.take_along_axis(values, index, axis=1, mode="promise_in_bounds")


def iota(shape, dim):
    return lax.broadcasted_iota(jnp.int32, shape, dim)


def split(values):
    high = values.astype(BF16)
    return high, (values - high.astype(F32)).astype(BF16)


def lanes_by_vector(z, values):
    total = jnp.sum(values, axis=1, keepdims=True)
    spread = jnp.broadcast_to(total, (ROWS, LANES))
    return jnp.sum(jnp.where(iota((ROWS, LANES), 1) == iota((ROWS, LANES), 0), spread, 0.0), axis=0, keepdims=True)


LOW, HIGH, FIRST_LIST, SECOND_LIST, CELL, OWNER, LOCAL, OTHER = range(8)


def prepare_kernel(
    z, pos_ref, count_ref, scale_ref, cell_ref, atom_ref, scount_ref, conn_ref,
    index_ref, corner_ref, table_ref, weight_ref,
):
    position = pos_ref[0]
    line = iota((1, LANES), 1)
    corner = jnp.zeros((1, LANES), jnp.int32)
    index_ref[...] = jnp.zeros_like(index_ref)
    live = count_ref[position]
    for c in range(z.slots):
        row = conn_ref[c : c + 1, :] + z.shift
        index_ref[c, :, : z.elem] = row
        corner = jnp.where(line == c, row[:, :1], corner)
        corner = jnp.where(line == z.slots + c, row[:, z.elem - 1 :], corner)
        weight = jnp.where(c < live, scale_ref[c], 0.0)
        weight_ref[c * ROWS : (c + 1) * ROWS, :] = jnp.zeros((ROWS, LANES), F32) + weight
    corner_ref[...] = corner
    nodes = (conn_ref[...] + z.shift).astype(F32)
    place = iota(nodes.shape, 1)
    middle = (place > 0) & (place < z.elem - 1)
    low = jnp.min(jnp.where(middle, nodes, 1.0 * z.window), axis=1, keepdims=True)
    high = jnp.max(jnp.where(middle, nodes, 0.0), axis=1, keepdims=True)
    lane, cell = iota((z.slots, LANES), 1), iota((z.slots, LANES), 0)

    def as_row(column):
        return jnp.sum(jnp.where(lane == cell, column, 0.0), axis=0, keepdims=True)

    rows = [as_row(low), as_row(high)]
    for margin in (z.rim, 2 * z.rim):
        good = jnp.where((low >= margin) & (high < z.window - margin), 1.0, 0.0)
        good = jnp.broadcast_to(good, (z.slots, LANES))
        number = cell.astype(F32)
        before = jnp.sum(jnp.where(lane < cell, as_row(good), 0.0), axis=1, keepdims=True)
        at = jnp.where(good > 0.5, before, z.slots - 1.0 - (number - before))
        rows.append(
            jnp.sum(jnp.where(lane.astype(F32) == at, number + z.slots * good, 0.0), axis=0, keepdims=True)
        )
    table = [row.astype(jnp.int32) for row in rows]
    facts = [jnp.zeros((1, LANES), jnp.int32)] * 3
    for s in range(z.entries):
        atom = atom_ref[s]
        owner = atom // z.owned
        for k, fact in enumerate((cell_ref[s], owner, atom - owner * z.owned)):
            facts[k] = jnp.where(line == s, fact, facts[k])
    other = jnp.where(line == 0, position, jnp.where(line == 1, scount_ref[position], 0))
    table_ref[...] = jnp.concatenate(table + facts + [other], axis=0)


def start_kernel(
    z, pos_ref, shift_ref, rhs_ref, precond_ref, potential_ref,
    p_ref, send_a_ref, send_b_ref, gamma_ref, diag_ref, shift_tile_ref,
):
    product = rhs_ref[...] * precond_ref[...]
    own = slice(z.rim, z.rim + z.nodes)
    head, tail = product[:, : z.rim], product[:, z.nodes - z.rim :]
    even = pos_ref[0] % 2 == 0
    send_a_ref[...] = jnp.where(even, tail, head)
    send_b_ref[...] = jnp.where(even, head, tail)
    p_ref[:, own] = product
    p_ref[:, z.window :] = jnp.zeros((ROWS, z.reach - z.window), F32)
    gamma_ref[...] = lanes_by_vector(z, product * rhs_ref[...])
    diag_ref[...] = jnp.zeros_like(diag_ref)
    diag_ref[0:1, own] = precond_ref[...]
    diag_ref[1:2, own] = potential_ref[...]
    row = iota((ROWS, LANES), 0)
    tile = jnp.zeros((ROWS, LANES), F32)
    for v in range(z.vectors):
        tile = jnp.where(row == v, shift_ref[v], tile)
    shift_tile_ref[...] = tile


def full_groups(z, table_ref, which):
    ends = [table_ref[which, g * z.together + z.together - 1] for g in range(z.slots // z.together)]
    return functools.reduce(jnp.add, [(end >= z.slots).astype(jnp.int32) for end in ends])


def gather_middle(z, groups, which, table_ref, index_ref, window_ref, u_ref):
    total = z.window // LANES
    tile = (ROWS, LANES)

    def some_cells(g, _):
        cells = [table_ref[which, g * z.together + i] for i in range(z.together)]
        cells = [jnp.where(c >= z.slots, c - z.slots, c) for c in cells]
        starts = [table_ref[LOW, c] >> 7 for c in cells]
        ends = [table_ref[HIGH, c] >> 7 for c in cells]
        passes = functools.reduce(jnp.maximum, [(e - s) // SPAN + 1 for s, e in zip(starts, ends)])

        def one_pass(k, values):
            values = list(values)
            for i, c in enumerate(cells):
                start = jnp.minimum(starts[i] + k * SPAN, total)
                for t in range(z.tiles):
                    index = jnp.broadcast_to(index_ref[c, :, t * LANES : (t + 1) * LANES], tile)
                    low, high = index & (LANES - 1), (index >> 7) - start
                    value = values[i * z.tiles + t]
                    for h in range(SPAN):
                        at = pl.ds(pl.multiple_of((start + h) * LANES, LANES), LANES)
                        value = jnp.where(high == h, lane_gather(window_ref[:, at], low), value)
                    values[i * z.tiles + t] = value
            return tuple(values)

        values = lax.fori_loop(0, passes, one_pass, (jnp.zeros(tile, F32),) * (z.together * z.tiles))
        for i, c in enumerate(cells):
            rows = pl.ds(pl.multiple_of(c * ROWS, ROWS), ROWS)
            for t in range(z.tiles):
                u_ref[rows, t * LANES : (t + 1) * LANES] = values[i * z.tiles + t]
        return 0

    lax.fori_loop(*groups, some_cells, 0)


def gather_corners(z, corner_ref, window_ref, weight_ref, u_ref, uw_ref):
    tile = (ROWS, LANES)
    corner = jnp.broadcast_to(corner_ref[...], tile)
    low, high = corner & (LANES - 1), corner >> 7
    chains = [jnp.zeros(tile, F32)] * CHAINS
    for h in range(z.window // LANES):
        got = lane_gather(window_ref[:, h * LANES : (h + 1) * LANES], low)
        chains[h % CHAINS] = jnp.where(high == h, got, chains[h % CHAINS])
    corners = functools.reduce(jnp.add, chains)
    lane = iota(tile, 1)
    last = (z.elem - 1) % LANES
    for c in range(z.slots):
        rows = slice(c * ROWS, (c + 1) * ROWS)
        weight = weight_ref[rows, :]
        for t in range(z.tiles):
            lanes = slice(t * LANES, (t + 1) * LANES)
            value = u_ref[rows, lanes]
            if t == 0:
                value = jnp.where(lane == 0, corners[:, c : c + 1], value)
            if t == z.tiles - 1:
                value = jnp.where(lane == last, corners[:, z.slots + c : z.slots + c + 1], value)
            u_ref[rows, lanes] = value
            uw_ref[rows, lanes] = value * weight


def stiffness_product(k_high_ref, k_low_ref, uw_ref, e_ref):
    k_high, k_low = k_high_ref[...], k_low_ref[...]
    u_high, u_low = split(uw_ref[...])
    dot = functools.partial(lax.dot_general, dimension_numbers=NT, preferred_element_type=F32)
    e_ref[...] = dot(u_high, k_high) + (dot(u_high, k_low) + dot(u_low, k_high))


def entry_facts(table_ref, s):
    return table_ref[OWNER, s], table_ref[LOCAL, s], s < table_ref[OTHER, 1]


def contributions(z, table_ref, pj_ref, u_ref):
    values = [u_ref[pl.ds(pl.multiple_of(table_ref[CELL, s] * ROWS, ROWS), ROWS), :] for s in range(z.entries)]
    sums = lax.dot_general(
        pj_ref[...], jnp.concatenate(values, axis=0), NT, precision=HIGHEST, preferred_element_type=F32
    )
    sums = jnp.concatenate([sums, jnp.zeros((sums.shape[0], LANES - sums.shape[1]), F32)], axis=1)
    lane, row = iota((ROWS, LANES), 1), iota((ROWS, LANES), 0)
    position = table_ref[OTHER, 0]
    parts = [jnp.zeros((ROWS, LANES), F32)] * 3
    for s in range(z.entries):
        owner, local, alive = entry_facts(table_ref, s)
        got = lane_gather(sums[s * ROWS : (s + 1) * ROWS], s * ROWS + lane % ROWS)
        here = (lane // ROWS % ROWS == row) & (lane // z.pairs == local) & alive
        for k in range(3):
            parts[k] = parts[k] + jnp.where(here & (owner == position - 1 + k), got, 0.0)
    return [jnp.sum(part, axis=0, keepdims=True) for part in parts]


def sides(position, near, far):
    even = position % 2 == 0
    return jnp.where(even, far, near), jnp.where(even, near, far)


def first_window_kernel(z, table_ref, p_ref, index_ref, u_ref):
    groups = 0, full_groups(z, table_ref, FIRST_LIST)
    gather_middle(z, groups, FIRST_LIST, table_ref, index_ref, p_ref, u_ref)


def first_kernel(
    z, table_ref, p_in_ref, u_in_ref, halo_a_ref, halo_b_ref, index_ref, corner_ref, weight_ref, projector_ref,
    coupling_ref, p_ref, out_ref, uw_ref, pj_ref, u_ref,
):
    own = slice(z.rim, z.rim + z.nodes)
    halo = sides(table_ref[OTHER, 0], halo_a_ref[...], halo_b_ref[...])
    p_ref[:, : z.rim], p_ref[:, z.rim + z.nodes : z.window] = halo
    p_ref[:, own] = p_in_ref[:, own]
    p_ref[:, z.window :] = p_in_ref[:, z.window :]
    u_ref[...] = u_in_ref[...]
    pj_ref[...] = jnp.zeros_like(pj_ref)
    pj_ref[:, : z.elem] = projector_ref[...]
    groups = full_groups(z, table_ref, FIRST_LIST), z.slots // z.together
    gather_middle(z, groups, FIRST_LIST, table_ref, index_ref, p_ref, u_ref)
    gather_corners(z, corner_ref, p_ref, weight_ref, u_ref, uw_ref)
    parts = contributions(z, table_ref, pj_ref, u_ref)
    small_lane, small_row = iota((ROWS, LANES), 1), iota((ROWS, LANES), 0)
    matrices = jnp.zeros((ROWS, LANES), F32)
    for atom in range(z.owned):
        block = jnp.concatenate([coupling_ref[atom], jnp.zeros((ROWS, LANES - z.channels), F32)], axis=1)
        got = lane_gather(block, small_lane % ROWS)
        matrices = jnp.where(small_lane // ROWS == atom * ROWS + small_row, got, matrices)
    message = jnp.concatenate(parts + [jnp.sum(matrices, axis=0, keepdims=True)], axis=0)
    for d in range(z.devices):
        out_ref[d] = message


def second_window_kernel(
    z, table_ref, p_ref, diag_ref, shift_ref, image_ref, index_ref, y_ref, q_ref, u_ref,
):
    y_ref[...] = image_ref[...] + (diag_ref[1:2, :] + shift_ref[:, :1]) * p_ref[:, : z.window]
    q_ref[:, : z.window] = y_ref[...] * diag_ref[0:1, :]
    q_ref[:, z.window :] = jnp.zeros((ROWS, z.reach - z.window), F32)
    groups = 0, full_groups(z, table_ref, SECOND_LIST)
    gather_middle(z, groups, SECOND_LIST, table_ref, index_ref, q_ref, u_ref)


def second_kernel(
    z, table_ref, y_in_ref, q_in_ref, u_in_ref, p_ref, diag_in_ref, shift_ref, gamma_ref, halo_a_ref, halo_b_ref,
    index_ref, corner_ref, weight_ref, k_high_ref, k_low_ref, pj_ref, y_ref, q_ref, out_ref, e_ref, diag_ref, u_ref, uw_ref,
):
    left, right = sides(table_ref[OTHER, 0], halo_a_ref[...], halo_b_ref[...])
    own = slice(z.rim, z.rim + z.nodes)
    ghosts = slice(0, z.rim), slice(z.rim + z.nodes, z.window)
    diag_ref[:, own] = diag_in_ref[:, own]
    diag_ref[:, ghosts[0]] = left[ROWS : ROWS + 2, : z.rim]
    diag_ref[:, ghosts[1]] = right[ROWS : ROWS + 2, z.rim :]
    y_ref[...] = y_in_ref[...]
    for ghost in ghosts:
        y_ref[:, ghost] += (diag_ref[1:2, ghost] - diag_in_ref[1:2, ghost]) * p_ref[:, ghost]
    y_ref[:, : 2 * z.rim] += left[:ROWS]
    y_ref[:, z.window - 2 * z.rim :] += right[:ROWS]
    q_ref[...] = q_in_ref[...]
    for rims in (slice(0, 2 * z.rim), slice(z.window - 2 * z.rim, z.window)):
        q_ref[:, rims] = y_ref[:, rims] * diag_ref[0:1, rims]
    u_ref[...] = u_in_ref[...]
    y, q = y_ref[:, own], q_ref[:, own]
    dots = [
        gamma_ref[...],
        lanes_by_vector(z, y * p_ref[:, own]),
        lanes_by_vector(z, y * q),
    ]
    energy = jnp.sum(q * q * (diag_ref[1:2, own] + shift_ref[:, :1]), axis=1, keepdims=True)
    groups = full_groups(z, table_ref, SECOND_LIST), z.slots // z.together
    gather_middle(z, groups, SECOND_LIST, table_ref, index_ref, q_ref, u_ref)
    gather_corners(z, corner_ref, q_ref, weight_ref, u_ref, uw_ref)
    parts = contributions(z, table_ref, pj_ref, u_ref)
    stiffness_product(k_high_ref, k_low_ref, uw_ref, e_ref)
    elements = jnp.zeros((ROWS, z.width), F32)
    for c in range(z.slots):
        rows = slice(c * ROWS, (c + 1) * ROWS)
        elements = elements + u_ref[rows, :] * e_ref[rows, :]
    energy = energy + jnp.sum(elements, axis=1, keepdims=True)
    dots.append(lanes_by_vector(z, energy))
    line = dots[0]
    for k in range(1, len(dots)):
        line = line + pltpu.roll(dots[k], k * ROWS, 1)
    message = jnp.concatenate(parts + [line], axis=0)
    for d in range(z.devices):
        out_ref[d] = message


class Scatter:
    def __init__(self, z, table_ref, index_ref, corner_ref, acc_ref):
        self.z, self.index_ref, self.corner_ref, self.acc_ref = z, index_ref, corner_ref, acc_ref
        self.table_ref = table_ref
        self.groups = z.window // WIDE
        self.pair = (2 * ROWS, LANES)
        sub = iota(self.pair, 0)
        self.lows = [(sub + k * 2 * ROWS).astype(jnp.int16) for k in range(WIDE // (2 * ROWS))]
        self.one, self.none = jnp.ones(self.pair, BF16), jnp.zeros(self.pair, BF16)
        self.lane = iota((ROWS, LANES), 1)
        self.end = (z.elem - 1) % LANES

    def two_parts(self, value):
        rounded = value.astype(BF16).astype(F32)
        return jnp.concatenate([rounded, value - rounded], axis=0).astype(BF16)

    def hot_rows(self, index):
        low = (index & (WIDE - 1)).astype(jnp.int16)
        return jnp.concatenate([jnp.where(low == k, self.one, self.none) for k in self.lows], axis=0)

    def masked(self, high, both, rows):
        high = high.astype(jnp.int16)
        return jnp.concatenate([jnp.where(high == jnp.int16(h), both, self.none) for h in range(rows)], axis=0)

    def product(self, lhs, hot):
        return lax.dot_general(lhs, hot, NT, preferred_element_type=F32)

    def start(self, sources):
        z = self.z
        corners = jnp.zeros((ROWS, LANES), F32)
        at = (z.tiles - 1) * LANES + self.end
        for cell, values in sources:
            corners = corners + jnp.where(self.lane == cell, values[:, 0:1], 0.0)
            corners = corners + jnp.where(self.lane == z.slots + cell, values[:, at : at + 1], 0.0)
        index = jnp.broadcast_to(self.corner_ref[...], self.pair)
        rows = self.groups * 2 * ROWS
        self.acc_ref[:rows, :] = self.product(
            self.masked(index >> 8, self.two_parts(corners), self.groups), self.hot_rows(index)
        )
        self.acc_ref[rows:, :] = jnp.zeros((BAND * 2 * ROWS, WIDE), F32)

    def add(self, cells, value_of):
        z = self.z
        starts = [self.table_ref[LOW, c] >> 8 for c in cells]
        ends = [self.table_ref[HIGH, c] >> 8 for c in cells]
        passes = functools.reduce(jnp.maximum, [(e - s) // BAND + 1 for s, e in zip(starts, ends)])

        def one_pass(k, _):
            for i, c in enumerate(cells):
                start = jnp.minimum(starts[i] + k * BAND, self.groups)
                lhs, hot = [], []
                for t in range(z.tiles):
                    index = jnp.broadcast_to(self.index_ref[c, :, t * LANES : (t + 1) * LANES], self.pair)
                    value = value_of(i, t)
                    if t == 0:
                        value = jnp.where(self.lane == 0, 0.0, value)
                    if t == z.tiles - 1:
                        value = jnp.where(self.lane == self.end, 0.0, value)
                    lhs.append(self.masked((index >> 8) - start, self.two_parts(value), BAND))
                    hot.append(self.hot_rows(index))
                to = pl.ds(pl.multiple_of(start * 2 * ROWS, 2 * ROWS), BAND * 2 * ROWS)
                self.acc_ref[to, :] += self.product(jnp.concatenate(lhs, axis=1), jnp.concatenate(hot, axis=1))
            return 0

        lax.fori_loop(0, passes, one_pass, 0)

    def result(self, h):
        at = h * 2 * ROWS
        return self.acc_ref[at : at + ROWS] + self.acc_ref[at + ROWS : at + 2 * ROWS]


def cells_kernel(z, multiply, table_ref, index_ref, corner_ref, *refs):
    if multiply:
        uw_ref, stiffness_ref, image_ref, k_high_ref, k_low_ref, e_ref, k_ref, acc_ref = refs
        k_ref[...] = jnp.zeros_like(k_ref)
        k_ref[: z.elem, : z.elem] = stiffness_ref[...]
        k_high_ref[...], k_low_ref[...] = split(k_ref[...])
        stiffness_product(k_high_ref, k_low_ref, uw_ref, e_ref)
    else:
        e_ref, image_ref, acc_ref = refs
    scatter = Scatter(z, table_ref, index_ref, corner_ref, acc_ref)
    scatter.start([(c, e_ref[c * ROWS : (c + 1) * ROWS, :]) for c in range(z.slots)])

    def some_cells(g, _):
        cells = [g * z.together + i for i in range(z.together)]

        def value_of(i, t):
            rows = pl.ds(pl.multiple_of(cells[i] * ROWS, ROWS), ROWS)
            return e_ref[rows, t * LANES : (t + 1) * LANES]

        scatter.add(cells, value_of)
        return 0

    lax.fori_loop(0, z.slots // z.together, some_cells, 0)
    for h in range(scatter.groups):
        image_ref[:, h * WIDE : (h + 1) * WIDE] = scatter.result(h)


def support_kernel(
    z, last, table_ref, sums_ref, coupling_ref, index_ref, corner_ref, pj_ref, diag_ref, cells_ref, *refs,
):
    if last:
        image_ref, send_a_ref, send_b_ref, dots_ref, support_ref, acc_ref = refs
    else:
        image_ref, send_a_ref, send_b_ref, support_ref, acc_ref = refs
    position = table_ref[OTHER, 0]
    wanted = (
        pltpu.roll(sums_ref[:, 0, :], z.devices - 1, 0) + sums_ref[:, 1, :] + pltpu.roll(sums_ref[:, 2, :], 1, 0)
    )
    coupling = coupling_ref[:, 3, :]
    shape = (z.devices, LANES)
    lane = iota(shape, 1)
    term = jnp.zeros(shape, F32)
    for j in range(z.channels):
        matrix = lane_gather(coupling, lane // ROWS * ROWS + j)
        vector = lane_gather(wanted, lane // z.pairs * z.pairs + j * ROWS + lane % ROWS)
        term = term + matrix * vector
    if last:
        energy = jnp.sum(term * wanted, axis=0, keepdims=True)
        energy = jnp.broadcast_to(energy, (ROWS, LANES))
        step = ROWS
        while step < LANES:
            energy = energy + pltpu.roll(energy, step, 1)
            step *= 2
        line = iota((1, LANES), 1)
        dots_ref[...] = jnp.sum(sums_ref[:, 3, :], axis=0, keepdims=True) + jnp.where(
            line // ROWS == 3, energy[0:1], 0.0
        )
    block = iota(shape, 0)
    small_lane, small_row = iota((ROWS, LANES), 1), iota((ROWS, LANES), 0)
    spread = []
    for s in range(z.entries):
        owner, local, alive = entry_facts(table_ref, s)
        mine = jnp.sum(jnp.where(block == owner, term, 0.0), axis=0, keepdims=True)
        got = lane_gather(
            jnp.broadcast_to(mine, (ROWS, LANES)), local * z.pairs + small_lane % ROWS * ROWS + small_row
        )
        spread.append(jnp.where((small_lane // ROWS == s) & alive, got, 0.0)[:, : z.entries * ROWS])
    support_ref[...] = jnp.dot(
        jnp.concatenate(spread, axis=0), pj_ref[...], precision=HIGHEST, preferred_element_type=F32
    )
    scatter = Scatter(z, table_ref, index_ref, corner_ref, acc_ref)
    cells = [table_ref[CELL, s] for s in range(z.entries)]
    scatter.start([(cell, support_ref[s * ROWS : (s + 1) * ROWS, :]) for s, cell in enumerate(cells)])
    for first in range(0, z.entries, z.together):
        some = cells[first : first + z.together]

        def value_of(i, t):
            s = first + i
            return support_ref[s * ROWS : (s + 1) * ROWS, t * LANES : (t + 1) * LANES]

        scatter.add(some, value_of)
    for h in range(scatter.groups):
        at = slice(h * WIDE, (h + 1) * WIDE)
        image_ref[:, at] = cells_ref[:, at] + scatter.result(h)
    even = position % 2 == 0
    ends = [slice(0, 2 * z.rim), slice(z.window - 2 * z.rim, z.window)]
    for source_ref, rows in ((image_ref, slice(0, ROWS)),) + (() if last else ((diag_ref, slice(ROWS, ROWS + 2)),)):
        low_rim, high_rim = (source_ref[:, end] for end in ends)
        send_a_ref[rows, :] = jnp.where(even, high_rim, low_rim)
        send_b_ref[rows, :] = jnp.where(even, low_rim, high_rim)


def last_kernel(
    z, rhs_ref, p_ref, diag_ref, shift_ref, y_ref, q_ref, image_ref, dots_ref, solution_ref, residual_ref, factor_ref,
):
    own = slice(z.rim, z.rim + z.nodes)
    lane, row = iota((ROWS, LANES), 1), iota((ROWS, LANES), 0)
    line = jnp.broadcast_to(dots_ref[...], (ROWS, LANES))

    def column(k):
        return jnp.sum(jnp.where(lane == k * ROWS + row, line, 0.0), axis=1, keepdims=True)

    gamma, py, qy, qq = (column(k) for k in range(4))
    alpha = gamma / py
    fresh = gamma - 2.0 * alpha * py + alpha * alpha * qy
    beta = fresh / gamma
    more = 1.0 + beta
    step = fresh / (more * more * py - 2.0 * more * alpha * qy + alpha * alpha * qq)
    p, q, y = p_ref[:, own], q_ref[:, own], y_ref[:, own]
    second = image_ref[:, own] + (diag_ref[1:2, own] + shift_ref[:, :1]) * q
    search = (p - alpha * q) + beta * p
    solution_ref[...] = alpha * p + step * search
    residual_ref[...] = (rhs_ref[...] - alpha * y) - step * (more * y - alpha * second)
    factor_ref[...] = jnp.broadcast_to(step * alpha, (ROWS, LANES))


def rim_kernel(z, table_ref, residual_in_ref, halo_a_ref, halo_b_ref, factor_ref, residual_ref):
    left, right = sides(table_ref[OTHER, 0], halo_a_ref[...], halo_b_ref[...])
    factor = factor_ref[:, :1]
    first, last = slice(0, z.rim), slice(z.nodes - z.rim, z.nodes)
    residual_ref[:, z.rim : z.nodes - z.rim] = residual_in_ref[:, z.rim : z.nodes - z.rim]
    residual_ref[:, first] = residual_in_ref[:, first] + factor * left[:, z.rim :]
    residual_ref[:, last] = residual_in_ref[:, last] + factor * right[:, : z.rim]


def on_device(
    rhs, potential, precond, shift, stiffness, cell_scale, conn, cell_count, projector, support_cell, support_atom,
    support_count, atom_matrix,
):
    count = lax.axis_size("dom")
    z = Sizes(count, rhs, conn, projector, atom_matrix)
    position = lax.axis_index("dom")
    pos = position.astype(jnp.int32).reshape(1)
    near = [(i, i ^ 1) for i in range(count)]
    far = [(i, j) for i in range(1, count - 1) for j in [i + 1 if i % 2 else i - 1]]

    def exchange(a, b):
        return lax.ppermute(a, "dom", near), lax.ppermute(b, "dom", far)

    def call(kernel, outs, scratch, scalars, *args, in_hbm=(), copied=False):
        if not copied:
            args = [pltpu.with_memory_space_constraint(x, pltpu.VMEM) for x in args]
        return pl.pallas_call(
            kernel,
            out_shape=[
                jax.ShapeDtypeStruct(s, d) if i in in_hbm else pltpu.VMEM(s, d) for i, (s, d) in enumerate(outs)
            ],
            in_specs=[SMEM] * len(scalars) + [VMEM] * len(args),
            out_specs=[VMEM] * len(outs),
            scratch_shapes=[pltpu.VMEM(s, d) for s, d in scratch],
            compiler_params=pltpu.CompilerParams(vmem_limit_bytes=16 * 1024 * 1024),
        )(*scalars, *args)

    flat_projector = projector.reshape(z.entries * z.channels, z.elem)
    cells = (z.slots * ROWS, z.width)
    window, reach, own = (z.vectors, z.window), (z.vectors, z.reach), (z.vectors, z.nodes)
    message = (z.devices, 4, LANES)
    square, entries = (z.width, z.width), (z.entries * ROWS, z.width)
    rim, more_rim = (z.vectors, 2 * z.rim), (z.vectors + 2, 2 * z.rim)
    acc = ((z.window // WIDE + BAND) * 2 * ROWS, WIDE)

    tile = (ROWS, LANES)
    p, send_a, send_b, gamma, diag, shift_tile = call(
        functools.partial(start_kernel, z),
        [(reach, F32), ((z.vectors, z.rim), F32), ((z.vectors, z.rim), F32), ((1, LANES), F32), ((2, z.window), F32),
         (tile, F32)],
        [],
        (pos, shift),
        rhs, precond[None, :], potential[None, :], copied=True,
    )
    halo = exchange(send_a, send_b)
    index, corner, table, weight = call(
        functools.partial(prepare_kernel, z),
        [((z.slots, 1, z.width), jnp.int32), ((1, LANES), jnp.int32), ((ROWS, LANES), jnp.int32),
         ((z.slots * ROWS, LANES), F32)],
        [],
        (pos, cell_count, cell_scale, support_cell, support_atom, support_count),
        conn,
    )
    (u,) = call(functools.partial(first_window_kernel, z), [(cells, F32)], [], (table,), p, index)
    p, sums, uw, pj = call(
        functools.partial(first_kernel, z),
        [(reach, F32), (message, F32), (cells, F32), (entries, F32)],
        [(cells, F32)],
        (table,),
        p, u, *halo, index, corner, weight, flat_projector, atom_matrix,
    )
    coupled = lax.all_to_all(sums, "dom", 0, 0)
    image, k_high, k_low = call(
        functools.partial(cells_kernel, z, True),
        [(window, F32), (square, BF16), (square, BF16)],
        [(cells, F32), (square, F32), (acc, F32)],
        (table,),
        index, corner, uw, stiffness,
    )
    image, send_a, send_b = call(
        functools.partial(support_kernel, z, False),
        [(window, F32), (more_rim, F32), (more_rim, F32)],
        [(entries, F32), (acc, F32)],
        (table,),
        coupled, coupled, index, corner, pj, diag, image,
    )
    halo = exchange(send_a, send_b)
    y, q, u = call(
        functools.partial(second_window_kernel, z),
        [(window, F32), (reach, F32), (cells, F32)],
        [],
        (table,),
        p, diag, shift_tile, image, index,
    )
    y, q, sums, e = call(
        functools.partial(second_kernel, z),
        [(window, F32), (reach, F32), (message, F32), (cells, F32)],
        [((2, z.window), F32), (cells, F32), (cells, F32)],
        (table,),
        y, q, u, p, diag, shift_tile, gamma, *halo, index, corner, weight, k_high, k_low, pj,
    )
    totals = lax.all_to_all(sums, "dom", 0, 0)
    (image,) = call(functools.partial(cells_kernel, z, False), [(window, F32)], [(acc, F32)], (table,), index, corner, e)
    image, send_a, send_b, dots = call(
        functools.partial(support_kernel, z, True),
        [(window, F32), (rim, F32), (rim, F32), ((1, LANES), F32)],
        [(entries, F32), (acc, F32)],
        (table,),
        totals, coupled, index, corner, pj, diag, image,
    )
    halo = exchange(send_a, send_b)
    answer, residual, factor = call(
        functools.partial(last_kernel, z),
        [(own, F32), (own, F32), (tile, F32)],
        [],
        (),
        rhs, p, diag, shift_tile, y, q, image, dots, in_hbm=(0,),
    )
    (residual,) = call(functools.partial(rim_kernel, z), [(own, F32)], [], (table,), residual, *halo, factor, in_hbm=(0,))
    return answer, residual


def solution(mesh):
    placed = (
        P(None, "dom"),
        P("dom"),
        P("dom"),
        P(),
        P(),
        P("dom"),
        P("dom", None),
        P(),
        P("dom", None, None),
        P("dom"),
        P("dom"),
        P(),
        P("dom", None, None),
    )
    return jax.shard_map(
        on_device,
        mesh=mesh,
        in_specs=placed,
        out_specs=(P(None, "dom"), P(None, "dom")),
        check_vma=False,
    )
```

```python
import functools

import jax
import jax.numpy as jnp
from jax import lax
from jax.experimental import pallas as pl
from jax.experimental.pallas import tpu as pltpu
from jax.sharding import PartitionSpec as P

LANES = 128
ROWS = 8
WIDE = 256
CHAINS = 4
SPAN = 14
BAND = 8
TOGETHER = 8
F32 = jnp.float32
BF16 = jnp.bfloat16
HIGHEST = lax.Precision.HIGHEST
NT = (((1,), (1,)), ((), ()))
VMEM = pl.BlockSpec(memory_space=pltpu.VMEM)
SMEM = pl.BlockSpec(memory_space=pltpu.SMEM)


def round_up(value, step):
    return -(-value // step) * step


class Sizes:
    def __init__(self, count, rhs, conn, projector, atom_matrix):
        self.devices = count
        self.vectors, self.nodes = rhs.shape
        self.slots, self.elem = conn.shape
        self.entries, self.channels = projector.shape[:2]
        self.owned = atom_matrix.shape[0]
        self.ghost = self.nodes // 16
        self.rim = round_up(self.ghost, WIDE)
        self.shift = self.rim - self.ghost
        self.window = self.nodes + 2 * self.rim
        self.width = round_up(self.elem, LANES)
        self.tiles = self.width // LANES
        self.pairs = self.channels * self.vectors
        self.reach = self.window + SPAN * LANES
        self.index_row = self.entries * self.channels
        self.rim_row = self.index_row + round_up(self.entries, ROWS)
        self.rim_pieces = -(-self.rim // self.width)
        self.message = self.rim_row + self.rim_pieces * ROWS
        assert self.elem + 3 <= self.width
        self.together = TOGETHER if self.slots % TOGETHER == 0 else 1
        assert self.vectors == ROWS and self.channels == ROWS and 2 * self.slots <= LANES
        assert self.nodes % WIDE == 0 and self.owned * self.pairs == LANES


def lane_gather(values, index):
    return jnp.take_along_axis(values, index, axis=1, mode="promise_in_bounds")


def iota(shape, dim):
    return lax.broadcasted_iota(jnp.int32, shape, dim)


def split(values):
    high = values.astype(BF16)
    return high, (values - high.astype(F32)).astype(BF16)


def lanes_by_vector(z, values):
    total = jnp.sum(values, axis=1, keepdims=True)
    spread = jnp.broadcast_to(total, (ROWS, LANES))
    return jnp.sum(jnp.where(iota((ROWS, LANES), 1) == iota((ROWS, LANES), 0), spread, 0.0), axis=0, keepdims=True)


LOW, HIGH, LIST, NOTHING, CELL, OWNER, LOCAL, OTHER = range(8)


def prepare_kernel(
    z, pos_ref, count_ref, scale_ref, cell_ref, atom_ref, scount_ref, conn_ref,
    index_ref, corner_ref, table_ref, weight_ref,
):
    position = pos_ref[0]
    line = iota((1, LANES), 1)
    corner = jnp.zeros((1, LANES), jnp.int32)
    index_ref[...] = jnp.zeros_like(index_ref)
    live = count_ref[position]
    for c in range(z.slots):
        row = conn_ref[c : c + 1, :] + z.shift
        index_ref[c, :, : z.elem] = row
        corner = jnp.where(line == c, row[:, :1], corner)
        corner = jnp.where(line == z.slots + c, row[:, z.elem - 1 :], corner)
        weight = jnp.where(c < live, scale_ref[c], 0.0)
        weight_ref[c * ROWS : (c + 1) * ROWS, :] = jnp.zeros((ROWS, LANES), F32) + weight
    corner_ref[...] = corner
    nodes = (conn_ref[...] + z.shift).astype(F32)
    place = iota(nodes.shape, 1)
    middle = (place > 0) & (place < z.elem - 1)
    low = jnp.min(jnp.where(middle, nodes, 1.0 * z.window), axis=1, keepdims=True)
    high = jnp.max(jnp.where(middle, nodes, 0.0), axis=1, keepdims=True)
    lane, cell = iota((z.slots, LANES), 1), iota((z.slots, LANES), 0)

    def as_row(column):
        return jnp.sum(jnp.where(lane == cell, column, 0.0), axis=0, keepdims=True)

    rows = [as_row(low), as_row(high)]
    good = jnp.where((low >= z.rim) & (high < z.window - z.rim), 1.0, 0.0)
    good = jnp.broadcast_to(good, (z.slots, LANES))
    number = cell.astype(F32)
    before = jnp.sum(jnp.where(lane < cell, as_row(good), 0.0), axis=1, keepdims=True)
    at = jnp.where(good > 0.5, before, z.slots - 1.0 - (number - before))
    rows.append(jnp.sum(jnp.where(lane.astype(F32) == at, number + z.slots * good, 0.0), axis=0, keepdims=True))
    rows.append(jnp.zeros((1, LANES), F32))
    table = [row.astype(jnp.int32) for row in rows]
    facts = [jnp.zeros((1, LANES), jnp.int32)] * 3
    for s in range(z.entries):
        atom = atom_ref[s]
        owner = atom // z.owned
        for k, fact in enumerate((cell_ref[s], owner, atom - owner * z.owned)):
            facts[k] = jnp.where(line == s, fact, facts[k])
    other = jnp.where(line == 0, position, jnp.where(line == 1, scount_ref[position], 0))
    table_ref[...] = jnp.concatenate(table + facts + [other], axis=0)


def start_kernel(
    z, pos_ref, cell_ref, atom_ref, scount_ref, rhs_ref, precond_ref, conn_ref, projector_ref,
    send_a_ref, send_b_ref, rhs_rim, precond_rim, conn_all, projector_all, sems,
):
    copies = [
        pltpu.make_async_copy(conn_ref, conn_all, sems.at[0]),
        pltpu.make_async_copy(projector_ref, projector_all, sems.at[1]),
    ]
    for k, first in enumerate((0, z.nodes - z.rim)):
        at, to = pl.ds(first, z.rim), pl.ds(k * z.rim, z.rim)
        copies.append(pltpu.make_async_copy(rhs_ref.at[:, at], rhs_rim.at[:, to], sems.at[2 + k]))
        copies.append(pltpu.make_async_copy(precond_ref.at[:, at], precond_rim.at[:, to], sems.at[4 + k]))
    for copy in copies:
        copy.start()
    for copy in copies:
        copy.wait()
    rims = rhs_rim[...] * precond_rim[...]
    head, tail = rims[:, : z.rim], rims[:, z.rim :]
    even = pos_ref[0] % 2 == 0
    sides = jnp.where(even, tail, head), jnp.where(even, head, tail)
    nodes = (conn_all[...] + z.shift).astype(F32)
    cell = iota(nodes.shape, 0)
    entry = iota((z.rim_row - z.index_row, z.width), 0)
    place = iota((z.rim_row - z.index_row, z.width), 1)
    rows = jnp.zeros((z.rim_row - z.index_row, z.width), F32)
    for s in range(z.entries):
        row = jnp.sum(jnp.where(cell == cell_ref[s], nodes, 0.0), axis=0, keepdims=True)
        row = jnp.concatenate([row, jnp.zeros((1, z.width - z.elem), F32)], axis=1)
        owner = atom_ref[s] // z.owned
        facts = owner, atom_ref[s] - owner * z.owned, (s < scount_ref[pos_ref[0]]).astype(jnp.int32)
        rows = jnp.where(entry == s, row, rows)
        for k, fact in enumerate(facts):
            rows = jnp.where((entry == s) & (place == z.elem + k), fact.astype(F32), rows)
    for ref, side in zip((send_a_ref, send_b_ref), sides):
        ref[...] = jnp.zeros_like(ref)
        ref[: z.index_row, : z.elem] = projector_all[...]
        ref[z.index_row : z.rim_row, :] = rows
        for k in range(z.rim_pieces):
            piece = side[:, k * z.width : min((k + 1) * z.width, z.rim)]
            ref[z.rim_row + k * ROWS : z.rim_row + (k + 1) * ROWS, : piece.shape[1]] = piece


def own_kernel(
    z, shift_ref, rhs_ref, precond_ref, potential_ref, p_ref, gamma_ref, diag_ref, shift_tile_ref,
):
    product = rhs_ref[...] * precond_ref[...]
    own = slice(z.rim, z.rim + z.nodes)
    p_ref[:, own] = product
    p_ref[:, z.window :] = jnp.zeros((ROWS, z.reach - z.window), F32)
    gamma_ref[...] = lanes_by_vector(z, product * rhs_ref[...])
    diag_ref[...] = jnp.zeros_like(diag_ref)
    diag_ref[0:1, own] = precond_ref[...]
    diag_ref[1:2, own] = potential_ref[...]
    row = iota((ROWS, LANES), 0)
    tile = jnp.zeros((ROWS, LANES), F32)
    for v in range(z.vectors):
        tile = jnp.where(row == v, shift_ref[v], tile)
    shift_tile_ref[...] = tile


def full_groups(z, table_ref):
    ends = [table_ref[LIST, g * z.together + z.together - 1] for g in range(z.slots // z.together)]
    return functools.reduce(jnp.add, [(end >= z.slots).astype(jnp.int32) for end in ends])


def gather_middle(z, groups, listed, table_ref, index_ref, window_ref, u_ref):
    total = z.window // LANES
    tile = (ROWS, LANES)

    def some_cells(g, _):
        cells = [g * z.together + i for i in range(z.together)]
        if listed:
            cells = [table_ref[LIST, c] for c in cells]
            cells = [jnp.where(c >= z.slots, c - z.slots, c) for c in cells]
        starts = [table_ref[LOW, c] >> 7 for c in cells]
        ends = [table_ref[HIGH, c] >> 7 for c in cells]
        passes = functools.reduce(jnp.maximum, [(e - s) // SPAN + 1 for s, e in zip(starts, ends)])

        def one_pass(k, values):
            values = list(values)
            for i, c in enumerate(cells):
                start = jnp.minimum(starts[i] + k * SPAN, total)
                for t in range(z.tiles):
                    index = jnp.broadcast_to(index_ref[c, :, t * LANES : (t + 1) * LANES], tile)
                    low, high = index & (LANES - 1), (index >> 7) - start
                    value = values[i * z.tiles + t]
                    for h in range(SPAN):
                        at = pl.ds(pl.multiple_of((start + h) * LANES, LANES), LANES)
                        value = jnp.where(high == h, lane_gather(window_ref[:, at], low), value)
                    values[i * z.tiles + t] = value
            return tuple(values)

        values = lax.fori_loop(0, passes, one_pass, (jnp.zeros(tile, F32),) * (z.together * z.tiles))
        for i, c in enumerate(cells):
            rows = pl.ds(pl.multiple_of(c * ROWS, ROWS), ROWS)
            for t in range(z.tiles):
                u_ref[rows, t * LANES : (t + 1) * LANES] = values[i * z.tiles + t]
        return 0

    lax.fori_loop(*groups, some_cells, 0)


def gather_corners(z, corner_ref, window_ref, weight_ref, u_ref, uw_ref):
    tile = (ROWS, LANES)
    corner = jnp.broadcast_to(corner_ref[...], tile)
    low, high = corner & (LANES - 1), corner >> 7
    chains = [jnp.zeros(tile, F32)] * CHAINS
    for h in range(z.window // LANES):
        got = lane_gather(window_ref[:, h * LANES : (h + 1) * LANES], low)
        chains[h % CHAINS] = jnp.where(high == h, got, chains[h % CHAINS])
    corners = functools.reduce(jnp.add, chains)
    lane = iota(tile, 1)
    last = (z.elem - 1) % LANES
    for c in range(z.slots):
        rows = slice(c * ROWS, (c + 1) * ROWS)
        weight = weight_ref[rows, :]
        for t in range(z.tiles):
            lanes = slice(t * LANES, (t + 1) * LANES)
            value = u_ref[rows, lanes]
            if t == 0:
                value = jnp.where(lane == 0, corners[:, c : c + 1], value)
            if t == z.tiles - 1:
                value = jnp.where(lane == last, corners[:, z.slots + c : z.slots + c + 1], value)
            u_ref[rows, lanes] = value
            uw_ref[rows, lanes] = value * weight


def stiffness_product(k_high_ref, k_low_ref, uw_ref, e_ref):
    k_high, k_low = k_high_ref[...], k_low_ref[...]
    u_high, u_low = split(uw_ref[...])
    dot = functools.partial(lax.dot_general, dimension_numbers=NT, preferred_element_type=F32)
    e_ref[...] = dot(u_high, k_high) + (dot(u_high, k_low) + dot(u_low, k_high))


def entry_facts(table_ref, s):
    return table_ref[OWNER, s], table_ref[LOCAL, s], s < table_ref[OTHER, 1]


def contributions(z, table_ref, pj_ref, u_ref):
    values = [u_ref[pl.ds(pl.multiple_of(table_ref[CELL, s] * ROWS, ROWS), ROWS), :] for s in range(z.entries)]
    sums = lax.dot_general(
        pj_ref[...], jnp.concatenate(values, axis=0), NT, precision=HIGHEST, preferred_element_type=F32
    )
    sums = jnp.concatenate([sums, jnp.zeros((sums.shape[0], LANES - sums.shape[1]), F32)], axis=1)
    lane, row = iota((ROWS, LANES), 1), iota((ROWS, LANES), 0)
    position = table_ref[OTHER, 0]
    parts = [jnp.zeros((ROWS, LANES), F32)] * 3
    for s in range(z.entries):
        owner, local, alive = entry_facts(table_ref, s)
        got = lane_gather(sums[s * ROWS : (s + 1) * ROWS], s * ROWS + lane % ROWS)
        here = (lane // ROWS % ROWS == row) & (lane // z.pairs == local) & alive
        for k in range(3):
            parts[k] = parts[k] + jnp.where(here & (owner == position - 1 + k), got, 0.0)
    return [jnp.sum(part, axis=0, keepdims=True) for part in parts]


def sides(position, near, far):
    even = position % 2 == 0
    return jnp.where(even, far, near), jnp.where(even, near, far)


def first_window_kernel(z, table_ref, p_ref, index_ref, u_ref):
    groups = 0, full_groups(z, table_ref)
    gather_middle(z, groups, True, table_ref, index_ref, p_ref, u_ref)


def first_kernel(
    z, table_ref, p_in_ref, u_in_ref, halo_a_ref, halo_b_ref, index_ref, corner_ref, weight_ref, projector_ref,
    coupling_ref, p_ref, out_ref, uw_ref, pj_ref, u_ref,
):
    own = slice(z.rim, z.rim + z.nodes)
    for k in range(z.rim_pieces):
        rows = slice(z.rim_row + k * ROWS, z.rim_row + (k + 1) * ROWS)
        at, to = k * z.width, min((k + 1) * z.width, z.rim)
        left, right = sides(table_ref[OTHER, 0], halo_a_ref[rows, : to - at], halo_b_ref[rows, : to - at])
        p_ref[:, at:to] = left
        p_ref[:, z.rim + z.nodes + at : z.rim + z.nodes + to] = right
    p_ref[:, own] = p_in_ref[:, own]
    p_ref[:, z.window :] = p_in_ref[:, z.window :]
    u_ref[...] = u_in_ref[...]
    pj_ref[...] = jnp.zeros_like(pj_ref)
    pj_ref[:, : z.elem] = projector_ref[...]
    groups = full_groups(z, table_ref), z.slots // z.together
    gather_middle(z, groups, True, table_ref, index_ref, p_ref, u_ref)
    gather_corners(z, corner_ref, p_ref, weight_ref, u_ref, uw_ref)
    parts = contributions(z, table_ref, pj_ref, u_ref)
    small_lane, small_row = iota((ROWS, LANES), 1), iota((ROWS, LANES), 0)
    matrices = jnp.zeros((ROWS, LANES), F32)
    for atom in range(z.owned):
        block = jnp.concatenate([coupling_ref[atom], jnp.zeros((ROWS, LANES - z.channels), F32)], axis=1)
        got = lane_gather(block, small_lane % ROWS)
        matrices = jnp.where(small_lane // ROWS == atom * ROWS + small_row, got, matrices)
    message = jnp.concatenate(parts + [jnp.sum(matrices, axis=0, keepdims=True)], axis=0)
    for d in range(z.devices):
        out_ref[d] = message


def second_kernel(
    z, table_ref, image_ref, p_ref, diag_in_ref, shift_ref, gamma_ref, halo_a_ref, halo_b_ref,
    index_ref, corner_ref, weight_ref, k_high_ref, k_low_ref, pj_ref, y_ref, q_ref, out_ref, e_ref, diag_ref, u_ref, uw_ref,
):
    left, right = sides(table_ref[OTHER, 0], halo_a_ref[...], halo_b_ref[...])
    own = slice(z.rim, z.rim + z.nodes)
    diag_ref[:, own] = diag_in_ref[:, own]
    diag_ref[:, : z.rim] = left[ROWS : ROWS + 2, : z.rim]
    diag_ref[:, z.rim + z.nodes :] = right[ROWS : ROWS + 2, z.rim :]
    y_ref[...] = image_ref[...] + (diag_ref[1:2, :] + shift_ref[:, :1]) * p_ref[:, : z.window]
    y_ref[:, : 2 * z.rim] += left[:ROWS]
    y_ref[:, z.window - 2 * z.rim :] += right[:ROWS]
    q_ref[:, : z.window] = y_ref[...] * diag_ref[0:1, :]
    q_ref[:, z.window :] = jnp.zeros((ROWS, z.reach - z.window), F32)
    y, q = y_ref[:, own], q_ref[:, own]
    dots = [
        gamma_ref[...],
        lanes_by_vector(z, y * p_ref[:, own]),
        lanes_by_vector(z, y * q),
    ]
    energy = jnp.sum(q * q * (diag_ref[1:2, own] + shift_ref[:, :1]), axis=1, keepdims=True)
    groups = 0, z.slots // z.together
    gather_middle(z, groups, False, table_ref, index_ref, q_ref, u_ref)
    gather_corners(z, corner_ref, q_ref, weight_ref, u_ref, uw_ref)
    parts = contributions(z, table_ref, pj_ref, u_ref)
    stiffness_product(k_high_ref, k_low_ref, uw_ref, e_ref)
    elements = jnp.zeros((ROWS, z.width), F32)
    for c in range(z.slots):
        rows = slice(c * ROWS, (c + 1) * ROWS)
        elements = elements + u_ref[rows, :] * e_ref[rows, :]
    energy = energy + jnp.sum(elements, axis=1, keepdims=True)
    dots.append(lanes_by_vector(z, energy))
    line = dots[0]
    for k in range(1, len(dots)):
        line = line + pltpu.roll(dots[k], k * ROWS, 1)
    message = jnp.concatenate(parts + [line], axis=0)
    for d in range(z.devices):
        out_ref[d] = message


class Scatter:
    def __init__(self, z, table_ref, index_ref, corner_ref, acc_ref):
        self.z, self.index_ref, self.corner_ref, self.acc_ref = z, index_ref, corner_ref, acc_ref
        self.table_ref = table_ref
        self.groups = z.window // WIDE
        self.pair = (2 * ROWS, LANES)
        sub = iota(self.pair, 0)
        self.lows = [(sub + k * 2 * ROWS).astype(jnp.int16) for k in range(WIDE // (2 * ROWS))]
        self.one, self.none = jnp.ones(self.pair, BF16), jnp.zeros(self.pair, BF16)
        self.lane = iota((ROWS, LANES), 1)
        self.end = (z.elem - 1) % LANES

    def two_parts(self, value):
        rounded = value.astype(BF16).astype(F32)
        return jnp.concatenate([rounded, value - rounded], axis=0).astype(BF16)

    def hot_rows(self, index):
        low = (index & (WIDE - 1)).astype(jnp.int16)
        return jnp.concatenate([jnp.where(low == k, self.one, self.none) for k in self.lows], axis=0)

    def masked(self, high, both, rows):
        high = high.astype(jnp.int16)
        return jnp.concatenate([jnp.where(high == jnp.int16(h), both, self.none) for h in range(rows)], axis=0)

    def product(self, lhs, hot):
        return lax.dot_general(lhs, hot, NT, preferred_element_type=F32)

    def start(self, sources):
        z = self.z
        corners = jnp.zeros((ROWS, LANES), F32)
        at = (z.tiles - 1) * LANES + self.end
        for cell, values in sources:
            corners = corners + jnp.where(self.lane == cell, values[:, 0:1], 0.0)
            corners = corners + jnp.where(self.lane == z.slots + cell, values[:, at : at + 1], 0.0)
        index = jnp.broadcast_to(self.corner_ref[...], self.pair)
        rows = self.groups * 2 * ROWS
        self.acc_ref[:rows, :] = self.product(
            self.masked(index >> 8, self.two_parts(corners), self.groups), self.hot_rows(index)
        )
        self.acc_ref[rows:, :] = jnp.zeros((BAND * 2 * ROWS, WIDE), F32)

    def add(self, cells, value_of):
        z = self.z
        starts = [self.table_ref[LOW, c] >> 8 for c in cells]
        ends = [self.table_ref[HIGH, c] >> 8 for c in cells]
        passes = functools.reduce(jnp.maximum, [(e - s) // BAND + 1 for s, e in zip(starts, ends)])

        def one_pass(k, _):
            for i, c in enumerate(cells):
                start = jnp.minimum(starts[i] + k * BAND, self.groups)
                lhs, hot = [], []
                for t in range(z.tiles):
                    index = jnp.broadcast_to(self.index_ref[c, :, t * LANES : (t + 1) * LANES], self.pair)
                    value = value_of(i, t)
                    if t == 0:
                        value = jnp.where(self.lane == 0, 0.0, value)
                    if t == z.tiles - 1:
                        value = jnp.where(self.lane == self.end, 0.0, value)
                    lhs.append(self.masked((index >> 8) - start, self.two_parts(value), BAND))
                    hot.append(self.hot_rows(index))
                to = pl.ds(pl.multiple_of(start * 2 * ROWS, 2 * ROWS), BAND * 2 * ROWS)
                self.acc_ref[to, :] += self.product(jnp.concatenate(lhs, axis=1), jnp.concatenate(hot, axis=1))
            return 0

        lax.fori_loop(0, passes, one_pass, 0)

    def add_rows(self, index, values, first, rows):
        lhs, hot = [], []
        for t in range(values.shape[1] // LANES):
            lanes = slice(t * LANES, (t + 1) * LANES)
            at = jnp.broadcast_to(index[:, lanes], self.pair)
            lhs.append(self.masked(at >> 8, self.two_parts(values[:, lanes]), rows))
            hot.append(self.hot_rows(at))
        to = slice(first * 2 * ROWS, (first + rows) * 2 * ROWS)
        self.acc_ref[to, :] += self.product(jnp.concatenate(lhs, axis=1), jnp.concatenate(hot, axis=1))

    def result(self, h):
        at = h * 2 * ROWS
        return self.acc_ref[at : at + ROWS] + self.acc_ref[at + ROWS : at + 2 * ROWS]


def cells_kernel(z, multiply, table_ref, index_ref, corner_ref, *refs):
    if multiply:
        uw_ref, stiffness_ref, diag_ref, image_ref, send_a_ref, send_b_ref, k_high_ref, k_low_ref, *refs = refs
        e_ref, k_ref, acc_ref = refs
        k_ref[...] = jnp.zeros_like(k_ref)
        k_ref[: z.elem, : z.elem] = stiffness_ref[...]
        k_high_ref[...], k_low_ref[...] = split(k_ref[...])
        stiffness_product(k_high_ref, k_low_ref, uw_ref, e_ref)
    else:
        e_ref, image_ref, send_a_ref, send_b_ref, acc_ref = refs
    scatter = Scatter(z, table_ref, index_ref, corner_ref, acc_ref)
    scatter.start([(c, e_ref[c * ROWS : (c + 1) * ROWS, :]) for c in range(z.slots)])

    def some_cells(g, _):
        cells = [g * z.together + i for i in range(z.together)]

        def value_of(i, t):
            rows = pl.ds(pl.multiple_of(cells[i] * ROWS, ROWS), ROWS)
            return e_ref[rows, t * LANES : (t + 1) * LANES]

        scatter.add(cells, value_of)
        return 0

    lax.fori_loop(0, z.slots // z.together, some_cells, 0)
    for h in range(scatter.groups):
        image_ref[:, h * WIDE : (h + 1) * WIDE] = scatter.result(h)
    even = table_ref[OTHER, 0] % 2 == 0
    ends = [slice(0, 2 * z.rim), slice(z.window - 2 * z.rim, z.window)]
    for source_ref, rows in ((image_ref, slice(0, ROWS)),) + (((diag_ref, slice(ROWS, ROWS + 2)),) if multiply else ()):
        low_rim, high_rim = (source_ref[:, end] for end in ends)
        send_a_ref[rows, :] = jnp.where(even, high_rim, low_rim)
        send_b_ref[rows, :] = jnp.where(even, low_rim, high_rim)


def support_kernel(
    z, last, table_ref, sums_ref, coupling_ref, index_ref, corner_ref, pj_ref, ext_a_ref, ext_b_ref,
    cells_ref, *refs,
):
    if last:
        image_ref, dots_ref, support_ref, acc_ref = refs
    else:
        image_ref, support_ref, acc_ref = refs
    position = table_ref[OTHER, 0]
    wanted = (
        pltpu.roll(sums_ref[:, 0, :], z.devices - 1, 0) + sums_ref[:, 1, :] + pltpu.roll(sums_ref[:, 2, :], 1, 0)
    )
    coupling = coupling_ref[:, 3, :]
    shape = (z.devices, LANES)
    lane = iota(shape, 1)
    term = jnp.zeros(shape, F32)
    for j in range(z.channels):
        matrix = lane_gather(coupling, lane // ROWS * ROWS + j)
        vector = lane_gather(wanted, lane // z.pairs * z.pairs + j * ROWS + lane % ROWS)
        term = term + matrix * vector
    if last:
        energy = jnp.sum(term * wanted, axis=0, keepdims=True)
        energy = jnp.broadcast_to(energy, (ROWS, LANES))
        step = ROWS
        while step < LANES:
            energy = energy + pltpu.roll(energy, step, 1)
            step *= 2
        line = iota((1, LANES), 1)
        dots_ref[...] = jnp.sum(sums_ref[:, 3, :], axis=0, keepdims=True) + jnp.where(
            line // ROWS == 3, energy[0:1], 0.0
        )
    block = iota(shape, 0)
    small_lane, small_row = iota((ROWS, LANES), 1), iota((ROWS, LANES), 0)

    def values(facts, projectors):
        spread = []
        for s, (owner, local, alive) in enumerate(facts):
            mine = jnp.sum(jnp.where(block == owner, term, 0.0), axis=0, keepdims=True)
            got = lane_gather(
                jnp.broadcast_to(mine, (ROWS, LANES)), local * z.pairs + small_lane % ROWS * ROWS + small_row
            )
            spread.append(jnp.where((small_lane // ROWS == s) & alive, got, 0.0)[:, : z.entries * ROWS])
        return jnp.dot(
            jnp.concatenate(spread, axis=0), projectors, precision=HIGHEST, preferred_element_type=F32
        )

    support_ref[...] = values([entry_facts(table_ref, s) for s in range(z.entries)], pj_ref[...])
    scatter = Scatter(z, table_ref, index_ref, corner_ref, acc_ref)
    cells = [table_ref[CELL, s] for s in range(z.entries)]
    scatter.start([(cell, support_ref[s * ROWS : (s + 1) * ROWS, :]) for s, cell in enumerate(cells)])
    for first in range(0, z.entries, z.together):
        some = cells[first : first + z.together]

        def value_of(i, t):
            s = first + i
            return support_ref[s * ROWS : (s + 1) * ROWS, t * LANES : (t + 1) * LANES]

        scatter.add(some, value_of)
    used = slice(0, z.rim_row)
    shared = 2 * z.rim // WIDE
    neighbours = sides(position, ext_a_ref[used, :], ext_b_ref[used, :])
    for ext, first, offset in zip(neighbours, (0, scatter.groups - shared), (z.window - 2 * z.rim, 0)):
        nodes = ext[z.index_row :].astype(jnp.int32)
        facts = []
        for s in range(z.entries):
            fact = [jnp.broadcast_to(nodes[s : s + 1, z.elem + k : z.elem + k + 1], (1, LANES)) for k in range(3)]
            facts.append((fact[0], fact[1], fact[2] > 0))
        rows = values(facts, jnp.where(iota((z.index_row, z.width), 1) < z.elem, ext[: z.index_row], 0.0))
        for s in range(0, z.entries, 2):
            index = jnp.concatenate([nodes[s : s + 1], nodes[s + 1 : s + 2]], axis=1) - offset
            pair = jnp.concatenate([rows[s * ROWS : (s + 1) * ROWS], rows[(s + 1) * ROWS : (s + 2) * ROWS]], axis=1)
            scatter.add_rows(index, pair, first, shared)
    for h in range(scatter.groups):
        at = slice(h * WIDE, (h + 1) * WIDE)
        image_ref[:, at] = cells_ref[:, at] + scatter.result(h)


def last_kernel(
    z, table_ref, rhs_ref, p_ref, diag_ref, shift_ref, y_ref, q_ref, image_ref, dots_ref, halo_a_ref, halo_b_ref,
    solution_ref, residual_ref,
):
    own = slice(z.rim, z.rim + z.nodes)
    lane, row = iota((ROWS, LANES), 1), iota((ROWS, LANES), 0)
    line = jnp.broadcast_to(dots_ref[...], (ROWS, LANES))

    def column(k):
        return jnp.sum(jnp.where(lane == k * ROWS + row, line, 0.0), axis=1, keepdims=True)

    gamma, py, qy, qq = (column(k) for k in range(4))
    alpha = gamma / py
    fresh = gamma - 2.0 * alpha * py + alpha * alpha * qy
    beta = fresh / gamma
    more = 1.0 + beta
    step = fresh / (more * more * py - 2.0 * more * alpha * qy + alpha * alpha * qq)
    p, q, y = p_ref[:, own], q_ref[:, own], y_ref[:, own]
    second = image_ref[:, own] + (diag_ref[1:2, own] + shift_ref[:, :1]) * q
    search = (p - alpha * q) + beta * p
    solution_ref[...] = alpha * p + step * search
    residual_ref[...] = (rhs_ref[...] - alpha * y) - step * (more * y - alpha * second)
    left, right = sides(table_ref[OTHER, 0], halo_a_ref[...], halo_b_ref[...])
    residual_ref[:, : z.rim] += step * alpha * left[:, z.rim :]
    residual_ref[:, z.nodes - z.rim :] += step * alpha * right[:, : z.rim]


def on_device(
    rhs, potential, precond, shift, stiffness, cell_scale, conn, cell_count, projector, support_cell, support_atom,
    support_count, atom_matrix,
):
    count = lax.axis_size("dom")
    z = Sizes(count, rhs, conn, projector, atom_matrix)
    position = lax.axis_index("dom")
    pos = position.astype(jnp.int32).reshape(1)
    near = [(i, i ^ 1) for i in range(count)]
    far = [(i, j) for i in range(1, count - 1) for j in [i + 1 if i % 2 else i - 1]]

    def exchange(a, b):
        return lax.ppermute(a, "dom", near), lax.ppermute(b, "dom", far)

    def call(kernel, outs, scratch, scalars, *args, in_hbm=(), by_hand=False):
        space = pltpu.HBM if by_hand else pltpu.VMEM
        args = [pltpu.with_memory_space_constraint(x, space) for x in args]
        return pl.pallas_call(
            kernel,
            out_shape=[
                jax.ShapeDtypeStruct(s, d) if i in in_hbm else pltpu.VMEM(s, d) for i, (s, d) in enumerate(outs)
            ],
            in_specs=[SMEM] * len(scalars) + [pl.BlockSpec(memory_space=space)] * len(args),
            out_specs=[VMEM] * len(outs),
            scratch_shapes=[pltpu.VMEM(*s) if isinstance(s, tuple) else s for s in scratch],
            compiler_params=pltpu.CompilerParams(vmem_limit_bytes=16 * 1024 * 1024),
        )(*scalars, *args)

    flat_projector = projector.reshape(z.entries * z.channels, z.elem)
    cells = (z.slots * ROWS, z.width)
    window, reach, own = (z.vectors, z.window), (z.vectors, z.reach), (z.vectors, z.nodes)
    message = (z.devices, 4, LANES)
    square, entries = (z.width, z.width), (z.entries * ROWS, z.width)
    rim, more_rim = (z.vectors, 2 * z.rim), (z.vectors + 2, 2 * z.rim)
    acc = ((z.window // WIDE + BAND) * 2 * ROWS, WIDE)

    tile = (ROWS, LANES)
    first_message = (z.message, z.width)
    ext = exchange(
        *call(
            functools.partial(start_kernel, z),
            [(first_message, F32)] * 2,
            [((z.vectors, 2 * z.rim), F32), ((1, 2 * z.rim), F32), (conn.shape, jnp.int32), (flat_projector.shape, F32),
             pltpu.SemaphoreType.DMA((6,))],
            (pos, support_cell, support_atom, support_count),
            rhs, precond[None, :], conn, flat_projector, by_hand=True,
        )
    )
    index, corner, table, weight = call(
        functools.partial(prepare_kernel, z),
        [((z.slots, 1, z.width), jnp.int32), ((1, LANES), jnp.int32), ((ROWS, LANES), jnp.int32),
         ((z.slots * ROWS, LANES), F32)],
        [],
        (pos, cell_count, cell_scale, support_cell, support_atom, support_count),
        conn,
    )
    p, gamma, diag, shift_tile = call(
        functools.partial(own_kernel, z),
        [(reach, F32), ((1, LANES), F32), ((2, z.window), F32), (tile, F32)],
        [],
        (shift,),
        rhs, precond[None, :], potential[None, :],
    )
    (u,) = call(functools.partial(first_window_kernel, z), [(cells, F32)], [], (table,), p, index)
    p, sums, uw, pj = call(
        functools.partial(first_kernel, z),
        [(reach, F32), (message, F32), (cells, F32), (entries, F32)],
        [(cells, F32)],
        (table,),
        p, u, *ext, index, corner, weight, flat_projector, atom_matrix,
    )
    coupled = lax.all_to_all(sums, "dom", 0, 0)
    image, send_a, send_b, k_high, k_low = call(
        functools.partial(cells_kernel, z, True),
        [(window, F32), (more_rim, F32), (more_rim, F32), (square, BF16), (square, BF16)],
        [(cells, F32), (square, F32), (acc, F32)],
        (table,),
        index, corner, uw, stiffness, diag,
    )
    halo = exchange(send_a, send_b)
    (image,) = call(
        functools.partial(support_kernel, z, False),
        [(window, F32)],
        [(entries, F32), (acc, F32)],
        (table,),
        coupled, coupled, index, corner, pj, *ext, image,
    )
    y, q, sums, e = call(
        functools.partial(second_kernel, z),
        [(window, F32), (reach, F32), (message, F32), (cells, F32)],
        [((2, z.window), F32), (cells, F32), (cells, F32)],
        (table,),
        image, p, diag, shift_tile, gamma, *halo, index, corner, weight, k_high, k_low, pj,
    )
    totals = lax.all_to_all(sums, "dom", 0, 0)
    image, send_a, send_b = call(
        functools.partial(cells_kernel, z, False), [(window, F32), (rim, F32), (rim, F32)], [(acc, F32)], (table,),
        index, corner, e,
    )
    halo = exchange(send_a, send_b)
    image, dots = call(
        functools.partial(support_kernel, z, True),
        [(window, F32), ((1, LANES), F32)],
        [(entries, F32), (acc, F32)],
        (table,),
        totals, coupled, index, corner, pj, *ext, image,
    )
    return tuple(
        call(
            functools.partial(last_kernel, z),
            [(own, F32), (own, F32)],
            [],
            (table,),
            rhs, p, diag, shift_tile, y, q, image, dots, *halo, in_hbm=(0, 1),
        )
    )


def solution(mesh):
    placed = (
        P(None, "dom"),
        P("dom"),
        P("dom"),
        P(),
        P(),
        P("dom"),
        P("dom", None),
        P(),
        P("dom", None, None),
        P("dom"),
        P("dom"),
        P(),
        P("dom", None, None),
    )
    return jax.shard_map(
        on_device,
        mesh=mesh,
        in_specs=placed,
        out_specs=(P(None, "dom"), P(None, "dom")),
        check_vma=False,
    )
```

```python
import functools

import jax
import jax.numpy as jnp
from jax import lax
from jax.experimental import pallas as pl
from jax.experimental.pallas import tpu as pltpu
from jax.sharding import PartitionSpec as P

LANES = 128
ROWS = 8
WIDE = 256
CHAINS = 4
SPAN = 14
BAND = 8
TOGETHER = 8
F32 = jnp.float32
BF16 = jnp.bfloat16
HIGHEST = lax.Precision.HIGHEST
NT = (((1,), (1,)), ((), ()))
VMEM = pl.BlockSpec(memory_space=pltpu.VMEM)
SMEM = pl.BlockSpec(memory_space=pltpu.SMEM)


def round_up(value, step):
    return -(-value // step) * step


class Sizes:
    def __init__(self, count, rhs, conn, projector, atom_matrix):
        self.devices = count
        self.vectors, self.nodes = rhs.shape
        self.slots, self.elem = conn.shape
        self.entries, self.channels = projector.shape[:2]
        self.owned = atom_matrix.shape[0]
        self.ghost = self.nodes // 16
        self.rim = round_up(self.ghost, WIDE)
        self.shift = self.rim - self.ghost
        self.window = self.nodes + 2 * self.rim
        self.width = round_up(self.elem, LANES)
        self.tiles = self.width // LANES
        self.pairs = self.channels * self.vectors
        self.low, self.high, self.list = 0, self.slots, 2 * self.slots
        self.cell = 3 * self.slots
        self.owner, self.local = self.cell + self.entries, self.cell + 2 * self.entries
        self.position = self.cell + 3 * self.entries
        assert self.position + 1 < LANES
        self.reach = self.window + SPAN * LANES
        self.index_row = self.entries * self.channels
        self.rim_row = self.index_row + round_up(self.entries, ROWS)
        self.rim_pieces = -(-self.rim // self.width)
        self.message = self.rim_row + self.rim_pieces * ROWS
        assert self.elem + 3 <= self.width
        self.together = TOGETHER if self.slots % TOGETHER == 0 else 1
        assert self.vectors == ROWS and self.channels == ROWS and 2 * self.slots <= LANES
        assert self.nodes % WIDE == 0 and self.owned * self.pairs == LANES


def lane_gather(values, index):
    return jnp.take_along_axis(values, index, axis=1, mode="promise_in_bounds")


def iota(shape, dim):
    return lax.broadcasted_iota(jnp.int32, shape, dim)


def split(values):
    high = values.astype(BF16)
    return high, (values - high.astype(F32)).astype(BF16)


def lanes_by_vector(z, values):
    total = jnp.sum(values, axis=1, keepdims=True)
    spread = jnp.broadcast_to(total, (ROWS, LANES))
    return jnp.sum(jnp.where(iota((ROWS, LANES), 1) == iota((ROWS, LANES), 0), spread, 0.0), axis=0, keepdims=True)


def prepare_kernel(
    z, pos_ref, count_ref, scale_ref, cell_ref, atom_ref, scount_ref, conn_ref,
    index_ref, corner_ref, table_ref, weight_ref,
):
    position = pos_ref[0]
    line = iota((1, LANES), 1)
    corner = jnp.zeros((1, LANES), jnp.int32)
    index_ref[...] = jnp.zeros_like(index_ref)
    live = count_ref[position]
    for c in range(z.slots):
        row = conn_ref[c : c + 1, :] + z.shift
        index_ref[c, :, : z.elem] = row
        corner = jnp.where(line == c, row[:, :1], corner)
        corner = jnp.where(line == z.slots + c, row[:, z.elem - 1 :], corner)
        weight = jnp.where(c < live, scale_ref[c], 0.0)
        weight_ref[c * ROWS : (c + 1) * ROWS, :] = jnp.zeros((ROWS, LANES), F32) + weight
    corner_ref[...] = corner
    nodes = (conn_ref[...] + z.shift).astype(F32)
    place = iota(nodes.shape, 1)
    middle = (place > 0) & (place < z.elem - 1)
    low = jnp.min(jnp.where(middle, nodes, 1.0 * z.window), axis=1, keepdims=True)
    high = jnp.max(jnp.where(middle, nodes, 0.0), axis=1, keepdims=True)
    lane, cell = iota((z.slots, LANES), 1), iota((z.slots, LANES), 0)

    def as_row(column, first=0):
        return jnp.sum(jnp.where(lane == cell + first, column, 0.0), axis=0, keepdims=True)

    good = jnp.where((low >= z.rim) & (high < z.window - z.rim), 1.0, 0.0)
    good = jnp.broadcast_to(good, (z.slots, LANES))
    number = cell.astype(F32)
    before = jnp.sum(jnp.where(lane < cell, as_row(good), 0.0), axis=1, keepdims=True)
    at = jnp.where(good > 0.5, before, z.slots - 1.0 - (number - before))
    listed = jnp.where(lane.astype(F32) == at + z.list, number + z.slots * good, 0.0)
    table = as_row(low, z.low) + as_row(high, z.high) + jnp.sum(listed, axis=0, keepdims=True)
    table = table.astype(jnp.int32)
    for s in range(z.entries):
        atom = atom_ref[s]
        owner = atom // z.owned
        for first, fact in ((z.cell, cell_ref[s]), (z.owner, owner), (z.local, atom - owner * z.owned)):
            table = jnp.where(line == first + s, fact, table)
    table = jnp.where(line == z.position, position, table)
    table_ref[...] = jnp.where(line == z.position + 1, scount_ref[position], table)


def start_kernel(
    z, pos_ref, cell_hbm, atom_hbm, scount_hbm, rhs_ref, precond_ref, conn_ref, projector_ref,
    send_a_ref, send_b_ref, rhs_rim, precond_rim, conn_all, projector_all, cell_ref, atom_ref, scount_ref, sems,
):
    lines = z.rim // LANES
    moves = [
        (cell_hbm, cell_ref), (atom_hbm, atom_ref), (scount_hbm, scount_ref), (conn_ref, conn_all),
        (projector_ref, projector_all),
    ]
    for k, first in enumerate((0, z.nodes - z.rim)):
        moves.append((rhs_ref.at[:, pl.ds(first, z.rim)], rhs_rim.at[k]))
        moves.append((precond_ref.at[pl.ds(first // LANES, lines), :], precond_rim.at[k]))
    copies = [pltpu.make_async_copy(source, to, sems.at[k]) for k, (source, to) in enumerate(moves)]
    for copy in copies:
        copy.start()
    for copy in copies:
        copy.wait()
    head, tail = (
        jnp.concatenate(
            [
                rhs_rim[k, :, i * LANES : (i + 1) * LANES] * precond_rim[k, i : i + 1, :]
                for i in range(lines)
            ],
            axis=1,
        )
        for k in range(2)
    )
    even = pos_ref[0] % 2 == 0
    sides = jnp.where(even, tail, head), jnp.where(even, head, tail)
    nodes = (conn_all[...] + z.shift).astype(F32)
    cell = iota(nodes.shape, 0)
    entry = iota((z.rim_row - z.index_row, z.width), 0)
    place = iota((z.rim_row - z.index_row, z.width), 1)
    rows = jnp.zeros((z.rim_row - z.index_row, z.width), F32)
    for s in range(z.entries):
        row = jnp.sum(jnp.where(cell == cell_ref[s], nodes, 0.0), axis=0, keepdims=True)
        row = jnp.concatenate([row, jnp.zeros((1, z.width - z.elem), F32)], axis=1)
        owner = atom_ref[s] // z.owned
        facts = owner, atom_ref[s] - owner * z.owned, (s < scount_ref[pos_ref[0]]).astype(jnp.int32)
        rows = jnp.where(entry == s, row, rows)
        for k, fact in enumerate(facts):
            rows = jnp.where((entry == s) & (place == z.elem + k), fact.astype(F32), rows)
    for ref, side in zip((send_a_ref, send_b_ref), sides):
        ref[...] = jnp.zeros_like(ref)
        ref[: z.index_row, : z.elem] = projector_all[...]
        ref[z.index_row : z.rim_row, :] = rows
        for k in range(z.rim_pieces):
            piece = side[:, k * z.width : min((k + 1) * z.width, z.rim)]
            ref[z.rim_row + k * ROWS : z.rim_row + (k + 1) * ROWS, : piece.shape[1]] = piece


def own_kernel(
    z, shift_ref, rhs_ref, precond_ref, potential_ref, p_ref, gamma_ref, diag_ref, shift_tile_ref,
):
    diag_ref[...] = jnp.zeros_like(diag_ref)
    gamma = jnp.zeros((ROWS, LANES), F32)
    for i in range(z.nodes // LANES):
        at = slice(i * LANES, (i + 1) * LANES)
        to = slice(z.rim + i * LANES, z.rim + (i + 1) * LANES)
        value = rhs_ref[:, at]
        scale = precond_ref[i : i + 1, :]
        product = value * scale
        p_ref[:, to] = product
        gamma = gamma + product * value
        diag_ref[0:1, to] = scale
        diag_ref[1:2, to] = potential_ref[i : i + 1, :]
    p_ref[:, z.window :] = jnp.zeros((ROWS, z.reach - z.window), F32)
    gamma_ref[...] = lanes_by_vector(z, gamma)
    row = iota((ROWS, LANES), 0)
    tile = jnp.zeros((ROWS, LANES), F32)
    for v in range(z.vectors):
        tile = jnp.where(row == v, shift_ref[v], tile)
    shift_tile_ref[...] = tile


def full_groups(z, table_ref):
    ends = [table_ref[0, z.list + g * z.together + z.together - 1] for g in range(z.slots // z.together)]
    return functools.reduce(jnp.add, [(end >= z.slots).astype(jnp.int32) for end in ends])


def gather_middle(z, groups, listed, table_ref, index_ref, window_ref, u_ref):
    total = z.window // LANES
    tile = (ROWS, LANES)

    def some_cells(g, _):
        cells = [g * z.together + i for i in range(z.together)]
        if listed:
            cells = [table_ref[0, z.list + c] for c in cells]
            cells = [jnp.where(c >= z.slots, c - z.slots, c) for c in cells]
        starts = [table_ref[0, z.low + c] >> 7 for c in cells]
        ends = [table_ref[0, z.high + c] >> 7 for c in cells]
        passes = functools.reduce(jnp.maximum, [(e - s) // SPAN + 1 for s, e in zip(starts, ends)])

        def one_pass(k, values):
            values = list(values)
            for i, c in enumerate(cells):
                start = jnp.minimum(starts[i] + k * SPAN, total)
                for t in range(z.tiles):
                    index = jnp.broadcast_to(index_ref[c, :, t * LANES : (t + 1) * LANES], tile)
                    low, high = index & (LANES - 1), (index >> 7) - start
                    value = values[i * z.tiles + t]
                    for h in range(SPAN):
                        at = pl.ds(pl.multiple_of((start + h) * LANES, LANES), LANES)
                        value = jnp.where(high == h, lane_gather(window_ref[:, at], low), value)
                    values[i * z.tiles + t] = value
            return tuple(values)

        values = lax.fori_loop(0, passes, one_pass, (jnp.zeros(tile, F32),) * (z.together * z.tiles))
        for i, c in enumerate(cells):
            rows = pl.ds(pl.multiple_of(c * ROWS, ROWS), ROWS)
            for t in range(z.tiles):
                u_ref[rows, t * LANES : (t + 1) * LANES] = values[i * z.tiles + t]
        return 0

    lax.fori_loop(*groups, some_cells, 0)


def gather_corners(z, corner_ref, window_ref, weight_ref, u_ref, uw_ref):
    tile = (ROWS, LANES)
    corner = jnp.broadcast_to(corner_ref[...], tile)
    low, high = corner & (LANES - 1), corner >> 7
    chains = [jnp.zeros(tile, F32)] * CHAINS
    for h in range(z.window // LANES):
        got = lane_gather(window_ref[:, h * LANES : (h + 1) * LANES], low)
        chains[h % CHAINS] = jnp.where(high == h, got, chains[h % CHAINS])
    corners = functools.reduce(jnp.add, chains)
    lane = iota(tile, 1)
    last = (z.elem - 1) % LANES
    for c in range(z.slots):
        rows = slice(c * ROWS, (c + 1) * ROWS)
        weight = weight_ref[rows, :]
        for t in range(z.tiles):
            lanes = slice(t * LANES, (t + 1) * LANES)
            value = u_ref[rows, lanes]
            if t == 0:
                value = jnp.where(lane == 0, corners[:, c : c + 1], value)
            if t == z.tiles - 1:
                value = jnp.where(lane == last, corners[:, z.slots + c : z.slots + c + 1], value)
            u_ref[rows, lanes] = value
            uw_ref[rows, lanes] = value * weight


def stiffness_product(k_high_ref, k_low_ref, uw_ref, e_ref):
    k_high, k_low = k_high_ref[...], k_low_ref[...]
    u_high, u_low = split(uw_ref[...])
    dot = functools.partial(lax.dot_general, dimension_numbers=NT, preferred_element_type=F32)
    e_ref[...] = dot(u_high, k_high) + (dot(u_high, k_low) + dot(u_low, k_high))


def entry_facts(z, table_ref, s):
    return table_ref[0, z.owner + s], table_ref[0, z.local + s], s < table_ref[0, z.position + 1]


def contributions(z, table_ref, pj_ref, u_ref):
    values = [u_ref[pl.ds(pl.multiple_of(table_ref[0, z.cell + s] * ROWS, ROWS), ROWS), :] for s in range(z.entries)]
    sums = lax.dot_general(
        pj_ref[...], jnp.concatenate(values, axis=0), NT, precision=HIGHEST, preferred_element_type=F32
    )
    sums = jnp.concatenate([sums, jnp.zeros((sums.shape[0], LANES - sums.shape[1]), F32)], axis=1)
    lane, row = iota((ROWS, LANES), 1), iota((ROWS, LANES), 0)
    position = table_ref[0, z.position]
    parts = [jnp.zeros((ROWS, LANES), F32)] * 3
    for s in range(z.entries):
        owner, local, alive = entry_facts(z, table_ref, s)
        got = lane_gather(sums[s * ROWS : (s + 1) * ROWS], s * ROWS + lane % ROWS)
        here = (lane // ROWS % ROWS == row) & (lane // z.pairs == local) & alive
        for k in range(3):
            parts[k] = parts[k] + jnp.where(here & (owner == position - 1 + k), got, 0.0)
    return [jnp.sum(part, axis=0, keepdims=True) for part in parts]


def sides(position, near, far):
    even = position % 2 == 0
    return jnp.where(even, far, near), jnp.where(even, near, far)


def first_window_kernel(z, table_ref, p_ref, index_ref, u_ref):
    groups = 0, full_groups(z, table_ref)
    gather_middle(z, groups, True, table_ref, index_ref, p_ref, u_ref)


def first_kernel(
    z, table_ref, p_in_ref, u_in_ref, halo_a_ref, halo_b_ref, index_ref, corner_ref, weight_ref, projector_ref,
    coupling_ref, p_ref, out_ref, uw_ref, pj_ref, u_ref,
):
    own = slice(z.rim, z.rim + z.nodes)
    for k in range(z.rim_pieces):
        rows = slice(z.rim_row + k * ROWS, z.rim_row + (k + 1) * ROWS)
        at, to = k * z.width, min((k + 1) * z.width, z.rim)
        left, right = sides(table_ref[0, z.position], halo_a_ref[rows, : to - at], halo_b_ref[rows, : to - at])
        p_ref[:, at:to] = left
        p_ref[:, z.rim + z.nodes + at : z.rim + z.nodes + to] = right
    p_ref[:, own] = p_in_ref[:, own]
    p_ref[:, z.window :] = p_in_ref[:, z.window :]
    u_ref[...] = u_in_ref[...]
    pj_ref[...] = jnp.zeros_like(pj_ref)
    pj_ref[:, : z.elem] = projector_ref[...]
    groups = full_groups(z, table_ref), z.slots // z.together
    gather_middle(z, groups, True, table_ref, index_ref, p_ref, u_ref)
    gather_corners(z, corner_ref, p_ref, weight_ref, u_ref, uw_ref)
    parts = contributions(z, table_ref, pj_ref, u_ref)
    small_lane, small_row = iota((ROWS, LANES), 1), iota((ROWS, LANES), 0)
    matrices = jnp.zeros((ROWS, LANES), F32)
    for atom in range(z.owned):
        block = jnp.concatenate([coupling_ref[atom], jnp.zeros((ROWS, LANES - z.channels), F32)], axis=1)
        got = lane_gather(block, small_lane % ROWS)
        matrices = jnp.where(small_lane // ROWS == atom * ROWS + small_row, got, matrices)
    message = jnp.concatenate(parts + [jnp.sum(matrices, axis=0, keepdims=True)], axis=0)
    for d in range(z.devices):
        out_ref[d] = message


def second_kernel(
    z, table_ref, image_ref, p_ref, diag_in_ref, shift_ref, gamma_ref, halo_a_ref, halo_b_ref,
    index_ref, corner_ref, weight_ref, k_high_ref, k_low_ref, pj_ref, y_ref, q_ref, out_ref, e_ref, diag_ref, u_ref, uw_ref,
):
    left, right = sides(table_ref[0, z.position], halo_a_ref[...], halo_b_ref[...])
    own = slice(z.rim, z.rim + z.nodes)
    diag_ref[:, own] = diag_in_ref[:, own]
    diag_ref[:, : z.rim] = left[ROWS : ROWS + 2, : z.rim]
    diag_ref[:, z.rim + z.nodes :] = right[ROWS : ROWS + 2, z.rim :]
    y_ref[...] = image_ref[...] + (diag_ref[1:2, :] + shift_ref[:, :1]) * p_ref[:, : z.window]
    y_ref[:, : 2 * z.rim] += left[:ROWS]
    y_ref[:, z.window - 2 * z.rim :] += right[:ROWS]
    q_ref[:, : z.window] = y_ref[...] * diag_ref[0:1, :]
    q_ref[:, z.window :] = jnp.zeros((ROWS, z.reach - z.window), F32)
    y, q = y_ref[:, own], q_ref[:, own]
    dots = [
        gamma_ref[...],
        lanes_by_vector(z, y * p_ref[:, own]),
        lanes_by_vector(z, y * q),
    ]
    energy = jnp.sum(q * q * (diag_ref[1:2, own] + shift_ref[:, :1]), axis=1, keepdims=True)
    groups = 0, z.slots // z.together
    gather_middle(z, groups, False, table_ref, index_ref, q_ref, u_ref)
    gather_corners(z, corner_ref, q_ref, weight_ref, u_ref, uw_ref)
    parts = contributions(z, table_ref, pj_ref, u_ref)
    stiffness_product(k_high_ref, k_low_ref, uw_ref, e_ref)
    elements = jnp.zeros((ROWS, z.width), F32)
    for c in range(z.slots):
        rows = slice(c * ROWS, (c + 1) * ROWS)
        elements = elements + u_ref[rows, :] * e_ref[rows, :]
    energy = energy + jnp.sum(elements, axis=1, keepdims=True)
    dots.append(lanes_by_vector(z, energy))
    line = dots[0]
    for k in range(1, len(dots)):
        line = line + pltpu.roll(dots[k], k * ROWS, 1)
    message = jnp.concatenate(parts + [line], axis=0)
    for d in range(z.devices):
        out_ref[d] = message


class Scatter:
    def __init__(self, z, table_ref, index_ref, corner_ref, acc_ref):
        self.z, self.index_ref, self.corner_ref, self.acc_ref = z, index_ref, corner_ref, acc_ref
        self.table_ref = table_ref
        self.groups = z.window // WIDE
        self.pair = (2 * ROWS, LANES)
        sub = iota(self.pair, 0)
        self.lows = [(sub + k * 2 * ROWS).astype(jnp.int16) for k in range(WIDE // (2 * ROWS))]
        self.one, self.none = jnp.ones(self.pair, BF16), jnp.zeros(self.pair, BF16)
        self.lane = iota((ROWS, LANES), 1)
        self.end = (z.elem - 1) % LANES

    def two_parts(self, value):
        rounded = value.astype(BF16).astype(F32)
        return jnp.concatenate([rounded, value - rounded], axis=0).astype(BF16)

    def hot_rows(self, index):
        low = (index & (WIDE - 1)).astype(jnp.int16)
        return jnp.concatenate([jnp.where(low == k, self.one, self.none) for k in self.lows], axis=0)

    def masked(self, high, both, rows):
        high = high.astype(jnp.int16)
        return jnp.concatenate([jnp.where(high == jnp.int16(h), both, self.none) for h in range(rows)], axis=0)

    def product(self, lhs, hot):
        return lax.dot_general(lhs, hot, NT, preferred_element_type=F32)

    def start(self, sources):
        z = self.z
        corners = jnp.zeros((ROWS, LANES), F32)
        at = (z.tiles - 1) * LANES + self.end
        for cell, values in sources:
            corners = corners + jnp.where(self.lane == cell, values[:, 0:1], 0.0)
            corners = corners + jnp.where(self.lane == z.slots + cell, values[:, at : at + 1], 0.0)
        index = jnp.broadcast_to(self.corner_ref[...], self.pair)
        rows = self.groups * 2 * ROWS
        self.acc_ref[:rows, :] = self.product(
            self.masked(index >> 8, self.two_parts(corners), self.groups), self.hot_rows(index)
        )
        self.acc_ref[rows:, :] = jnp.zeros((BAND * 2 * ROWS, WIDE), F32)

    def add(self, cells, value_of):
        z = self.z
        starts = [self.table_ref[0, z.low + c] >> 8 for c in cells]
        ends = [self.table_ref[0, z.high + c] >> 8 for c in cells]
        passes = functools.reduce(jnp.maximum, [(e - s) // BAND + 1 for s, e in zip(starts, ends)])

        def one_pass(k, _):
            for i, c in enumerate(cells):
                start = jnp.minimum(starts[i] + k * BAND, self.groups)
                lhs, hot = [], []
                for t in range(z.tiles):
                    index = jnp.broadcast_to(self.index_ref[c, :, t * LANES : (t + 1) * LANES], self.pair)
                    value = value_of(i, t)
                    if t == 0:
                        value = jnp.where(self.lane == 0, 0.0, value)
                    if t == z.tiles - 1:
                        value = jnp.where(self.lane == self.end, 0.0, value)
                    lhs.append(self.masked((index >> 8) - start, self.two_parts(value), BAND))
                    hot.append(self.hot_rows(index))
                to = pl.ds(pl.multiple_of(start * 2 * ROWS, 2 * ROWS), BAND * 2 * ROWS)
                self.acc_ref[to, :] += self.product(jnp.concatenate(lhs, axis=1), jnp.concatenate(hot, axis=1))
            return 0

        lax.fori_loop(0, passes, one_pass, 0)

    def add_rows(self, index, values, first, rows):
        lhs, hot = [], []
        for t in range(values.shape[1] // LANES):
            lanes = slice(t * LANES, (t + 1) * LANES)
            at = jnp.broadcast_to(index[:, lanes], self.pair)
            lhs.append(self.masked(at >> 8, self.two_parts(values[:, lanes]), rows))
            hot.append(self.hot_rows(at))
        to = slice(first * 2 * ROWS, (first + rows) * 2 * ROWS)
        self.acc_ref[to, :] += self.product(jnp.concatenate(lhs, axis=1), jnp.concatenate(hot, axis=1))

    def result(self, h):
        at = h * 2 * ROWS
        return self.acc_ref[at : at + ROWS] + self.acc_ref[at + ROWS : at + 2 * ROWS]


def cells_kernel(z, multiply, table_ref, index_ref, corner_ref, *refs):
    if multiply:
        uw_ref, stiffness_ref, diag_ref, image_ref, send_a_ref, send_b_ref, k_high_ref, k_low_ref, *refs = refs
        e_ref, k_ref, acc_ref = refs
        k_ref[...] = jnp.zeros_like(k_ref)
        k_ref[: z.elem, : z.elem] = stiffness_ref[...]
        k_high_ref[...], k_low_ref[...] = split(k_ref[...])
        stiffness_product(k_high_ref, k_low_ref, uw_ref, e_ref)
    else:
        e_ref, image_ref, send_a_ref, send_b_ref, acc_ref = refs
    scatter = Scatter(z, table_ref, index_ref, corner_ref, acc_ref)
    scatter.start([(c, e_ref[c * ROWS : (c + 1) * ROWS, :]) for c in range(z.slots)])

    def some_cells(g, _):
        cells = [g * z.together + i for i in range(z.together)]

        def value_of(i, t):
            rows = pl.ds(pl.multiple_of(cells[i] * ROWS, ROWS), ROWS)
            return e_ref[rows, t * LANES : (t + 1) * LANES]

        scatter.add(cells, value_of)
        return 0

    lax.fori_loop(0, z.slots // z.together, some_cells, 0)
    for h in range(scatter.groups):
        image_ref[:, h * WIDE : (h + 1) * WIDE] = scatter.result(h)
    even = table_ref[0, z.position] % 2 == 0
    ends = [slice(0, 2 * z.rim), slice(z.window - 2 * z.rim, z.window)]
    for source_ref, rows in ((image_ref, slice(0, ROWS)),) + (((diag_ref, slice(ROWS, ROWS + 2)),) if multiply else ()):
        low_rim, high_rim = (source_ref[:, end] for end in ends)
        send_a_ref[rows, :] = jnp.where(even, high_rim, low_rim)
        send_b_ref[rows, :] = jnp.where(even, low_rim, high_rim)


def support_kernel(
    z, last, table_ref, sums_ref, coupling_ref, index_ref, corner_ref, pj_ref, ext_a_ref, ext_b_ref,
    cells_ref, *refs,
):
    if last:
        image_ref, dots_ref, support_ref, acc_ref = refs
    else:
        image_ref, support_ref, acc_ref = refs
    position = table_ref[0, z.position]
    wanted = (
        pltpu.roll(sums_ref[:, 0, :], z.devices - 1, 0) + sums_ref[:, 1, :] + pltpu.roll(sums_ref[:, 2, :], 1, 0)
    )
    coupling = coupling_ref[:, 3, :]
    shape = (z.devices, LANES)
    lane = iota(shape, 1)
    term = jnp.zeros(shape, F32)
    for j in range(z.channels):
        matrix = lane_gather(coupling, lane // ROWS * ROWS + j)
        vector = lane_gather(wanted, lane // z.pairs * z.pairs + j * ROWS + lane % ROWS)
        term = term + matrix * vector
    if last:
        energy = jnp.sum(term * wanted, axis=0, keepdims=True)
        energy = jnp.broadcast_to(energy, (ROWS, LANES))
        step = ROWS
        while step < LANES:
            energy = energy + pltpu.roll(energy, step, 1)
            step *= 2
        line = iota((1, LANES), 1)
        dots_ref[...] = jnp.sum(sums_ref[:, 3, :], axis=0, keepdims=True) + jnp.where(
            line // ROWS == 3, energy[0:1], 0.0
        )
    block = iota(shape, 0)
    small_lane, small_row = iota((ROWS, LANES), 1), iota((ROWS, LANES), 0)

    def values(facts, projectors):
        spread = []
        for s, (owner, local, alive) in enumerate(facts):
            mine = jnp.sum(jnp.where(block == owner, term, 0.0), axis=0, keepdims=True)
            got = lane_gather(
                jnp.broadcast_to(mine, (ROWS, LANES)), local * z.pairs + small_lane % ROWS * ROWS + small_row
            )
            spread.append(jnp.where((small_lane // ROWS == s) & alive, got, 0.0)[:, : z.entries * ROWS])
        return jnp.dot(
            jnp.concatenate(spread, axis=0), projectors, precision=HIGHEST, preferred_element_type=F32
        )

    support_ref[...] = values([entry_facts(z, table_ref, s) for s in range(z.entries)], pj_ref[...])
    scatter = Scatter(z, table_ref, index_ref, corner_ref, acc_ref)
    cells = [table_ref[0, z.cell + s] for s in range(z.entries)]
    scatter.start([(cell, support_ref[s * ROWS : (s + 1) * ROWS, :]) for s, cell in enumerate(cells)])
    for first in range(0, z.entries, z.together):
        some = cells[first : first + z.together]

        def value_of(i, t):
            s = first + i
            return support_ref[s * ROWS : (s + 1) * ROWS, t * LANES : (t + 1) * LANES]

        scatter.add(some, value_of)
    used = slice(0, z.rim_row)
    shared = 2 * z.rim // WIDE
    neighbours = sides(position, ext_a_ref[used, :], ext_b_ref[used, :])
    for ext, first, offset in zip(neighbours, (0, scatter.groups - shared), (z.window - 2 * z.rim, 0)):
        nodes = ext[z.index_row :].astype(jnp.int32)
        facts = []
        for s in range(z.entries):
            fact = [jnp.broadcast_to(nodes[s : s + 1, z.elem + k : z.elem + k + 1], (1, LANES)) for k in range(3)]
            facts.append((fact[0], fact[1], fact[2] > 0))
        rows = values(facts, jnp.where(iota((z.index_row, z.width), 1) < z.elem, ext[: z.index_row], 0.0))
        for s in range(0, z.entries, 2):
            index = jnp.concatenate([nodes[s : s + 1], nodes[s + 1 : s + 2]], axis=1) - offset
            pair = jnp.concatenate([rows[s * ROWS : (s + 1) * ROWS], rows[(s + 1) * ROWS : (s + 2) * ROWS]], axis=1)
            scatter.add_rows(index, pair, first, shared)
    for h in range(scatter.groups):
        at = slice(h * WIDE, (h + 1) * WIDE)
        image_ref[:, at] = cells_ref[:, at] + scatter.result(h)


def last_kernel(
    z, table_ref, rhs_ref, p_ref, diag_ref, shift_ref, y_ref, q_ref, image_ref, dots_ref, halo_a_ref, halo_b_ref,
    solution_ref, residual_ref,
):
    own = slice(z.rim, z.rim + z.nodes)
    lane, row = iota((ROWS, LANES), 1), iota((ROWS, LANES), 0)
    line = jnp.broadcast_to(dots_ref[...], (ROWS, LANES))

    def column(k):
        return jnp.sum(jnp.where(lane == k * ROWS + row, line, 0.0), axis=1, keepdims=True)

    gamma, py, qy, qq = (column(k) for k in range(4))
    alpha = gamma / py
    fresh = gamma - 2.0 * alpha * py + alpha * alpha * qy
    beta = fresh / gamma
    more = 1.0 + beta
    step = fresh / (more * more * py - 2.0 * more * alpha * qy + alpha * alpha * qq)
    p, q, y = p_ref[:, own], q_ref[:, own], y_ref[:, own]
    second = image_ref[:, own] + (diag_ref[1:2, own] + shift_ref[:, :1]) * q
    search = (p - alpha * q) + beta * p
    solution_ref[...] = alpha * p + step * search
    residual_ref[...] = (rhs_ref[...] - alpha * y) - step * (more * y - alpha * second)
    left, right = sides(table_ref[0, z.position], halo_a_ref[...], halo_b_ref[...])
    residual_ref[:, : z.rim] += step * alpha * left[:, z.rim :]
    residual_ref[:, z.nodes - z.rim :] += step * alpha * right[:, : z.rim]


def on_device(
    rhs, potential, precond, shift, stiffness, cell_scale, conn, cell_count, projector, support_cell, support_atom,
    support_count, atom_matrix,
):
    count = lax.axis_size("dom")
    z = Sizes(count, rhs, conn, projector, atom_matrix)
    position = lax.axis_index("dom")
    pos = position.astype(jnp.int32).reshape(1)
    near = [(i, i ^ 1) for i in range(count)]
    far = [(i, j) for i in range(1, count - 1) for j in [i + 1 if i % 2 else i - 1]]

    def exchange(a, b):
        return lax.ppermute(a, "dom", near), lax.ppermute(b, "dom", far)

    def call(kernel, outs, scratch, scalars, *args, in_hbm=(), by_hand=False):
        space = pltpu.HBM if by_hand else pltpu.VMEM
        args = [pltpu.with_memory_space_constraint(x, space) for x in args]
        return pl.pallas_call(
            kernel,
            out_shape=[
                jax.ShapeDtypeStruct(s, d) if i in in_hbm else pltpu.VMEM(s, d) for i, (s, d) in enumerate(outs)
            ],
            in_specs=[SMEM] * len(scalars) + [pl.BlockSpec(memory_space=space)] * len(args),
            out_specs=[VMEM] * len(outs),
            scratch_shapes=[pltpu.VMEM(*s) if isinstance(s, tuple) else s for s in scratch],
            compiler_params=pltpu.CompilerParams(vmem_limit_bytes=16 * 1024 * 1024),
        )(*scalars, *args)

    flat_projector = projector.reshape(z.entries * z.channels, z.elem)
    cells = (z.slots * ROWS, z.width)
    window, reach, own = (z.vectors, z.window), (z.vectors, z.reach), (z.vectors, z.nodes)
    message = (z.devices, 4, LANES)
    square, entries = (z.width, z.width), (z.entries * ROWS, z.width)
    rim, more_rim = (z.vectors, 2 * z.rim), (z.vectors + 2, 2 * z.rim)
    acc = ((z.window // WIDE + BAND) * 2 * ROWS, WIDE)

    precond_lines = precond.reshape(-1, LANES)
    tile = (ROWS, LANES)
    first_message = (z.message, z.width)
    ext = exchange(
        *call(
            functools.partial(start_kernel, z),
            [(first_message, F32)] * 2,
            [((2, z.vectors, z.rim), F32), ((2, z.rim // LANES, LANES), F32), (conn.shape, jnp.int32),
             (flat_projector.shape, F32), pltpu.SMEM(support_cell.shape, jnp.int32),
             pltpu.SMEM(support_atom.shape, jnp.int32), pltpu.SMEM(support_count.shape, jnp.int32),
             pltpu.SemaphoreType.DMA((9,))],
            (pos,),
            support_cell, support_atom, support_count, rhs, precond_lines, conn, flat_projector, by_hand=True,
        )
    )
    index, corner, table, weight = call(
        functools.partial(prepare_kernel, z),
        [((z.slots, 1, z.width), jnp.int32), ((1, LANES), jnp.int32), ((1, LANES), jnp.int32),
         ((z.slots * ROWS, LANES), F32)],
        [],
        (pos, cell_count, cell_scale, support_cell, support_atom, support_count),
        conn,
    )
    p, gamma, diag, shift_tile = call(
        functools.partial(own_kernel, z),
        [(reach, F32), ((1, LANES), F32), ((2, z.window), F32), (tile, F32)],
        [],
        (shift,),
        rhs, precond_lines, potential.reshape(-1, LANES),
    )
    (u,) = call(functools.partial(first_window_kernel, z), [(cells, F32)], [], (table,), p, index)
    p, sums, uw, pj = call(
        functools.partial(first_kernel, z),
        [(reach, F32), (message, F32), (cells, F32), (entries, F32)],
        [(cells, F32)],
        (table,),
        p, u, *ext, index, corner, weight, flat_projector, atom_matrix,
    )
    coupled = lax.all_to_all(sums, "dom", 0, 0)
    image, send_a, send_b, k_high, k_low = call(
        functools.partial(cells_kernel, z, True),
        [(window, F32), (more_rim, F32), (more_rim, F32), (square, BF16), (square, BF16)],
        [(cells, F32), (square, F32), (acc, F32)],
        (table,),
        index, corner, uw, stiffness, diag,
    )
    halo = exchange(send_a, send_b)
    (image,) = call(
        functools.partial(support_kernel, z, False),
        [(window, F32)],
        [(entries, F32), (acc, F32)],
        (table,),
        coupled, coupled, index, corner, pj, *ext, image,
    )
    y, q, sums, e = call(
        functools.partial(second_kernel, z),
        [(window, F32), (reach, F32), (message, F32), (cells, F32)],
        [((2, z.window), F32), (cells, F32), (cells, F32)],
        (table,),
        image, p, diag, shift_tile, gamma, *halo, index, corner, weight, k_high, k_low, pj,
    )
    totals = lax.all_to_all(sums, "dom", 0, 0)
    image, send_a, send_b = call(
        functools.partial(cells_kernel, z, False), [(window, F32), (rim, F32), (rim, F32)], [(acc, F32)], (table,),
        index, corner, e,
    )
    halo = exchange(send_a, send_b)
    image, dots = call(
        functools.partial(support_kernel, z, True),
        [(window, F32), ((1, LANES), F32)],
        [(entries, F32), (acc, F32)],
        (table,),
        totals, coupled, index, corner, pj, *ext, image,
    )
    return tuple(
        call(
            functools.partial(last_kernel, z),
            [(own, F32), (own, F32)],
            [],
            (table,),
            rhs, p, diag, shift_tile, y, q, image, dots, *halo, in_hbm=(0, 1),
        )
    )


def solution(mesh):
    placed = (
        P(None, "dom"),
        P("dom"),
        P("dom"),
        P(),
        P(),
        P("dom"),
        P("dom", None),
        P(),
        P("dom", None, None),
        P("dom"),
        P("dom"),
        P(),
        P("dom", None, None),
    )
    return jax.shard_map(
        on_device,
        mesh=mesh,
        in_specs=placed,
        out_specs=(P(None, "dom"), P(None, "dom")),
        check_vma=False,
    )
```

```python
import functools

import jax
import jax.numpy as jnp
from jax import lax
from jax.experimental import pallas as pl
from jax.experimental.pallas import tpu as pltpu
from jax.sharding import PartitionSpec as P

LANES = 128
ROWS = 8
WIDE = 256
CHAINS = 4
SPAN = 14
BAND = 8
TOGETHER = 8
F32 = jnp.float32
BF16 = jnp.bfloat16
HIGHEST = lax.Precision.HIGHEST
NT = (((1,), (1,)), ((), ()))
VMEM = pl.BlockSpec(memory_space=pltpu.VMEM)
SMEM = pl.BlockSpec(memory_space=pltpu.SMEM)


def round_up(value, step):
    return -(-value // step) * step


class Sizes:
    def __init__(self, count, rhs, conn, projector, atom_matrix):
        self.devices = count
        self.vectors, self.nodes = rhs.shape
        self.slots, self.elem = conn.shape
        self.entries, self.channels = projector.shape[:2]
        self.owned = atom_matrix.shape[0]
        self.ghost = self.nodes // 16
        self.rim = round_up(self.ghost, WIDE)
        self.shift = self.rim - self.ghost
        self.window = self.nodes + 2 * self.rim
        self.width = round_up(self.elem, LANES)
        self.tiles = self.width // LANES
        self.pairs = self.channels * self.vectors
        self.low, self.high, self.list = 0, self.slots, 2 * self.slots
        self.cell = 3 * self.slots
        self.owner, self.local = self.cell + self.entries, self.cell + 2 * self.entries
        self.position = self.cell + 3 * self.entries
        self.beside = 2 * self.slots
        assert self.position + 1 < LANES and self.beside + 4 * self.entries <= LANES
        self.reach = self.window + SPAN * LANES
        self.index_row = self.entries * self.channels
        self.rim_row = self.index_row + round_up(self.entries, ROWS)
        self.rim_pieces = -(-self.rim // self.width)
        self.message = self.rim_row + self.rim_pieces * ROWS
        assert self.elem + 5 <= self.width and 2 * self.entries <= self.slots
        self.together = TOGETHER if self.slots % TOGETHER == 0 else 1
        assert self.vectors == ROWS and self.channels == ROWS and 2 * self.slots <= LANES
        assert self.nodes % WIDE == 0 and self.owned * self.pairs == LANES


def lane_gather(values, index):
    return jnp.take_along_axis(values, index, axis=1, mode="promise_in_bounds")


def iota(shape, dim):
    return lax.broadcasted_iota(jnp.int32, shape, dim)


def split(values):
    high = values.astype(BF16)
    return high, (values - high.astype(F32)).astype(BF16)


def lanes_by_vector(z, values):
    total = jnp.sum(values, axis=1, keepdims=True)
    spread = jnp.broadcast_to(total, (ROWS, LANES))
    return jnp.sum(jnp.where(iota((ROWS, LANES), 1) == iota((ROWS, LANES), 0), spread, 0.0), axis=0, keepdims=True)


def prepare_kernel(
    z, pos_ref, count_ref, scale_ref, cell_ref, atom_ref, scount_ref, conn_ref,
    index_ref, corner_ref, table_ref, weight_ref,
):
    position = pos_ref[0]
    line = iota((1, LANES), 1)
    corner = jnp.zeros((1, LANES), jnp.int32)
    index_ref[...] = jnp.zeros_like(index_ref)
    live = count_ref[position]
    for c in range(z.slots):
        row = conn_ref[c : c + 1, :] + z.shift
        index_ref[c, :, : z.elem] = row
        corner = jnp.where(line == c, row[:, :1], corner)
        corner = jnp.where(line == z.slots + c, row[:, z.elem - 1 :], corner)
        weight = jnp.where(c < live, scale_ref[c], 0.0)
        weight_ref[c * ROWS : (c + 1) * ROWS, :] = jnp.zeros((ROWS, LANES), F32) + weight
    corner_ref[...] = corner
    nodes = (conn_ref[...] + z.shift).astype(F32)
    place = iota(nodes.shape, 1)
    middle = (place > 0) & (place < z.elem - 1)
    low = jnp.min(jnp.where(middle, nodes, 1.0 * z.window), axis=1, keepdims=True)
    high = jnp.max(jnp.where(middle, nodes, 0.0), axis=1, keepdims=True)
    lane, cell = iota((z.slots, LANES), 1), iota((z.slots, LANES), 0)

    def as_row(column, first=0):
        return jnp.sum(jnp.where(lane == cell + first, column, 0.0), axis=0, keepdims=True)

    good = jnp.where((low >= z.rim) & (high < z.window - z.rim), 1.0, 0.0)
    good = jnp.broadcast_to(good, (z.slots, LANES))
    number = cell.astype(F32)
    before = jnp.sum(jnp.where(lane < cell, as_row(good), 0.0), axis=1, keepdims=True)
    at = jnp.where(good > 0.5, before, z.slots - 1.0 - (number - before))
    listed = jnp.where(lane.astype(F32) == at + z.list, number + z.slots * good, 0.0)
    table = as_row(low, z.low) + as_row(high, z.high) + jnp.sum(listed, axis=0, keepdims=True)
    table = table.astype(jnp.int32)
    for s in range(z.entries):
        atom = atom_ref[s]
        owner = atom // z.owned
        for first, fact in ((z.cell, cell_ref[s]), (z.owner, owner), (z.local, atom - owner * z.owned)):
            table = jnp.where(line == first + s, fact, table)
    table = jnp.where(line == z.position, position, table)
    table_ref[...] = jnp.where(line == z.position + 1, scount_ref[position], table)


def start_kernel(
    z, pos_ref, cell_hbm, atom_hbm, scount_hbm, shift_hbm, rhs_ref, precond_ref, conn_ref, projector_ref,
    send_a_ref, send_b_ref, shift_tile_ref, rhs_rim, precond_rim, conn_all, projector_all, cell_ref, atom_ref,
    scount_ref, shift_ref, sems,
):
    lines = z.rim // LANES
    moves = [
        (cell_hbm, cell_ref), (atom_hbm, atom_ref), (scount_hbm, scount_ref), (shift_hbm, shift_ref),
        (conn_ref, conn_all), (projector_ref, projector_all),
    ]
    for k, first in enumerate((0, z.nodes - z.rim)):
        moves.append((rhs_ref.at[:, pl.ds(first, z.rim)], rhs_rim.at[k]))
        moves.append((precond_ref.at[pl.ds(first // LANES, lines), :], precond_rim.at[k]))
    copies = [pltpu.make_async_copy(source, to, sems.at[k]) for k, (source, to) in enumerate(moves)]
    for copy in copies:
        copy.start()
    for copy in copies:
        copy.wait()
    row = iota((ROWS, LANES), 0)
    tile = jnp.zeros((ROWS, LANES), F32)
    for v in range(z.vectors):
        tile = jnp.where(row == v, shift_ref[v], tile)
    shift_tile_ref[...] = tile
    head, tail = (
        jnp.concatenate(
            [
                rhs_rim[k, :, i * LANES : (i + 1) * LANES] * precond_rim[k, i : i + 1, :]
                for i in range(lines)
            ],
            axis=1,
        )
        for k in range(2)
    )
    even = pos_ref[0] % 2 == 0
    sides = jnp.where(even, tail, head), jnp.where(even, head, tail)
    nodes = (conn_all[...] + z.shift).astype(F32)
    cell = iota(nodes.shape, 0)
    entry = iota((z.rim_row - z.index_row, z.width), 0)
    place = iota((z.rim_row - z.index_row, z.width), 1)
    rows = jnp.zeros((z.rim_row - z.index_row, z.width), F32)
    for s in range(z.entries):
        row = jnp.sum(jnp.where(cell == cell_ref[s], nodes, 0.0), axis=0, keepdims=True)
        row = jnp.concatenate([row, jnp.zeros((1, z.width - z.elem), F32)], axis=1)
        owner = atom_ref[s] // z.owned
        facts = owner, atom_ref[s] - owner * z.owned, (s < scount_ref[pos_ref[0]]).astype(jnp.int32)
        rows = jnp.where(entry == s, row, rows)
        for k, fact in enumerate(facts):
            rows = jnp.where((entry == s) & (place == z.elem + k), fact.astype(F32), rows)
    middle = (place > 0) & (place < z.elem - 1)
    low = jnp.min(jnp.where(middle, rows, 1.0 * z.window), axis=1, keepdims=True)
    high = jnp.max(jnp.where(middle, rows, 0.0), axis=1, keepdims=True)
    rows = jnp.where(place == z.elem + 3, low, jnp.where(place == z.elem + 4, high, rows))
    for ref, side in zip((send_a_ref, send_b_ref), sides):
        ref[...] = jnp.zeros_like(ref)
        ref[: z.index_row, : z.elem] = projector_all[...]
        ref[z.index_row : z.rim_row, :] = rows
        for k in range(z.rim_pieces):
            piece = side[:, k * z.width : min((k + 1) * z.width, z.rim)]
            ref[z.rim_row + k * ROWS : z.rim_row + (k + 1) * ROWS, : piece.shape[1]] = piece


def own_kernel(
    z, rhs_ref, precond_ref, potential_ref, p_ref, gamma_ref, diag_ref,
):
    diag_ref[...] = jnp.zeros_like(diag_ref)
    gamma = jnp.zeros((ROWS, LANES), F32)
    for i in range(z.nodes // LANES):
        at = slice(i * LANES, (i + 1) * LANES)
        to = slice(z.rim + i * LANES, z.rim + (i + 1) * LANES)
        value = rhs_ref[:, at]
        scale = precond_ref[i : i + 1, :]
        product = value * scale
        p_ref[:, to] = product
        gamma = gamma + product * value
        diag_ref[0:1, to] = scale
        diag_ref[1:2, to] = potential_ref[i : i + 1, :]
    p_ref[:, z.window :] = jnp.zeros((ROWS, z.reach - z.window), F32)
    gamma_ref[...] = lanes_by_vector(z, gamma)


def full_groups(z, table_ref):
    ends = [table_ref[0, z.list + g * z.together + z.together - 1] for g in range(z.slots // z.together)]
    return functools.reduce(jnp.add, [(end >= z.slots).astype(jnp.int32) for end in ends])


def gather_middle(z, groups, listed, table_ref, index_ref, window_ref, u_ref):
    total = z.window // LANES
    tile = (ROWS, LANES)

    def some_cells(g, _):
        cells = [g * z.together + i for i in range(z.together)]
        if listed:
            cells = [table_ref[0, z.list + c] for c in cells]
            cells = [jnp.where(c >= z.slots, c - z.slots, c) for c in cells]
        starts = [table_ref[0, z.low + c] >> 7 for c in cells]
        ends = [table_ref[0, z.high + c] >> 7 for c in cells]
        passes = functools.reduce(jnp.maximum, [(e - s) // SPAN + 1 for s, e in zip(starts, ends)])

        def one_pass(k, values):
            values = list(values)
            for i, c in enumerate(cells):
                start = jnp.minimum(starts[i] + k * SPAN, total)
                for t in range(z.tiles):
                    index = jnp.broadcast_to(index_ref[c, :, t * LANES : (t + 1) * LANES], tile)
                    low, high = index & (LANES - 1), (index >> 7) - start
                    value = values[i * z.tiles + t]
                    for h in range(SPAN):
                        at = pl.ds(pl.multiple_of((start + h) * LANES, LANES), LANES)
                        value = jnp.where(high == h, lane_gather(window_ref[:, at], low), value)
                    values[i * z.tiles + t] = value
            return tuple(values)

        values = lax.fori_loop(0, passes, one_pass, (jnp.zeros(tile, F32),) * (z.together * z.tiles))
        for i, c in enumerate(cells):
            rows = pl.ds(pl.multiple_of(c * ROWS, ROWS), ROWS)
            for t in range(z.tiles):
                u_ref[rows, t * LANES : (t + 1) * LANES] = values[i * z.tiles + t]
        return 0

    lax.fori_loop(*groups, some_cells, 0)


def gather_corners(z, corner_ref, window_ref, weight_ref, u_ref, uw_ref):
    tile = (ROWS, LANES)
    corner = jnp.broadcast_to(corner_ref[...], tile)
    low, high = corner & (LANES - 1), corner >> 7
    chains = [jnp.zeros(tile, F32)] * CHAINS
    for h in range(z.window // LANES):
        got = lane_gather(window_ref[:, h * LANES : (h + 1) * LANES], low)
        chains[h % CHAINS] = jnp.where(high == h, got, chains[h % CHAINS])
    corners = functools.reduce(jnp.add, chains)
    lane = iota(tile, 1)
    last = (z.elem - 1) % LANES
    for c in range(z.slots):
        rows = slice(c * ROWS, (c + 1) * ROWS)
        weight = weight_ref[rows, :]
        for t in range(z.tiles):
            lanes = slice(t * LANES, (t + 1) * LANES)
            value = u_ref[rows, lanes]
            if t == 0:
                value = jnp.where(lane == 0, corners[:, c : c + 1], value)
            if t == z.tiles - 1:
                value = jnp.where(lane == last, corners[:, z.slots + c : z.slots + c + 1], value)
            u_ref[rows, lanes] = value
            uw_ref[rows, lanes] = value * weight


def stiffness_product(k_high_ref, k_low_ref, uw_ref, e_ref):
    k_high, k_low = k_high_ref[...], k_low_ref[...]
    u_high, u_low = split(uw_ref[...])
    dot = functools.partial(lax.dot_general, dimension_numbers=NT, preferred_element_type=F32)
    e_ref[...] = dot(u_high, k_high) + (dot(u_high, k_low) + dot(u_low, k_high))


def entry_facts(z, table_ref, s):
    return table_ref[0, z.owner + s], table_ref[0, z.local + s], s < table_ref[0, z.position + 1]


def contributions(z, table_ref, pj_ref, u_ref):
    values = [u_ref[pl.ds(pl.multiple_of(table_ref[0, z.cell + s] * ROWS, ROWS), ROWS), :] for s in range(z.entries)]
    sums = lax.dot_general(
        pj_ref[...], jnp.concatenate(values, axis=0), NT, precision=HIGHEST, preferred_element_type=F32
    )
    sums = jnp.concatenate([sums, jnp.zeros((sums.shape[0], LANES - sums.shape[1]), F32)], axis=1)
    lane, row = iota((ROWS, LANES), 1), iota((ROWS, LANES), 0)
    position = table_ref[0, z.position]
    parts = [jnp.zeros((ROWS, LANES), F32)] * 3
    for s in range(z.entries):
        owner, local, alive = entry_facts(z, table_ref, s)
        got = lane_gather(sums[s * ROWS : (s + 1) * ROWS], s * ROWS + lane % ROWS)
        here = (lane // ROWS % ROWS == row) & (lane // z.pairs == local) & alive
        for k in range(3):
            parts[k] = parts[k] + jnp.where(here & (owner == position - 1 + k), got, 0.0)
    return [jnp.sum(part, axis=0, keepdims=True) for part in parts]


def sides(position, near, far):
    even = position % 2 == 0
    return jnp.where(even, far, near), jnp.where(even, near, far)


def first_window_kernel(z, table_ref, p_ref, index_ref, u_ref):
    groups = 0, full_groups(z, table_ref)
    gather_middle(z, groups, True, table_ref, index_ref, p_ref, u_ref)


def first_kernel(
    z, table_ref, table_row_ref, p_in_ref, u_in_ref, halo_a_ref, halo_b_ref, index_ref, corner_ref, weight_ref,
    projector_ref, coupling_ref, p_ref, out_ref, uw_ref, pj_ref, marked_ref, beside_ref, u_ref,
):
    rows = slice(z.index_row, z.index_row + z.entries)
    marked = table_row_ref[...]
    line = iota((1, LANES), 1)
    left, right = sides(table_ref[0, z.position], halo_a_ref[rows, :], halo_b_ref[rows, :])
    for s in range(z.entries):
        high = left[s : s + 1, z.elem + 4 : z.elem + 5]
        marked = jnp.where(line == z.list + s, (high >= z.window - 2 * z.rim).astype(jnp.int32), marked)
        low = right[s : s + 1, z.elem + 3 : z.elem + 4]
        marked = jnp.where(line == z.list + z.entries + s, (low < 2 * z.rim).astype(jnp.int32), marked)
    marked_ref[...] = marked
    beside = corner_ref[...]
    for k, (side, move) in enumerate(((left, -z.nodes), (right, z.nodes))):
        side = side.astype(jnp.int32) + move
        for s in range(z.entries):
            lane = z.beside + 2 * z.entries * k + s
            beside = jnp.where(line == lane, side[s : s + 1, :1], beside)
            beside = jnp.where(line == lane + z.entries, side[s : s + 1, z.elem - 1 : z.elem], beside)
    beside_ref[...] = beside
    own = slice(z.rim, z.rim + z.nodes)
    for k in range(z.rim_pieces):
        rows = slice(z.rim_row + k * ROWS, z.rim_row + (k + 1) * ROWS)
        at, to = k * z.width, min((k + 1) * z.width, z.rim)
        left, right = sides(table_ref[0, z.position], halo_a_ref[rows, : to - at], halo_b_ref[rows, : to - at])
        p_ref[:, at:to] = left
        p_ref[:, z.rim + z.nodes + at : z.rim + z.nodes + to] = right
    p_ref[:, own] = p_in_ref[:, own]
    p_ref[:, z.window :] = p_in_ref[:, z.window :]
    u_ref[...] = u_in_ref[...]
    pj_ref[...] = jnp.zeros_like(pj_ref)
    pj_ref[:, : z.elem] = projector_ref[...]
    groups = full_groups(z, table_ref), z.slots // z.together
    gather_middle(z, groups, True, table_ref, index_ref, p_ref, u_ref)
    gather_corners(z, corner_ref, p_ref, weight_ref, u_ref, uw_ref)
    parts = contributions(z, table_ref, pj_ref, u_ref)
    small_lane, small_row = iota((ROWS, LANES), 1), iota((ROWS, LANES), 0)
    matrices = jnp.zeros((ROWS, LANES), F32)
    for atom in range(z.owned):
        block = jnp.concatenate([coupling_ref[atom], jnp.zeros((ROWS, LANES - z.channels), F32)], axis=1)
        got = lane_gather(block, small_lane % ROWS)
        matrices = jnp.where(small_lane // ROWS == atom * ROWS + small_row, got, matrices)
    message = jnp.concatenate(parts + [jnp.sum(matrices, axis=0, keepdims=True)], axis=0)
    for d in range(z.devices):
        out_ref[d] = message


def second_kernel(
    z, table_ref, image_ref, p_ref, diag_in_ref, shift_ref, gamma_ref, halo_a_ref, halo_b_ref,
    index_ref, corner_ref, weight_ref, k_high_ref, k_low_ref, pj_ref, y_ref, q_ref, out_ref, e_ref, diag_ref, u_ref, uw_ref,
):
    left, right = sides(table_ref[0, z.position], halo_a_ref[...], halo_b_ref[...])
    own = slice(z.rim, z.rim + z.nodes)
    diag_ref[:, own] = diag_in_ref[:, own]
    diag_ref[:, : z.rim] = left[ROWS : ROWS + 2, : z.rim]
    diag_ref[:, z.rim + z.nodes :] = right[ROWS : ROWS + 2, z.rim :]
    y_ref[...] = image_ref[...] + (diag_ref[1:2, :] + shift_ref[:, :1]) * p_ref[:, : z.window]
    y_ref[:, : 2 * z.rim] += left[:ROWS]
    y_ref[:, z.window - 2 * z.rim :] += right[:ROWS]
    q_ref[:, : z.window] = y_ref[...] * diag_ref[0:1, :]
    q_ref[:, z.window :] = jnp.zeros((ROWS, z.reach - z.window), F32)
    y, q = y_ref[:, own], q_ref[:, own]
    dots = [
        gamma_ref[...],
        lanes_by_vector(z, y * p_ref[:, own]),
        lanes_by_vector(z, y * q),
    ]
    energy = jnp.sum(q * q * (diag_ref[1:2, own] + shift_ref[:, :1]), axis=1, keepdims=True)
    groups = 0, z.slots // z.together
    gather_middle(z, groups, False, table_ref, index_ref, q_ref, u_ref)
    gather_corners(z, corner_ref, q_ref, weight_ref, u_ref, uw_ref)
    parts = contributions(z, table_ref, pj_ref, u_ref)
    stiffness_product(k_high_ref, k_low_ref, uw_ref, e_ref)
    elements = jnp.zeros((ROWS, z.width), F32)
    for c in range(z.slots):
        rows = slice(c * ROWS, (c + 1) * ROWS)
        elements = elements + u_ref[rows, :] * e_ref[rows, :]
    energy = energy + jnp.sum(elements, axis=1, keepdims=True)
    dots.append(lanes_by_vector(z, energy))
    line = dots[0]
    for k in range(1, len(dots)):
        line = line + pltpu.roll(dots[k], k * ROWS, 1)
    message = jnp.concatenate(parts + [line], axis=0)
    for d in range(z.devices):
        out_ref[d] = message


class Scatter:
    def __init__(self, z, table_ref, index_ref, corner_ref, acc_ref):
        self.z, self.index_ref, self.corner_ref, self.acc_ref = z, index_ref, corner_ref, acc_ref
        self.table_ref = table_ref
        self.groups = z.window // WIDE
        self.pair = (2 * ROWS, LANES)
        sub = iota(self.pair, 0)
        self.lows = [(sub + k * 2 * ROWS).astype(jnp.int16) for k in range(WIDE // (2 * ROWS))]
        self.one, self.none = jnp.ones(self.pair, BF16), jnp.zeros(self.pair, BF16)
        self.lane = iota((ROWS, LANES), 1)
        self.end = (z.elem - 1) % LANES

    def two_parts(self, value):
        rounded = value.astype(BF16).astype(F32)
        return jnp.concatenate([rounded, value - rounded], axis=0).astype(BF16)

    def hot_rows(self, index):
        low = (index & (WIDE - 1)).astype(jnp.int16)
        return jnp.concatenate([jnp.where(low == k, self.one, self.none) for k in self.lows], axis=0)

    def masked(self, high, both, rows):
        high = high.astype(jnp.int16)
        return jnp.concatenate([jnp.where(high == jnp.int16(h), both, self.none) for h in range(rows)], axis=0)

    def product(self, lhs, hot):
        return lax.dot_general(lhs, hot, NT, preferred_element_type=F32)

    def start(self, sources, beside=()):
        z = self.z
        corners = jnp.zeros((ROWS, LANES), F32)
        at = (z.tiles - 1) * LANES + self.end
        for cell, values in sources:
            corners = corners + jnp.where(self.lane == cell, values[:, 0:1], 0.0)
            corners = corners + jnp.where(self.lane == z.slots + cell, values[:, at : at + 1], 0.0)
        for s, values in enumerate(beside):
            lane = z.beside + s + s // z.entries * z.entries
            corners = jnp.where(self.lane == lane, values[:, 0:1], corners)
            corners = jnp.where(self.lane == lane + z.entries, values[:, at : at + 1], corners)
        index = jnp.broadcast_to(self.corner_ref[...], self.pair)
        rows = self.groups * 2 * ROWS
        self.acc_ref[:rows, :] = self.product(
            self.masked(index >> 8, self.two_parts(corners), self.groups), self.hot_rows(index)
        )
        self.acc_ref[rows:, :] = jnp.zeros((BAND * 2 * ROWS, WIDE), F32)

    def add(self, cells, value_of):
        z = self.z
        starts = [self.table_ref[0, z.low + c] >> 8 for c in cells]
        ends = [self.table_ref[0, z.high + c] >> 8 for c in cells]
        passes = functools.reduce(jnp.maximum, [(e - s) // BAND + 1 for s, e in zip(starts, ends)])

        def one_pass(k, _):
            for i, c in enumerate(cells):
                start = jnp.minimum(starts[i] + k * BAND, self.groups)
                lhs, hot = [], []
                for t in range(z.tiles):
                    index = jnp.broadcast_to(self.index_ref[c, :, t * LANES : (t + 1) * LANES], self.pair)
                    value = value_of(i, t)
                    if t == 0:
                        value = jnp.where(self.lane == 0, 0.0, value)
                    if t == z.tiles - 1:
                        value = jnp.where(self.lane == self.end, 0.0, value)
                    lhs.append(self.masked((index >> 8) - start, self.two_parts(value), BAND))
                    hot.append(self.hot_rows(index))
                to = pl.ds(pl.multiple_of(start * 2 * ROWS, 2 * ROWS), BAND * 2 * ROWS)
                self.acc_ref[to, :] += self.product(jnp.concatenate(lhs, axis=1), jnp.concatenate(hot, axis=1))
            return 0

        lax.fori_loop(0, passes, one_pass, 0)

    def add_rows(self, index, values, first, rows):
        lhs, hot = [], []
        for t in range(values.shape[1] // LANES):
            lanes = slice(t * LANES, (t + 1) * LANES)
            at = jnp.broadcast_to(index[:, lanes], self.pair)
            lhs.append(self.masked(at >> 8, self.two_parts(values[:, lanes]), rows))
            hot.append(self.hot_rows(at))
        to = slice(first * 2 * ROWS, (first + rows) * 2 * ROWS)
        self.acc_ref[to, :] += self.product(jnp.concatenate(lhs, axis=1), jnp.concatenate(hot, axis=1))

    def result(self, h):
        at = h * 2 * ROWS
        return self.acc_ref[at : at + ROWS] + self.acc_ref[at + ROWS : at + 2 * ROWS]


def cells_kernel(z, multiply, table_ref, index_ref, corner_ref, *refs):
    if multiply:
        uw_ref, stiffness_ref, diag_ref, image_ref, send_a_ref, send_b_ref, k_high_ref, k_low_ref, *refs = refs
        e_ref, k_ref, acc_ref = refs
        k_ref[...] = jnp.zeros_like(k_ref)
        k_ref[: z.elem, : z.elem] = stiffness_ref[...]
        k_high_ref[...], k_low_ref[...] = split(k_ref[...])
        stiffness_product(k_high_ref, k_low_ref, uw_ref, e_ref)
    else:
        e_ref, image_ref, send_a_ref, send_b_ref, acc_ref = refs
    scatter = Scatter(z, table_ref, index_ref, corner_ref, acc_ref)
    scatter.start([(c, e_ref[c * ROWS : (c + 1) * ROWS, :]) for c in range(z.slots)])

    def some_cells(g, _):
        cells = [g * z.together + i for i in range(z.together)]

        def value_of(i, t):
            rows = pl.ds(pl.multiple_of(cells[i] * ROWS, ROWS), ROWS)
            return e_ref[rows, t * LANES : (t + 1) * LANES]

        scatter.add(cells, value_of)
        return 0

    lax.fori_loop(0, z.slots // z.together, some_cells, 0)
    for h in range(scatter.groups):
        image_ref[:, h * WIDE : (h + 1) * WIDE] = scatter.result(h)
    even = table_ref[0, z.position] % 2 == 0
    ends = [slice(0, 2 * z.rim), slice(z.window - 2 * z.rim, z.window)]
    for source_ref, rows in ((image_ref, slice(0, ROWS)),) + (((diag_ref, slice(ROWS, ROWS + 2)),) if multiply else ()):
        low_rim, high_rim = (source_ref[:, end] for end in ends)
        send_a_ref[rows, :] = jnp.where(even, high_rim, low_rim)
        send_b_ref[rows, :] = jnp.where(even, low_rim, high_rim)


def support_kernel(
    z, last, table_ref, sums_ref, coupling_ref, index_ref, corner_ref, pj_ref, ext_a_ref, ext_b_ref,
    cells_ref, *refs,
):
    if last:
        image_ref, dots_ref, support_ref, nodes_ref, acc_ref = refs
    else:
        image_ref, support_ref, nodes_ref, acc_ref = refs
    position = table_ref[0, z.position]
    wanted = (
        pltpu.roll(sums_ref[:, 0, :], z.devices - 1, 0) + sums_ref[:, 1, :] + pltpu.roll(sums_ref[:, 2, :], 1, 0)
    )
    coupling = coupling_ref[:, 3, :]
    shape = (z.devices, LANES)
    lane = iota(shape, 1)
    term = jnp.zeros(shape, F32)
    for j in range(z.channels):
        matrix = lane_gather(coupling, lane // ROWS * ROWS + j)
        vector = lane_gather(wanted, lane // z.pairs * z.pairs + j * ROWS + lane % ROWS)
        term = term + matrix * vector
    if last:
        energy = jnp.sum(term * wanted, axis=0, keepdims=True)
        energy = jnp.broadcast_to(energy, (ROWS, LANES))
        step = ROWS
        while step < LANES:
            energy = energy + pltpu.roll(energy, step, 1)
            step *= 2
        line = iota((1, LANES), 1)
        dots_ref[...] = jnp.sum(sums_ref[:, 3, :], axis=0, keepdims=True) + jnp.where(
            line // ROWS == 3, energy[0:1], 0.0
        )
    block = iota(shape, 0)
    small_lane, small_row = iota((ROWS, LANES), 1), iota((ROWS, LANES), 0)

    def values(facts, projectors):
        spread = []
        for s, (owner, local, alive) in enumerate(facts):
            mine = jnp.sum(jnp.where(block == owner, term, 0.0), axis=0, keepdims=True)
            got = lane_gather(
                jnp.broadcast_to(mine, (ROWS, LANES)), local * z.pairs + small_lane % ROWS * ROWS + small_row
            )
            spread.append(jnp.where((small_lane // ROWS == s) & alive, got, 0.0)[:, : z.entries * ROWS])
        return jnp.dot(
            jnp.concatenate(spread, axis=0), projectors, precision=HIGHEST, preferred_element_type=F32
        )

    count = z.entries * ROWS
    support_ref[:count, :] = values([entry_facts(z, table_ref, s) for s in range(z.entries)], pj_ref[...])
    used = slice(0, z.rim_row)
    for side, ext in enumerate(sides(position, ext_a_ref[used, :], ext_b_ref[used, :])):
        nodes = ext[z.index_row :].astype(jnp.int32)
        facts = []
        for s in range(z.entries):
            fact = [jnp.broadcast_to(nodes[s : s + 1, z.elem + k : z.elem + k + 1], (1, LANES)) for k in range(3)]
            facts.append((fact[0], fact[1], fact[2] > 0))
        projectors = jnp.where(iota((z.index_row, z.width), 1) < z.elem, ext[: z.index_row], 0.0)
        support_ref[(side + 1) * count : (side + 2) * count, :] = values(facts, projectors)
        nodes_ref[side] = nodes
    scatter = Scatter(z, table_ref, index_ref, corner_ref, acc_ref)
    cells = [table_ref[0, z.cell + s] for s in range(z.entries)]
    blocks = [support_ref[s * ROWS : (s + 1) * ROWS, :] for s in range(3 * z.entries)]
    scatter.start(list(zip(cells, blocks)), blocks[z.entries :])
    for first in range(0, z.entries, z.together):
        some = cells[first : first + z.together]

        def value_of(i, t):
            s = first + i
            return support_ref[s * ROWS : (s + 1) * ROWS, t * LANES : (t + 1) * LANES]

        scatter.add(some, value_of)
    shared = 2 * z.rim // WIDE
    place = iota((ROWS, z.width), 1)
    middle = (place > 0) & (place < z.elem - 1)
    for side, (first, offset) in enumerate(((0, z.window - 2 * z.rim), (scatter.groups - shared, 0))):
        for s in range(z.entries):

            @pl.when(table_ref[0, z.list + side * z.entries + s] > 0)
            def _():
                at = ((side + 1) * z.entries + s) * ROWS
                value = jnp.where(middle, support_ref[at : at + ROWS, :], 0.0)
                scatter.add_rows(nodes_ref[side, s : s + 1, :] - offset, value, first, shared)

    for h in range(scatter.groups):
        at = slice(h * WIDE, (h + 1) * WIDE)
        image_ref[:, at] = cells_ref[:, at] + scatter.result(h)


def last_kernel(
    z, table_ref, rhs_ref, p_ref, diag_ref, shift_ref, y_ref, q_ref, image_ref, dots_ref, halo_a_ref, halo_b_ref,
    solution_ref, residual_ref,
):
    own = slice(z.rim, z.rim + z.nodes)
    lane, row = iota((ROWS, LANES), 1), iota((ROWS, LANES), 0)
    line = jnp.broadcast_to(dots_ref[...], (ROWS, LANES))

    def column(k):
        return jnp.sum(jnp.where(lane == k * ROWS + row, line, 0.0), axis=1, keepdims=True)

    gamma, py, qy, qq = (column(k) for k in range(4))
    alpha = gamma / py
    fresh = gamma - 2.0 * alpha * py + alpha * alpha * qy
    beta = fresh / gamma
    more = 1.0 + beta
    step = fresh / (more * more * py - 2.0 * more * alpha * qy + alpha * alpha * qq)
    p, q, y = p_ref[:, own], q_ref[:, own], y_ref[:, own]
    second = image_ref[:, own] + (diag_ref[1:2, own] + shift_ref[:, :1]) * q
    search = (p - alpha * q) + beta * p
    solution_ref[...] = alpha * p + step * search
    residual_ref[...] = (rhs_ref[...] - alpha * y) - step * (more * y - alpha * second)
    left, right = sides(table_ref[0, z.position], halo_a_ref[...], halo_b_ref[...])
    residual_ref[:, : z.rim] += step * alpha * left[:, z.rim :]
    residual_ref[:, z.nodes - z.rim :] += step * alpha * right[:, : z.rim]


def on_device(
    rhs, potential, precond, shift, stiffness, cell_scale, conn, cell_count, projector, support_cell, support_atom,
    support_count, atom_matrix,
):
    count = lax.axis_size("dom")
    z = Sizes(count, rhs, conn, projector, atom_matrix)
    position = lax.axis_index("dom")
    pos = position.astype(jnp.int32).reshape(1)
    near = [(i, i ^ 1) for i in range(count)]
    far = [(i, j) for i in range(1, count - 1) for j in [i + 1 if i % 2 else i - 1]]

    def exchange(a, b):
        return lax.ppermute(a, "dom", near), lax.ppermute(b, "dom", far)

    def call(kernel, outs, scratch, scalars, *args, in_hbm=(), by_hand=False):
        space = pltpu.HBM if by_hand else pltpu.VMEM
        args = [pltpu.with_memory_space_constraint(x, space) for x in args]
        return pl.pallas_call(
            kernel,
            out_shape=[
                jax.ShapeDtypeStruct(s, d) if i in in_hbm else pltpu.VMEM(s, d) for i, (s, d) in enumerate(outs)
            ],
            in_specs=[SMEM] * len(scalars) + [pl.BlockSpec(memory_space=space)] * len(args),
            out_specs=[VMEM] * len(outs),
            scratch_shapes=[pltpu.VMEM(*s) if isinstance(s, tuple) else s for s in scratch],
            compiler_params=pltpu.CompilerParams(vmem_limit_bytes=16 * 1024 * 1024),
        )(*scalars, *args)

    flat_projector = projector.reshape(z.entries * z.channels, z.elem)
    cells = (z.slots * ROWS, z.width)
    window, reach, own = (z.vectors, z.window), (z.vectors, z.reach), (z.vectors, z.nodes)
    message = (z.devices, 4, LANES)
    square, entries = (z.width, z.width), (z.entries * ROWS, z.width)
    rim, more_rim = (z.vectors, 2 * z.rim), (z.vectors + 2, 2 * z.rim)
    acc = ((z.window // WIDE + BAND) * 2 * ROWS, WIDE)
    support_scratch = [
        ((3 * z.entries * ROWS, z.width), F32), ((2, z.rim_row - z.index_row, z.width), jnp.int32), (acc, F32),
    ]

    precond_lines = precond.reshape(-1, LANES)
    tile = (ROWS, LANES)
    first_message = (z.message, z.width)
    send_a, send_b, shift_tile = call(
            functools.partial(start_kernel, z),
            [(first_message, F32), (first_message, F32), (tile, F32)],
            [((2, z.vectors, z.rim), F32), ((2, z.rim // LANES, LANES), F32), (conn.shape, jnp.int32),
             (flat_projector.shape, F32), pltpu.SMEM(support_cell.shape, jnp.int32),
             pltpu.SMEM(support_atom.shape, jnp.int32), pltpu.SMEM(support_count.shape, jnp.int32),
             pltpu.SMEM(shift.shape, F32), pltpu.SemaphoreType.DMA((10,))],
            (pos,),
            support_cell, support_atom, support_count, shift, rhs, precond_lines, conn, flat_projector, by_hand=True,
    )
    ext = exchange(send_a, send_b)
    index, corner, table, weight = call(
        functools.partial(prepare_kernel, z),
        [((z.slots, 1, z.width), jnp.int32), ((1, LANES), jnp.int32), ((1, LANES), jnp.int32),
         ((z.slots * ROWS, LANES), F32)],
        [],
        (pos, cell_count, cell_scale, support_cell, support_atom, support_count),
        conn,
    )
    p, gamma, diag = call(
        functools.partial(own_kernel, z),
        [(reach, F32), ((1, LANES), F32), ((2, z.window), F32)],
        [],
        (),
        rhs, precond_lines, potential.reshape(-1, LANES),
    )
    (u,) = call(functools.partial(first_window_kernel, z), [(cells, F32)], [], (table,), p, index)
    p, sums, uw, pj, marked, beside = call(
        functools.partial(first_kernel, z),
        [(reach, F32), (message, F32), (cells, F32), (entries, F32), ((1, LANES), jnp.int32),
         ((1, LANES), jnp.int32)],
        [(cells, F32)],
        (table,),
        table, p, u, *ext, index, corner, weight, flat_projector, atom_matrix,
    )
    coupled = lax.all_to_all(sums, "dom", 0, 0)
    image, send_a, send_b, k_high, k_low = call(
        functools.partial(cells_kernel, z, True),
        [(window, F32), (more_rim, F32), (more_rim, F32), (square, BF16), (square, BF16)],
        [(cells, F32), (square, F32), (acc, F32)],
        (table,),
        index, corner, uw, stiffness, diag,
    )
    halo = exchange(send_a, send_b)
    (image,) = call(
        functools.partial(support_kernel, z, False),
        [(window, F32)],
        support_scratch,
        (marked,),
        coupled, coupled, index, beside, pj, *ext, image,
    )
    y, q, sums, e = call(
        functools.partial(second_kernel, z),
        [(window, F32), (reach, F32), (message, F32), (cells, F32)],
        [((2, z.window), F32), (cells, F32), (cells, F32)],
        (table,),
        image, p, diag, shift_tile, gamma, *halo, index, corner, weight, k_high, k_low, pj,
    )
    totals = lax.all_to_all(sums, "dom", 0, 0)
    image, send_a, send_b = call(
        functools.partial(cells_kernel, z, False), [(window, F32), (rim, F32), (rim, F32)], [(acc, F32)], (table,),
        index, corner, e,
    )
    halo = exchange(send_a, send_b)
    image, dots = call(
        functools.partial(support_kernel, z, True),
        [(window, F32), ((1, LANES), F32)],
        support_scratch,
        (marked,),
        totals, coupled, index, beside, pj, *ext, image,
    )
    return tuple(
        call(
            functools.partial(last_kernel, z),
            [(own, F32), (own, F32)],
            [],
            (table,),
            rhs, p, diag, shift_tile, y, q, image, dots, *halo, in_hbm=(0, 1),
        )
    )


def solution(mesh):
    placed = (
        P(None, "dom"),
        P("dom"),
        P("dom"),
        P(),
        P(),
        P("dom"),
        P("dom", None),
        P(),
        P("dom", None, None),
        P("dom"),
        P("dom"),
        P(),
        P("dom", None, None),
    )
    return jax.shard_map(
        on_device,
        mesh=mesh,
        in_specs=placed,
        out_specs=(P(None, "dom"), P(None, "dom")),
        check_vma=False,
    )
```

```python
import functools

import jax
import jax.numpy as jnp
from jax import lax
from jax.experimental import pallas as pl
from jax.experimental.pallas import tpu as pltpu
from jax.sharding import PartitionSpec as P

LANES = 128
ROWS = 8
BITS = 8
WIDE = 1 << BITS
NARROW = 7
CHAINS = 4
SPAN = 14
BAND = 8
BESIDE = 4
TOGETHER = 8
F32 = jnp.float32
BF16 = jnp.bfloat16
HIGHEST = lax.Precision.HIGHEST
NT = (((1,), (1,)), ((), ()))
VMEM = pl.BlockSpec(memory_space=pltpu.VMEM)
SMEM = pl.BlockSpec(memory_space=pltpu.SMEM)


def round_up(value, step):
    return -(-value // step) * step


class Sizes:
    def __init__(self, count, rhs, conn, projector, atom_matrix):
        self.devices = count
        self.vectors, self.nodes = rhs.shape
        self.slots, self.elem = conn.shape
        self.entries, self.channels = projector.shape[:2]
        self.owned = atom_matrix.shape[0]
        self.ghost = self.nodes // 16
        self.rim = round_up(self.ghost, 2 * LANES)
        self.shift = self.rim - self.ghost
        self.window = self.nodes + 2 * self.rim
        self.width = round_up(self.elem, LANES)
        self.tiles = self.width // LANES
        self.pairs = self.channels * self.vectors
        self.low, self.high, self.list = 0, self.slots, 2 * self.slots
        self.cell = 3 * self.slots
        self.owner, self.local = self.cell + self.entries, self.cell + 2 * self.entries
        self.position = self.cell + 3 * self.entries
        self.beside = 2 * self.slots
        assert self.position + 1 < LANES and self.beside + 4 * self.entries <= LANES
        self.reach = self.window + SPAN * LANES
        self.index_row = self.entries * self.channels
        self.rim_row = self.index_row + round_up(self.entries, ROWS)
        self.rim_pieces = -(-self.rim // self.width)
        self.message = self.rim_row + self.rim_pieces * ROWS
        assert self.elem + 3 <= self.width and self.entries % BESIDE == 0
        self.together = TOGETHER if self.slots % TOGETHER == 0 else 1
        assert self.vectors == ROWS and self.channels == ROWS and 2 * self.slots <= LANES
        assert self.nodes % WIDE == 0 and self.owned * self.pairs == LANES


def lane_gather(values, index):
    return jnp.take_along_axis(values, index, axis=1, mode="promise_in_bounds")


def iota(shape, dim):
    return lax.broadcasted_iota(jnp.int32, shape, dim)


def split(values):
    high = values.astype(BF16)
    return high, (values - high.astype(F32)).astype(BF16)


def lanes_by_vector(z, values):
    total = jnp.sum(values, axis=1, keepdims=True)
    spread = jnp.broadcast_to(total, (ROWS, LANES))
    return jnp.sum(jnp.where(iota((ROWS, LANES), 1) == iota((ROWS, LANES), 0), spread, 0.0), axis=0, keepdims=True)


def prepare_kernel(
    z, pos_ref, count_ref, scale_ref, cell_ref, atom_ref, scount_ref, conn_ref,
    index_ref, corner_ref, table_ref, weight_ref,
):
    position = pos_ref[0]
    line = iota((1, LANES), 1)
    corner = jnp.zeros((1, LANES), jnp.int32)
    index_ref[...] = jnp.zeros_like(index_ref)
    live = count_ref[position]
    for c in range(z.slots):
        row = conn_ref[c : c + 1, :] + z.shift
        index_ref[c, :, : z.elem] = row
        corner = jnp.where(line == c, row[:, :1], corner)
        corner = jnp.where(line == z.slots + c, row[:, z.elem - 1 :], corner)
        weight = jnp.where(c < live, scale_ref[c], 0.0)
        weight_ref[c * ROWS : (c + 1) * ROWS, :] = jnp.zeros((ROWS, LANES), F32) + weight
    corner_ref[...] = corner
    nodes = (conn_ref[...] + z.shift).astype(F32)
    place = iota(nodes.shape, 1)
    middle = (place > 0) & (place < z.elem - 1)
    low = jnp.min(jnp.where(middle, nodes, 1.0 * z.window), axis=1, keepdims=True)
    high = jnp.max(jnp.where(middle, nodes, 0.0), axis=1, keepdims=True)
    lane, cell = iota((z.slots, LANES), 1), iota((z.slots, LANES), 0)

    def as_row(column, first=0):
        return jnp.sum(jnp.where(lane == cell + first, column, 0.0), axis=0, keepdims=True)

    good = jnp.where((low >= z.rim) & (high < z.window - z.rim), 1.0, 0.0)
    good = jnp.broadcast_to(good, (z.slots, LANES))
    number = cell.astype(F32)
    before = jnp.sum(jnp.where(lane < cell, as_row(good), 0.0), axis=1, keepdims=True)
    at = jnp.where(good > 0.5, before, z.slots - 1.0 - (number - before))
    listed = jnp.where(lane.astype(F32) == at + z.list, number + z.slots * good, 0.0)
    table = as_row(low, z.low) + as_row(high, z.high) + jnp.sum(listed, axis=0, keepdims=True)
    table = table.astype(jnp.int32)
    for s in range(z.entries):
        atom = atom_ref[s]
        owner = atom // z.owned
        for first, fact in ((z.cell, cell_ref[s]), (z.owner, owner), (z.local, atom - owner * z.owned)):
            table = jnp.where(line == first + s, fact, table)
    table = jnp.where(line == z.position, position, table)
    table_ref[...] = jnp.where(line == z.position + 1, scount_ref[position], table)


def start_kernel(
    z, pos_ref, cell_hbm, atom_hbm, scount_hbm, shift_hbm, rhs_ref, precond_ref, conn_ref, projector_ref,
    send_a_ref, send_b_ref, shift_tile_ref, rhs_rim, precond_rim, conn_all, projector_all, cell_ref, atom_ref,
    scount_ref, shift_ref, sems,
):
    lines = z.rim // LANES
    moves = [
        (cell_hbm, cell_ref), (atom_hbm, atom_ref), (scount_hbm, scount_ref), (shift_hbm, shift_ref),
        (conn_ref, conn_all), (projector_ref, projector_all),
    ]
    for k, first in enumerate((0, z.nodes - z.rim)):
        moves.append((rhs_ref.at[:, pl.ds(first, z.rim)], rhs_rim.at[k]))
        moves.append((precond_ref.at[pl.ds(first // LANES, lines), :], precond_rim.at[k]))
    copies = [pltpu.make_async_copy(source, to, sems.at[k]) for k, (source, to) in enumerate(moves)]
    for copy in copies:
        copy.start()
    for copy in copies:
        copy.wait()
    row = iota((ROWS, LANES), 0)
    tile = jnp.zeros((ROWS, LANES), F32)
    for v in range(z.vectors):
        tile = jnp.where(row == v, shift_ref[v], tile)
    shift_tile_ref[...] = tile
    head, tail = (
        jnp.concatenate(
            [
                rhs_rim[k, :, i * LANES : (i + 1) * LANES] * precond_rim[k, i : i + 1, :]
                for i in range(lines)
            ],
            axis=1,
        )
        for k in range(2)
    )
    even = pos_ref[0] % 2 == 0
    sides = jnp.where(even, tail, head), jnp.where(even, head, tail)
    nodes = (conn_all[...] + z.shift).astype(F32)
    cell = iota(nodes.shape, 0)
    entry = iota((z.rim_row - z.index_row, z.width), 0)
    place = iota((z.rim_row - z.index_row, z.width), 1)
    rows = jnp.zeros((z.rim_row - z.index_row, z.width), F32)
    for s in range(z.entries):
        row = jnp.sum(jnp.where(cell == cell_ref[s], nodes, 0.0), axis=0, keepdims=True)
        row = jnp.concatenate([row, jnp.zeros((1, z.width - z.elem), F32)], axis=1)
        owner = atom_ref[s] // z.owned
        facts = owner, atom_ref[s] - owner * z.owned, (s < scount_ref[pos_ref[0]]).astype(jnp.int32)
        rows = jnp.where(entry == s, row, rows)
        for k, fact in enumerate(facts):
            rows = jnp.where((entry == s) & (place == z.elem + k), fact.astype(F32), rows)
    for ref, side in zip((send_a_ref, send_b_ref), sides):
        ref[...] = jnp.zeros_like(ref)
        ref[: z.index_row, : z.elem] = projector_all[...]
        ref[z.index_row : z.rim_row, :] = rows
        for k in range(z.rim_pieces):
            piece = side[:, k * z.width : min((k + 1) * z.width, z.rim)]
            ref[z.rim_row + k * ROWS : z.rim_row + (k + 1) * ROWS, : piece.shape[1]] = piece


def own_kernel(
    z, rhs_ref, precond_ref, potential_ref, p_ref, gamma_ref, diag_ref,
):
    diag_ref[...] = jnp.zeros_like(diag_ref)
    gamma = jnp.zeros((ROWS, LANES), F32)
    for i in range(z.nodes // LANES):
        at = slice(i * LANES, (i + 1) * LANES)
        to = slice(z.rim + i * LANES, z.rim + (i + 1) * LANES)
        value = rhs_ref[:, at]
        scale = precond_ref[i : i + 1, :]
        product = value * scale
        p_ref[:, to] = product
        gamma = gamma + product * value
        diag_ref[0:1, to] = scale
        diag_ref[1:2, to] = potential_ref[i : i + 1, :]
    p_ref[:, z.window :] = jnp.zeros((ROWS, z.reach - z.window), F32)
    gamma_ref[...] = lanes_by_vector(z, gamma)


def full_groups(z, table_ref):
    ends = [table_ref[0, z.list + g * z.together + z.together - 1] for g in range(z.slots // z.together)]
    return functools.reduce(jnp.add, [(end >= z.slots).astype(jnp.int32) for end in ends])


def split_window(z, window_ref, parts_ref):
    count = z.window // WIDE
    for h in range(count):
        value = window_ref[:, h * WIDE : (h + 1) * WIDE]
        rounded = value.astype(BF16).astype(F32)
        both = jnp.concatenate([rounded, value - rounded], axis=0).astype(BF16)
        parts_ref[h * 2 * ROWS : (h + 1) * 2 * ROWS, :] = both
    parts_ref[count * 2 * ROWS :, :] = jnp.zeros((BAND * 2 * ROWS, WIDE), BF16)


def gather_middle(z, groups, listed, table_ref, index_ref, window_ref, u_ref, parts_ref=None):
    total = z.window // LANES
    tile = (ROWS, LANES)
    pair = (2 * ROWS, LANES)
    sub = iota(pair, 0)
    lows = [(sub + n * 2 * ROWS).astype(jnp.int16) for n in range(WIDE // (2 * ROWS))]
    one, none = jnp.ones(pair, BF16), jnp.zeros(pair, BF16)

    def product_tile(c, k):
        start = jnp.minimum((table_ref[0, z.low + c] >> BITS) + k * BAND, z.window // WIDE)
        index = index_ref[c, :, (z.tiles - 1) * LANES : z.tiles * LANES]
        low = (jnp.broadcast_to(index, pair) & (WIDE - 1)).astype(jnp.int16)
        hot = jnp.concatenate([jnp.where(low == n, one, none) for n in lows], axis=0)
        rows = pl.ds(pl.multiple_of(start * 2 * ROWS, 2 * ROWS), BAND * 2 * ROWS)
        got = jnp.dot(parts_ref[rows, :], hot, preferred_element_type=F32)
        high = (jnp.broadcast_to(index, tile) >> BITS) - start
        value = jnp.zeros(tile, F32)
        for h in range(BAND):
            at = h * 2 * ROWS
            value = jnp.where(high == h, got[at : at + ROWS] + got[at + ROWS : at + 2 * ROWS], value)
        return value

    def some_cells(g, _):
        cells = [g * z.together + i for i in range(z.together)]
        if listed:
            cells = [table_ref[0, z.list + c] for c in cells]
            cells = [jnp.where(c >= z.slots, c - z.slots, c) for c in cells]
        starts = [table_ref[0, z.low + c] >> 7 for c in cells]
        ends = [table_ref[0, z.high + c] >> 7 for c in cells]
        passes = functools.reduce(jnp.maximum, [(e - s) // SPAN + 1 for s, e in zip(starts, ends)])

        def one_pass(k, values):
            values = list(values)
            for i, c in enumerate(cells):
                start = jnp.minimum(starts[i] + k * SPAN, total)
                for t in range(z.tiles):
                    if parts_ref is not None and t == z.tiles - 1:
                        values[i * z.tiles + t] += product_tile(c, k)
                        continue
                    index = jnp.broadcast_to(index_ref[c, :, t * LANES : (t + 1) * LANES], tile)
                    low, high = index & (LANES - 1), (index >> 7) - start
                    value = values[i * z.tiles + t]
                    for h in range(SPAN):
                        at = pl.ds(pl.multiple_of((start + h) * LANES, LANES), LANES)
                        value = jnp.where(high == h, lane_gather(window_ref[:, at], low), value)
                    values[i * z.tiles + t] = value
            return tuple(values)

        values = lax.fori_loop(0, passes, one_pass, (jnp.zeros(tile, F32),) * (z.together * z.tiles))
        for i, c in enumerate(cells):
            rows = pl.ds(pl.multiple_of(c * ROWS, ROWS), ROWS)
            for t in range(z.tiles):
                u_ref[rows, t * LANES : (t + 1) * LANES] = values[i * z.tiles + t]
        return 0

    lax.fori_loop(*groups, some_cells, 0)


def gather_corners(z, corner_ref, window_ref, weight_ref, u_ref, uw_ref):
    tile = (ROWS, LANES)
    corner = jnp.broadcast_to(corner_ref[...], tile)
    low, high = corner & (LANES - 1), corner >> 7
    chains = [jnp.zeros(tile, F32)] * CHAINS
    for h in range(z.window // LANES):
        got = lane_gather(window_ref[:, h * LANES : (h + 1) * LANES], low)
        chains[h % CHAINS] = jnp.where(high == h, got, chains[h % CHAINS])
    corners = functools.reduce(jnp.add, chains)
    lane = iota(tile, 1)
    last = (z.elem - 1) % LANES
    for c in range(z.slots):
        rows = slice(c * ROWS, (c + 1) * ROWS)
        weight = weight_ref[rows, :]
        for t in range(z.tiles):
            lanes = slice(t * LANES, (t + 1) * LANES)
            value = u_ref[rows, lanes]
            if t == 0:
                value = jnp.where(lane == 0, corners[:, c : c + 1], value)
            if t == z.tiles - 1:
                value = jnp.where(lane == last, corners[:, z.slots + c : z.slots + c + 1], value)
            u_ref[rows, lanes] = value
            uw_ref[rows, lanes] = value * weight


def stiffness_product(k_high_ref, k_low_ref, uw_ref, e_ref):
    k_high, k_low = k_high_ref[...], k_low_ref[...]
    u_high, u_low = split(uw_ref[...])
    dot = functools.partial(lax.dot_general, dimension_numbers=NT, preferred_element_type=F32)
    e_ref[...] = dot(u_high, k_high) + (dot(u_high, k_low) + dot(u_low, k_high))


def entry_facts(z, table_ref, s):
    return table_ref[0, z.owner + s], table_ref[0, z.local + s], s < table_ref[0, z.position + 1]


def contributions(z, table_ref, pj_ref, u_ref):
    values = [u_ref[pl.ds(pl.multiple_of(table_ref[0, z.cell + s] * ROWS, ROWS), ROWS), :] for s in range(z.entries)]
    sums = lax.dot_general(
        pj_ref[...], jnp.concatenate(values, axis=0), NT, precision=HIGHEST, preferred_element_type=F32
    )
    sums = jnp.concatenate([sums, jnp.zeros((sums.shape[0], LANES - sums.shape[1]), F32)], axis=1)
    lane, row = iota((ROWS, LANES), 1), iota((ROWS, LANES), 0)
    position = table_ref[0, z.position]
    parts = [jnp.zeros((ROWS, LANES), F32)] * 3
    for s in range(z.entries):
        owner, local, alive = entry_facts(z, table_ref, s)
        got = lane_gather(sums[s * ROWS : (s + 1) * ROWS], s * ROWS + lane % ROWS)
        here = (lane // ROWS % ROWS == row) & (lane // z.pairs == local) & alive
        for k in range(3):
            parts[k] = parts[k] + jnp.where(here & (owner == position - 1 + k), got, 0.0)
    return [jnp.sum(part, axis=0, keepdims=True) for part in parts]


def sides(position, near, far):
    even = position % 2 == 0
    return jnp.where(even, far, near), jnp.where(even, near, far)


def first_window_kernel(z, table_ref, p_ref, index_ref, u_ref):
    groups = 0, full_groups(z, table_ref)
    gather_middle(z, groups, True, table_ref, index_ref, p_ref, u_ref)


def first_kernel(
    z, table_ref, p_in_ref, u_in_ref, halo_a_ref, halo_b_ref, index_ref, corner_ref, weight_ref,
    projector_ref, coupling_ref, p_ref, out_ref, uw_ref, pj_ref, beside_ref, u_ref,
):
    rows = slice(z.index_row, z.index_row + z.entries)
    line = iota((1, LANES), 1)
    left, right = sides(table_ref[0, z.position], halo_a_ref[rows, :], halo_b_ref[rows, :])
    beside = corner_ref[...]
    for k, (side, move) in enumerate(((left, -z.nodes), (right, z.nodes))):
        side = side.astype(jnp.int32) + move
        for s in range(z.entries):
            lane = z.beside + 2 * z.entries * k + s
            beside = jnp.where(line == lane, side[s : s + 1, :1], beside)
            beside = jnp.where(line == lane + z.entries, side[s : s + 1, z.elem - 1 : z.elem], beside)
    beside_ref[...] = beside
    own = slice(z.rim, z.rim + z.nodes)
    for k in range(z.rim_pieces):
        rows = slice(z.rim_row + k * ROWS, z.rim_row + (k + 1) * ROWS)
        at, to = k * z.width, min((k + 1) * z.width, z.rim)
        left, right = sides(table_ref[0, z.position], halo_a_ref[rows, : to - at], halo_b_ref[rows, : to - at])
        p_ref[:, at:to] = left
        p_ref[:, z.rim + z.nodes + at : z.rim + z.nodes + to] = right
    p_ref[:, own] = p_in_ref[:, own]
    p_ref[:, z.window :] = p_in_ref[:, z.window :]
    u_ref[...] = u_in_ref[...]
    pj_ref[...] = jnp.zeros_like(pj_ref)
    pj_ref[:, : z.elem] = projector_ref[...]
    groups = full_groups(z, table_ref), z.slots // z.together
    gather_middle(z, groups, True, table_ref, index_ref, p_ref, u_ref)
    gather_corners(z, corner_ref, p_ref, weight_ref, u_ref, uw_ref)
    parts = contributions(z, table_ref, pj_ref, u_ref)
    small_lane, small_row = iota((ROWS, LANES), 1), iota((ROWS, LANES), 0)
    matrices = jnp.zeros((ROWS, LANES), F32)
    for atom in range(z.owned):
        block = jnp.concatenate([coupling_ref[atom], jnp.zeros((ROWS, LANES - z.channels), F32)], axis=1)
        got = lane_gather(block, small_lane % ROWS)
        matrices = jnp.where(small_lane // ROWS == atom * ROWS + small_row, got, matrices)
    message = jnp.concatenate(parts + [jnp.sum(matrices, axis=0, keepdims=True)], axis=0)
    for d in range(z.devices):
        out_ref[d] = message


def second_kernel(
    z, table_ref, image_ref, p_ref, diag_in_ref, shift_ref, gamma_ref, halo_a_ref, halo_b_ref,
    index_ref, corner_ref, weight_ref, k_high_ref, k_low_ref, pj_ref, y_ref, q_ref, out_ref, e_ref, diag_ref, u_ref, uw_ref,
    parts_ref,
):
    left, right = sides(table_ref[0, z.position], halo_a_ref[...], halo_b_ref[...])
    own = slice(z.rim, z.rim + z.nodes)
    diag_ref[:, own] = diag_in_ref[:, own]
    diag_ref[:, : z.rim] = left[ROWS : ROWS + 2, : z.rim]
    diag_ref[:, z.rim + z.nodes :] = right[ROWS : ROWS + 2, z.rim :]
    y_ref[...] = image_ref[...] + (diag_ref[1:2, :] + shift_ref[:, :1]) * p_ref[:, : z.window]
    y_ref[:, : 2 * z.rim] += left[:ROWS]
    y_ref[:, z.window - 2 * z.rim :] += right[:ROWS]
    q_ref[:, : z.window] = y_ref[...] * diag_ref[0:1, :]
    q_ref[:, z.window :] = jnp.zeros((ROWS, z.reach - z.window), F32)
    y, q = y_ref[:, own], q_ref[:, own]
    dots = [
        gamma_ref[...],
        lanes_by_vector(z, y * p_ref[:, own]),
        lanes_by_vector(z, y * q),
    ]
    energy = jnp.sum(q * q * (diag_ref[1:2, own] + shift_ref[:, :1]), axis=1, keepdims=True)
    groups = 0, z.slots // z.together
    split_window(z, q_ref, parts_ref)
    gather_middle(z, groups, False, table_ref, index_ref, q_ref, u_ref, parts_ref)
    gather_corners(z, corner_ref, q_ref, weight_ref, u_ref, uw_ref)
    parts = contributions(z, table_ref, pj_ref, u_ref)
    stiffness_product(k_high_ref, k_low_ref, uw_ref, e_ref)
    elements = jnp.zeros((ROWS, z.width), F32)
    for c in range(z.slots):
        rows = slice(c * ROWS, (c + 1) * ROWS)
        elements = elements + u_ref[rows, :] * e_ref[rows, :]
    energy = energy + jnp.sum(elements, axis=1, keepdims=True)
    dots.append(lanes_by_vector(z, energy))
    line = dots[0]
    for k in range(1, len(dots)):
        line = line + pltpu.roll(dots[k], k * ROWS, 1)
    message = jnp.concatenate(parts + [line], axis=0)
    for d in range(z.devices):
        out_ref[d] = message


def band_of(bits):
    return BAND if bits == BITS else SPAN


def acc_shape(z, bits):
    return ((z.window >> bits) + band_of(bits)) * 2 * ROWS, 1 << bits


class Scatter:
    def __init__(self, z, bits, table_ref, index_ref, corner_ref, acc_ref):
        self.bits, self.wide, self.band = bits, 1 << bits, band_of(bits)
        self.z, self.index_ref, self.corner_ref, self.acc_ref = z, index_ref, corner_ref, acc_ref
        self.table_ref = table_ref
        self.groups = z.window // self.wide
        self.pair = (2 * ROWS, LANES)
        sub = iota(self.pair, 0)
        self.lows = [(sub + k * 2 * ROWS).astype(jnp.int16) for k in range(self.wide // (2 * ROWS))]
        self.one, self.none = jnp.ones(self.pair, BF16), jnp.zeros(self.pair, BF16)
        self.lane = iota((ROWS, LANES), 1)
        self.end = (z.elem - 1) % LANES

    def two_parts(self, value):
        rounded = value.astype(BF16).astype(F32)
        return jnp.concatenate([rounded, value - rounded], axis=0).astype(BF16)

    def hot_rows(self, index):
        low = (index & (self.wide - 1)).astype(jnp.int16)
        return jnp.concatenate([jnp.where(low == k, self.one, self.none) for k in self.lows], axis=0)

    def masked(self, high, both, rows):
        high = high.astype(jnp.int16)
        return jnp.concatenate([jnp.where(high == jnp.int16(h), both, self.none) for h in range(rows)], axis=0)

    def product(self, lhs, hot):
        return lax.dot_general(lhs, hot, NT, preferred_element_type=F32)

    def start(self, sources, beside=()):
        z = self.z
        corners = jnp.zeros((ROWS, LANES), F32)
        at = (z.tiles - 1) * LANES + self.end
        for cell, values in sources:
            corners = corners + jnp.where(self.lane == cell, values[:, 0:1], 0.0)
            corners = corners + jnp.where(self.lane == z.slots + cell, values[:, at : at + 1], 0.0)
        for s, values in enumerate(beside):
            lane = z.beside + s + s // z.entries * z.entries
            corners = jnp.where(self.lane == lane, values[:, 0:1], corners)
            corners = jnp.where(self.lane == lane + z.entries, values[:, at : at + 1], corners)
        index = jnp.broadcast_to(self.corner_ref[...], self.pair)
        rows = self.groups * 2 * ROWS
        self.acc_ref[:rows, :] = self.product(
            self.masked(index >> self.bits, self.two_parts(corners), self.groups), self.hot_rows(index)
        )
        self.acc_ref[rows:, :] = jnp.zeros((self.band * 2 * ROWS, self.wide), F32)

    def add(self, cells, value_of):
        z = self.z
        starts = [self.table_ref[0, z.low + c] >> self.bits for c in cells]
        ends = [self.table_ref[0, z.high + c] >> self.bits for c in cells]
        passes = functools.reduce(jnp.maximum, [(e - s) // self.band + 1 for s, e in zip(starts, ends)])

        def one_pass(k, _):
            for i, c in enumerate(cells):
                start = jnp.minimum(starts[i] + k * self.band, self.groups)
                lhs, hot = [], []
                for t in range(z.tiles):
                    index = jnp.broadcast_to(self.index_ref[c, :, t * LANES : (t + 1) * LANES], self.pair)
                    value = value_of(i, t)
                    if t == 0:
                        value = jnp.where(self.lane == 0, 0.0, value)
                    if t == z.tiles - 1:
                        value = jnp.where(self.lane == self.end, 0.0, value)
                    lhs.append(self.masked((index >> self.bits) - start, self.two_parts(value), self.band))
                    hot.append(self.hot_rows(index))
                to = pl.ds(pl.multiple_of(start * 2 * ROWS, 2 * ROWS), self.band * 2 * ROWS)
                self.acc_ref[to, :] += self.product(jnp.concatenate(lhs, axis=1), jnp.concatenate(hot, axis=1))
            return 0

        lax.fori_loop(0, passes, one_pass, 0)

    def add_rows(self, index, values, first, rows):
        lhs, hot = [], []
        for t in range(values.shape[1] // LANES):
            lanes = slice(t * LANES, (t + 1) * LANES)
            at = jnp.broadcast_to(index[:, lanes], self.pair)
            lhs.append(self.masked(at >> self.bits, self.two_parts(values[:, lanes]), rows))
            hot.append(self.hot_rows(at))
        to = slice(first * 2 * ROWS, (first + rows) * 2 * ROWS)
        self.acc_ref[to, :] += self.product(jnp.concatenate(lhs, axis=1), jnp.concatenate(hot, axis=1))

    def result(self, h):
        at = h * 2 * ROWS
        return self.acc_ref[at : at + ROWS] + self.acc_ref[at + ROWS : at + 2 * ROWS]


def cells_kernel(z, multiply, table_ref, index_ref, corner_ref, *refs):
    if multiply:
        uw_ref, stiffness_ref, diag_ref, image_ref, send_a_ref, send_b_ref, k_high_ref, k_low_ref, *refs = refs
        e_ref, k_ref, acc_ref = refs
        k_ref[...] = jnp.zeros_like(k_ref)
        k_ref[: z.elem, : z.elem] = stiffness_ref[...]
        k_high_ref[...], k_low_ref[...] = split(k_ref[...])
        stiffness_product(k_high_ref, k_low_ref, uw_ref, e_ref)
    else:
        e_ref, image_ref, send_a_ref, send_b_ref, acc_ref = refs
    scatter = Scatter(z, BITS, table_ref, index_ref, corner_ref, acc_ref)
    scatter.start([(c, e_ref[c * ROWS : (c + 1) * ROWS, :]) for c in range(z.slots)])

    def some_cells(g, _):
        cells = [g * z.together + i for i in range(z.together)]

        def value_of(i, t):
            rows = pl.ds(pl.multiple_of(cells[i] * ROWS, ROWS), ROWS)
            return e_ref[rows, t * LANES : (t + 1) * LANES]

        scatter.add(cells, value_of)
        return 0

    lax.fori_loop(0, z.slots // z.together, some_cells, 0)
    for h in range(scatter.groups):
        image_ref[:, h * WIDE : (h + 1) * WIDE] = scatter.result(h)
    even = table_ref[0, z.position] % 2 == 0
    ends = [slice(0, 2 * z.rim), slice(z.window - 2 * z.rim, z.window)]
    for source_ref, rows in ((image_ref, slice(0, ROWS)),) + (((diag_ref, slice(ROWS, ROWS + 2)),) if multiply else ()):
        low_rim, high_rim = (source_ref[:, end] for end in ends)
        send_a_ref[rows, :] = jnp.where(even, high_rim, low_rim)
        send_b_ref[rows, :] = jnp.where(even, low_rim, high_rim)


def support_kernel(
    z, last, table_ref, sums_ref, coupling_ref, index_ref, corner_ref, pj_ref, ext_a_ref, ext_b_ref,
    cells_ref, *refs,
):
    if last:
        image_ref, dots_ref, support_ref, nodes_ref, acc_ref = refs
    else:
        image_ref, support_ref, nodes_ref, acc_ref = refs
    position = table_ref[0, z.position]
    wanted = (
        pltpu.roll(sums_ref[:, 0, :], z.devices - 1, 0) + sums_ref[:, 1, :] + pltpu.roll(sums_ref[:, 2, :], 1, 0)
    )
    coupling = coupling_ref[:, 3, :]
    shape = (z.devices, LANES)
    lane = iota(shape, 1)
    term = jnp.zeros(shape, F32)
    for j in range(z.channels):
        matrix = lane_gather(coupling, lane // ROWS * ROWS + j)
        vector = lane_gather(wanted, lane // z.pairs * z.pairs + j * ROWS + lane % ROWS)
        term = term + matrix * vector
    if last:
        energy = jnp.sum(term * wanted, axis=0, keepdims=True)
        energy = jnp.broadcast_to(energy, (ROWS, LANES))
        step = ROWS
        while step < LANES:
            energy = energy + pltpu.roll(energy, step, 1)
            step *= 2
        line = iota((1, LANES), 1)
        dots_ref[...] = jnp.sum(sums_ref[:, 3, :], axis=0, keepdims=True) + jnp.where(
            line // ROWS == 3, energy[0:1], 0.0
        )
    block = iota(shape, 0)
    small_lane, small_row = iota((ROWS, LANES), 1), iota((ROWS, LANES), 0)

    def values(facts, projectors):
        spread = []
        for s, (owner, local, alive) in enumerate(facts):
            mine = jnp.sum(jnp.where(block == owner, term, 0.0), axis=0, keepdims=True)
            got = lane_gather(
                jnp.broadcast_to(mine, (ROWS, LANES)), local * z.pairs + small_lane % ROWS * ROWS + small_row
            )
            spread.append(jnp.where((small_lane // ROWS == s) & alive, got, 0.0)[:, : z.entries * ROWS])
        return jnp.dot(
            jnp.concatenate(spread, axis=0), projectors, precision=HIGHEST, preferred_element_type=F32
        )

    count = z.entries * ROWS
    support_ref[:count, :] = values([entry_facts(z, table_ref, s) for s in range(z.entries)], pj_ref[...])
    used = slice(0, z.rim_row)
    for side, ext in enumerate(sides(position, ext_a_ref[used, :], ext_b_ref[used, :])):
        nodes = ext[z.index_row :].astype(jnp.int32)
        facts = []
        for s in range(z.entries):
            fact = [jnp.broadcast_to(nodes[s : s + 1, z.elem + k : z.elem + k + 1], (1, LANES)) for k in range(3)]
            facts.append((fact[0], fact[1], fact[2] > 0))
        projectors = jnp.where(iota((z.index_row, z.width), 1) < z.elem, ext[: z.index_row], 0.0)
        support_ref[(side + 1) * count : (side + 2) * count, :] = values(facts, projectors)
        nodes_ref[side] = nodes
    scatter = Scatter(z, NARROW, table_ref, index_ref, corner_ref, acc_ref)
    cells = [table_ref[0, z.cell + s] for s in range(z.entries)]
    blocks = [support_ref[s * ROWS : (s + 1) * ROWS, :] for s in range(3 * z.entries)]
    scatter.start(list(zip(cells, blocks)), blocks[z.entries :])
    for first in range(0, z.entries, z.together):
        some = cells[first : first + z.together]

        def value_of(i, t):
            s = first + i
            return support_ref[s * ROWS : (s + 1) * ROWS, t * LANES : (t + 1) * LANES]

        scatter.add(some, value_of)
    shared = 2 * z.rim // scatter.wide
    place = iota((ROWS, z.width), 1)
    middle = (place > 0) & (place < z.elem - 1)
    for side, (first, offset) in enumerate(((0, z.window - 2 * z.rim), (scatter.groups - shared, 0))):
        for s in range(0, z.entries, BESIDE):
            some = range(s, s + BESIDE)
            base = (side + 1) * z.entries
            value = [jnp.where(middle, support_ref[(base + i) * ROWS : (base + i + 1) * ROWS, :], 0.0) for i in some]
            index = [nodes_ref[side, i : i + 1, :] - offset for i in some]
            scatter.add_rows(jnp.concatenate(index, axis=1), jnp.concatenate(value, axis=1), first, shared)
    for h in range(scatter.groups):
        at = slice(h * scatter.wide, (h + 1) * scatter.wide)
        image_ref[:, at] = cells_ref[:, at] + scatter.result(h)


def last_kernel(
    z, table_ref, rhs_ref, p_ref, diag_ref, shift_ref, y_ref, q_ref, image_ref, dots_ref, halo_a_ref, halo_b_ref,
    solution_ref, residual_ref,
):
    own = slice(z.rim, z.rim + z.nodes)
    lane, row = iota((ROWS, LANES), 1), iota((ROWS, LANES), 0)
    line = jnp.broadcast_to(dots_ref[...], (ROWS, LANES))

    def column(k):
        return jnp.sum(jnp.where(lane == k * ROWS + row, line, 0.0), axis=1, keepdims=True)

    gamma, py, qy, qq = (column(k) for k in range(4))
    alpha = gamma / py
    fresh = gamma - 2.0 * alpha * py + alpha * alpha * qy
    beta = fresh / gamma
    more = 1.0 + beta
    step = fresh / (more * more * py - 2.0 * more * alpha * qy + alpha * alpha * qq)
    p, q, y = p_ref[:, own], q_ref[:, own], y_ref[:, own]
    second = image_ref[:, own] + (diag_ref[1:2, own] + shift_ref[:, :1]) * q
    search = (p - alpha * q) + beta * p
    solution_ref[...] = alpha * p + step * search
    residual_ref[...] = (rhs_ref[...] - alpha * y) - step * (more * y - alpha * second)
    left, right = sides(table_ref[0, z.position], halo_a_ref[...], halo_b_ref[...])
    residual_ref[:, : z.rim] += step * alpha * left[:, z.rim :]
    residual_ref[:, z.nodes - z.rim :] += step * alpha * right[:, : z.rim]


def on_device(
    rhs, potential, precond, shift, stiffness, cell_scale, conn, cell_count, projector, support_cell, support_atom,
    support_count, atom_matrix,
):
    count = lax.axis_size("dom")
    z = Sizes(count, rhs, conn, projector, atom_matrix)
    position = lax.axis_index("dom")
    pos = position.astype(jnp.int32).reshape(1)
    near = [(i, i ^ 1) for i in range(count)]
    far = [(i, j) for i in range(1, count - 1) for j in [i + 1 if i % 2 else i - 1]]

    def exchange(a, b):
        return lax.ppermute(a, "dom", near), lax.ppermute(b, "dom", far)

    def call(kernel, outs, scratch, scalars, *args, in_hbm=(), by_hand=False):
        space = pltpu.HBM if by_hand else pltpu.VMEM
        args = [pltpu.with_memory_space_constraint(x, space) for x in args]
        return pl.pallas_call(
            kernel,
            out_shape=[
                jax.ShapeDtypeStruct(s, d) if i in in_hbm else pltpu.VMEM(s, d) for i, (s, d) in enumerate(outs)
            ],
            in_specs=[SMEM] * len(scalars) + [pl.BlockSpec(memory_space=space)] * len(args),
            out_specs=[VMEM] * len(outs),
            scratch_shapes=[pltpu.VMEM(*s) if isinstance(s, tuple) else s for s in scratch],
            compiler_params=pltpu.CompilerParams(vmem_limit_bytes=16 * 1024 * 1024),
        )(*scalars, *args)

    flat_projector = projector.reshape(z.entries * z.channels, z.elem)
    cells = (z.slots * ROWS, z.width)
    window, reach, own = (z.vectors, z.window), (z.vectors, z.reach), (z.vectors, z.nodes)
    message = (z.devices, 4, LANES)
    square, entries = (z.width, z.width), (z.entries * ROWS, z.width)
    rim, more_rim = (z.vectors, 2 * z.rim), (z.vectors + 2, 2 * z.rim)
    acc = acc_shape(z, BITS)
    support_scratch = [
        ((3 * z.entries * ROWS, z.width), F32), ((2, z.rim_row - z.index_row, z.width), jnp.int32),
        (acc_shape(z, NARROW), F32),
    ]

    precond_lines = precond.reshape(-1, LANES)
    tile = (ROWS, LANES)
    first_message = (z.message, z.width)
    send_a, send_b, shift_tile = call(
            functools.partial(start_kernel, z),
            [(first_message, F32), (first_message, F32), (tile, F32)],
            [((2, z.vectors, z.rim), F32), ((2, z.rim // LANES, LANES), F32), (conn.shape, jnp.int32),
             (flat_projector.shape, F32), pltpu.SMEM(support_cell.shape, jnp.int32),
             pltpu.SMEM(support_atom.shape, jnp.int32), pltpu.SMEM(support_count.shape, jnp.int32),
             pltpu.SMEM(shift.shape, F32), pltpu.SemaphoreType.DMA((10,))],
            (pos,),
            support_cell, support_atom, support_count, shift, rhs, precond_lines, conn, flat_projector, by_hand=True,
    )
    ext = exchange(send_a, send_b)
    index, corner, table, weight = call(
        functools.partial(prepare_kernel, z),
        [((z.slots, 1, z.width), jnp.int32), ((1, LANES), jnp.int32), ((1, LANES), jnp.int32),
         ((z.slots * ROWS, LANES), F32)],
        [],
        (pos, cell_count, cell_scale, support_cell, support_atom, support_count),
        conn,
    )
    p, gamma, diag = call(
        functools.partial(own_kernel, z),
        [(reach, F32), ((1, LANES), F32), ((2, z.window), F32)],
        [],
        (),
        rhs, precond_lines, potential.reshape(-1, LANES),
    )
    (u,) = call(functools.partial(first_window_kernel, z), [(cells, F32)], [], (table,), p, index)
    p, sums, uw, pj, beside = call(
        functools.partial(first_kernel, z),
        [(reach, F32), (message, F32), (cells, F32), (entries, F32), ((1, LANES), jnp.int32)],
        [(cells, F32)],
        (table,),
        p, u, *ext, index, corner, weight, flat_projector, atom_matrix,
    )
    coupled = lax.all_to_all(sums, "dom", 0, 0)
    image, send_a, send_b, k_high, k_low = call(
        functools.partial(cells_kernel, z, True),
        [(window, F32), (more_rim, F32), (more_rim, F32), (square, BF16), (square, BF16)],
        [(cells, F32), (square, F32), (acc, F32)],
        (table,),
        index, corner, uw, stiffness, diag,
    )
    halo = exchange(send_a, send_b)
    (image,) = call(
        functools.partial(support_kernel, z, False),
        [(window, F32)],
        support_scratch,
        (table,),
        coupled, coupled, index, beside, pj, *ext, image,
    )
    y, q, sums, e = call(
        functools.partial(second_kernel, z),
        [(window, F32), (reach, F32), (message, F32), (cells, F32)],
        [((2, z.window), F32), (cells, F32), (cells, F32), (acc, BF16)],
        (table,),
        image, p, diag, shift_tile, gamma, *halo, index, corner, weight, k_high, k_low, pj,
    )
    totals = lax.all_to_all(sums, "dom", 0, 0)
    image, send_a, send_b = call(
        functools.partial(cells_kernel, z, False), [(window, F32), (rim, F32), (rim, F32)], [(acc, F32)], (table,),
        index, corner, e,
    )
    halo = exchange(send_a, send_b)
    image, dots = call(
        functools.partial(support_kernel, z, True),
        [(window, F32), ((1, LANES), F32)],
        support_scratch,
        (table,),
        totals, coupled, index, beside, pj, *ext, image,
    )
    return tuple(
        call(
            functools.partial(last_kernel, z),
            [(own, F32), (own, F32)],
            [],
            (table,),
            rhs, p, diag, shift_tile, y, q, image, dots, *halo, in_hbm=(0, 1),
        )
    )


def solution(mesh):
    placed = (
        P(None, "dom"),
        P("dom"),
        P("dom"),
        P(),
        P(),
        P("dom"),
        P("dom", None),
        P(),
        P("dom", None, None),
        P("dom"),
        P("dom"),
        P(),
        P("dom", None, None),
    )
    return jax.shard_map(
        on_device,
        mesh=mesh,
        in_specs=placed,
        out_specs=(P(None, "dom"), P(None, "dom")),
        check_vma=False,
    )
```

```python
import functools

import jax
import jax.numpy as jnp
from jax import lax
from jax.experimental import pallas as pl
from jax.experimental.pallas import tpu as pltpu
from jax.sharding import PartitionSpec as P

LANES = 128
ROWS = 8
BITS = 7
WIDE = 1 << BITS
NARROW = 7
CHAINS = 4
SPAN = 14
BAND = 14
BESIDE = 4
TOGETHER = 8
MANY = 32
F32 = jnp.float32
BF16 = jnp.bfloat16
HIGHEST = lax.Precision.HIGHEST
NT = (((1,), (1,)), ((), ()))
VMEM = pl.BlockSpec(memory_space=pltpu.VMEM)
SMEM = pl.BlockSpec(memory_space=pltpu.SMEM)


def round_up(value, step):
    return -(-value // step) * step


class Sizes:
    def __init__(self, count, rhs, conn, projector, atom_matrix):
        self.devices = count
        self.vectors, self.nodes = rhs.shape
        self.slots, self.elem = conn.shape
        self.entries, self.channels = projector.shape[:2]
        self.owned = atom_matrix.shape[0]
        self.ghost = self.nodes // 16
        self.rim = round_up(self.ghost, 2 * LANES)
        self.shift = self.rim - self.ghost
        self.window = self.nodes + 2 * self.rim
        self.width = round_up(self.elem, LANES)
        self.tiles = self.width // LANES
        self.pairs = self.channels * self.vectors
        self.low, self.high, self.list = 0, self.slots, 2 * self.slots
        self.cell = 3 * self.slots
        self.owner, self.local = self.cell + self.entries, self.cell + 2 * self.entries
        self.position = self.cell + 3 * self.entries
        self.beside = 2 * self.slots
        assert self.position + 1 < LANES and self.beside + 4 * self.entries <= LANES
        self.reach = self.window + SPAN * LANES
        self.index_row = self.entries * self.channels
        self.rim_row = self.index_row + round_up(self.entries, ROWS)
        self.rim_pieces = -(-self.rim // self.width)
        self.message = self.rim_row + self.rim_pieces * ROWS
        assert self.elem + 3 <= self.width and self.entries % BESIDE == 0
        self.together = TOGETHER if self.slots % TOGETHER == 0 else 1
        self.many = MANY if self.slots % MANY == 0 else 1
        assert self.vectors == ROWS and self.channels == ROWS and 2 * self.slots <= LANES
        assert self.nodes % WIDE == 0 and self.owned * self.pairs == LANES


def lane_gather(values, index):
    return jnp.take_along_axis(values, index, axis=1, mode="promise_in_bounds")


def iota(shape, dim):
    return lax.broadcasted_iota(jnp.int32, shape, dim)


def split(values):
    high = values.astype(BF16)
    return high, (values - high.astype(F32)).astype(BF16)


def lanes_by_vector(z, values):
    total = jnp.sum(values, axis=1, keepdims=True)
    spread = jnp.broadcast_to(total, (ROWS, LANES))
    return jnp.sum(jnp.where(iota((ROWS, LANES), 1) == iota((ROWS, LANES), 0), spread, 0.0), axis=0, keepdims=True)


def prepare_kernel(
    z, pos_ref, count_ref, scale_ref, cell_ref, atom_ref, scount_ref, conn_ref,
    index_ref, corner_ref, table_ref, weight_ref,
):
    position = pos_ref[0]
    line = iota((1, LANES), 1)
    corner = jnp.zeros((1, LANES), jnp.int32)
    index_ref[...] = jnp.zeros_like(index_ref)
    live = count_ref[position]
    for c in range(z.slots):
        row = conn_ref[c : c + 1, :] + z.shift
        index_ref[c, :, : z.elem] = row
        corner = jnp.where(line == c, row[:, :1], corner)
        corner = jnp.where(line == z.slots + c, row[:, z.elem - 1 :], corner)
        weight = jnp.where(c < live, scale_ref[c], 0.0)
        weight_ref[c * ROWS : (c + 1) * ROWS, :] = jnp.zeros((ROWS, LANES), F32) + weight
    corner_ref[...] = corner
    nodes = (conn_ref[...] + z.shift).astype(F32)
    place = iota(nodes.shape, 1)
    middle = (place > 0) & (place < z.elem - 1)
    low = jnp.min(jnp.where(middle, nodes, 1.0 * z.window), axis=1, keepdims=True)
    high = jnp.max(jnp.where(middle, nodes, 0.0), axis=1, keepdims=True)
    lane, cell = iota((z.slots, LANES), 1), iota((z.slots, LANES), 0)

    def as_row(column, first=0):
        return jnp.sum(jnp.where(lane == cell + first, column, 0.0), axis=0, keepdims=True)

    good = jnp.where((low >= z.rim) & (high < z.window - z.rim), 1.0, 0.0)
    good = jnp.broadcast_to(good, (z.slots, LANES))
    number = cell.astype(F32)
    before = jnp.sum(jnp.where(lane < cell, as_row(good), 0.0), axis=1, keepdims=True)
    at = jnp.where(good > 0.5, before, z.slots - 1.0 - (number - before))
    listed = jnp.where(lane.astype(F32) == at + z.list, number + z.slots * good, 0.0)
    table = as_row(low, z.low) + as_row(high, z.high) + jnp.sum(listed, axis=0, keepdims=True)
    table = table.astype(jnp.int32)
    for s in range(z.entries):
        atom = atom_ref[s]
        owner = atom // z.owned
        for first, fact in ((z.cell, cell_ref[s]), (z.owner, owner), (z.local, atom - owner * z.owned)):
            table = jnp.where(line == first + s, fact, table)
    table = jnp.where(line == z.position, position, table)
    table_ref[...] = jnp.where(line == z.position + 1, scount_ref[position], table)


def start_kernel(
    z, pos_ref, cell_hbm, atom_hbm, scount_hbm, shift_hbm, rhs_ref, precond_ref, conn_ref, projector_ref,
    send_a_ref, send_b_ref, shift_tile_ref, rhs_rim, precond_rim, conn_all, projector_all, cell_ref, atom_ref,
    scount_ref, shift_ref, sems,
):
    lines = z.rim // LANES
    moves = [
        (cell_hbm, cell_ref), (atom_hbm, atom_ref), (scount_hbm, scount_ref), (shift_hbm, shift_ref),
        (conn_ref, conn_all), (projector_ref, projector_all),
    ]
    for k, first in enumerate((0, z.nodes - z.rim)):
        moves.append((rhs_ref.at[:, pl.ds(first, z.rim)], rhs_rim.at[k]))
        moves.append((precond_ref.at[pl.ds(first // LANES, lines), :], precond_rim.at[k]))
    copies = [pltpu.make_async_copy(source, to, sems.at[k]) for k, (source, to) in enumerate(moves)]
    for copy in copies:
        copy.start()
    for copy in copies:
        copy.wait()
    row = iota((ROWS, LANES), 0)
    tile = jnp.zeros((ROWS, LANES), F32)
    for v in range(z.vectors):
        tile = jnp.where(row == v, shift_ref[v], tile)
    shift_tile_ref[...] = tile
    head, tail = (
        jnp.concatenate(
            [
                rhs_rim[k, :, i * LANES : (i + 1) * LANES] * precond_rim[k, i : i + 1, :]
                for i in range(lines)
            ],
            axis=1,
        )
        for k in range(2)
    )
    even = pos_ref[0] % 2 == 0
    sides = jnp.where(even, tail, head), jnp.where(even, head, tail)
    nodes = (conn_all[...] + z.shift).astype(F32)
    cell = iota(nodes.shape, 0)
    entry = iota((z.rim_row - z.index_row, z.width), 0)
    place = iota((z.rim_row - z.index_row, z.width), 1)
    rows = jnp.zeros((z.rim_row - z.index_row, z.width), F32)
    for s in range(z.entries):
        row = jnp.sum(jnp.where(cell == cell_ref[s], nodes, 0.0), axis=0, keepdims=True)
        row = jnp.concatenate([row, jnp.zeros((1, z.width - z.elem), F32)], axis=1)
        owner = atom_ref[s] // z.owned
        facts = owner, atom_ref[s] - owner * z.owned, (s < scount_ref[pos_ref[0]]).astype(jnp.int32)
        rows = jnp.where(entry == s, row, rows)
        for k, fact in enumerate(facts):
            rows = jnp.where((entry == s) & (place == z.elem + k), fact.astype(F32), rows)
    for ref, side in zip((send_a_ref, send_b_ref), sides):
        ref[...] = jnp.zeros_like(ref)
        ref[: z.index_row, : z.elem] = projector_all[...]
        ref[z.index_row : z.rim_row, :] = rows
        for k in range(z.rim_pieces):
            piece = side[:, k * z.width : min((k + 1) * z.width, z.rim)]
            ref[z.rim_row + k * ROWS : z.rim_row + (k + 1) * ROWS, : piece.shape[1]] = piece


def own_kernel(
    z, rhs_ref, precond_ref, potential_ref, p_ref, gamma_ref, diag_ref,
):
    diag_ref[...] = jnp.zeros_like(diag_ref)
    gamma = jnp.zeros((ROWS, LANES), F32)
    for i in range(z.nodes // LANES):
        at = slice(i * LANES, (i + 1) * LANES)
        to = slice(z.rim + i * LANES, z.rim + (i + 1) * LANES)
        value = rhs_ref[:, at]
        scale = precond_ref[i : i + 1, :]
        product = value * scale
        p_ref[:, to] = product
        gamma = gamma + product * value
        diag_ref[0:1, to] = scale
        diag_ref[1:2, to] = potential_ref[i : i + 1, :]
    p_ref[:, z.window :] = jnp.zeros((ROWS, z.reach - z.window), F32)
    gamma_ref[...] = lanes_by_vector(z, gamma)


def full_groups(z, table_ref):
    ends = [table_ref[0, z.list + g * z.together + z.together - 1] for g in range(z.slots // z.together)]
    return functools.reduce(jnp.add, [(end >= z.slots).astype(jnp.int32) for end in ends])


def split_window(z, window_ref, parts_ref):
    count = z.window // WIDE
    for h in range(count):
        value = window_ref[:, h * WIDE : (h + 1) * WIDE]
        rounded = value.astype(BF16).astype(F32)
        both = jnp.concatenate([rounded, value - rounded], axis=0).astype(BF16)
        parts_ref[h * 2 * ROWS : (h + 1) * 2 * ROWS, :] = both
    parts_ref[count * 2 * ROWS :, :] = jnp.zeros((BAND * 2 * ROWS, WIDE), BF16)


def gather_middle(z, groups, listed, table_ref, index_ref, window_ref, u_ref, parts_ref=None):
    total = z.window // LANES
    tile = (ROWS, LANES)
    pair = (2 * ROWS, LANES)
    sub = iota(pair, 0)
    lows = [(sub + n * 2 * ROWS).astype(jnp.int16) for n in range(WIDE // (2 * ROWS))]
    one, none = jnp.ones(pair, BF16), jnp.zeros(pair, BF16)

    def product_tile(c, k):
        start = jnp.minimum((table_ref[0, z.low + c] >> BITS) + k * BAND, z.window // WIDE)
        index = index_ref[c, :, (z.tiles - 1) * LANES : z.tiles * LANES]
        low = (jnp.broadcast_to(index, pair) & (WIDE - 1)).astype(jnp.int16)
        hot = jnp.concatenate([jnp.where(low == n, one, none) for n in lows], axis=0)
        rows = pl.ds(pl.multiple_of(start * 2 * ROWS, 2 * ROWS), BAND * 2 * ROWS)
        got = jnp.dot(parts_ref[rows, :], hot, preferred_element_type=F32)
        high = (jnp.broadcast_to(index, tile) >> BITS) - start
        value = jnp.zeros(tile, F32)
        for h in range(BAND):
            at = h * 2 * ROWS
            value = jnp.where(high == h, got[at : at + ROWS] + got[at + ROWS : at + 2 * ROWS], value)
        return value

    size = z.together if listed else z.many

    def some_cells(g, _):
        cells = [g * size + i for i in range(size)]
        if listed:
            cells = [table_ref[0, z.list + c] for c in cells]
            cells = [jnp.where(c >= z.slots, c - z.slots, c) for c in cells]
        starts = [table_ref[0, z.low + c] >> 7 for c in cells]
        ends = [table_ref[0, z.high + c] >> 7 for c in cells]
        passes = functools.reduce(jnp.maximum, [(e - s) // SPAN + 1 for s, e in zip(starts, ends)])

        def one_pass(k, values):
            values = list(values)
            for i, c in enumerate(cells):
                start = jnp.minimum(starts[i] + k * SPAN, total)
                for t in range(z.tiles):
                    if parts_ref is not None and t == z.tiles - 1:
                        values[i * z.tiles + t] += product_tile(c, k)
                        continue
                    index = jnp.broadcast_to(index_ref[c, :, t * LANES : (t + 1) * LANES], tile)
                    low, high = index & (LANES - 1), (index >> 7) - start
                    value = values[i * z.tiles + t]
                    for h in range(SPAN):
                        at = pl.ds(pl.multiple_of((start + h) * LANES, LANES), LANES)
                        value = jnp.where(high == h, lane_gather(window_ref[:, at], low), value)
                    values[i * z.tiles + t] = value
            return tuple(values)

        values = lax.fori_loop(0, passes, one_pass, (jnp.zeros(tile, F32),) * (size * z.tiles))
        for i, c in enumerate(cells):
            rows = pl.ds(pl.multiple_of(c * ROWS, ROWS), ROWS)
            for t in range(z.tiles):
                u_ref[rows, t * LANES : (t + 1) * LANES] = values[i * z.tiles + t]
        return 0

    lax.fori_loop(*groups, some_cells, 0)


def gather_corners(z, corner_ref, window_ref, weight_ref, u_ref, uw_ref):
    tile = (ROWS, LANES)
    corner = jnp.broadcast_to(corner_ref[...], tile)
    low, high = corner & (LANES - 1), corner >> 7
    chains = [jnp.zeros(tile, F32)] * CHAINS
    for h in range(z.window // LANES):
        got = lane_gather(window_ref[:, h * LANES : (h + 1) * LANES], low)
        chains[h % CHAINS] = jnp.where(high == h, got, chains[h % CHAINS])
    corners = functools.reduce(jnp.add, chains)
    lane = iota(tile, 1)
    last = (z.elem - 1) % LANES
    for c in range(z.slots):
        rows = slice(c * ROWS, (c + 1) * ROWS)
        weight = weight_ref[rows, :]
        for t in range(z.tiles):
            lanes = slice(t * LANES, (t + 1) * LANES)
            value = u_ref[rows, lanes]
            if t == 0:
                value = jnp.where(lane == 0, corners[:, c : c + 1], value)
            if t == z.tiles - 1:
                value = jnp.where(lane == last, corners[:, z.slots + c : z.slots + c + 1], value)
            u_ref[rows, lanes] = value
            uw_ref[rows, lanes] = value * weight


def stiffness_product(k_high_ref, k_low_ref, uw_ref, e_ref):
    k_high, k_low = k_high_ref[...], k_low_ref[...]
    u_high, u_low = split(uw_ref[...])
    dot = functools.partial(lax.dot_general, dimension_numbers=NT, preferred_element_type=F32)
    e_ref[...] = dot(u_high, k_high) + (dot(u_high, k_low) + dot(u_low, k_high))


def entry_facts(z, table_ref, s):
    return table_ref[0, z.owner + s], table_ref[0, z.local + s], s < table_ref[0, z.position + 1]


def contributions(z, table_ref, pj_ref, u_ref):
    values = [u_ref[pl.ds(pl.multiple_of(table_ref[0, z.cell + s] * ROWS, ROWS), ROWS), :] for s in range(z.entries)]
    sums = lax.dot_general(
        pj_ref[...], jnp.concatenate(values, axis=0), NT, precision=HIGHEST, preferred_element_type=F32
    )
    sums = jnp.concatenate([sums, jnp.zeros((sums.shape[0], LANES - sums.shape[1]), F32)], axis=1)
    lane, row = iota((ROWS, LANES), 1), iota((ROWS, LANES), 0)
    position = table_ref[0, z.position]
    parts = [jnp.zeros((ROWS, LANES), F32)] * 3
    for s in range(z.entries):
        owner, local, alive = entry_facts(z, table_ref, s)
        got = lane_gather(sums[s * ROWS : (s + 1) * ROWS], s * ROWS + lane % ROWS)
        here = (lane // ROWS % ROWS == row) & (lane // z.pairs == local) & alive
        for k in range(3):
            parts[k] = parts[k] + jnp.where(here & (owner == position - 1 + k), got, 0.0)
    return [jnp.sum(part, axis=0, keepdims=True) for part in parts]


def sides(position, near, far):
    even = position % 2 == 0
    return jnp.where(even, far, near), jnp.where(even, near, far)


def first_window_kernel(z, table_ref, p_ref, index_ref, u_ref):
    groups = 0, full_groups(z, table_ref)
    gather_middle(z, groups, True, table_ref, index_ref, p_ref, u_ref)


def first_kernel(
    z, table_ref, p_in_ref, u_in_ref, halo_a_ref, halo_b_ref, index_ref, corner_ref, weight_ref,
    projector_ref, coupling_ref, p_ref, out_ref, uw_ref, pj_ref, beside_ref, u_ref,
):
    rows = slice(z.index_row, z.index_row + z.entries)
    line = iota((1, LANES), 1)
    left, right = sides(table_ref[0, z.position], halo_a_ref[rows, :], halo_b_ref[rows, :])
    beside = corner_ref[...]
    for k, (side, move) in enumerate(((left, -z.nodes), (right, z.nodes))):
        side = side.astype(jnp.int32) + move
        for s in range(z.entries):
            lane = z.beside + 2 * z.entries * k + s
            beside = jnp.where(line == lane, side[s : s + 1, :1], beside)
            beside = jnp.where(line == lane + z.entries, side[s : s + 1, z.elem - 1 : z.elem], beside)
    beside_ref[...] = beside
    own = slice(z.rim, z.rim + z.nodes)
    for k in range(z.rim_pieces):
        rows = slice(z.rim_row + k * ROWS, z.rim_row + (k + 1) * ROWS)
        at, to = k * z.width, min((k + 1) * z.width, z.rim)
        left, right = sides(table_ref[0, z.position], halo_a_ref[rows, : to - at], halo_b_ref[rows, : to - at])
        p_ref[:, at:to] = left
        p_ref[:, z.rim + z.nodes + at : z.rim + z.nodes + to] = right
    p_ref[:, own] = p_in_ref[:, own]
    p_ref[:, z.window :] = p_in_ref[:, z.window :]
    u_ref[...] = u_in_ref[...]
    pj_ref[...] = jnp.zeros_like(pj_ref)
    pj_ref[:, : z.elem] = projector_ref[...]
    groups = full_groups(z, table_ref), z.slots // z.together
    gather_middle(z, groups, True, table_ref, index_ref, p_ref, u_ref)
    gather_corners(z, corner_ref, p_ref, weight_ref, u_ref, uw_ref)
    parts = contributions(z, table_ref, pj_ref, u_ref)
    small_lane, small_row = iota((ROWS, LANES), 1), iota((ROWS, LANES), 0)
    matrices = jnp.zeros((ROWS, LANES), F32)
    for atom in range(z.owned):
        block = jnp.concatenate([coupling_ref[atom], jnp.zeros((ROWS, LANES - z.channels), F32)], axis=1)
        got = lane_gather(block, small_lane % ROWS)
        matrices = jnp.where(small_lane // ROWS == atom * ROWS + small_row, got, matrices)
    message = jnp.concatenate(parts + [jnp.sum(matrices, axis=0, keepdims=True)], axis=0)
    for d in range(z.devices):
        out_ref[d] = message


def second_kernel(
    z, table_ref, image_ref, p_ref, diag_in_ref, shift_ref, gamma_ref, halo_a_ref, halo_b_ref,
    index_ref, corner_ref, weight_ref, k_high_ref, k_low_ref, pj_ref, y_ref, q_ref, out_ref, e_ref, diag_ref, u_ref, uw_ref,
    parts_ref,
):
    left, right = sides(table_ref[0, z.position], halo_a_ref[...], halo_b_ref[...])
    own = slice(z.rim, z.rim + z.nodes)
    diag_ref[:, own] = diag_in_ref[:, own]
    diag_ref[:, : z.rim] = left[ROWS : ROWS + 2, : z.rim]
    diag_ref[:, z.rim + z.nodes :] = right[ROWS : ROWS + 2, z.rim :]
    y_ref[...] = image_ref[...] + (diag_ref[1:2, :] + shift_ref[:, :1]) * p_ref[:, : z.window]
    y_ref[:, : 2 * z.rim] += left[:ROWS]
    y_ref[:, z.window - 2 * z.rim :] += right[:ROWS]
    q_ref[:, : z.window] = y_ref[...] * diag_ref[0:1, :]
    q_ref[:, z.window :] = jnp.zeros((ROWS, z.reach - z.window), F32)
    y, q = y_ref[:, own], q_ref[:, own]
    dots = [
        gamma_ref[...],
        lanes_by_vector(z, y * p_ref[:, own]),
        lanes_by_vector(z, y * q),
    ]
    energy = jnp.sum(q * q * (diag_ref[1:2, own] + shift_ref[:, :1]), axis=1, keepdims=True)
    groups = 0, z.slots // z.many
    split_window(z, q_ref, parts_ref)
    gather_middle(z, groups, False, table_ref, index_ref, q_ref, u_ref, parts_ref)
    gather_corners(z, corner_ref, q_ref, weight_ref, u_ref, uw_ref)
    parts = contributions(z, table_ref, pj_ref, u_ref)
    stiffness_product(k_high_ref, k_low_ref, uw_ref, e_ref)
    elements = jnp.zeros((ROWS, z.width), F32)
    for c in range(z.slots):
        rows = slice(c * ROWS, (c + 1) * ROWS)
        elements = elements + u_ref[rows, :] * e_ref[rows, :]
    energy = energy + jnp.sum(elements, axis=1, keepdims=True)
    dots.append(lanes_by_vector(z, energy))
    line = dots[0]
    for k in range(1, len(dots)):
        line = line + pltpu.roll(dots[k], k * ROWS, 1)
    message = jnp.concatenate(parts + [line], axis=0)
    for d in range(z.devices):
        out_ref[d] = message


def band_of(bits):
    return BAND if bits == BITS else SPAN


def acc_shape(z, bits):
    return ((z.window >> bits) + band_of(bits)) * 2 * ROWS, 1 << bits


class Scatter:
    def __init__(self, z, bits, table_ref, index_ref, corner_ref, acc_ref):
        self.bits, self.wide, self.band = bits, 1 << bits, band_of(bits)
        self.z, self.index_ref, self.corner_ref, self.acc_ref = z, index_ref, corner_ref, acc_ref
        self.table_ref = table_ref
        self.groups = z.window // self.wide
        self.pair = (2 * ROWS, LANES)
        sub = iota(self.pair, 0)
        self.lows = [(sub + k * 2 * ROWS).astype(jnp.int16) for k in range(self.wide // (2 * ROWS))]
        self.one, self.none = jnp.ones(self.pair, BF16), jnp.zeros(self.pair, BF16)
        self.lane = iota((ROWS, LANES), 1)
        self.end = (z.elem - 1) % LANES

    def two_parts(self, value):
        rounded = value.astype(BF16).astype(F32)
        return jnp.concatenate([rounded, value - rounded], axis=0).astype(BF16)

    def hot_rows(self, index):
        low = (index & (self.wide - 1)).astype(jnp.int16)
        return jnp.concatenate([jnp.where(low == k, self.one, self.none) for k in self.lows], axis=0)

    def masked(self, high, both, rows):
        high = high.astype(jnp.int16)
        return jnp.concatenate([jnp.where(high == jnp.int16(h), both, self.none) for h in range(rows)], axis=0)

    def product(self, lhs, hot):
        return lax.dot_general(lhs, hot, NT, preferred_element_type=F32)

    def start(self, sources, beside=()):
        z = self.z
        corners = jnp.zeros((ROWS, LANES), F32)
        at = (z.tiles - 1) * LANES + self.end
        for cell, values in sources:
            corners = corners + jnp.where(self.lane == cell, values[:, 0:1], 0.0)
            corners = corners + jnp.where(self.lane == z.slots + cell, values[:, at : at + 1], 0.0)
        for s, values in enumerate(beside):
            lane = z.beside + s + s // z.entries * z.entries
            corners = jnp.where(self.lane == lane, values[:, 0:1], corners)
            corners = jnp.where(self.lane == lane + z.entries, values[:, at : at + 1], corners)
        index = jnp.broadcast_to(self.corner_ref[...], self.pair)
        rows = self.groups * 2 * ROWS
        self.acc_ref[:rows, :] = self.product(
            self.masked(index >> self.bits, self.two_parts(corners), self.groups), self.hot_rows(index)
        )
        self.acc_ref[rows:, :] = jnp.zeros((self.band * 2 * ROWS, self.wide), F32)

    def add(self, cells, value_of):
        z = self.z
        starts = [self.table_ref[0, z.low + c] >> self.bits for c in cells]
        ends = [self.table_ref[0, z.high + c] >> self.bits for c in cells]
        passes = functools.reduce(jnp.maximum, [(e - s) // self.band + 1 for s, e in zip(starts, ends)])

        def one_pass(k, _):
            for i, c in enumerate(cells):
                start = jnp.minimum(starts[i] + k * self.band, self.groups)
                lhs, hot = [], []
                for t in range(z.tiles):
                    index = jnp.broadcast_to(self.index_ref[c, :, t * LANES : (t + 1) * LANES], self.pair)
                    value = value_of(i, t)
                    if t == 0:
                        value = jnp.where(self.lane == 0, 0.0, value)
                    if t == z.tiles - 1:
                        value = jnp.where(self.lane == self.end, 0.0, value)
                    lhs.append(self.masked((index >> self.bits) - start, self.two_parts(value), self.band))
                    hot.append(self.hot_rows(index))
                to = pl.ds(pl.multiple_of(start * 2 * ROWS, 2 * ROWS), self.band * 2 * ROWS)
                self.acc_ref[to, :] += self.product(jnp.concatenate(lhs, axis=1), jnp.concatenate(hot, axis=1))
            return 0

        lax.fori_loop(0, passes, one_pass, 0)

    def add_rows(self, index, values, first, rows):
        lhs, hot = [], []
        for t in range(values.shape[1] // LANES):
            lanes = slice(t * LANES, (t + 1) * LANES)
            at = jnp.broadcast_to(index[:, lanes], self.pair)
            lhs.append(self.masked(at >> self.bits, self.two_parts(values[:, lanes]), rows))
            hot.append(self.hot_rows(at))
        to = slice(first * 2 * ROWS, (first + rows) * 2 * ROWS)
        self.acc_ref[to, :] += self.product(jnp.concatenate(lhs, axis=1), jnp.concatenate(hot, axis=1))

    def result(self, h):
        at = h * 2 * ROWS
        return self.acc_ref[at : at + ROWS] + self.acc_ref[at + ROWS : at + 2 * ROWS]


def cells_kernel(z, multiply, table_ref, index_ref, corner_ref, *refs):
    if multiply:
        uw_ref, stiffness_ref, diag_ref, image_ref, send_a_ref, send_b_ref, k_high_ref, k_low_ref, *refs = refs
        e_ref, k_ref, acc_ref = refs
        k_ref[...] = jnp.zeros_like(k_ref)
        k_ref[: z.elem, : z.elem] = stiffness_ref[...]
        k_high_ref[...], k_low_ref[...] = split(k_ref[...])
        stiffness_product(k_high_ref, k_low_ref, uw_ref, e_ref)
    else:
        e_ref, image_ref, send_a_ref, send_b_ref, acc_ref = refs
    scatter = Scatter(z, BITS, table_ref, index_ref, corner_ref, acc_ref)
    scatter.start([(c, e_ref[c * ROWS : (c + 1) * ROWS, :]) for c in range(z.slots)])

    def some_cells(g, _):
        cells = [g * z.many + i for i in range(z.many)]

        def value_of(i, t):
            rows = pl.ds(pl.multiple_of(cells[i] * ROWS, ROWS), ROWS)
            return e_ref[rows, t * LANES : (t + 1) * LANES]

        scatter.add(cells, value_of)
        return 0

    lax.fori_loop(0, z.slots // z.many, some_cells, 0)
    for h in range(scatter.groups):
        image_ref[:, h * WIDE : (h + 1) * WIDE] = scatter.result(h)
    even = table_ref[0, z.position] % 2 == 0
    ends = [slice(0, 2 * z.rim), slice(z.window - 2 * z.rim, z.window)]
    for source_ref, rows in ((image_ref, slice(0, ROWS)),) + (((diag_ref, slice(ROWS, ROWS + 2)),) if multiply else ()):
        low_rim, high_rim = (source_ref[:, end] for end in ends)
        send_a_ref[rows, :] = jnp.where(even, high_rim, low_rim)
        send_b_ref[rows, :] = jnp.where(even, low_rim, high_rim)


def support_kernel(
    z, last, table_ref, sums_ref, coupling_ref, index_ref, corner_ref, pj_ref, ext_a_ref, ext_b_ref,
    cells_ref, *refs,
):
    if last:
        image_ref, dots_ref, support_ref, nodes_ref, acc_ref = refs
    else:
        image_ref, support_ref, nodes_ref, acc_ref = refs
    position = table_ref[0, z.position]
    wanted = (
        pltpu.roll(sums_ref[:, 0, :], z.devices - 1, 0) + sums_ref[:, 1, :] + pltpu.roll(sums_ref[:, 2, :], 1, 0)
    )
    coupling = coupling_ref[:, 3, :]
    shape = (z.devices, LANES)
    lane = iota(shape, 1)
    term = jnp.zeros(shape, F32)
    for j in range(z.channels):
        matrix = lane_gather(coupling, lane // ROWS * ROWS + j)
        vector = lane_gather(wanted, lane // z.pairs * z.pairs + j * ROWS + lane % ROWS)
        term = term + matrix * vector
    if last:
        energy = jnp.sum(term * wanted, axis=0, keepdims=True)
        energy = jnp.broadcast_to(energy, (ROWS, LANES))
        step = ROWS
        while step < LANES:
            energy = energy + pltpu.roll(energy, step, 1)
            step *= 2
        line = iota((1, LANES), 1)
        dots_ref[...] = jnp.sum(sums_ref[:, 3, :], axis=0, keepdims=True) + jnp.where(
            line // ROWS == 3, energy[0:1], 0.0
        )
    block = iota(shape, 0)
    small_lane, small_row = iota((ROWS, LANES), 1), iota((ROWS, LANES), 0)

    def values(facts, projectors):
        spread = []
        for s, (owner, local, alive) in enumerate(facts):
            mine = jnp.sum(jnp.where(block == owner, term, 0.0), axis=0, keepdims=True)
            got = lane_gather(
                jnp.broadcast_to(mine, (ROWS, LANES)), local * z.pairs + small_lane % ROWS * ROWS + small_row
            )
            spread.append(jnp.where((small_lane // ROWS == s) & alive, got, 0.0)[:, : z.entries * ROWS])
        return jnp.dot(
            jnp.concatenate(spread, axis=0), projectors, precision=HIGHEST, preferred_element_type=F32
        )

    count = z.entries * ROWS
    support_ref[:count, :] = values([entry_facts(z, table_ref, s) for s in range(z.entries)], pj_ref[...])
    used = slice(0, z.rim_row)
    for side, ext in enumerate(sides(position, ext_a_ref[used, :], ext_b_ref[used, :])):
        nodes = ext[z.index_row :].astype(jnp.int32)
        facts = []
        for s in range(z.entries):
            fact = [jnp.broadcast_to(nodes[s : s + 1, z.elem + k : z.elem + k + 1], (1, LANES)) for k in range(3)]
            facts.append((fact[0], fact[1], fact[2] > 0))
        projectors = jnp.where(iota((z.index_row, z.width), 1) < z.elem, ext[: z.index_row], 0.0)
        support_ref[(side + 1) * count : (side + 2) * count, :] = values(facts, projectors)
        nodes_ref[side] = nodes
    scatter = Scatter(z, NARROW, table_ref, index_ref, corner_ref, acc_ref)
    cells = [table_ref[0, z.cell + s] for s in range(z.entries)]
    blocks = [support_ref[s * ROWS : (s + 1) * ROWS, :] for s in range(3 * z.entries)]
    scatter.start(list(zip(cells, blocks)), blocks[z.entries :])
    for first in range(0, z.entries, z.together):
        some = cells[first : first + z.together]

        def value_of(i, t):
            s = first + i
            return support_ref[s * ROWS : (s + 1) * ROWS, t * LANES : (t + 1) * LANES]

        scatter.add(some, value_of)
    shared = 2 * z.rim // scatter.wide
    place = iota((ROWS, z.width), 1)
    middle = (place > 0) & (place < z.elem - 1)
    for side, (first, offset) in enumerate(((0, z.window - 2 * z.rim), (scatter.groups - shared, 0))):
        for s in range(0, z.entries, BESIDE):
            some = range(s, s + BESIDE)
            base = (side + 1) * z.entries
            value = [jnp.where(middle, support_ref[(base + i) * ROWS : (base + i + 1) * ROWS, :], 0.0) for i in some]
            index = [nodes_ref[side, i : i + 1, :] - offset for i in some]
            scatter.add_rows(jnp.concatenate(index, axis=1), jnp.concatenate(value, axis=1), first, shared)
    for h in range(scatter.groups):
        at = slice(h * scatter.wide, (h + 1) * scatter.wide)
        image_ref[:, at] = cells_ref[:, at] + scatter.result(h)


def last_kernel(
    z, table_ref, rhs_ref, p_ref, diag_ref, shift_ref, y_ref, q_ref, image_ref, dots_ref, halo_a_ref, halo_b_ref,
    solution_ref, residual_ref,
):
    own = slice(z.rim, z.rim + z.nodes)
    lane, row = iota((ROWS, LANES), 1), iota((ROWS, LANES), 0)
    line = jnp.broadcast_to(dots_ref[...], (ROWS, LANES))

    def column(k):
        return jnp.sum(jnp.where(lane == k * ROWS + row, line, 0.0), axis=1, keepdims=True)

    gamma, py, qy, qq = (column(k) for k in range(4))
    alpha = gamma / py
    fresh = gamma - 2.0 * alpha * py + alpha * alpha * qy
    beta = fresh / gamma
    more = 1.0 + beta
    step = fresh / (more * more * py - 2.0 * more * alpha * qy + alpha * alpha * qq)
    p, q, y = p_ref[:, own], q_ref[:, own], y_ref[:, own]
    second = image_ref[:, own] + (diag_ref[1:2, own] + shift_ref[:, :1]) * q
    search = (p - alpha * q) + beta * p
    solution_ref[...] = alpha * p + step * search
    residual_ref[...] = (rhs_ref[...] - alpha * y) - step * (more * y - alpha * second)
    left, right = sides(table_ref[0, z.position], halo_a_ref[...], halo_b_ref[...])
    residual_ref[:, : z.rim] += step * alpha * left[:, z.rim :]
    residual_ref[:, z.nodes - z.rim :] += step * alpha * right[:, : z.rim]


def on_device(
    rhs, potential, precond, shift, stiffness, cell_scale, conn, cell_count, projector, support_cell, support_atom,
    support_count, atom_matrix,
):
    count = lax.axis_size("dom")
    z = Sizes(count, rhs, conn, projector, atom_matrix)
    position = lax.axis_index("dom")
    pos = position.astype(jnp.int32).reshape(1)
    near = [(i, i ^ 1) for i in range(count)]
    far = [(i, j) for i in range(1, count - 1) for j in [i + 1 if i % 2 else i - 1]]

    def exchange(a, b):
        return lax.ppermute(a, "dom", near), lax.ppermute(b, "dom", far)

    def call(kernel, outs, scratch, scalars, *args, in_hbm=(), by_hand=False):
        space = pltpu.HBM if by_hand else pltpu.VMEM
        args = [pltpu.with_memory_space_constraint(x, space) for x in args]
        return pl.pallas_call(
            kernel,
            out_shape=[
                jax.ShapeDtypeStruct(s, d) if i in in_hbm else pltpu.VMEM(s, d) for i, (s, d) in enumerate(outs)
            ],
            in_specs=[SMEM] * len(scalars) + [pl.BlockSpec(memory_space=space)] * len(args),
            out_specs=[VMEM] * len(outs),
            scratch_shapes=[pltpu.VMEM(*s) if isinstance(s, tuple) else s for s in scratch],
            compiler_params=pltpu.CompilerParams(vmem_limit_bytes=16 * 1024 * 1024),
        )(*scalars, *args)

    flat_projector = projector.reshape(z.entries * z.channels, z.elem)
    cells = (z.slots * ROWS, z.width)
    window, reach, own = (z.vectors, z.window), (z.vectors, z.reach), (z.vectors, z.nodes)
    message = (z.devices, 4, LANES)
    square, entries = (z.width, z.width), (z.entries * ROWS, z.width)
    rim, more_rim = (z.vectors, 2 * z.rim), (z.vectors + 2, 2 * z.rim)
    acc = acc_shape(z, BITS)
    support_scratch = [
        ((3 * z.entries * ROWS, z.width), F32), ((2, z.rim_row - z.index_row, z.width), jnp.int32),
        (acc_shape(z, NARROW), F32),
    ]

    precond_lines = precond.reshape(-1, LANES)
    tile = (ROWS, LANES)
    first_message = (z.message, z.width)
    send_a, send_b, shift_tile = call(
            functools.partial(start_kernel, z),
            [(first_message, F32), (first_message, F32), (tile, F32)],
            [((2, z.vectors, z.rim), F32), ((2, z.rim // LANES, LANES), F32), (conn.shape, jnp.int32),
             (flat_projector.shape, F32), pltpu.SMEM(support_cell.shape, jnp.int32),
             pltpu.SMEM(support_atom.shape, jnp.int32), pltpu.SMEM(support_count.shape, jnp.int32),
             pltpu.SMEM(shift.shape, F32), pltpu.SemaphoreType.DMA((10,))],
            (pos,),
            support_cell, support_atom, support_count, shift, rhs, precond_lines, conn, flat_projector, by_hand=True,
    )
    ext = exchange(send_a, send_b)
    index, corner, table, weight = call(
        functools.partial(prepare_kernel, z),
        [((z.slots, 1, z.width), jnp.int32), ((1, LANES), jnp.int32), ((1, LANES), jnp.int32),
         ((z.slots * ROWS, LANES), F32)],
        [],
        (pos, cell_count, cell_scale, support_cell, support_atom, support_count),
        conn,
    )
    p, gamma, diag = call(
        functools.partial(own_kernel, z),
        [(reach, F32), ((1, LANES), F32), ((2, z.window), F32)],
        [],
        (),
        rhs, precond_lines, potential.reshape(-1, LANES),
    )
    (u,) = call(functools.partial(first_window_kernel, z), [(cells, F32)], [], (table,), p, index)
    p, sums, uw, pj, beside = call(
        functools.partial(first_kernel, z),
        [(reach, F32), (message, F32), (cells, F32), (entries, F32), ((1, LANES), jnp.int32)],
        [(cells, F32)],
        (table,),
        p, u, *ext, index, corner, weight, flat_projector, atom_matrix,
    )
    coupled = lax.all_to_all(sums, "dom", 0, 0)
    image, send_a, send_b, k_high, k_low = call(
        functools.partial(cells_kernel, z, True),
        [(window, F32), (more_rim, F32), (more_rim, F32), (square, BF16), (square, BF16)],
        [(cells, F32), (square, F32), (acc, F32)],
        (table,),
        index, corner, uw, stiffness, diag,
    )
    halo = exchange(send_a, send_b)
    (image,) = call(
        functools.partial(support_kernel, z, False),
        [(window, F32)],
        support_scratch,
        (table,),
        coupled, coupled, index, beside, pj, *ext, image,
    )
    y, q, sums, e = call(
        functools.partial(second_kernel, z),
        [(window, F32), (reach, F32), (message, F32), (cells, F32)],
        [((2, z.window), F32), (cells, F32), (cells, F32), (acc, BF16)],
        (table,),
        image, p, diag, shift_tile, gamma, *halo, index, corner, weight, k_high, k_low, pj,
    )
    totals = lax.all_to_all(sums, "dom", 0, 0)
    image, send_a, send_b = call(
        functools.partial(cells_kernel, z, False), [(window, F32), (rim, F32), (rim, F32)], [(acc, F32)], (table,),
        index, corner, e,
    )
    halo = exchange(send_a, send_b)
    image, dots = call(
        functools.partial(support_kernel, z, True),
        [(window, F32), ((1, LANES), F32)],
        support_scratch,
        (table,),
        totals, coupled, index, beside, pj, *ext, image,
    )
    return tuple(
        call(
            functools.partial(last_kernel, z),
            [(own, F32), (own, F32)],
            [],
            (table,),
            rhs, p, diag, shift_tile, y, q, image, dots, *halo, in_hbm=(0, 1),
        )
    )


def solution(mesh):
    placed = (
        P(None, "dom"),
        P("dom"),
        P("dom"),
        P(),
        P(),
        P("dom"),
        P("dom", None),
        P(),
        P("dom", None, None),
        P("dom"),
        P("dom"),
        P(),
        P("dom", None, None),
    )
    return jax.shard_map(
        on_device,
        mesh=mesh,
        in_specs=placed,
        out_specs=(P(None, "dom"), P(None, "dom")),
        check_vma=False,
    )
```

```python
import functools

import jax
import jax.numpy as jnp
from jax import lax
from jax.experimental import pallas as pl
from jax.experimental.pallas import tpu as pltpu
from jax.sharding import PartitionSpec as P

LANES = 128
ROWS = 8
BITS = 7
WIDE = 1 << BITS
NARROW = 7
CHAINS = 4
SPAN = 14
BAND = 14
BESIDE = 4
TOGETHER = 8
MANY = 32
F32 = jnp.float32
BF16 = jnp.bfloat16
HIGHEST = lax.Precision.HIGHEST
NT = (((1,), (1,)), ((), ()))
VMEM = pl.BlockSpec(memory_space=pltpu.VMEM)
SMEM = pl.BlockSpec(memory_space=pltpu.SMEM)


def round_up(value, step):
    return -(-value // step) * step


class Sizes:
    def __init__(self, count, rhs, conn, projector, atom_matrix):
        self.devices = count
        self.vectors, self.nodes = rhs.shape
        self.slots, self.elem = conn.shape
        self.entries, self.channels = projector.shape[:2]
        self.owned = atom_matrix.shape[0]
        self.ghost = self.nodes // 16
        self.rim = round_up(self.ghost, 2 * LANES)
        self.shift = self.rim - self.ghost
        self.window = self.nodes + 2 * self.rim
        self.width = round_up(self.elem, LANES)
        self.tiles = self.width // LANES
        self.pairs = self.channels * self.vectors
        self.pieces = 4 if self.nodes % (4 * LANES) == 0 and self.nodes // 4 >= self.rim else 1
        self.low, self.high, self.list = 0, self.slots, 2 * self.slots
        self.cell = 3 * self.slots
        self.owner, self.local = self.cell + self.entries, self.cell + 2 * self.entries
        self.position = self.cell + 3 * self.entries
        self.beside = 2 * self.slots
        assert self.position + 1 < LANES and self.beside + 4 * self.entries <= LANES
        self.reach = self.window + SPAN * LANES
        self.index_row = self.entries * self.channels
        self.rim_row = self.index_row + round_up(self.entries, ROWS)
        self.rim_pieces = -(-self.rim // self.width)
        self.message = self.rim_row + self.rim_pieces * ROWS
        assert self.elem + 3 <= self.width and self.entries % BESIDE == 0
        self.together = TOGETHER if self.slots % TOGETHER == 0 else 1
        self.many = MANY if self.slots % MANY == 0 else 1
        assert self.vectors == ROWS and self.channels == ROWS and 2 * self.slots <= LANES
        assert self.nodes % WIDE == 0 and self.owned * self.pairs == LANES


def lane_gather(values, index):
    return jnp.take_along_axis(values, index, axis=1, mode="promise_in_bounds")


def iota(shape, dim):
    return lax.broadcasted_iota(jnp.int32, shape, dim)


def split(values):
    high = values.astype(BF16)
    return high, (values - high.astype(F32)).astype(BF16)


def lanes_by_vector(z, values):
    total = jnp.sum(values, axis=1, keepdims=True)
    spread = jnp.broadcast_to(total, (ROWS, LANES))
    return jnp.sum(jnp.where(iota((ROWS, LANES), 1) == iota((ROWS, LANES), 0), spread, 0.0), axis=0, keepdims=True)


def prepare_kernel(
    z, pos_ref, count_ref, scale_ref, cell_ref, atom_ref, scount_ref, conn_ref,
    index_ref, corner_ref, table_ref, weight_ref,
):
    position = pos_ref[0]
    line = iota((1, LANES), 1)
    corner = jnp.zeros((1, LANES), jnp.int32)
    index_ref[...] = jnp.zeros_like(index_ref)
    live = count_ref[position]
    for c in range(z.slots):
        row = conn_ref[c : c + 1, :] + z.shift
        index_ref[c, :, : z.elem] = row
        corner = jnp.where(line == c, row[:, :1], corner)
        corner = jnp.where(line == z.slots + c, row[:, z.elem - 1 :], corner)
        weight = jnp.where(c < live, scale_ref[c], 0.0)
        weight_ref[c * ROWS : (c + 1) * ROWS, :] = jnp.zeros((ROWS, LANES), F32) + weight
    corner_ref[...] = corner
    nodes = (conn_ref[...] + z.shift).astype(F32)
    place = iota(nodes.shape, 1)
    middle = (place > 0) & (place < z.elem - 1)
    low = jnp.min(jnp.where(middle, nodes, 1.0 * z.window), axis=1, keepdims=True)
    high = jnp.max(jnp.where(middle, nodes, 0.0), axis=1, keepdims=True)
    lane, cell = iota((z.slots, LANES), 1), iota((z.slots, LANES), 0)

    def as_row(column, first=0):
        return jnp.sum(jnp.where(lane == cell + first, column, 0.0), axis=0, keepdims=True)

    good = jnp.where((low >= z.rim) & (high < z.window - z.rim), 1.0, 0.0)
    good = jnp.broadcast_to(good, (z.slots, LANES))
    number = cell.astype(F32)
    before = jnp.sum(jnp.where(lane < cell, as_row(good), 0.0), axis=1, keepdims=True)
    at = jnp.where(good > 0.5, before, z.slots - 1.0 - (number - before))
    listed = jnp.where(lane.astype(F32) == at + z.list, number + z.slots * good, 0.0)
    table = as_row(low, z.low) + as_row(high, z.high) + jnp.sum(listed, axis=0, keepdims=True)
    table = table.astype(jnp.int32)
    for s in range(z.entries):
        atom = atom_ref[s]
        owner = atom // z.owned
        for first, fact in ((z.cell, cell_ref[s]), (z.owner, owner), (z.local, atom - owner * z.owned)):
            table = jnp.where(line == first + s, fact, table)
    table = jnp.where(line == z.position, position, table)
    table_ref[...] = jnp.where(line == z.position + 1, scount_ref[position], table)


def start_kernel(
    z, pos_ref, cell_hbm, atom_hbm, scount_hbm, shift_hbm, rhs_ref, precond_ref, conn_ref, projector_ref,
    send_a_ref, send_b_ref, shift_tile_ref, rhs_rim, precond_rim, conn_all, projector_all, cell_ref, atom_ref,
    scount_ref, shift_ref, sems,
):
    lines = z.rim // LANES
    moves = [
        (cell_hbm, cell_ref), (atom_hbm, atom_ref), (scount_hbm, scount_ref), (shift_hbm, shift_ref),
        (conn_ref, conn_all), (projector_ref, projector_all),
    ]
    for k, first in enumerate((0, z.nodes - z.rim)):
        moves.append((rhs_ref.at[:, pl.ds(first, z.rim)], rhs_rim.at[k]))
        moves.append((precond_ref.at[pl.ds(first // LANES, lines), :], precond_rim.at[k]))
    copies = [pltpu.make_async_copy(source, to, sems.at[k]) for k, (source, to) in enumerate(moves)]
    for copy in copies:
        copy.start()
    for copy in copies:
        copy.wait()
    row = iota((ROWS, LANES), 0)
    tile = jnp.zeros((ROWS, LANES), F32)
    for v in range(z.vectors):
        tile = jnp.where(row == v, shift_ref[v], tile)
    shift_tile_ref[:ROWS, :] = tile
    shift_tile_ref[ROWS:, :] = jnp.zeros((ROWS, LANES), F32) + jnp.where(pos_ref[0] % 2 == 0, 1.0, 0.0)
    head, tail = (
        jnp.concatenate(
            [
                rhs_rim[k, :, i * LANES : (i + 1) * LANES] * precond_rim[k, i : i + 1, :]
                for i in range(lines)
            ],
            axis=1,
        )
        for k in range(2)
    )
    even = pos_ref[0] % 2 == 0
    sides = jnp.where(even, tail, head), jnp.where(even, head, tail)
    nodes = (conn_all[...] + z.shift).astype(F32)
    cell = iota(nodes.shape, 0)
    entry = iota((z.rim_row - z.index_row, z.width), 0)
    place = iota((z.rim_row - z.index_row, z.width), 1)
    rows = jnp.zeros((z.rim_row - z.index_row, z.width), F32)
    for s in range(z.entries):
        row = jnp.sum(jnp.where(cell == cell_ref[s], nodes, 0.0), axis=0, keepdims=True)
        row = jnp.concatenate([row, jnp.zeros((1, z.width - z.elem), F32)], axis=1)
        owner = atom_ref[s] // z.owned
        facts = owner, atom_ref[s] - owner * z.owned, (s < scount_ref[pos_ref[0]]).astype(jnp.int32)
        rows = jnp.where(entry == s, row, rows)
        for k, fact in enumerate(facts):
            rows = jnp.where((entry == s) & (place == z.elem + k), fact.astype(F32), rows)
    for ref, side in zip((send_a_ref, send_b_ref), sides):
        ref[...] = jnp.zeros_like(ref)
        ref[: z.index_row, : z.elem] = projector_all[...]
        ref[z.index_row : z.rim_row, :] = rows
        for k in range(z.rim_pieces):
            piece = side[:, k * z.width : min((k + 1) * z.width, z.rim)]
            ref[z.rim_row + k * ROWS : z.rim_row + (k + 1) * ROWS, : piece.shape[1]] = piece


def own_kernel(
    z, rhs_ref, precond_ref, potential_ref, p_ref, gamma_ref, diag_ref,
):
    diag_ref[...] = jnp.zeros_like(diag_ref)
    gamma = jnp.zeros((ROWS, LANES), F32)
    for i in range(z.nodes // LANES):
        at = slice(i * LANES, (i + 1) * LANES)
        to = slice(z.rim + i * LANES, z.rim + (i + 1) * LANES)
        value = rhs_ref[:, at]
        scale = precond_ref[i : i + 1, :]
        product = value * scale
        p_ref[:, to] = product
        gamma = gamma + product * value
        diag_ref[0:1, to] = scale
        diag_ref[1:2, to] = potential_ref[i : i + 1, :]
    p_ref[:, z.window :] = jnp.zeros((ROWS, z.reach - z.window), F32)
    gamma_ref[...] = lanes_by_vector(z, gamma)


def full_groups(z, table_ref):
    ends = [table_ref[0, z.list + g * z.together + z.together - 1] for g in range(z.slots // z.together)]
    return functools.reduce(jnp.add, [(end >= z.slots).astype(jnp.int32) for end in ends])


def split_window(z, window_ref, parts_ref):
    count = z.window // WIDE
    for h in range(count):
        value = window_ref[:, h * WIDE : (h + 1) * WIDE]
        rounded = value.astype(BF16).astype(F32)
        both = jnp.concatenate([rounded, value - rounded], axis=0).astype(BF16)
        parts_ref[h * 2 * ROWS : (h + 1) * 2 * ROWS, :] = both
    parts_ref[count * 2 * ROWS :, :] = jnp.zeros((BAND * 2 * ROWS, WIDE), BF16)


def gather_middle(z, groups, listed, table_ref, index_ref, window_ref, u_ref, parts_ref=None):
    total = z.window // LANES
    tile = (ROWS, LANES)
    pair = (2 * ROWS, LANES)
    sub = iota(pair, 0)
    lows = [(sub + n * 2 * ROWS).astype(jnp.int16) for n in range(WIDE // (2 * ROWS))]
    one, none = jnp.ones(pair, BF16), jnp.zeros(pair, BF16)

    def product_tile(c, k, t):
        start = jnp.minimum((table_ref[0, z.low + c] >> BITS) + k * BAND, z.window // WIDE)
        index = index_ref[c, :, t * LANES : (t + 1) * LANES]
        low = (jnp.broadcast_to(index, pair) & (WIDE - 1)).astype(jnp.int16)
        hot = jnp.concatenate([jnp.where(low == n, one, none) for n in lows], axis=0)
        rows = pl.ds(pl.multiple_of(start * 2 * ROWS, 2 * ROWS), BAND * 2 * ROWS)
        got = jnp.dot(parts_ref[rows, :], hot, preferred_element_type=F32)
        high = (jnp.broadcast_to(index, tile) >> BITS) - start
        value = jnp.zeros(tile, F32)
        for h in range(BAND):
            at = h * 2 * ROWS
            value = jnp.where(high == h, got[at : at + ROWS] + got[at + ROWS : at + 2 * ROWS], value)
        return value

    size = z.together if listed else z.many

    def some_cells(g, _):
        cells = [g * size + i for i in range(size)]
        if listed:
            cells = [table_ref[0, z.list + c] for c in cells]
            cells = [jnp.where(c >= z.slots, c - z.slots, c) for c in cells]
        starts = [table_ref[0, z.low + c] >> 7 for c in cells]
        ends = [table_ref[0, z.high + c] >> 7 for c in cells]
        passes = functools.reduce(jnp.maximum, [(e - s) // SPAN + 1 for s, e in zip(starts, ends)])

        def one_pass(k, values):
            values = list(values)
            for i, c in enumerate(cells):
                start = jnp.minimum(starts[i] + k * SPAN, total)
                for t in range(z.tiles):
                    if parts_ref is not None and t >= z.tiles - 2:
                        values[i * z.tiles + t] += product_tile(c, k, t)
                        continue
                    index = jnp.broadcast_to(index_ref[c, :, t * LANES : (t + 1) * LANES], tile)
                    low, high = index & (LANES - 1), (index >> 7) - start
                    value = values[i * z.tiles + t]
                    for h in range(SPAN):
                        at = pl.ds(pl.multiple_of((start + h) * LANES, LANES), LANES)
                        value = jnp.where(high == h, lane_gather(window_ref[:, at], low), value)
                    values[i * z.tiles + t] = value
            return tuple(values)

        values = lax.fori_loop(0, passes, one_pass, (jnp.zeros(tile, F32),) * (size * z.tiles))
        for i, c in enumerate(cells):
            rows = pl.ds(pl.multiple_of(c * ROWS, ROWS), ROWS)
            for t in range(z.tiles):
                u_ref[rows, t * LANES : (t + 1) * LANES] = values[i * z.tiles + t]
        return 0

    lax.fori_loop(*groups, some_cells, 0)


def gather_corners(z, corner_ref, window_ref, weight_ref, u_ref, uw_ref):
    tile = (ROWS, LANES)
    corner = jnp.broadcast_to(corner_ref[...], tile)
    low, high = corner & (LANES - 1), corner >> 7
    chains = [jnp.zeros(tile, F32)] * CHAINS
    for h in range(z.window // LANES):
        got = lane_gather(window_ref[:, h * LANES : (h + 1) * LANES], low)
        chains[h % CHAINS] = jnp.where(high == h, got, chains[h % CHAINS])
    corners = functools.reduce(jnp.add, chains)
    lane = iota(tile, 1)
    last = (z.elem - 1) % LANES
    for c in range(z.slots):
        rows = slice(c * ROWS, (c + 1) * ROWS)
        weight = weight_ref[rows, :]
        for t in range(z.tiles):
            lanes = slice(t * LANES, (t + 1) * LANES)
            value = u_ref[rows, lanes]
            if t == 0:
                value = jnp.where(lane == 0, corners[:, c : c + 1], value)
            if t == z.tiles - 1:
                value = jnp.where(lane == last, corners[:, z.slots + c : z.slots + c + 1], value)
            u_ref[rows, lanes] = value
            uw_ref[rows, lanes] = value * weight


def stiffness_product(k_high_ref, k_low_ref, uw_ref, e_ref):
    k_high, k_low = k_high_ref[...], k_low_ref[...]
    u_high, u_low = split(uw_ref[...])
    dot = functools.partial(lax.dot_general, dimension_numbers=NT, preferred_element_type=F32)
    e_ref[...] = dot(u_high, k_high) + (dot(u_high, k_low) + dot(u_low, k_high))


def entry_facts(z, table_ref, s):
    return table_ref[0, z.owner + s], table_ref[0, z.local + s], s < table_ref[0, z.position + 1]


def contributions(z, table_ref, pj_ref, u_ref):
    values = [u_ref[pl.ds(pl.multiple_of(table_ref[0, z.cell + s] * ROWS, ROWS), ROWS), :] for s in range(z.entries)]
    sums = lax.dot_general(
        pj_ref[...], jnp.concatenate(values, axis=0), NT, precision=HIGHEST, preferred_element_type=F32
    )
    sums = jnp.concatenate([sums, jnp.zeros((sums.shape[0], LANES - sums.shape[1]), F32)], axis=1)
    lane, row = iota((ROWS, LANES), 1), iota((ROWS, LANES), 0)
    position = table_ref[0, z.position]
    parts = [jnp.zeros((ROWS, LANES), F32)] * 3
    for s in range(z.entries):
        owner, local, alive = entry_facts(z, table_ref, s)
        got = lane_gather(sums[s * ROWS : (s + 1) * ROWS], s * ROWS + lane % ROWS)
        here = (lane // ROWS % ROWS == row) & (lane // z.pairs == local) & alive
        for k in range(3):
            parts[k] = parts[k] + jnp.where(here & (owner == position - 1 + k), got, 0.0)
    return [jnp.sum(part, axis=0, keepdims=True) for part in parts]


def sides(position, near, far):
    even = position % 2 == 0
    return jnp.where(even, far, near), jnp.where(even, near, far)


def first_window_kernel(z, table_ref, p_ref, index_ref, u_ref):
    groups = 0, full_groups(z, table_ref)
    gather_middle(z, groups, True, table_ref, index_ref, p_ref, u_ref)


def first_kernel(
    z, table_ref, p_in_ref, u_in_ref, halo_a_ref, halo_b_ref, index_ref, corner_ref, weight_ref,
    projector_ref, coupling_ref, p_ref, out_ref, uw_ref, pj_ref, beside_ref, u_ref,
):
    rows = slice(z.index_row, z.index_row + z.entries)
    line = iota((1, LANES), 1)
    left, right = sides(table_ref[0, z.position], halo_a_ref[rows, :], halo_b_ref[rows, :])
    beside = corner_ref[...]
    for k, (side, move) in enumerate(((left, -z.nodes), (right, z.nodes))):
        side = side.astype(jnp.int32) + move
        for s in range(z.entries):
            lane = z.beside + 2 * z.entries * k + s
            beside = jnp.where(line == lane, side[s : s + 1, :1], beside)
            beside = jnp.where(line == lane + z.entries, side[s : s + 1, z.elem - 1 : z.elem], beside)
    beside_ref[...] = beside
    own = slice(z.rim, z.rim + z.nodes)
    for k in range(z.rim_pieces):
        rows = slice(z.rim_row + k * ROWS, z.rim_row + (k + 1) * ROWS)
        at, to = k * z.width, min((k + 1) * z.width, z.rim)
        left, right = sides(table_ref[0, z.position], halo_a_ref[rows, : to - at], halo_b_ref[rows, : to - at])
        p_ref[:, at:to] = left
        p_ref[:, z.rim + z.nodes + at : z.rim + z.nodes + to] = right
    p_ref[:, own] = p_in_ref[:, own]
    p_ref[:, z.window :] = p_in_ref[:, z.window :]
    u_ref[...] = u_in_ref[...]
    pj_ref[...] = jnp.zeros_like(pj_ref)
    pj_ref[:, : z.elem] = projector_ref[...]
    groups = full_groups(z, table_ref), z.slots // z.together
    gather_middle(z, groups, True, table_ref, index_ref, p_ref, u_ref)
    gather_corners(z, corner_ref, p_ref, weight_ref, u_ref, uw_ref)
    parts = contributions(z, table_ref, pj_ref, u_ref)
    small_lane, small_row = iota((ROWS, LANES), 1), iota((ROWS, LANES), 0)
    matrices = jnp.zeros((ROWS, LANES), F32)
    for atom in range(z.owned):
        block = jnp.concatenate([coupling_ref[atom], jnp.zeros((ROWS, LANES - z.channels), F32)], axis=1)
        got = lane_gather(block, small_lane % ROWS)
        matrices = jnp.where(small_lane // ROWS == atom * ROWS + small_row, got, matrices)
    message = jnp.concatenate(parts + [jnp.sum(matrices, axis=0, keepdims=True)], axis=0)
    for d in range(z.devices):
        out_ref[d] = message


def second_kernel(
    z, table_ref, image_ref, p_ref, diag_in_ref, shift_ref, gamma_ref, halo_a_ref, halo_b_ref,
    index_ref, corner_ref, weight_ref, k_high_ref, k_low_ref, pj_ref, y_ref, q_ref, out_ref, e_ref, diag_ref, u_ref, uw_ref,
    parts_ref,
):
    left, right = sides(table_ref[0, z.position], halo_a_ref[...], halo_b_ref[...])
    own = slice(z.rim, z.rim + z.nodes)
    diag_ref[:, own] = diag_in_ref[:, own]
    diag_ref[:, : z.rim] = left[ROWS : ROWS + 2, : z.rim]
    diag_ref[:, z.rim + z.nodes :] = right[ROWS : ROWS + 2, z.rim :]
    y_ref[...] = image_ref[...] + (diag_ref[1:2, :] + shift_ref[:ROWS, :1]) * p_ref[:, : z.window]
    y_ref[:, : 2 * z.rim] += left[:ROWS]
    y_ref[:, z.window - 2 * z.rim :] += right[:ROWS]
    q_ref[:, : z.window] = y_ref[...] * diag_ref[0:1, :]
    q_ref[:, z.window :] = jnp.zeros((ROWS, z.reach - z.window), F32)
    y, q = y_ref[:, own], q_ref[:, own]
    dots = [
        gamma_ref[...],
        lanes_by_vector(z, y * p_ref[:, own]),
        lanes_by_vector(z, y * q),
    ]
    energy = jnp.sum(q * q * (diag_ref[1:2, own] + shift_ref[:ROWS, :1]), axis=1, keepdims=True)
    groups = 0, z.slots // z.many
    split_window(z, q_ref, parts_ref)
    gather_middle(z, groups, False, table_ref, index_ref, q_ref, u_ref, parts_ref)
    gather_corners(z, corner_ref, q_ref, weight_ref, u_ref, uw_ref)
    parts = contributions(z, table_ref, pj_ref, u_ref)
    stiffness_product(k_high_ref, k_low_ref, uw_ref, e_ref)
    elements = jnp.zeros((ROWS, z.width), F32)
    for c in range(z.slots):
        rows = slice(c * ROWS, (c + 1) * ROWS)
        elements = elements + u_ref[rows, :] * e_ref[rows, :]
    energy = energy + jnp.sum(elements, axis=1, keepdims=True)
    dots.append(lanes_by_vector(z, energy))
    line = dots[0]
    for k in range(1, len(dots)):
        line = line + pltpu.roll(dots[k], k * ROWS, 1)
    message = jnp.concatenate(parts + [line], axis=0)
    for d in range(z.devices):
        out_ref[d] = message


def band_of(bits):
    return BAND if bits == BITS else SPAN


def acc_shape(z, bits):
    return ((z.window >> bits) + band_of(bits)) * 2 * ROWS, 1 << bits


class Scatter:
    def __init__(self, z, bits, table_ref, index_ref, corner_ref, acc_ref):
        self.bits, self.wide, self.band = bits, 1 << bits, band_of(bits)
        self.z, self.index_ref, self.corner_ref, self.acc_ref = z, index_ref, corner_ref, acc_ref
        self.table_ref = table_ref
        self.groups = z.window // self.wide
        self.pair = (2 * ROWS, LANES)
        sub = iota(self.pair, 0)
        self.lows = [(sub + k * 2 * ROWS).astype(jnp.int16) for k in range(self.wide // (2 * ROWS))]
        self.one, self.none = jnp.ones(self.pair, BF16), jnp.zeros(self.pair, BF16)
        self.lane = iota((ROWS, LANES), 1)
        self.end = (z.elem - 1) % LANES

    def two_parts(self, value):
        rounded = value.astype(BF16).astype(F32)
        return jnp.concatenate([rounded, value - rounded], axis=0).astype(BF16)

    def hot_rows(self, index):
        low = (index & (self.wide - 1)).astype(jnp.int16)
        return jnp.concatenate([jnp.where(low == k, self.one, self.none) for k in self.lows], axis=0)

    def masked(self, high, both, rows):
        high = high.astype(jnp.int16)
        return jnp.concatenate([jnp.where(high == jnp.int16(h), both, self.none) for h in range(rows)], axis=0)

    def product(self, lhs, hot):
        return lax.dot_general(lhs, hot, NT, preferred_element_type=F32)

    def start(self, sources, beside=()):
        z = self.z
        corners = jnp.zeros((ROWS, LANES), F32)
        at = (z.tiles - 1) * LANES + self.end
        for cell, values in sources:
            corners = corners + jnp.where(self.lane == cell, values[:, 0:1], 0.0)
            corners = corners + jnp.where(self.lane == z.slots + cell, values[:, at : at + 1], 0.0)
        for s, values in enumerate(beside):
            lane = z.beside + s + s // z.entries * z.entries
            corners = jnp.where(self.lane == lane, values[:, 0:1], corners)
            corners = jnp.where(self.lane == lane + z.entries, values[:, at : at + 1], corners)
        index = jnp.broadcast_to(self.corner_ref[...], self.pair)
        rows = self.groups * 2 * ROWS
        self.acc_ref[:rows, :] = self.product(
            self.masked(index >> self.bits, self.two_parts(corners), self.groups), self.hot_rows(index)
        )
        self.acc_ref[rows:, :] = jnp.zeros((self.band * 2 * ROWS, self.wide), F32)

    def add(self, cells, value_of):
        z = self.z
        starts = [self.table_ref[0, z.low + c] >> self.bits for c in cells]
        ends = [self.table_ref[0, z.high + c] >> self.bits for c in cells]
        passes = functools.reduce(jnp.maximum, [(e - s) // self.band + 1 for s, e in zip(starts, ends)])

        def one_pass(k, _):
            for i, c in enumerate(cells):
                start = jnp.minimum(starts[i] + k * self.band, self.groups)
                lhs, hot = [], []
                for t in range(z.tiles):
                    index = jnp.broadcast_to(self.index_ref[c, :, t * LANES : (t + 1) * LANES], self.pair)
                    value = value_of(i, t)
                    if t == 0:
                        value = jnp.where(self.lane == 0, 0.0, value)
                    if t == z.tiles - 1:
                        value = jnp.where(self.lane == self.end, 0.0, value)
                    lhs.append(self.masked((index >> self.bits) - start, self.two_parts(value), self.band))
                    hot.append(self.hot_rows(index))
                to = pl.ds(pl.multiple_of(start * 2 * ROWS, 2 * ROWS), self.band * 2 * ROWS)
                self.acc_ref[to, :] += self.product(jnp.concatenate(lhs, axis=1), jnp.concatenate(hot, axis=1))
            return 0

        lax.fori_loop(0, passes, one_pass, 0)

    def add_rows(self, index, values, first, rows):
        lhs, hot = [], []
        for t in range(values.shape[1] // LANES):
            lanes = slice(t * LANES, (t + 1) * LANES)
            at = jnp.broadcast_to(index[:, lanes], self.pair)
            lhs.append(self.masked(at >> self.bits, self.two_parts(values[:, lanes]), rows))
            hot.append(self.hot_rows(at))
        to = slice(first * 2 * ROWS, (first + rows) * 2 * ROWS)
        self.acc_ref[to, :] += self.product(jnp.concatenate(lhs, axis=1), jnp.concatenate(hot, axis=1))

    def result(self, h):
        at = h * 2 * ROWS
        return self.acc_ref[at : at + ROWS] + self.acc_ref[at + ROWS : at + 2 * ROWS]


def cells_kernel(z, multiply, table_ref, index_ref, corner_ref, *refs):
    if multiply:
        uw_ref, stiffness_ref, diag_ref, image_ref, send_a_ref, send_b_ref, k_high_ref, k_low_ref, *refs = refs
        e_ref, k_ref, acc_ref = refs
        k_ref[...] = jnp.zeros_like(k_ref)
        k_ref[: z.elem, : z.elem] = stiffness_ref[...]
        k_high_ref[...], k_low_ref[...] = split(k_ref[...])
        stiffness_product(k_high_ref, k_low_ref, uw_ref, e_ref)
    else:
        e_ref, image_ref, send_a_ref, send_b_ref, acc_ref = refs
    scatter = Scatter(z, BITS, table_ref, index_ref, corner_ref, acc_ref)
    scatter.start([(c, e_ref[c * ROWS : (c + 1) * ROWS, :]) for c in range(z.slots)])

    def some_cells(g, _):
        cells = [g * z.many + i for i in range(z.many)]

        def value_of(i, t):
            rows = pl.ds(pl.multiple_of(cells[i] * ROWS, ROWS), ROWS)
            return e_ref[rows, t * LANES : (t + 1) * LANES]

        scatter.add(cells, value_of)
        return 0

    lax.fori_loop(0, z.slots // z.many, some_cells, 0)
    for h in range(scatter.groups):
        image_ref[:, h * WIDE : (h + 1) * WIDE] = scatter.result(h)
    even = table_ref[0, z.position] % 2 == 0
    ends = [slice(0, 2 * z.rim), slice(z.window - 2 * z.rim, z.window)]
    for source_ref, rows in ((image_ref, slice(0, ROWS)),) + (((diag_ref, slice(ROWS, ROWS + 2)),) if multiply else ()):
        low_rim, high_rim = (source_ref[:, end] for end in ends)
        send_a_ref[rows, :] = jnp.where(even, high_rim, low_rim)
        send_b_ref[rows, :] = jnp.where(even, low_rim, high_rim)


def support_kernel(
    z, last, table_ref, sums_ref, coupling_ref, index_ref, corner_ref, pj_ref, ext_a_ref, ext_b_ref,
    cells_ref, *refs,
):
    if last:
        image_ref, dots_ref, support_ref, nodes_ref, acc_ref = refs
    else:
        image_ref, support_ref, nodes_ref, acc_ref = refs
    position = table_ref[0, z.position]
    parts = [sums_ref[:, k, :] for k in range(3)]
    coupling = coupling_ref[:, 3, :]
    wanted = pltpu.roll(parts[0], z.devices - 1, 0) + parts[1] + pltpu.roll(parts[2], 1, 0)
    block = iota((z.devices, LANES), 0)
    if not last:
        near = iota((ROWS, LANES), 0)

        def nearby(values):
            rows = [jnp.sum(jnp.where(block == position - 2 + k, values, 0.0), axis=0, keepdims=True) for k in range(5)]
            return functools.reduce(
                jnp.add, [jnp.where(near == k, jnp.broadcast_to(row, near.shape), 0.0) for k, row in enumerate(rows)]
            )

        wanted, coupling = nearby(wanted), nearby(coupling)
        block = near + (position - 2)
    shape = wanted.shape
    lane = iota(shape, 1)
    term = jnp.zeros(shape, F32)
    for j in range(z.channels):
        matrix = lane_gather(coupling, lane // ROWS * ROWS + j)
        vector = lane_gather(wanted, lane // z.pairs * z.pairs + j * ROWS + lane % ROWS)
        term = term + matrix * vector
    if last:
        energy = jnp.sum(term * wanted, axis=0, keepdims=True)
        energy = jnp.broadcast_to(energy, (ROWS, LANES))
        step = ROWS
        while step < LANES:
            energy = energy + pltpu.roll(energy, step, 1)
            step *= 2
        line = iota((1, LANES), 1)
        dots_ref[...] = jnp.sum(sums_ref[:, 3, :], axis=0, keepdims=True) + jnp.where(
            line // ROWS == 3, energy[0:1], 0.0
        )
    small_lane, small_row = iota((ROWS, LANES), 1), iota((ROWS, LANES), 0)

    def values(facts, projectors):
        spread = []
        for s, (owner, local, alive) in enumerate(facts):
            mine = jnp.sum(jnp.where(block == owner, term, 0.0), axis=0, keepdims=True)
            got = lane_gather(
                jnp.broadcast_to(mine, (ROWS, LANES)), local * z.pairs + small_lane % ROWS * ROWS + small_row
            )
            spread.append(jnp.where((small_lane // ROWS == s) & alive, got, 0.0)[:, : z.entries * ROWS])
        return jnp.dot(
            jnp.concatenate(spread, axis=0), projectors, precision=HIGHEST, preferred_element_type=F32
        )

    count = z.entries * ROWS
    support_ref[:count, :] = values([entry_facts(z, table_ref, s) for s in range(z.entries)], pj_ref[...])
    used = slice(0, z.rim_row)
    for side, ext in enumerate(sides(position, ext_a_ref[used, :], ext_b_ref[used, :])):
        nodes = ext[z.index_row :].astype(jnp.int32)
        facts = []
        for s in range(z.entries):
            fact = [jnp.broadcast_to(nodes[s : s + 1, z.elem + k : z.elem + k + 1], (1, LANES)) for k in range(3)]
            facts.append((fact[0], fact[1], fact[2] > 0))
        projectors = jnp.where(iota((z.index_row, z.width), 1) < z.elem, ext[: z.index_row], 0.0)
        support_ref[(side + 1) * count : (side + 2) * count, :] = values(facts, projectors)
        nodes_ref[side] = nodes
    scatter = Scatter(z, NARROW, table_ref, index_ref, corner_ref, acc_ref)
    cells = [table_ref[0, z.cell + s] for s in range(z.entries)]
    blocks = [support_ref[s * ROWS : (s + 1) * ROWS, :] for s in range(3 * z.entries)]
    scatter.start(list(zip(cells, blocks)), blocks[z.entries :])
    for first in range(0, z.entries, z.together):
        some = cells[first : first + z.together]

        def value_of(i, t):
            s = first + i
            return support_ref[s * ROWS : (s + 1) * ROWS, t * LANES : (t + 1) * LANES]

        scatter.add(some, value_of)
    shared = 2 * z.rim // scatter.wide
    place = iota((ROWS, z.width), 1)
    middle = (place > 0) & (place < z.elem - 1)
    for side, (first, offset) in enumerate(((0, z.window - 2 * z.rim), (scatter.groups - shared, 0))):
        for s in range(0, z.entries, BESIDE):
            some = range(s, s + BESIDE)
            base = (side + 1) * z.entries
            value = [jnp.where(middle, support_ref[(base + i) * ROWS : (base + i + 1) * ROWS, :], 0.0) for i in some]
            index = [nodes_ref[side, i : i + 1, :] - offset for i in some]
            scatter.add_rows(jnp.concatenate(index, axis=1), jnp.concatenate(value, axis=1), first, shared)
    for h in range(scatter.groups):
        at = slice(h * scatter.wide, (h + 1) * scatter.wide)
        image_ref[:, at] = cells_ref[:, at] + scatter.result(h)


def last_kernel(
    z, rhs_ref, p_ref, diag_ref, shift_ref, y_ref, q_ref, image_ref, dots_ref, halo_a_ref, halo_b_ref,
    solution_hbm, residual_hbm, solution_ref, residual_ref, sems,
):
    lane, row = iota((ROWS, LANES), 1), iota((ROWS, LANES), 0)
    line = jnp.broadcast_to(dots_ref[...], (ROWS, LANES))

    def column(k):
        return jnp.sum(jnp.where(lane == k * ROWS + row, line, 0.0), axis=1, keepdims=True)

    gamma, py, qy, qq = (column(k) for k in range(4))
    alpha = gamma / py
    fresh = gamma - 2.0 * alpha * py + alpha * alpha * qy
    beta = fresh / gamma
    more = 1.0 + beta
    step = fresh / (more * more * py - 2.0 * more * alpha * qy + alpha * alpha * qq)
    even = shift_ref[ROWS:, :1] > 0.5
    a, b = halo_a_ref[...], halo_b_ref[...]
    left, right = jnp.where(even, b, a)[:, z.rim :], jnp.where(even, a, b)[:, : z.rim]
    size = z.nodes // z.pieces
    copies = []
    for k in range(z.pieces):
        at, own = slice(k * size, (k + 1) * size), slice(z.rim + k * size, z.rim + (k + 1) * size)
        p, q, y = p_ref[:, own], q_ref[:, own], y_ref[:, own]
        second = image_ref[:, own] + (diag_ref[1:2, own] + shift_ref[:ROWS, :1]) * q
        search = (p - alpha * q) + beta * p
        solution_ref[:, at] = alpha * p + step * search
        residual_ref[:, at] = (rhs_ref[:, at] - alpha * y) - step * (more * y - alpha * second)
        if k == 0:
            residual_ref[:, : z.rim] += step * alpha * left
        if k == z.pieces - 1:
            residual_ref[:, z.nodes - z.rim :] += step * alpha * right
        for n, (source, to) in enumerate(((solution_ref, solution_hbm), (residual_ref, residual_hbm))):
            part = pl.ds(k * size, size)
            copies.append(pltpu.make_async_copy(source.at[:, part], to.at[:, part], sems.at[2 * k + n]))
            copies[-1].start()
    for copy in copies:
        copy.wait()


def on_device(
    rhs, potential, precond, shift, stiffness, cell_scale, conn, cell_count, projector, support_cell, support_atom,
    support_count, atom_matrix,
):
    count = lax.axis_size("dom")
    z = Sizes(count, rhs, conn, projector, atom_matrix)
    position = lax.axis_index("dom")
    pos = position.astype(jnp.int32).reshape(1)
    near = [(i, i ^ 1) for i in range(count)]
    far = [(i, j) for i in range(1, count - 1) for j in [i + 1 if i % 2 else i - 1]]

    def exchange(a, b):
        return lax.ppermute(a, "dom", near), lax.ppermute(b, "dom", far)

    def call(kernel, outs, scratch, scalars, *args, in_hbm=(), by_hand=False):
        space = pltpu.HBM if by_hand else pltpu.VMEM
        args = [pltpu.with_memory_space_constraint(x, space) for x in args]
        return pl.pallas_call(
            kernel,
            out_shape=[
                jax.ShapeDtypeStruct(s, d) if i in in_hbm else pltpu.VMEM(s, d) for i, (s, d) in enumerate(outs)
            ],
            in_specs=[SMEM] * len(scalars) + [pl.BlockSpec(memory_space=space)] * len(args),
            out_specs=[VMEM] * len(outs),
            scratch_shapes=[pltpu.VMEM(*s) if isinstance(s, tuple) else s for s in scratch],
            compiler_params=pltpu.CompilerParams(vmem_limit_bytes=16 * 1024 * 1024),
        )(*scalars, *args)

    flat_projector = projector.reshape(z.entries * z.channels, z.elem)
    cells = (z.slots * ROWS, z.width)
    window, reach, own = (z.vectors, z.window), (z.vectors, z.reach), (z.vectors, z.nodes)
    message = (z.devices, 4, LANES)
    square, entries = (z.width, z.width), (z.entries * ROWS, z.width)
    rim, more_rim = (z.vectors, 2 * z.rim), (z.vectors + 2, 2 * z.rim)
    acc = acc_shape(z, BITS)
    support_scratch = [
        ((3 * z.entries * ROWS, z.width), F32), ((2, z.rim_row - z.index_row, z.width), jnp.int32),
        (acc_shape(z, NARROW), F32),
    ]

    precond_lines = precond.reshape(-1, LANES)
    tile = (ROWS, LANES)
    first_message = (z.message, z.width)
    send_a, send_b, shift_tile = call(
            functools.partial(start_kernel, z),
            [(first_message, F32), (first_message, F32), ((2 * ROWS, LANES), F32)],
            [((2, z.vectors, z.rim), F32), ((2, z.rim // LANES, LANES), F32), (conn.shape, jnp.int32),
             (flat_projector.shape, F32), pltpu.SMEM(support_cell.shape, jnp.int32),
             pltpu.SMEM(support_atom.shape, jnp.int32), pltpu.SMEM(support_count.shape, jnp.int32),
             pltpu.SMEM(shift.shape, F32), pltpu.SemaphoreType.DMA((10,))],
            (pos,),
            support_cell, support_atom, support_count, shift, rhs, precond_lines, conn, flat_projector, by_hand=True,
    )
    ext = exchange(send_a, send_b)
    index, corner, table, weight = call(
        functools.partial(prepare_kernel, z),
        [((z.slots, 1, z.width), jnp.int32), ((1, LANES), jnp.int32), ((1, LANES), jnp.int32),
         ((z.slots * ROWS, LANES), F32)],
        [],
        (pos, cell_count, cell_scale, support_cell, support_atom, support_count),
        conn,
    )
    p, gamma, diag = call(
        functools.partial(own_kernel, z),
        [(reach, F32), ((1, LANES), F32), ((2, z.window), F32)],
        [],
        (),
        rhs, precond_lines, potential.reshape(-1, LANES),
    )
    (u,) = call(functools.partial(first_window_kernel, z), [(cells, F32)], [], (table,), p, index)
    p, sums, uw, pj, beside = call(
        functools.partial(first_kernel, z),
        [(reach, F32), (message, F32), (cells, F32), (entries, F32), ((1, LANES), jnp.int32)],
        [(cells, F32)],
        (table,),
        p, u, *ext, index, corner, weight, flat_projector, atom_matrix,
    )
    coupled = lax.all_to_all(sums, "dom", 0, 0)
    image, send_a, send_b, k_high, k_low = call(
        functools.partial(cells_kernel, z, True),
        [(window, F32), (more_rim, F32), (more_rim, F32), (square, BF16), (square, BF16)],
        [(cells, F32), (square, F32), (acc, F32)],
        (table,),
        index, corner, uw, stiffness, diag,
    )
    halo = exchange(send_a, send_b)
    (image,) = call(
        functools.partial(support_kernel, z, False),
        [(window, F32)],
        support_scratch,
        (table,),
        coupled, coupled, index, beside, pj, *ext, image,
    )
    y, q, sums, e = call(
        functools.partial(second_kernel, z),
        [(window, F32), (reach, F32), (message, F32), (cells, F32)],
        [((2, z.window), F32), (cells, F32), (cells, F32), (acc, BF16)],
        (table,),
        image, p, diag, shift_tile, gamma, *halo, index, corner, weight, k_high, k_low, pj,
    )
    totals = lax.all_to_all(sums, "dom", 0, 0)
    image, send_a, send_b = call(
        functools.partial(cells_kernel, z, False), [(window, F32), (rim, F32), (rim, F32)], [(acc, F32)], (table,),
        index, corner, e,
    )
    halo = exchange(send_a, send_b)
    image, dots = call(
        functools.partial(support_kernel, z, True),
        [(window, F32), ((1, LANES), F32)],
        support_scratch,
        (table,),
        totals, coupled, index, beside, pj, *ext, image,
    )
    values = rhs, p, diag, shift_tile, y, q, image, dots, *halo
    return tuple(
        pl.pallas_call(
            functools.partial(last_kernel, z),
            out_shape=[jax.ShapeDtypeStruct(own, F32)] * 2,
            in_specs=[VMEM] * len(values),
            out_specs=[pl.BlockSpec(memory_space=pl.ANY)] * 2,
            scratch_shapes=[pltpu.VMEM(own, F32)] * 2 + [pltpu.SemaphoreType.DMA((2 * z.pieces,))],
            compiler_params=pltpu.CompilerParams(vmem_limit_bytes=16 * 1024 * 1024),
        )(*[pltpu.with_memory_space_constraint(x, pltpu.VMEM) for x in values])
    )


def solution(mesh):
    placed = (
        P(None, "dom"),
        P("dom"),
        P("dom"),
        P(),
        P(),
        P("dom"),
        P("dom", None),
        P(),
        P("dom", None, None),
        P("dom"),
        P("dom"),
        P(),
        P("dom", None, None),
    )
    return jax.shard_map(
        on_device,
        mesh=mesh,
        in_specs=placed,
        out_specs=(P(None, "dom"), P(None, "dom")),
        check_vma=False,
    )
```

```python
import functools

import jax
import jax.numpy as jnp
from jax import lax
from jax.experimental import pallas as pl
from jax.experimental.pallas import tpu as pltpu
from jax.sharding import PartitionSpec as P

LANES = 128
ROWS = 8
BITS = 7
WIDE = 1 << BITS
NARROW = 7
CHAINS = 4
SPAN = 14
BAND = 14
BESIDE = 4
TOGETHER = 8
MANY = 32
F32 = jnp.float32
BF16 = jnp.bfloat16
HIGHEST = lax.Precision.HIGHEST
NT = (((1,), (1,)), ((), ()))
VMEM = pl.BlockSpec(memory_space=pltpu.VMEM)
SMEM = pl.BlockSpec(memory_space=pltpu.SMEM)


def round_up(value, step):
    return -(-value // step) * step


class Sizes:
    def __init__(self, count, rhs, conn, projector, atom_matrix):
        self.devices = count
        self.vectors, self.nodes = rhs.shape
        self.slots, self.elem = conn.shape
        self.entries, self.channels = projector.shape[:2]
        self.owned = atom_matrix.shape[0]
        self.ghost = self.nodes // 16
        self.rim = round_up(self.ghost, 2 * LANES)
        self.shift = self.rim - self.ghost
        self.window = self.nodes + 2 * self.rim
        self.width = round_up(self.elem, LANES)
        self.tiles = self.width // LANES
        self.pairs = self.channels * self.vectors
        self.pieces = 4 if self.nodes % (4 * LANES) == 0 and self.nodes // 4 >= self.rim else 1
        self.low, self.high, self.list = 0, self.slots, 2 * self.slots
        self.cell = 3 * self.slots
        self.owner, self.local = self.cell + self.entries, self.cell + 2 * self.entries
        self.position = self.cell + 3 * self.entries
        self.beside = 2 * self.slots
        assert self.position + 1 < LANES and self.beside + 4 * self.entries <= LANES
        self.reach = self.window + SPAN * LANES
        self.index_row = self.entries * self.channels
        self.rim_row = self.index_row + round_up(self.entries, ROWS)
        self.rim_pieces = -(-self.rim // self.width)
        self.message = self.rim_row + self.rim_pieces * ROWS
        assert self.elem + 3 <= self.width and self.entries % BESIDE == 0
        self.together = TOGETHER if self.slots % TOGETHER == 0 else 1
        self.many = MANY if self.slots % MANY == 0 else 1
        assert self.vectors == ROWS and self.channels == ROWS and 2 * self.slots <= LANES
        assert self.nodes % WIDE == 0 and self.owned * self.pairs == LANES


def lane_gather(values, index):
    return jnp.take_along_axis(values, index, axis=1, mode="promise_in_bounds")


def iota(shape, dim):
    return lax.broadcasted_iota(jnp.int32, shape, dim)


def split(values):
    high = values.astype(BF16)
    return high, (values - high.astype(F32)).astype(BF16)


def lanes_by_vector(z, values):
    total = jnp.sum(values, axis=1, keepdims=True)
    spread = jnp.broadcast_to(total, (ROWS, LANES))
    return jnp.sum(jnp.where(iota((ROWS, LANES), 1) == iota((ROWS, LANES), 0), spread, 0.0), axis=0, keepdims=True)


def prepare_kernel(
    z, pos_ref, count_ref, scale_ref, cell_ref, atom_ref, scount_ref, conn_ref,
    index_ref, corner_ref, table_ref, weight_ref,
):
    position = pos_ref[0]
    line = iota((1, LANES), 1)
    corner = jnp.zeros((1, LANES), jnp.int32)
    index_ref[...] = jnp.zeros_like(index_ref)
    live = count_ref[position]
    for c in range(z.slots):
        row = conn_ref[c : c + 1, :] + z.shift
        index_ref[c, :, : z.elem] = row
        corner = jnp.where(line == c, row[:, :1], corner)
        corner = jnp.where(line == z.slots + c, row[:, z.elem - 1 :], corner)
        weight = jnp.where(c < live, scale_ref[c], 0.0)
        weight_ref[c * ROWS : (c + 1) * ROWS, :] = jnp.zeros((ROWS, LANES), F32) + weight
    corner_ref[...] = corner
    nodes = (conn_ref[...] + z.shift).astype(F32)
    place = iota(nodes.shape, 1)
    middle = (place > 0) & (place < z.elem - 1)
    low = jnp.min(jnp.where(middle, nodes, 1.0 * z.window), axis=1, keepdims=True)
    high = jnp.max(jnp.where(middle, nodes, 0.0), axis=1, keepdims=True)
    lane, cell = iota((z.slots, LANES), 1), iota((z.slots, LANES), 0)

    def as_row(column, first=0):
        return jnp.sum(jnp.where(lane == cell + first, column, 0.0), axis=0, keepdims=True)

    good = jnp.where((low >= z.rim) & (high < z.window - z.rim), 1.0, 0.0)
    good = jnp.broadcast_to(good, (z.slots, LANES))
    number = cell.astype(F32)
    before = jnp.sum(jnp.where(lane < cell, as_row(good), 0.0), axis=1, keepdims=True)
    at = jnp.where(good > 0.5, before, z.slots - 1.0 - (number - before))
    listed = jnp.where(lane.astype(F32) == at + z.list, number + z.slots * good, 0.0)
    table = as_row(low, z.low) + as_row(high, z.high) + jnp.sum(listed, axis=0, keepdims=True)
    table = table.astype(jnp.int32)
    for s in range(z.entries):
        atom = atom_ref[s]
        owner = atom // z.owned
        for first, fact in ((z.cell, cell_ref[s]), (z.owner, owner), (z.local, atom - owner * z.owned)):
            table = jnp.where(line == first + s, fact, table)
    table = jnp.where(line == z.position, position, table)
    table_ref[...] = jnp.where(line == z.position + 1, scount_ref[position], table)


def start_kernel(
    z, pos_ref, cell_hbm, atom_hbm, scount_hbm, shift_hbm, rhs_ref, precond_ref, conn_ref, projector_ref,
    send_a_ref, send_b_ref, shift_tile_ref, rhs_rim, precond_rim, conn_all, projector_all, cell_ref, atom_ref,
    scount_ref, shift_ref, sems,
):
    lines = z.rim // LANES
    moves = [
        (cell_hbm, cell_ref), (atom_hbm, atom_ref), (scount_hbm, scount_ref), (shift_hbm, shift_ref),
        (conn_ref, conn_all), (projector_ref, projector_all),
    ]
    for k, first in enumerate((0, z.nodes - z.rim)):
        moves.append((rhs_ref.at[:, pl.ds(first, z.rim)], rhs_rim.at[k]))
        moves.append((precond_ref.at[pl.ds(first // LANES, lines), :], precond_rim.at[k]))
    copies = [pltpu.make_async_copy(source, to, sems.at[k]) for k, (source, to) in enumerate(moves)]
    for copy in copies:
        copy.start()
    for copy in copies:
        copy.wait()
    row = iota((ROWS, LANES), 0)
    tile = jnp.zeros((ROWS, LANES), F32)
    for v in range(z.vectors):
        tile = jnp.where(row == v, shift_ref[v], tile)
    shift_tile_ref[:ROWS, :] = tile
    shift_tile_ref[ROWS:, :] = jnp.zeros((ROWS, LANES), F32) + jnp.where(pos_ref[0] % 2 == 0, 1.0, 0.0)
    head, tail = (
        jnp.concatenate(
            [
                rhs_rim[k, :, i * LANES : (i + 1) * LANES] * precond_rim[k, i : i + 1, :]
                for i in range(lines)
            ],
            axis=1,
        )
        for k in range(2)
    )
    even = pos_ref[0] % 2 == 0
    sides = jnp.where(even, tail, head), jnp.where(even, head, tail)
    nodes = (conn_all[...] + z.shift).astype(F32)
    cell = iota(nodes.shape, 0)
    entry = iota((z.rim_row - z.index_row, z.width), 0)
    place = iota((z.rim_row - z.index_row, z.width), 1)
    rows = jnp.zeros((z.rim_row - z.index_row, z.width), F32)
    for s in range(z.entries):
        row = jnp.sum(jnp.where(cell == cell_ref[s], nodes, 0.0), axis=0, keepdims=True)
        row = jnp.concatenate([row, jnp.zeros((1, z.width - z.elem), F32)], axis=1)
        owner = atom_ref[s] // z.owned
        facts = owner, atom_ref[s] - owner * z.owned, (s < scount_ref[pos_ref[0]]).astype(jnp.int32)
        rows = jnp.where(entry == s, row, rows)
        for k, fact in enumerate(facts):
            rows = jnp.where((entry == s) & (place == z.elem + k), fact.astype(F32), rows)
    for ref, side in zip((send_a_ref, send_b_ref), sides):
        ref[...] = jnp.zeros_like(ref)
        ref[: z.index_row, : z.elem] = projector_all[...]
        ref[z.index_row : z.rim_row, :] = rows
        for k in range(z.rim_pieces):
            piece = side[:, k * z.width : min((k + 1) * z.width, z.rim)]
            ref[z.rim_row + k * ROWS : z.rim_row + (k + 1) * ROWS, : piece.shape[1]] = piece


def own_kernel(
    z, rhs_ref, precond_ref, potential_ref, p_ref, gamma_ref, diag_ref,
):
    diag_ref[...] = jnp.zeros_like(diag_ref)
    gamma = jnp.zeros((ROWS, LANES), F32)
    for i in range(z.nodes // LANES):
        at = slice(i * LANES, (i + 1) * LANES)
        to = slice(z.rim + i * LANES, z.rim + (i + 1) * LANES)
        value = rhs_ref[:, at]
        scale = precond_ref[i : i + 1, :]
        product = value * scale
        p_ref[:, to] = product
        gamma = gamma + product * value
        diag_ref[0:1, to] = scale
        diag_ref[1:2, to] = potential_ref[i : i + 1, :]
    p_ref[:, z.window :] = jnp.zeros((ROWS, z.reach - z.window), F32)
    gamma_ref[...] = lanes_by_vector(z, gamma)


def full_groups(z, table_ref):
    ends = [table_ref[0, z.list + g * z.together + z.together - 1] for g in range(z.slots // z.together)]
    return functools.reduce(jnp.add, [(end >= z.slots).astype(jnp.int32) for end in ends])


def split_window(z, window_ref, parts_ref):
    count = z.window // WIDE
    for h in range(count):
        value = window_ref[:, h * WIDE : (h + 1) * WIDE]
        rounded = value.astype(BF16).astype(F32)
        both = jnp.concatenate([rounded, value - rounded], axis=0).astype(BF16)
        parts_ref[h * 2 * ROWS : (h + 1) * 2 * ROWS, :] = both
    parts_ref[count * 2 * ROWS :, :] = jnp.zeros((BAND * 2 * ROWS, WIDE), BF16)


def gather_middle(z, groups, listed, table_ref, index_ref, window_ref, u_ref, parts_ref=None):
    total = z.window // LANES
    tile = (ROWS, LANES)
    pair = (2 * ROWS, LANES)
    sub = iota(pair, 0)
    lows = [(sub + n * 2 * ROWS).astype(jnp.int16) for n in range(WIDE // (2 * ROWS))]
    one, none = jnp.ones(pair, BF16), jnp.zeros(pair, BF16)

    def product_tile(c, k, t):
        start = jnp.minimum((table_ref[0, z.low + c] >> BITS) + k * BAND, z.window // WIDE)
        index = index_ref[c, :, t * LANES : (t + 1) * LANES]
        low = (jnp.broadcast_to(index, pair) & (WIDE - 1)).astype(jnp.int16)
        hot = jnp.concatenate([jnp.where(low == n, one, none) for n in lows], axis=0)
        rows = pl.ds(pl.multiple_of(start * 2 * ROWS, 2 * ROWS), BAND * 2 * ROWS)
        got = jnp.dot(parts_ref[rows, :], hot, preferred_element_type=F32)
        high = (jnp.broadcast_to(index, tile) >> BITS) - start
        value = jnp.zeros(tile, F32)
        for h in range(BAND):
            at = h * 2 * ROWS
            value = jnp.where(high == h, got[at : at + ROWS] + got[at + ROWS : at + 2 * ROWS], value)
        return value

    size = z.together if listed else z.many

    def some_cells(g, _):
        cells = [g * size + i for i in range(size)]
        if listed:
            cells = [table_ref[0, z.list + c] for c in cells]
            cells = [jnp.where(c >= z.slots, c - z.slots, c) for c in cells]
        starts = [table_ref[0, z.low + c] >> 7 for c in cells]
        ends = [table_ref[0, z.high + c] >> 7 for c in cells]
        passes = functools.reduce(jnp.maximum, [(e - s) // SPAN + 1 for s, e in zip(starts, ends)])

        def one_pass(k, values):
            values = list(values)
            for i, c in enumerate(cells):
                start = jnp.minimum(starts[i] + k * SPAN, total)
                for t in range(z.tiles):
                    if parts_ref is not None and t >= z.tiles - 2:
                        values[i * z.tiles + t] += product_tile(c, k, t)
                        continue
                    index = jnp.broadcast_to(index_ref[c, :, t * LANES : (t + 1) * LANES], tile)
                    low, high = index & (LANES - 1), (index >> 7) - start
                    value = values[i * z.tiles + t]
                    for h in range(SPAN):
                        at = pl.ds(pl.multiple_of((start + h) * LANES, LANES), LANES)
                        value = jnp.where(high == h, lane_gather(window_ref[:, at], low), value)
                    values[i * z.tiles + t] = value
            return tuple(values)

        values = lax.fori_loop(0, passes, one_pass, (jnp.zeros(tile, F32),) * (size * z.tiles))
        for i, c in enumerate(cells):
            rows = pl.ds(pl.multiple_of(c * ROWS, ROWS), ROWS)
            for t in range(z.tiles):
                u_ref[rows, t * LANES : (t + 1) * LANES] = values[i * z.tiles + t]
        return 0

    lax.fori_loop(*groups, some_cells, 0)


def gather_corners(z, corner_ref, window_ref, weight_ref, u_ref, uw_ref):
    tile = (ROWS, LANES)
    corner = jnp.broadcast_to(corner_ref[...], tile)
    low, high = corner & (LANES - 1), corner >> 7
    chains = [jnp.zeros(tile, F32)] * CHAINS
    for h in range(z.window // LANES):
        got = lane_gather(window_ref[:, h * LANES : (h + 1) * LANES], low)
        chains[h % CHAINS] = jnp.where(high == h, got, chains[h % CHAINS])
    corners = functools.reduce(jnp.add, chains)
    lane = iota(tile, 1)
    last = (z.elem - 1) % LANES
    for c in range(z.slots):
        rows = slice(c * ROWS, (c + 1) * ROWS)
        weight = weight_ref[rows, :]
        for t in range(z.tiles):
            lanes = slice(t * LANES, (t + 1) * LANES)
            value = u_ref[rows, lanes]
            if t == 0:
                value = jnp.where(lane == 0, corners[:, c : c + 1], value)
            if t == z.tiles - 1:
                value = jnp.where(lane == last, corners[:, z.slots + c : z.slots + c + 1], value)
            u_ref[rows, lanes] = value
            uw_ref[rows, lanes] = value * weight


def stiffness_product(k_high_ref, k_low_ref, uw_ref, e_ref):
    k_high, k_low = k_high_ref[...], k_low_ref[...]
    u_high, u_low = split(uw_ref[...])
    dot = functools.partial(lax.dot_general, dimension_numbers=NT, preferred_element_type=F32)
    e_ref[...] = dot(u_high, k_high) + (dot(u_high, k_low) + dot(u_low, k_high))


def entry_facts(z, table_ref, s):
    return table_ref[0, z.owner + s], table_ref[0, z.local + s], s < table_ref[0, z.position + 1]


def contributions(z, table_ref, pj_ref, u_ref):
    values = [u_ref[pl.ds(pl.multiple_of(table_ref[0, z.cell + s] * ROWS, ROWS), ROWS), :] for s in range(z.entries)]
    sums = lax.dot_general(
        pj_ref[...], jnp.concatenate(values, axis=0), NT, precision=HIGHEST, preferred_element_type=F32
    )
    sums = jnp.concatenate([sums, jnp.zeros((sums.shape[0], LANES - sums.shape[1]), F32)], axis=1)
    lane, row = iota((ROWS, LANES), 1), iota((ROWS, LANES), 0)
    position = table_ref[0, z.position]
    parts = [jnp.zeros((ROWS, LANES), F32)] * 3
    for s in range(z.entries):
        owner, local, alive = entry_facts(z, table_ref, s)
        got = lane_gather(sums[s * ROWS : (s + 1) * ROWS], s * ROWS + lane % ROWS)
        here = (lane // ROWS % ROWS == row) & (lane // z.pairs == local) & alive
        for k in range(3):
            parts[k] = parts[k] + jnp.where(here & (owner == position - 1 + k), got, 0.0)
    return [jnp.sum(part, axis=0, keepdims=True) for part in parts]


def sides(position, near, far):
    even = position % 2 == 0
    return jnp.where(even, far, near), jnp.where(even, near, far)


def first_window_kernel(z, table_ref, p_ref, index_ref, u_ref):
    groups = 0, full_groups(z, table_ref)
    gather_middle(z, groups, True, table_ref, index_ref, p_ref, u_ref)


def first_kernel(
    z, table_ref, p_in_ref, u_in_ref, halo_a_ref, halo_b_ref, index_ref, corner_ref, weight_ref,
    projector_ref, coupling_ref, p_ref, out_ref, uw_ref, pj_ref, beside_ref, u_ref, parts_ref,
):
    rows = slice(z.index_row, z.index_row + z.entries)
    line = iota((1, LANES), 1)
    left, right = sides(table_ref[0, z.position], halo_a_ref[rows, :], halo_b_ref[rows, :])
    beside = corner_ref[...]
    for k, (side, move) in enumerate(((left, -z.nodes), (right, z.nodes))):
        side = side.astype(jnp.int32) + move
        for s in range(z.entries):
            lane = z.beside + 2 * z.entries * k + s
            beside = jnp.where(line == lane, side[s : s + 1, :1], beside)
            beside = jnp.where(line == lane + z.entries, side[s : s + 1, z.elem - 1 : z.elem], beside)
    beside_ref[...] = beside
    own = slice(z.rim, z.rim + z.nodes)
    for k in range(z.rim_pieces):
        rows = slice(z.rim_row + k * ROWS, z.rim_row + (k + 1) * ROWS)
        at, to = k * z.width, min((k + 1) * z.width, z.rim)
        left, right = sides(table_ref[0, z.position], halo_a_ref[rows, : to - at], halo_b_ref[rows, : to - at])
        p_ref[:, at:to] = left
        p_ref[:, z.rim + z.nodes + at : z.rim + z.nodes + to] = right
    p_ref[:, own] = p_in_ref[:, own]
    p_ref[:, z.window :] = p_in_ref[:, z.window :]
    u_ref[...] = u_in_ref[...]
    pj_ref[...] = jnp.zeros_like(pj_ref)
    pj_ref[:, : z.elem] = projector_ref[...]
    groups = full_groups(z, table_ref), z.slots // z.together
    split_window(z, p_ref, parts_ref)
    gather_middle(z, groups, True, table_ref, index_ref, p_ref, u_ref, parts_ref)
    gather_corners(z, corner_ref, p_ref, weight_ref, u_ref, uw_ref)
    parts = contributions(z, table_ref, pj_ref, u_ref)
    small_lane, small_row = iota((ROWS, LANES), 1), iota((ROWS, LANES), 0)
    matrices = jnp.zeros((ROWS, LANES), F32)
    for atom in range(z.owned):
        block = jnp.concatenate([coupling_ref[atom], jnp.zeros((ROWS, LANES - z.channels), F32)], axis=1)
        got = lane_gather(block, small_lane % ROWS)
        matrices = jnp.where(small_lane // ROWS == atom * ROWS + small_row, got, matrices)
    message = jnp.concatenate(parts + [jnp.sum(matrices, axis=0, keepdims=True)], axis=0)
    for d in range(z.devices):
        out_ref[d] = message


def second_kernel(
    z, table_ref, image_ref, p_ref, diag_in_ref, shift_ref, gamma_ref, halo_a_ref, halo_b_ref,
    index_ref, corner_ref, weight_ref, k_high_ref, k_low_ref, pj_ref, y_ref, q_ref, out_ref, e_ref, diag_ref, u_ref, uw_ref,
    parts_ref,
):
    left, right = sides(table_ref[0, z.position], halo_a_ref[...], halo_b_ref[...])
    own = slice(z.rim, z.rim + z.nodes)
    diag_ref[:, own] = diag_in_ref[:, own]
    diag_ref[:, : z.rim] = left[ROWS : ROWS + 2, : z.rim]
    diag_ref[:, z.rim + z.nodes :] = right[ROWS : ROWS + 2, z.rim :]
    y_ref[...] = image_ref[...] + (diag_ref[1:2, :] + shift_ref[:ROWS, :1]) * p_ref[:, : z.window]
    y_ref[:, : 2 * z.rim] += left[:ROWS]
    y_ref[:, z.window - 2 * z.rim :] += right[:ROWS]
    q_ref[:, : z.window] = y_ref[...] * diag_ref[0:1, :]
    q_ref[:, z.window :] = jnp.zeros((ROWS, z.reach - z.window), F32)
    y, q = y_ref[:, own], q_ref[:, own]
    dots = [
        gamma_ref[...],
        lanes_by_vector(z, y * p_ref[:, own]),
        lanes_by_vector(z, y * q),
    ]
    energy = jnp.sum(q * q * (diag_ref[1:2, own] + shift_ref[:ROWS, :1]), axis=1, keepdims=True)
    groups = 0, z.slots // z.many
    split_window(z, q_ref, parts_ref)
    gather_middle(z, groups, False, table_ref, index_ref, q_ref, u_ref, parts_ref)
    gather_corners(z, corner_ref, q_ref, weight_ref, u_ref, uw_ref)
    parts = contributions(z, table_ref, pj_ref, u_ref)
    stiffness_product(k_high_ref, k_low_ref, uw_ref, e_ref)
    elements = jnp.zeros((ROWS, z.width), F32)
    for c in range(z.slots):
        rows = slice(c * ROWS, (c + 1) * ROWS)
        elements = elements + u_ref[rows, :] * e_ref[rows, :]
    energy = energy + jnp.sum(elements, axis=1, keepdims=True)
    dots.append(lanes_by_vector(z, energy))
    line = dots[0]
    for k in range(1, len(dots)):
        line = line + pltpu.roll(dots[k], k * ROWS, 1)
    message = jnp.concatenate(parts + [line], axis=0)
    for d in range(z.devices):
        out_ref[d] = message


def band_of(bits):
    return BAND if bits == BITS else SPAN


def acc_shape(z, bits):
    return ((z.window >> bits) + band_of(bits)) * 2 * ROWS, 1 << bits


class Scatter:
    def __init__(self, z, bits, table_ref, index_ref, corner_ref, acc_ref):
        self.bits, self.wide, self.band = bits, 1 << bits, band_of(bits)
        self.z, self.index_ref, self.corner_ref, self.acc_ref = z, index_ref, corner_ref, acc_ref
        self.table_ref = table_ref
        self.groups = z.window // self.wide
        self.pair = (2 * ROWS, LANES)
        sub = iota(self.pair, 0)
        self.lows = [(sub + k * 2 * ROWS).astype(jnp.int16) for k in range(self.wide // (2 * ROWS))]
        self.one, self.none = jnp.ones(self.pair, BF16), jnp.zeros(self.pair, BF16)
        self.lane = iota((ROWS, LANES), 1)
        self.end = (z.elem - 1) % LANES

    def two_parts(self, value):
        rounded = value.astype(BF16).astype(F32)
        return jnp.concatenate([rounded, value - rounded], axis=0).astype(BF16)

    def hot_rows(self, index):
        low = (index & (self.wide - 1)).astype(jnp.int16)
        return jnp.concatenate([jnp.where(low == k, self.one, self.none) for k in self.lows], axis=0)

    def masked(self, high, both, rows):
        high = high.astype(jnp.int16)
        return jnp.concatenate([jnp.where(high == jnp.int16(h), both, self.none) for h in range(rows)], axis=0)

    def product(self, lhs, hot):
        return lax.dot_general(lhs, hot, NT, preferred_element_type=F32)

    def start(self, sources, beside=()):
        z = self.z
        corners = jnp.zeros((ROWS, LANES), F32)
        at = (z.tiles - 1) * LANES + self.end
        for cell, values in sources:
            corners = corners + jnp.where(self.lane == cell, values[:, 0:1], 0.0)
            corners = corners + jnp.where(self.lane == z.slots + cell, values[:, at : at + 1], 0.0)
        for s, values in enumerate(beside):
            lane = z.beside + s + s // z.entries * z.entries
            corners = jnp.where(self.lane == lane, values[:, 0:1], corners)
            corners = jnp.where(self.lane == lane + z.entries, values[:, at : at + 1], corners)
        index = jnp.broadcast_to(self.corner_ref[...], self.pair)
        rows = self.groups * 2 * ROWS
        self.acc_ref[:rows, :] = self.product(
            self.masked(index >> self.bits, self.two_parts(corners), self.groups), self.hot_rows(index)
        )
        self.acc_ref[rows:, :] = jnp.zeros((self.band * 2 * ROWS, self.wide), F32)

    def add(self, cells, value_of):
        z = self.z
        starts = [self.table_ref[0, z.low + c] >> self.bits for c in cells]
        ends = [self.table_ref[0, z.high + c] >> self.bits for c in cells]
        passes = functools.reduce(jnp.maximum, [(e - s) // self.band + 1 for s, e in zip(starts, ends)])

        def one_pass(k, _):
            for i, c in enumerate(cells):
                start = jnp.minimum(starts[i] + k * self.band, self.groups)
                lhs, hot = [], []
                for t in range(z.tiles):
                    index = jnp.broadcast_to(self.index_ref[c, :, t * LANES : (t + 1) * LANES], self.pair)
                    value = value_of(i, t)
                    if t == 0:
                        value = jnp.where(self.lane == 0, 0.0, value)
                    if t == z.tiles - 1:
                        value = jnp.where(self.lane == self.end, 0.0, value)
                    lhs.append(self.masked((index >> self.bits) - start, self.two_parts(value), self.band))
                    hot.append(self.hot_rows(index))
                to = pl.ds(pl.multiple_of(start * 2 * ROWS, 2 * ROWS), self.band * 2 * ROWS)
                self.acc_ref[to, :] += self.product(jnp.concatenate(lhs, axis=1), jnp.concatenate(hot, axis=1))
            return 0

        lax.fori_loop(0, passes, one_pass, 0)

    def add_rows(self, index, values, first, rows):
        lhs, hot = [], []
        for t in range(values.shape[1] // LANES):
            lanes = slice(t * LANES, (t + 1) * LANES)
            at = jnp.broadcast_to(index[:, lanes], self.pair)
            lhs.append(self.masked(at >> self.bits, self.two_parts(values[:, lanes]), rows))
            hot.append(self.hot_rows(at))
        to = slice(first * 2 * ROWS, (first + rows) * 2 * ROWS)
        self.acc_ref[to, :] += self.product(jnp.concatenate(lhs, axis=1), jnp.concatenate(hot, axis=1))

    def result(self, h):
        at = h * 2 * ROWS
        return self.acc_ref[at : at + ROWS] + self.acc_ref[at + ROWS : at + 2 * ROWS]


def cells_kernel(z, multiply, table_ref, index_ref, corner_ref, *refs):
    if multiply:
        uw_ref, stiffness_ref, diag_ref, image_ref, send_a_ref, send_b_ref, k_high_ref, k_low_ref, *refs = refs
        e_ref, k_ref, acc_ref = refs
        k_ref[...] = jnp.zeros_like(k_ref)
        k_ref[: z.elem, : z.elem] = stiffness_ref[...]
        k_high_ref[...], k_low_ref[...] = split(k_ref[...])
        stiffness_product(k_high_ref, k_low_ref, uw_ref, e_ref)
    else:
        e_ref, image_ref, send_a_ref, send_b_ref, acc_ref = refs
    scatter = Scatter(z, BITS, table_ref, index_ref, corner_ref, acc_ref)
    scatter.start([(c, e_ref[c * ROWS : (c + 1) * ROWS, :]) for c in range(z.slots)])

    def some_cells(g, _):
        cells = [g * z.many + i for i in range(z.many)]

        def value_of(i, t):
            rows = pl.ds(pl.multiple_of(cells[i] * ROWS, ROWS), ROWS)
            return e_ref[rows, t * LANES : (t + 1) * LANES]

        scatter.add(cells, value_of)
        return 0

    lax.fori_loop(0, z.slots // z.many, some_cells, 0)
    for h in range(scatter.groups):
        image_ref[:, h * WIDE : (h + 1) * WIDE] = scatter.result(h)
    even = table_ref[0, z.position] % 2 == 0
    ends = [slice(0, 2 * z.rim), slice(z.window - 2 * z.rim, z.window)]
    for source_ref, rows in ((image_ref, slice(0, ROWS)),) + (((diag_ref, slice(ROWS, ROWS + 2)),) if multiply else ()):
        low_rim, high_rim = (source_ref[:, end] for end in ends)
        send_a_ref[rows, :] = jnp.where(even, high_rim, low_rim)
        send_b_ref[rows, :] = jnp.where(even, low_rim, high_rim)


def support_kernel(
    z, last, table_ref, sums_ref, coupling_ref, index_ref, corner_ref, pj_ref, ext_a_ref, ext_b_ref,
    cells_ref, *refs,
):
    if last:
        image_ref, dots_ref, support_ref, nodes_ref, acc_ref = refs
    else:
        image_ref, support_ref, nodes_ref, acc_ref = refs
    position = table_ref[0, z.position]
    parts = [sums_ref[:, k, :] for k in range(3)]
    coupling = coupling_ref[:, 3, :]
    wanted = pltpu.roll(parts[0], z.devices - 1, 0) + parts[1] + pltpu.roll(parts[2], 1, 0)
    block = iota((z.devices, LANES), 0)
    if not last:
        near = iota((ROWS, LANES), 0)

        def nearby(values):
            rows = [jnp.sum(jnp.where(block == position - 2 + k, values, 0.0), axis=0, keepdims=True) for k in range(5)]
            return functools.reduce(
                jnp.add, [jnp.where(near == k, jnp.broadcast_to(row, near.shape), 0.0) for k, row in enumerate(rows)]
            )

        wanted, coupling = nearby(wanted), nearby(coupling)
        block = near + (position - 2)
    shape = wanted.shape
    lane = iota(shape, 1)
    term = jnp.zeros(shape, F32)
    for j in range(z.channels):
        matrix = lane_gather(coupling, lane // ROWS * ROWS + j)
        vector = lane_gather(wanted, lane // z.pairs * z.pairs + j * ROWS + lane % ROWS)
        term = term + matrix * vector
    if last:
        energy = jnp.sum(term * wanted, axis=0, keepdims=True)
        energy = jnp.broadcast_to(energy, (ROWS, LANES))
        step = ROWS
        while step < LANES:
            energy = energy + pltpu.roll(energy, step, 1)
            step *= 2
        line = iota((1, LANES), 1)
        dots_ref[...] = jnp.sum(sums_ref[:, 3, :], axis=0, keepdims=True) + jnp.where(
            line // ROWS == 3, energy[0:1], 0.0
        )
    small_lane, small_row = iota((ROWS, LANES), 1), iota((ROWS, LANES), 0)

    def values(facts, projectors):
        spread = []
        for s, (owner, local, alive) in enumerate(facts):
            mine = jnp.sum(jnp.where(block == owner, term, 0.0), axis=0, keepdims=True)
            got = lane_gather(
                jnp.broadcast_to(mine, (ROWS, LANES)), local * z.pairs + small_lane % ROWS * ROWS + small_row
            )
            spread.append(jnp.where((small_lane // ROWS == s) & alive, got, 0.0)[:, : z.entries * ROWS])
        return jnp.dot(
            jnp.concatenate(spread, axis=0), projectors, precision=HIGHEST, preferred_element_type=F32
        )

    count = z.entries * ROWS
    support_ref[:count, :] = values([entry_facts(z, table_ref, s) for s in range(z.entries)], pj_ref[...])
    used = slice(0, z.rim_row)
    for side, ext in enumerate(sides(position, ext_a_ref[used, :], ext_b_ref[used, :])):
        nodes = ext[z.index_row :].astype(jnp.int32)
        facts = []
        for s in range(z.entries):
            fact = [jnp.broadcast_to(nodes[s : s + 1, z.elem + k : z.elem + k + 1], (1, LANES)) for k in range(3)]
            facts.append((fact[0], fact[1], fact[2] > 0))
        projectors = jnp.where(iota((z.index_row, z.width), 1) < z.elem, ext[: z.index_row], 0.0)
        support_ref[(side + 1) * count : (side + 2) * count, :] = values(facts, projectors)
        nodes_ref[side] = nodes
    scatter = Scatter(z, NARROW, table_ref, index_ref, corner_ref, acc_ref)
    cells = [table_ref[0, z.cell + s] for s in range(z.entries)]
    blocks = [support_ref[s * ROWS : (s + 1) * ROWS, :] for s in range(3 * z.entries)]
    scatter.start(list(zip(cells, blocks)), blocks[z.entries :])
    for first in range(0, z.entries, z.together):
        some = cells[first : first + z.together]

        def value_of(i, t):
            s = first + i
            return support_ref[s * ROWS : (s + 1) * ROWS, t * LANES : (t + 1) * LANES]

        scatter.add(some, value_of)
    shared = 2 * z.rim // scatter.wide
    place = iota((ROWS, z.width), 1)
    middle = (place > 0) & (place < z.elem - 1)
    for side, (first, offset) in enumerate(((0, z.window - 2 * z.rim), (scatter.groups - shared, 0))):
        for s in range(0, z.entries, BESIDE):
            some = range(s, s + BESIDE)
            base = (side + 1) * z.entries
            value = [jnp.where(middle, support_ref[(base + i) * ROWS : (base + i + 1) * ROWS, :], 0.0) for i in some]
            index = [nodes_ref[side, i : i + 1, :] - offset for i in some]
            scatter.add_rows(jnp.concatenate(index, axis=1), jnp.concatenate(value, axis=1), first, shared)
    for h in range(scatter.groups):
        at = slice(h * scatter.wide, (h + 1) * scatter.wide)
        image_ref[:, at] = cells_ref[:, at] + scatter.result(h)


def last_kernel(
    z, rhs_ref, p_ref, diag_ref, shift_ref, y_ref, q_ref, image_ref, dots_ref, halo_a_ref, halo_b_ref,
    solution_hbm, residual_hbm, solution_ref, residual_ref, sems,
):
    lane, row = iota((ROWS, LANES), 1), iota((ROWS, LANES), 0)
    line = jnp.broadcast_to(dots_ref[...], (ROWS, LANES))

    def column(k):
        return jnp.sum(jnp.where(lane == k * ROWS + row, line, 0.0), axis=1, keepdims=True)

    gamma, py, qy, qq = (column(k) for k in range(4))
    alpha = gamma / py
    fresh = gamma - 2.0 * alpha * py + alpha * alpha * qy
    beta = fresh / gamma
    more = 1.0 + beta
    step = fresh / (more * more * py - 2.0 * more * alpha * qy + alpha * alpha * qq)
    even = shift_ref[ROWS:, :1] > 0.5
    a, b = halo_a_ref[...], halo_b_ref[...]
    left, right = jnp.where(even, b, a)[:, z.rim :], jnp.where(even, a, b)[:, : z.rim]
    size = z.nodes // z.pieces
    copies = []
    for k in range(z.pieces):
        at, own = slice(k * size, (k + 1) * size), slice(z.rim + k * size, z.rim + (k + 1) * size)
        p, q, y = p_ref[:, own], q_ref[:, own], y_ref[:, own]
        second = image_ref[:, own] + (diag_ref[1:2, own] + shift_ref[:ROWS, :1]) * q
        search = (p - alpha * q) + beta * p
        solution_ref[:, at] = alpha * p + step * search
        residual_ref[:, at] = (rhs_ref[:, at] - alpha * y) - step * (more * y - alpha * second)
        if k == 0:
            residual_ref[:, : z.rim] += step * alpha * left
        if k == z.pieces - 1:
            residual_ref[:, z.nodes - z.rim :] += step * alpha * right
        for n, (source, to) in enumerate(((solution_ref, solution_hbm), (residual_ref, residual_hbm))):
            part = pl.ds(k * size, size)
            copies.append(pltpu.make_async_copy(source.at[:, part], to.at[:, part], sems.at[2 * k + n]))
            copies[-1].start()
    for copy in copies:
        copy.wait()


def on_device(
    rhs, potential, precond, shift, stiffness, cell_scale, conn, cell_count, projector, support_cell, support_atom,
    support_count, atom_matrix,
):
    count = lax.axis_size("dom")
    z = Sizes(count, rhs, conn, projector, atom_matrix)
    position = lax.axis_index("dom")
    pos = position.astype(jnp.int32).reshape(1)
    near = [(i, i ^ 1) for i in range(count)]
    far = [(i, j) for i in range(1, count - 1) for j in [i + 1 if i % 2 else i - 1]]

    def exchange(a, b):
        return lax.ppermute(a, "dom", near), lax.ppermute(b, "dom", far)

    def call(kernel, outs, scratch, scalars, *args, in_hbm=(), by_hand=False):
        space = pltpu.HBM if by_hand else pltpu.VMEM
        args = [pltpu.with_memory_space_constraint(x, space) for x in args]
        return pl.pallas_call(
            kernel,
            out_shape=[
                jax.ShapeDtypeStruct(s, d) if i in in_hbm else pltpu.VMEM(s, d) for i, (s, d) in enumerate(outs)
            ],
            in_specs=[SMEM] * len(scalars) + [pl.BlockSpec(memory_space=space)] * len(args),
            out_specs=[VMEM] * len(outs),
            scratch_shapes=[pltpu.VMEM(*s) if isinstance(s, tuple) else s for s in scratch],
            compiler_params=pltpu.CompilerParams(vmem_limit_bytes=16 * 1024 * 1024),
        )(*scalars, *args)

    flat_projector = projector.reshape(z.entries * z.channels, z.elem)
    cells = (z.slots * ROWS, z.width)
    window, reach, own = (z.vectors, z.window), (z.vectors, z.reach), (z.vectors, z.nodes)
    message = (z.devices, 4, LANES)
    square, entries = (z.width, z.width), (z.entries * ROWS, z.width)
    rim, more_rim = (z.vectors, 2 * z.rim), (z.vectors + 2, 2 * z.rim)
    acc = acc_shape(z, BITS)
    support_scratch = [
        ((3 * z.entries * ROWS, z.width), F32), ((2, z.rim_row - z.index_row, z.width), jnp.int32),
        (acc_shape(z, NARROW), F32),
    ]

    precond_lines = precond.reshape(-1, LANES)
    tile = (ROWS, LANES)
    first_message = (z.message, z.width)
    send_a, send_b, shift_tile = call(
            functools.partial(start_kernel, z),
            [(first_message, F32), (first_message, F32), ((2 * ROWS, LANES), F32)],
            [((2, z.vectors, z.rim), F32), ((2, z.rim // LANES, LANES), F32), (conn.shape, jnp.int32),
             (flat_projector.shape, F32), pltpu.SMEM(support_cell.shape, jnp.int32),
             pltpu.SMEM(support_atom.shape, jnp.int32), pltpu.SMEM(support_count.shape, jnp.int32),
             pltpu.SMEM(shift.shape, F32), pltpu.SemaphoreType.DMA((10,))],
            (pos,),
            support_cell, support_atom, support_count, shift, rhs, precond_lines, conn, flat_projector, by_hand=True,
    )
    ext = exchange(send_a, send_b)
    index, corner, table, weight = call(
        functools.partial(prepare_kernel, z),
        [((z.slots, 1, z.width), jnp.int32), ((1, LANES), jnp.int32), ((1, LANES), jnp.int32),
         ((z.slots * ROWS, LANES), F32)],
        [],
        (pos, cell_count, cell_scale, support_cell, support_atom, support_count),
        conn,
    )
    p, gamma, diag = call(
        functools.partial(own_kernel, z),
        [(reach, F32), ((1, LANES), F32), ((2, z.window), F32)],
        [],
        (),
        rhs, precond_lines, potential.reshape(-1, LANES),
    )
    (u,) = call(functools.partial(first_window_kernel, z), [(cells, F32)], [], (table,), p, index)
    p, sums, uw, pj, beside = call(
        functools.partial(first_kernel, z),
        [(reach, F32), (message, F32), (cells, F32), (entries, F32), ((1, LANES), jnp.int32)],
        [(cells, F32), (acc, BF16)],
        (table,),
        p, u, *ext, index, corner, weight, flat_projector, atom_matrix,
    )
    coupled = lax.all_to_all(sums, "dom", 0, 0)
    image, send_a, send_b, k_high, k_low = call(
        functools.partial(cells_kernel, z, True),
        [(window, F32), (more_rim, F32), (more_rim, F32), (square, BF16), (square, BF16)],
        [(cells, F32), (square, F32), (acc, F32)],
        (table,),
        index, corner, uw, stiffness, diag,
    )
    halo = exchange(send_a, send_b)
    (image,) = call(
        functools.partial(support_kernel, z, False),
        [(window, F32)],
        support_scratch,
        (table,),
        coupled, coupled, index, beside, pj, *ext, image,
    )
    y, q, sums, e = call(
        functools.partial(second_kernel, z),
        [(window, F32), (reach, F32), (message, F32), (cells, F32)],
        [((2, z.window), F32), (cells, F32), (cells, F32), (acc, BF16)],
        (table,),
        image, p, diag, shift_tile, gamma, *halo, index, corner, weight, k_high, k_low, pj,
    )
    totals = lax.all_to_all(sums, "dom", 0, 0)
    image, send_a, send_b = call(
        functools.partial(cells_kernel, z, False), [(window, F32), (rim, F32), (rim, F32)], [(acc, F32)], (table,),
        index, corner, e,
    )
    halo = exchange(send_a, send_b)
    image, dots = call(
        functools.partial(support_kernel, z, True),
        [(window, F32), ((1, LANES), F32)],
        support_scratch,
        (table,),
        totals, coupled, index, beside, pj, *ext, image,
    )
    values = rhs, p, diag, shift_tile, y, q, image, dots, *halo
    return tuple(
        pl.pallas_call(
            functools.partial(last_kernel, z),
            out_shape=[jax.ShapeDtypeStruct(own, F32)] * 2,
            in_specs=[VMEM] * len(values),
            out_specs=[pl.BlockSpec(memory_space=pl.ANY)] * 2,
            scratch_shapes=[pltpu.VMEM(own, F32)] * 2 + [pltpu.SemaphoreType.DMA((2 * z.pieces,))],
            compiler_params=pltpu.CompilerParams(vmem_limit_bytes=16 * 1024 * 1024),
        )(*[pltpu.with_memory_space_constraint(x, pltpu.VMEM) for x in values])
    )


def solution(mesh):
    placed = (
        P(None, "dom"),
        P("dom"),
        P("dom"),
        P(),
        P(),
        P("dom"),
        P("dom", None),
        P(),
        P("dom", None, None),
        P("dom"),
        P("dom"),
        P(),
        P("dom", None, None),
    )
    return jax.shard_map(
        on_device,
        mesh=mesh,
        in_specs=placed,
        out_specs=(P(None, "dom"), P(None, "dom")),
        check_vma=False,
    )
```
